32 devices in a mesh: dp: 4 (over z), row: 4 (over y, core), col: 2 (over x).
Axes of the slice: x: 2, y: 2, z: 4, core: 2. Of those that a mesh axis runs over, the one named last changes fastest.
Arguments:
- inputs: bfloat16 [8, 1024, 768], P(('dp', 'col'), 'row'), may hold values from -6 to 6
- cotangent: bfloat16 [8, 1024, 768], P(('dp', 'col'), 'row'), may hold values from -6 to 6
- gain_attn: float32 [768], replicated, may hold values from 0.5 to 1.5
- gain_ffn: float32 [768], replicated, may hold values from 0.5 to 1.5
- attn_in: bfloat16 [3, 768, 768], P(None, None, 'row'), may hold values from -0.21875 to 0.21875
- attn_out: bfloat16 [768, 768], P('row'), may hold values from -3 to 3
- expert_gate: bfloat16 [8, 768, 2048], P('col', None, 'row'), may hold values from -0.21875 to 0.21875
- expert_up: bfloat16 [8, 768, 2048], P('col', None, 'row'), may hold values from -0.21875 to 0.21875
- expert_down: bfloat16 [8, 2048, 768], P('col', 'row'), may hold values from -0.125 to 0.125
- const_vectors: bfloat16 [2, 768], replicated, may hold values from -6 to 6
- gate_values: float32 [8, 1024, 2], P(('dp', 'col'), 'row'), may hold values from 0.25 to 1
- routes: int32 [4, 2048, 2], P('dp'), may hold values from 0 to 11, as said below
- priority: int32 [4, 2048], P('dp'), may hold values from 0 to 2047, each once within a row
- pieces: int32 [8, 1024], P(('dp', 'col')), may hold values from 0 to 2, as said below
Outputs:
- block_output: bfloat16 [8, 1024, 768], P(('dp', 'col'), 'row')
- input_grad: float32 [8, 1024, 768], P(('dp', 'col'), 'row')
- gain_attn_grad: float32 [768], replicated
- gain_ffn_grad: float32 [768], replicated
- attn_in_grad: float32 [3, 768, 768], P(None, None, 'row')
- attn_out_grad: float32 [768, 768], P('row')
- gate_weight_grad: float32 [8, 768, 2048], P('col', None, 'row')
- up_weight_grad: float32 [8, 768, 2048], P('col', None, 'row')
- down_weight_grad: float32 [8, 2048, 768], P('col', 'row')
- const_grad: float32 [2, 768], replicated
- gates_grad: float32 [8, 1024, 2], P(('dp', 'col'), 'row')
The draws below stay inside these ranges and needn't reach their ends.
Inputs may be any that keep to these rules, and one draw needn't show every extreme that they name: The two routes of a token name different experts: 0 to 7 are feed-forward experts, 8 the zero expert, 9 the copy expert, the last two the constant experts. The 256 tokens of one device (an aligned block of rows of a group) name one expert at most 88 times; in each group some feed-forward expert is named exactly 88 times in every such block. `priority`: each row is a permutation of the group's tokens; a pair of a token with a lower value takes its expert's slot first. `pieces`: 0 marks text; each positive value marks one picture piece of 256 consecutive tokens within one sequence.
All inputs are finite; a program needn't handle non-finite values.
Results may differ from the reference program's by a relative error of at most 0.015.
Values may be sent and summed in bfloat16 or wider, within the bound.
No kernel may reach another device: no remote copies, remote signals or barrier semaphores. Data moves between devices by JAX's collectives and lax.ppermute only.
A program may use at most 192 MiB of HBM per device.

```python
import math
import jax
import jax.numpy as jnp
from jax import lax

D = 768
HEADS = 12
HEAD_DIM = 64
FF = 2048
E_FFN = 8
EXPERTS = 12
PIECE = 256
TOK_DEV = 256
GROUPS = 4
SEQ = 1024
SEQS = 8
TOK_GRP = 2048
CAP = 426
MOST = 88


def shared_field(key):
    return jax.random.normal(jax.random.fold_in(key, 31), (SEQS, SEQ, D), jnp.float32)


def draw_inputs(key, part):
    return jnp.clip(shared_field(key), -6.0, 6.0).astype(jnp.bfloat16)


def draw_cotangent(key, part):
    noise_key = jax.random.fold_in(key, 37)
    noise_part = jax.random.normal(noise_key, (SEQS, SEQ, D), jnp.float32)
    mixed = 0.7 * shared_field(key) + 0.7 * noise_part
    return jnp.clip(mixed, -6.0, 6.0).astype(jnp.bfloat16)


def route_block(block_key, hot_expert):
    remaining = 2 * TOK_DEV - MOST
    base_count = remaining // (EXPERTS - 1)
    swing_size = base_count // 3
    shift_key, perm_key, flip_key = jax.random.split(block_key, 3)
    shifts = jax.random.randint(shift_key, ((EXPERTS - 2) // 2,), -swing_size, swing_size + 1)
    paired = jnp.stack([base_count + shifts, base_count - shifts], axis=1).reshape(-1)
    others = jnp.concatenate([paired, jnp.full((1,), remaining - (EXPERTS - 2) * base_count, jnp.int32)])
    expert_ids = jnp.arange(EXPERTS, dtype=jnp.int32)
    other_index = jnp.clip(expert_ids - (expert_ids > hot_expert).astype(jnp.int32), 0, EXPERTS - 2)
    counts = jnp.where(expert_ids == hot_expert, MOST, others[other_index])
    bounds = jnp.cumsum(counts)
    positions = jnp.arange(2 * TOK_DEV, dtype=jnp.int32)
    listed = jnp.sum((positions[:, None] >= bounds[None, :]).astype(jnp.int32), axis=1)
    pair_rows = jnp.stack([listed[:TOK_DEV], listed[TOK_DEV:]], axis=1)
    pair_rows = pair_rows[jax.random.permutation(perm_key, TOK_DEV)]
    flip_bits = jax.random.randint(flip_key, (TOK_DEV, 1), 0, 2)
    return jnp.where(flip_bits == 1, pair_rows[:, ::-1], pair_rows).astype(jnp.int32)


def route_group(group_key):
    hot_key, block_key = jax.random.split(group_key)
    hot_expert = jax.random.randint(hot_key, (), 0, E_FFN)
    block_keys = jax.random.split(block_key, TOK_GRP // TOK_DEV)
    blocks = jax.vmap(route_block, in_axes=(0, None))(block_keys, hot_expert)
    return blocks.reshape(TOK_GRP, 2)


def draw_routes(key, part):
    return jax.vmap(route_group)(jax.random.split(jax.random.fold_in(key, 11), GROUPS))


def draw_pieces(key, part):
    windows = SEQ // (2 * PIECE)
    present_key, offset_key = jax.random.split(jax.random.fold_in(key, 23))
    present = jax.random.randint(present_key, (SEQS, windows), 0, 4) > 0
    offsets = jax.random.randint(offset_key, (SEQS, windows), 0, PIECE + 1)
    position = jnp.arange(SEQ, dtype=jnp.int32)
    window_ids = position // (2 * PIECE)
    inside = position % (2 * PIECE)
    starts = offsets[:, window_ids]
    hit_rows = present[:, window_ids] & (inside[None, :] >= starts) & (inside[None, :] < starts + PIECE)
    return jnp.where(hit_rows, window_ids[None, :] + 1, 0).astype(jnp.int32)


def shard_levels(stream_key, dims, cuts, least, largest):
    gain, own = 1.0, jax.random.fold_in(stream_key, 6)
    for dim, shards_of in cuts:
        heights = jnp.exp(jax.random.uniform(jax.random.fold_in(own, dim), (shards_of,), jnp.float32, least / len(cuts), largest / len(cuts)))
        gain = gain * jnp.repeat(heights, dims[dim] // shards_of).reshape([-1 if axis == dim else 1 for axis in range(len(dims))])
    return gain


def centred(stream_key, extent, scale, limit, cuts=(), kind=jnp.bfloat16):
    level = shard_levels(stream_key, extent, cuts, -0.22, 0.18) if cuts else 1.0
    values = jax.random.normal(stream_key, extent, jnp.float32) * scale * level
    return jnp.minimum(jnp.maximum(values, -limit), limit).astype(kind)


def setup_inputs(seed: int = 0) -> dict:
    arg_keys = jax.random.split(jax.random.key(seed), 15)
    inputs = draw_inputs(jax.random.fold_in(arg_keys[14], 71), 0)
    cotangent = draw_cotangent(jax.random.fold_in(arg_keys[14], 71), 0)
    gain_attn = jnp.clip(1.0 + 0.1 * jax.random.normal(arg_keys[2], (D,), jnp.float32), 0.5, 1.5)
    gain_ffn = jnp.clip(1.0 + 0.1 * jax.random.normal(arg_keys[3], (D,), jnp.float32), 0.5, 1.5)
    attn_in = centred(arg_keys[4], (3, D, D), D ** -0.5, 0.21875, ((2, 4),))
    attn_out = centred(arg_keys[5], (D, D), (max(D // 192, 1)) ** -0.5, 3.0, ((0, 4),))
    expert_gate = centred(arg_keys[6], (E_FFN, D, FF), D ** -0.5, 0.21875, ((0, 2), (2, 4)))
    expert_up = centred(arg_keys[7], (E_FFN, D, FF), D ** -0.5, 0.21875, ((0, 2), (2, 4)))
    expert_down = centred(arg_keys[8], (E_FFN, FF, D), FF ** -0.5, 0.125, ((0, 2), (1, 4)))
    const_vectors = centred(arg_keys[9], (2, D), 1.0, 6.0)
    gate_values = jnp.clip(0.25 + 0.75 * jax.random.uniform(arg_keys[10], (SEQS, SEQ, 2), jnp.float32) ** shard_levels(arg_keys[10], (SEQS, SEQ, 2), ((0, 8), (1, 4)), -0.2, 0.2), 0.25, 1.0)
    routes = draw_routes(jax.random.fold_in(arg_keys[14], 71), 0)
    priority = jax.vmap(lambda own: jax.random.permutation(own, TOK_GRP))(jax.random.split(arg_keys[12], GROUPS)).reshape((GROUPS, TOK_GRP)).astype(jnp.int32)
    pieces = draw_pieces(jax.random.fold_in(arg_keys[14], 71), 0)
    return dict(inputs=inputs, cotangent=cotangent, gain_attn=gain_attn, gain_ffn=gain_ffn, attn_in=attn_in, attn_out=attn_out, expert_gate=expert_gate, expert_up=expert_up, expert_down=expert_down, const_vectors=const_vectors, gate_values=gate_values, routes=routes, priority=priority, pieces=pieces)


@jax.custom_vjp
def low(v):
    return lax.optimization_barrier(v.astype(jnp.bfloat16)).astype(jnp.float32)

@jax.custom_vjp
def low_back(v):
    return v

def low_keep(v):
    return (low(v), None)

def low_pass(kept, grad):
    return (grad,)

def back_keep(v):
    return (v, None)

def back_low(kept, grad):
    return (low(grad),)
low.defvjp(low_keep, low_pass)
low_back.defvjp(back_keep, back_low)
highest = lax.Precision.HIGHEST
norm_eps = 1e-05
masked_score = -1e+30

def rms_norm(tensor, scale_gain):
    inverse = lax.rsqrt(lax.optimization_barrier(jnp.mean(tensor * tensor, axis=-1, keepdims=True)) + norm_eps)
    return tensor * inverse * scale_gain

def rotary_tables(length, half_width):
    position = jnp.arange(length).astype(jnp.float32)
    frequency = 10000.0 ** (-jnp.arange(half_width).astype(jnp.float32) / half_width)
    angles = position[:, None] * frequency[None, :]
    return (jnp.cos(angles), jnp.sin(angles))

def rotate(tensor, cosine, sine_table):
    half_width = tensor.shape[-1] // 2
    first_half = tensor[..., :half_width]
    second_half = tensor[..., half_width:]
    cosine_part = cosine[:, None, :]
    sine_part = sine_table[:, None, :]
    return jnp.concatenate([first_half * cosine_part - second_half * sine_part, second_half * cosine_part + first_half * sine_part], axis=-1)

def slot_tables(route_rows, priority_rows, capacity):
    total_rows = route_rows.shape[0]
    by_priority = jnp.zeros((total_rows,), jnp.int32).at[priority_rows].set(jnp.arange(total_rows, dtype=jnp.int32))
    ordered = route_rows[by_priority]
    expert_ids = jnp.arange(EXPERTS, dtype=jnp.int32)
    onehot = lax.optimization_barrier(jnp.sum((ordered[:, :, None] == expert_ids[None, None, :]).astype(jnp.int32), axis=1))
    before = jnp.cumsum(onehot, axis=0) - onehot
    slot_ordered = jnp.take_along_axis(before, ordered, axis=1)
    slot_ids = slot_ordered[priority_rows]
    kept_pairs = (slot_ids < capacity) & (route_rows < E_FFN)
    return (slot_ids, kept_pairs)

def dispatch_index(route_rows, slot_ids, kept_pairs):
    total_rows = route_rows.shape[0]
    target = jnp.where(kept_pairs, route_rows * CAP + slot_ids, E_FFN * CAP).astype(jnp.int32)
    pair_tokens = jnp.arange(2 * total_rows, dtype=jnp.int32) // 2
    slot_table = jnp.full((E_FFN * CAP + 1,), total_rows, jnp.int32).at[target.reshape(-1)].set(pair_tokens)
    return (slot_table[:E_FFN * CAP], target)

def attend(normed, weight_in, weight_out, piece_rows):
    groups = normed.shape[0]
    head_shape = (groups, SEQ, HEADS, HEAD_DIM)
    cosine, sine_table = rotary_tables(SEQ, HEAD_DIM // 2)
    query_lin = low_back(jnp.einsum('gsd,de->gse', normed, weight_in[0], precision=highest))
    key_lin = low_back(jnp.einsum('gsd,de->gse', normed, weight_in[1], precision=highest))
    value_lin = low_back(jnp.einsum('gsd,de->gse', normed, weight_in[2], precision=highest))
    queries = low(rotate(query_lin.reshape(head_shape), cosine, sine_table))
    key_rows = low(rotate(key_lin.reshape(head_shape), cosine, sine_table))
    value_rows = low(value_lin.reshape(head_shape))
    raw_scores = jnp.einsum('gqhd,gkhd->ghqk', queries, key_rows, precision=highest) * HEAD_DIM ** (-0.5)
    scores = low_back(raw_scores)
    position = jnp.arange(SEQ)
    causal = position[:, None] >= position[None, :]
    same_piece = (piece_rows[:, :, None] == piece_rows[:, None, :]) & (piece_rows[:, :, None] > 0)
    allowed = causal[None] | same_piece
    scores = jnp.where(allowed[:, None], scores, masked_score)
    soft_probs = low(jax.nn.softmax(scores, axis=-1))
    mixed_heads = jnp.einsum('ghqk,gkhd->gqhd', soft_probs, value_rows, precision=highest).reshape(groups, SEQ, D)
    mixed_heads = low(low_back(mixed_heads))
    return low_back(jnp.einsum('gse,ed->gsd', mixed_heads, weight_out, precision=highest))

def experts(normed, slot_table, target, gate_rows, route_rows, weight_gate, weight_up, weight_down, consts):
    padded = jnp.concatenate([normed, jnp.zeros((1, D), jnp.float32)], axis=0)
    rows_in = padded[slot_table].reshape(E_FFN, CAP, D)
    gate_pre = low_back(jnp.einsum('ecd,edf->ecf', rows_in, weight_gate, precision=highest))
    up_pre = low_back(jnp.einsum('ecd,edf->ecf', rows_in, weight_up, precision=highest))
    hidden = low(jax.nn.silu(gate_pre) * up_pre)
    result = low(low_back(jnp.einsum('ecf,efd->ecd', hidden, weight_down, precision=highest)))
    flat_rows = jnp.concatenate([result.reshape(E_FFN * CAP, D), jnp.zeros((1, D), jnp.float32)], axis=0)
    chosen = flat_rows[target]
    copy_flag = (route_rows == E_FFN + 1).astype(jnp.float32)[..., None]
    first_const = (route_rows == E_FFN + 2).astype(jnp.float32)[..., None]
    second_const = (route_rows == E_FFN + 3).astype(jnp.float32)[..., None]
    branch = chosen + copy_flag * normed[:, None, :] + first_const * consts[0] + second_const * consts[1]
    return lax.optimization_barrier(jnp.sum(gate_rows[..., None] * branch, axis=1))

def reference(inputs, cotangent, gain_attn, gain_ffn, attn_in, attn_out, expert_gate, expert_up, expert_down, const_vectors, gate_values, routes, priority, pieces):
    slot_ids, kept_pairs = jax.vmap(slot_tables, in_axes=(0, 0, None))(routes, priority, CAP)
    slot_table, target = jax.vmap(dispatch_index)(routes, slot_ids, kept_pairs)
    group_size = math.gcd(SEQS, max(1, 4096 // SEQ))

    def forward(inputs_f, gain_one, gain_two, weight_in, weight_out, weight_gate, weight_up, weight_down, consts, gate_rows):
        normed = low(rms_norm(inputs_f, gain_one))

        def attend_group(bundle):
            return attend(bundle[0], weight_in, weight_out, bundle[1])
        attended = lax.map(jax.checkpoint(attend_group), (normed.reshape(SEQS // group_size, group_size, SEQ, D), pieces.reshape(SEQS // group_size, group_size, SEQ)))
        resid = inputs_f + attended.reshape(SEQS, SEQ, D)
        normed_two = low(rms_norm(resid, gain_two))

        def expert_group(bundle):
            return experts(bundle[0], bundle[1], bundle[2], bundle[3], bundle[4], weight_gate, weight_up, weight_down, consts)
        moe = lax.map(jax.checkpoint(expert_group), (normed_two.reshape(GROUPS, TOK_GRP, D), slot_table, target, gate_rows.reshape(GROUPS, TOK_GRP, 2), routes))
        return resid + moe.reshape(SEQS, SEQ, D)
    floats = (inputs.astype(jnp.float32), gain_attn.astype(jnp.float32), gain_ffn.astype(jnp.float32), attn_in.astype(jnp.float32), attn_out.astype(jnp.float32), expert_gate.astype(jnp.float32), expert_up.astype(jnp.float32), expert_down.astype(jnp.float32), const_vectors.astype(jnp.float32), gate_values.astype(jnp.float32))
    result, pullback = jax.vjp(forward, *floats)
    grads = pullback(cotangent.astype(jnp.float32))
    return (result.astype(jnp.bfloat16), grads[0], grads[1], grads[2], grads[3], grads[4], grads[5], grads[6], grads[7], grads[8], grads[9])
```

```python
import functools

import jax
import jax.numpy as jnp
import numpy as np
from jax import lax
from jax.experimental import pallas as pl
from jax.experimental.pallas import tpu as pltpu
from jax.sharding import Mesh
from jax.sharding import PartitionSpec as P

D = 768
HEAD_DIM = 64
E_FFN = 8
MOST = 88
SEG = 96
TAB = 8
TILE_OWN = 192
TILE_ALL = 256
CALL_TOKENS = 8192

norm_eps = 1e-05
masked_score = -1e30
bf16 = jnp.bfloat16
f32 = jnp.float32
VMEM_MAX = 60 * 1024 * 1024


def dot(a, b, ca=1, cb=0):
    return lax.dot_general(a, b, (((ca,), (cb,)), ((), ())), preferred_element_type=f32)


def params(**kw):
    return pltpu.CompilerParams(vmem_limit_bytes=VMEM_MAX, **kw)


VM = pl.BlockSpec(memory_space=pltpu.VMEM)
SM = pl.BlockSpec(memory_space=pltpu.SMEM)
HB = pl.BlockSpec(memory_space=pl.ANY)


def shift(value, axis, step):
    count = lax.axis_size(axis)
    return lax.ppermute(value, axis, [(i, (i + step) % count) for i in range(count)])


def normed(rows, gain):
    inverse = lax.rsqrt(jnp.mean(rows * rows, axis=-1, keepdims=True) + norm_eps)
    unit = rows * inverse
    return unit, inverse, (unit * gain).astype(bf16)


def rotary_numpy(length, heads):
    half = HEAD_DIM // 2
    frequency = (10000.0 ** (-np.arange(half, dtype=np.float32) / half)).astype(np.float32)
    angles = np.arange(length, dtype=np.float32)[:, None] * frequency[None, :]
    cosine = np.tile(np.cos(angles), (1, 2 * heads)).astype(np.float32)
    sine = np.tile(np.sin(angles), (1, 2 * heads)).astype(np.float32)
    return cosine, sine


def partner_matrix(width):
    i = lax.broadcasted_iota(jnp.int32, (width, width), 0)
    j = lax.broadcasted_iota(jnp.int32, (width, width), 1)
    low = (j % HEAD_DIM) < HEAD_DIM // 2
    minus = jnp.where(low & (i == j + HEAD_DIM // 2), -1.0, 0.0)
    plus = jnp.where((~low) & (i == j - HEAD_DIM // 2), 1.0, 0.0)
    return (minus + plus).astype(bf16)


def eye(width):
    i = lax.broadcasted_iota(jnp.int32, (width, width), 0)
    j = lax.broadcasted_iota(jnp.int32, (width, width), 1)
    return jnp.where(i == j, 1.0, 0.0).astype(bf16)


def route_kernel(cap, base_ref, routes_ref, prio_ref, gates_ref, cot_ref, out_ref):
    total = prio_ref.shape[1]
    toks = cot_ref.shape[0]
    base = pl.multiple_of(base_ref[0], toks)
    prio = prio_ref[...].astype(f32)
    own_row = prio_ref[:, pl.ds(base, toks)].astype(f32)
    own_col = jnp.broadcast_to(own_row, (8, toks)).T[:, :1]
    earlier = jnp.where(prio < own_col, 1.0, 0.0).astype(bf16)
    ids = lax.broadcasted_iota(jnp.int32, (16, total), 0)
    named = (routes_ref[0:1, :] == ids) | (routes_ref[1:2, :] == ids)
    slots = dot(jnp.where(named, 1.0, 0.0).astype(bf16), earlier, 1, 1)
    own_ids = lax.broadcasted_iota(jnp.int32, (16, toks), 0)
    first = routes_ref[0:1, pl.ds(base, toks)] == own_ids
    second = routes_ref[1:2, pl.ds(base, toks)] == own_ids
    kept = (first | second) & (own_ids < E_FFN) & (slots < cap)
    before_i = lax.broadcasted_iota(jnp.int32, (toks, toks), 0)
    before_j = lax.broadcasted_iota(jnp.int32, (toks, toks), 1)
    lower = jnp.where(before_i < before_j, 1.0, 0.0).astype(bf16)
    rank = dot(jnp.where(kept, 1.0, 0.0).astype(bf16), lower)
    rank = jnp.where(kept, rank, -1.0)
    gate = jnp.where(first, gates_ref[0:1, :], 0.0) + jnp.where(second, gates_ref[1:2, :], 0.0)
    high = gate.astype(bf16)
    rest = (gate - high.astype(f32)).astype(bf16)
    out_ref[0:toks, :] = cot_ref[...]
    out_ref[toks : toks + TAB, 0:toks] = rank[:TAB].astype(bf16)
    out_ref[toks : toks + TAB, toks : 2 * toks] = high[:TAB]
    out_ref[toks : toks + TAB, 2 * toks : 3 * toks] = rest[:TAB]


def attn_fwd_kernel(
    heads,
    place_ref,
    x0,
    x1,
    x2,
    x3,
    gain_ref,
    w_ref,
    cos_ref,
    sin_ref,
    prow_ref,
    pcol_ref,
    q_ref,
    k_ref,
    v_ref,
    pt_ref,
    m0,
    m1,
    m2,
    m3,
    bias_ref,
    pbuf,
    obuf,
    sems,
):
    toks = x0.shape[0]
    width = heads * HEAD_DIM
    slots = 4
    seq = slots * toks
    swap = partner_matrix(width)
    wq, wk, wv = w_ref[0], w_ref[1], w_ref[2]
    wq_swap = dot(wq, swap).astype(bf16)
    wk_swap = dot(wk, swap).astype(bf16)
    for slot, x_ref in enumerate((x0, x1, x2, x3)):
        start = pl.multiple_of(place_ref[slot] * toks, toks)
        rows = pl.ds(start, toks)
        _, _, act = normed(x_ref[...].astype(f32), gain_ref[...])
        cosine, sine = cos_ref[rows, :], sin_ref[rows, :]
        queries = (dot(act, wq) * cosine + dot(act, wq_swap) * sine).astype(bf16)
        queries = (queries.astype(f32) * HEAD_DIM**-0.5).astype(bf16)
        keys = (dot(act, wk) * cosine + dot(act, wk_swap) * sine).astype(bf16)
        values = dot(act, wv).astype(bf16)
        for h in range(heads):
            cols = slice(h * HEAD_DIM, (h + 1) * HEAD_DIM)
            q_ref[h, rows, :] = queries[:, cols]
            k_ref[h, rows, :] = keys[:, cols]
            v_ref[h, rows, :] = values[:, cols]

    def copy_out(step):
        return pltpu.make_async_copy(pbuf.at[step % 2], pt_ref.at[step], sems.at[step % 2])

    def step_body(step, carry):
        block = step // heads
        h = step % heads
        cols = pl.ds(pl.multiple_of(block * toks, toks), toks)

        @pl.when(h == 0)
        def _():
            kpos = lax.broadcasted_iota(jnp.int32, (seq, toks), 0)
            qpos = lax.broadcasted_iota(jnp.int32, (seq, toks), 1) + block * toks
            qp = prow_ref[:, cols]
            same = (pcol_ref[...] == qp) & (qp > 0)
            bias_ref[...] = jnp.where((kpos <= qpos) | same, 0.0, masked_score)

        scores = dot(k_ref[h], q_ref[h, cols, :], 1, 1) + bias_ref[...]
        peak = jnp.max(scores, axis=0, keepdims=True)
        weights = jnp.exp(scores - peak)
        mass = jnp.sum(weights, axis=0, keepdims=True)
        probs = (weights * (1.0 / mass)).astype(bf16)

        @pl.when(step >= 2)
        def _():
            copy_out(step - 2).wait()

        pbuf[step % 2] = probs
        copy_out(step).start()
        obuf[block, pl.ds(pl.multiple_of(h * HEAD_DIM, HEAD_DIM), HEAD_DIM), :] = dot(
            v_ref[h], probs, 0, 0
        )
        return carry

    lax.fori_loop(0, slots * heads, step_body, 0)
    for slot, m_ref in enumerate((m0, m1, m2, m3)):
        m_ref[...] = obuf[place_ref[slot]].T.astype(bf16)
    copy_out(slots * heads - 2).wait()
    copy_out(slots * heads - 1).wait()


def attn_bwd_kernel(
    heads,
    place_ref,
    x0,
    x1,
    x2,
    x3,
    g0,
    g1,
    g2,
    g3,
    gain_ref,
    w_ref,
    cos_ref,
    sin_ref,
    cost_ref,
    sint_ref,
    q_ref,
    k_ref,
    v_ref,
    pt_ref,
    keep_ref,
    send_ref,
    dw_ref,
    gg_ref,
    act_ref,
    go_ref,
    qcat_ref,
    kcat_ref,
    dk_ref,
    dv_ref,
    dqt_ref,
    dlin_ref,
    pbuf,
    sems,
):
    toks = x0.shape[0]
    width = heads * HEAD_DIM
    slots = 4
    total_steps = slots * heads

    def copy_in(step):
        return pltpu.make_async_copy(pt_ref.at[step], pbuf.at[step % 2], sems.at[step % 2])

    copy_in(0).start()
    copy_in(1).start()
    swap = partner_matrix(HEAD_DIM)
    both = jnp.concatenate([eye(HEAD_DIM), swap], axis=1)
    swap_i = lax.broadcasted_iota(jnp.int32, (2 * HEAD_DIM, HEAD_DIM), 0)
    swap_j = lax.broadcasted_iota(jnp.int32, (2 * HEAD_DIM, HEAD_DIM), 1)
    low = ((swap_i - HEAD_DIM) < HEAD_DIM // 2) & (swap_i >= HEAD_DIM)
    high = (swap_i - HEAD_DIM) >= HEAD_DIM // 2
    stacked = (
        jnp.where(swap_i == swap_j, 1.0, 0.0)
        + jnp.where(low & (swap_j == swap_i - HEAD_DIM + HEAD_DIM // 2), -1.0, 0.0)
        + jnp.where(high & (swap_j == swap_i - HEAD_DIM - HEAD_DIM // 2), 1.0, 0.0)
    ).astype(bf16)
    for slot, (x_ref, g_ref) in enumerate(zip((x0, x1, x2, x3), (g0, g1, g2, g3))):
        rows = pl.ds(pl.multiple_of(place_ref[slot] * toks, toks), toks)
        _, _, act = normed(x_ref[...].astype(f32), gain_ref[...])
        act_ref[rows, :] = act
        for h in range(heads):
            go_ref[h, rows, :] = g_ref[:, h * HEAD_DIM : (h + 1) * HEAD_DIM]
    for h in range(heads):
        qcat_ref[h] = dot(q_ref[h], both).astype(bf16)
        kcat_ref[h] = dot(stacked, k_ref[h], 1, 1).astype(bf16)
    dk_ref[...] = jnp.zeros(dk_ref.shape, f32)
    dv_ref[...] = jnp.zeros(dv_ref.shape, f32)

    def step_body(step, carry):
        block = step // heads
        h = step % heads
        cols = pl.ds(pl.multiple_of(block * toks, toks), toks)
        copy_in(step).wait()
        probs = pbuf[step % 2]
        grad_out = go_ref[h, cols, :]
        grad_probs = dot(v_ref[h], grad_out, 1, 1)
        probs_f = probs.astype(f32)
        inner = jnp.sum(probs_f * grad_probs, axis=0, keepdims=True)
        grad_scores = (probs_f * (grad_probs - inner)).astype(bf16)
        dv_ref[h] += dot(probs, grad_out)
        dk_ref[h] += dot(grad_scores, qcat_ref[h, cols, :])
        dqt_ref[block, h] = dot(kcat_ref[h], grad_scores)

        @pl.when(step + 2 < total_steps)
        def _():
            copy_in(step + 2).start()

        return carry

    lax.fori_loop(0, total_steps, step_body, 0)
    for h in range(heads):
        cols = slice(h * HEAD_DIM, (h + 1) * HEAD_DIM)
        for block in range(slots):
            rows = slice(block * toks, (block + 1) * toks)
            both_t = dqt_ref[block, h]
            lin_t = (
                both_t[:HEAD_DIM] * cost_ref[:, rows] - both_t[HEAD_DIM:] * sint_ref[:, rows]
            ) * HEAD_DIM**-0.5
            dlin_ref[0, rows, cols] = lin_t.T.astype(bf16)
        cosine, sine = cos_ref[:, :HEAD_DIM], sin_ref[:, :HEAD_DIM]
        dlin_ref[1, :, cols] = (
            dk_ref[h, :, :HEAD_DIM] * cosine - dk_ref[h, :, HEAD_DIM:] * sine
        ).astype(bf16)
        dlin_ref[2, :, cols] = dv_ref[h].astype(bf16)
    for k in range(3):
        dw_ref[k] = dot(dlin_ref[k], act_ref[...], 0, 0).astype(bf16)
    gain_grad = jnp.zeros((1, D), f32)
    for slot, x_ref in enumerate((x0, x1, x2, x3)):
        rows = pl.ds(pl.multiple_of(place_ref[slot] * toks, toks), toks)
        part = dot(dlin_ref[0, rows, :], w_ref[0], 1, 1)
        part += dot(dlin_ref[1, rows, :], w_ref[1], 1, 1)
        part += dot(dlin_ref[2, rows, :], w_ref[2], 1, 1)
        unit, _, _ = normed(x_ref[...].astype(f32), gain_ref[...])
        gain_grad += jnp.sum(part * unit, axis=0, keepdims=True)
        if slot % 2 == 0:
            keep_ref[slot // 2] = part.astype(bf16)
        else:
            send_ref[slot // 2] = part.astype(bf16)
    gg_ref[...] = gain_grad


def out_proj_kernel(x_ref, m0, m1, m2, m3, w0, w1, w2, w3, gain_ref, resid_ref, n_ref):
    attended = dot(m0[...], w0[...])
    attended += dot(m1[...], w1[...])
    attended += dot(m2[...], w2[...])
    attended += dot(m3[...], w3[...])
    resid = x_ref[...].astype(f32) + attended
    resid_ref[...] = resid
    _, _, act = normed(resid, gain_ref[...])
    n_ref[...] = act


def mid_kernel(
    dx_ref,
    cot_ref,
    resid_ref,
    routes_ref,
    gates_ref,
    gain_ref,
    m0,
    m1,
    m2,
    m3,
    w0,
    w1,
    w2,
    w3,
    gres_ref,
    g0,
    g1,
    g2,
    g3,
    o0,
    o1,
    o2,
    o3,
    sums_ref,
):
    cot = cot_ref[...].astype(f32)
    routes = routes_ref[...]
    gates = gates_ref[...]

    def weight(expert):
        return jnp.sum(jnp.where(routes == expert, gates, 0.0), axis=1, keepdims=True)

    grad = dx_ref[...].astype(f32) + weight(E_FFN + 1) * cot
    unit, inverse, _ = normed(resid_ref[...], gain_ref[...])
    grad_unit = grad * gain_ref[...]
    grad_resid = cot + inverse * (
        grad_unit - unit * jnp.mean(grad_unit * unit, axis=-1, keepdims=True)
    )
    gres_ref[...] = grad_resid
    grad_att = grad_resid.astype(bf16)
    for m_ref, w_ref, g_ref, o_ref in zip(
        (m0, m1, m2, m3), (w0, w1, w2, w3), (g0, g1, g2, g3), (o0, o1, o2, o3)
    ):
        g_ref[...] = dot(grad_att, w_ref[...], 1, 1).astype(bf16)
        o_ref[...] = dot(m_ref[...], grad_att, 0, 0).astype(bf16)
    sums_ref[...] = jnp.zeros(sums_ref.shape, f32)
    sums_ref[0:1, :] = jnp.sum(grad * unit, axis=0, keepdims=True)
    sums_ref[1:2, :] = jnp.sum(weight(E_FFN + 2) * cot, axis=0, keepdims=True)
    sums_ref[2:3, :] = jnp.sum(weight(E_FFN + 3) * cot, axis=0, keepdims=True)


def out_kernel(y_ref, cot_ref, resid_ref, n_ref, routes_ref, gates_ref, const_ref, out_ref, gg_ref):
    toks = cot_ref.shape[0]
    cot = cot_ref[...].astype(f32)
    routes = routes_ref[...]
    gates = gates_ref[...]
    act = n_ref[...].astype(f32)
    consts = const_ref[...].astype(f32)

    def weight(expert):
        return jnp.sum(jnp.where(routes == expert, gates, 0.0), axis=1, keepdims=True)

    moe = y_ref[0:toks, :].astype(f32) + weight(E_FFN + 1) * act
    moe += weight(E_FFN + 2) * consts[0:1] + weight(E_FFN + 3) * consts[1:2]
    out_ref[...] = (resid_ref[...] + moe).astype(bf16)
    dots = [
        jnp.sum(cot * act, axis=1, keepdims=True),
        jnp.sum(cot * consts[0:1], axis=1, keepdims=True),
        jnp.sum(cot * consts[1:2], axis=1, keepdims=True),
    ]
    table = y_ref[toks : toks + TAB, 0:toks].astype(f32).T
    result = jnp.zeros(routes.shape, f32)
    for e in range(E_FFN):
        result += jnp.where(routes == e, table[:, e : e + 1], 0.0)
    for k, value in enumerate(dots):
        result += jnp.where(routes == E_FFN + 1 + k, value, 0.0)
    gg_ref[...] = result


def last_kernel(gno_a, gno_b, x_ref, gres_ref, gain_ref, out_ref):
    grad = gno_a[...].astype(f32) + gno_b[...].astype(f32)
    unit, inverse, _ = normed(x_ref[...].astype(f32), gain_ref[...])
    grad_unit = grad * gain_ref[...]
    out_ref[...] = gres_ref[...] + inverse * (
        grad_unit - unit * jnp.mean(grad_unit * unit, axis=-1, keepdims=True)
    )


def dispatch_block(first, experts, x, p_ref, tab_ref, rows_ref, gate_ref, offs, starts, block):
    toks = x.shape[0]
    tab_ref[...] = p_ref[toks : toks + TAB, :].astype(f32)
    want = lax.broadcasted_iota(jnp.int32, (SEG, toks), 0).astype(f32)
    hots, weights, counts = [], [], []
    for i in range(experts):
        row = tab_ref[pl.ds(first + i, 1), :]
        rank = row[:, 0:toks]
        gate = row[:, toks : 2 * toks] + row[:, 2 * toks : 3 * toks]
        match = want == rank
        hots.append(jnp.where(match, 1.0, 0.0).astype(bf16))
        weights.append(jnp.sum(jnp.where(match, gate, 0.0), axis=1, keepdims=True))
        counts.append(jnp.max(rank).astype(jnp.int32) + 1)
    hot = jnp.concatenate(hots, axis=0)
    rows_x = dot(hot, x).astype(bf16)
    rows_c = dot(hot, p_ref[0:toks, :])
    for i in range(experts):
        off = offs[i]
        if starts is not None:
            starts[block, i] = off
        at = pl.ds(pl.multiple_of(off, 16), SEG)
        seg = slice(i * SEG, (i + 1) * SEG)
        rows_ref[i, at, 0:D] = rows_x[seg]
        rows_ref[i, at, D : 2 * D] = (rows_c[seg] * weights[i]).astype(bf16)
        if gate_ref is not None:
            gate_ref[i, at, :] = jnp.broadcast_to(weights[i], (SEG, 128))
        offs[i] = off + ((counts[i] + 15) // 16) * 16


def expert_acts(rows, wg, wu, wd):
    act, grad = rows[:, :D], rows[:, D:]
    gate_pre = dot(act, wg)
    up_pre = dot(act, wu)
    grad_hidden = dot(grad, wd, 1, 1)
    sig = 1.0 / (1.0 + jnp.exp(-gate_pre))
    silu = gate_pre * sig
    hidden = (silu * up_pre).astype(bf16)
    grad_gate = (grad_hidden * up_pre * sig * (1.0 + gate_pre * (1.0 - sig))).astype(bf16)
    grad_up = (grad_hidden * silu).astype(bf16)
    return act, grad, hidden, grad_hidden, grad_gate, grad_up


def own_kernel(nb, tile, first_ref, *refs):
    xs, ps = refs[:nb], refs[nb : 2 * nb]
    wg_h, wu_h, wd_h, dxa, dxb, ya, yb = refs[2 * nb : 2 * nb + 7]
    (
        xbuf,
        pbuf,
        wg,
        wu,
        wd,
        rows_ref,
        gate_ref,
        tab_ref,
        dxbuf,
        ybuf,
        offs,
        starts,
        tok_sems,
        w_sems,
        out_sems,
    ) = refs[2 * nb + 7 :]
    experts = wg.shape[0]
    toks = xbuf.shape[1]
    half = nb // 2
    first = first_ref[0]
    x_copies = [pltpu.make_async_copy(xs[b], xbuf.at[b], tok_sems.at[0, b]) for b in range(nb)]
    p_copies = [pltpu.make_async_copy(ps[b], pbuf.at[b], tok_sems.at[1, b]) for b in range(nb)]
    w_copies = [
        pltpu.make_async_copy(src, dst, w_sems.at[k])
        for k, (src, dst) in enumerate(((wg_h, wg), (wu_h, wu), (wd_h, wd)))
    ]
    for b in range(nb):
        x_copies[b].start()
        p_copies[b].start()
    for copy in w_copies:
        copy.start()
    for i in range(experts):
        offs[i] = 0

    def dispatch_body(b, carry):
        pltpu.make_async_copy(xs[0], xbuf.at[b], tok_sems.at[0, b]).wait()
        pltpu.make_async_copy(ps[0], pbuf.at[b], tok_sems.at[1, b]).wait()
        dispatch_block(
            first, experts, xbuf[b], pbuf.at[b], tab_ref, rows_ref, gate_ref, offs, starts, b
        )
        return carry

    lax.fori_loop(0, nb, dispatch_body, 0)
    for i in range(experts):
        at = pl.ds(pl.multiple_of(offs[i], 16), tile)
        rows_ref[i, at, :] = jnp.zeros((tile, 2 * D), bf16)
        gate_ref[i, at, :] = jnp.zeros((tile, 128), f32)
    for copy in w_copies:
        copy.wait()

    def expert_body(e, carry):
        def tile_body(j, inner):
            at = pl.ds(pl.multiple_of(j * tile, 16), tile)
            rows = rows_ref[e, at, :]
            _, _, hidden, grad_hidden, grad_gate, grad_up = expert_acts(rows, wg[e], wu[e], wd[e])
            weight = gate_ref[e, at, :]
            product = jnp.sum(hidden.astype(f32) * grad_hidden, axis=1, keepdims=True)
            gate_ref[e, at, :] = jnp.where(weight > 0.0, product / jnp.maximum(weight, 0.125), 0.0)
            rows_ref[e, at, 0:D] = (
                dot(grad_gate, wg[e], 1, 1) + dot(grad_up, wu[e], 1, 1)
            ).astype(bf16)
            rows_ref[e, at, D : 2 * D] = (dot(hidden, wd[e]) * weight[:, :1]).astype(bf16)
            return inner

        return lax.fori_loop(0, (offs[e] + tile - 1) // tile, tile_body, carry)

    lax.fori_loop(0, experts, expert_body, 0)

    def out_copies(b, slot):
        near = b < half
        return near, (
            pltpu.make_async_copy(dxbuf.at[slot], dxa.at[b % half], out_sems.at[0, slot]),
            pltpu.make_async_copy(ybuf.at[slot], ya.at[b % half], out_sems.at[1, slot]),
        ), (
            pltpu.make_async_copy(dxbuf.at[slot], dxb.at[b % half], out_sems.at[0, slot]),
            pltpu.make_async_copy(ybuf.at[slot], yb.at[b % half], out_sems.at[1, slot]),
        )

    def wait_slot(slot):
        pltpu.make_async_copy(dxbuf.at[slot], dxa.at[0], out_sems.at[0, slot]).wait()
        pltpu.make_async_copy(ybuf.at[slot], ya.at[0], out_sems.at[1, slot]).wait()

    want = lax.broadcasted_iota(jnp.int32, (SEG, toks), 0).astype(f32)
    tab_rows = lax.broadcasted_iota(jnp.int32, (TAB, toks), 0)

    def combine_body(b, carry):
        slot = b % 2

        @pl.when(b >= 2)
        def _():
            wait_slot(slot)

        tab_ref[...] = pbuf[b, toks : toks + TAB, :].astype(f32)
        hots, segs = [], []
        table = jnp.zeros((TAB, toks), f32)
        for i in range(experts):
            rank = tab_ref[pl.ds(first + i, 1), 0:toks]
            match = jnp.where(want == rank, 1.0, 0.0)
            at = pl.ds(pl.multiple_of(starts[b, i], 16), SEG)
            hots.append(match.astype(bf16))
            segs.append(rows_ref[i, at, :])
            line = jnp.sum(match * gate_ref[i, at, :][:, :1], axis=0, keepdims=True)
            table += jnp.where(tab_rows == first + i, line, 0.0)
        result = dot(jnp.concatenate(hots, axis=0), jnp.concatenate(segs, axis=0), 0, 0)
        dxbuf[slot] = result[:, :D].astype(bf16)
        ybuf[slot, 0:toks, :] = result[:, D:].astype(bf16)
        ybuf[slot, toks : toks + TAB, 0:toks] = table.astype(bf16)
        ybuf[slot, toks : toks + TAB, toks:] = jnp.zeros((TAB, D - toks), bf16)
        near, here, there = out_copies(b, slot)

        @pl.when(near)
        def _():
            here[0].start()
            here[1].start()

        @pl.when(jnp.logical_not(near))
        def _():
            there[0].start()
            there[1].start()

        return carry

    lax.fori_loop(0, nb, combine_body, 0)
    wait_slot(0)
    wait_slot(1)


def weight_kernel(pieces, tile, first_ref, *refs):
    count = len(pieces)
    xs, ps = refs[:count], refs[count : 2 * count]
    wg_h, wu_h, wd_h, og, ou, od = refs[2 * count : 2 * count + 6]
    (
        xbuf,
        pbuf,
        wg,
        wu,
        wd,
        rows_ref,
        tab_ref,
        ag,
        au,
        ad,
        offs,
        tok_sems,
        w_sems,
        out_sems,
    ) = refs[2 * count + 6 :]
    experts = wg.shape[0]
    ring = xbuf.shape[0]
    first = first_ref[0]
    total = sum(pieces)
    w_copies = [
        pltpu.make_async_copy(src, dst, w_sems.at[k])
        for k, (src, dst) in enumerate(((wg_h, wg), (wu_h, wu), (wd_h, wd)))
    ]

    def start_block(b):
        slot = b % ring
        begin = 0
        for n, x_ref, p_ref in zip(pieces, xs, ps):

            @pl.when((b >= begin) & (b < begin + n))
            def _(begin=begin, x_ref=x_ref, p_ref=p_ref):
                pltpu.make_async_copy(x_ref.at[b - begin], xbuf.at[slot], tok_sems.at[0, slot]).start()
                pltpu.make_async_copy(p_ref.at[b - begin], pbuf.at[slot], tok_sems.at[1, slot]).start()

            begin += n

    for b in range(ring - 1):
        start_block(jnp.int32(b))
    for copy in w_copies:
        copy.start()
    for i in range(experts):
        offs[i] = 0

    def dispatch_body(b, carry):
        slot = b % ring
        pltpu.make_async_copy(xs[0].at[0], xbuf.at[slot], tok_sems.at[0, slot]).wait()
        pltpu.make_async_copy(ps[0].at[0], pbuf.at[slot], tok_sems.at[1, slot]).wait()

        @pl.when(b + ring - 1 < total)
        def _():
            start_block(b + ring - 1)

        dispatch_block(
            first, experts, xbuf[slot], pbuf.at[slot], tab_ref, rows_ref, None, offs, None, b
        )
        return carry

    lax.fori_loop(0, total, dispatch_body, 0)
    for i in range(experts):
        rows_ref[i, pl.ds(pl.multiple_of(offs[i], 16), tile), :] = jnp.zeros((tile, 2 * D), bf16)
    for copy in w_copies:
        copy.wait()

    def out_copies(e):
        return [
            pltpu.make_async_copy(src, dst.at[e], out_sems.at[k])
            for k, (src, dst) in enumerate(((ag, og), (au, ou), (ad, od)))
        ]

    def expert_body(e, carry):
        def tile_body(j, inner):
            rows = rows_ref[e, pl.ds(pl.multiple_of(j * tile, 16), tile), :]
            act, grad, hidden, _, grad_gate, grad_up = expert_acts(rows, wg[e], wu[e], wd[e])
            part = dot(act, jnp.concatenate([grad_gate, grad_up], axis=1), 0, 0)
            width = grad_gate.shape[1]
            down = dot(hidden, grad, 0, 0)

            @pl.when(j == 0)
            def _():
                @pl.when(e > 0)
                def _():
                    for copy in out_copies(e - 1):
                        copy.wait()

                ag[...] = part[:, :width]
                au[...] = part[:, width:]
                ad[...] = down

            @pl.when(j > 0)
            def _():
                ag[...] += part[:, :width]
                au[...] += part[:, width:]
                ad[...] += down

            return inner

        tiles = jnp.maximum((offs[e] + tile - 1) // tile, 1)
        lax.fori_loop(0, tiles, tile_body, carry)
        for copy in out_copies(e):
            copy.start()
        return carry

    lax.fori_loop(0, experts, expert_body, 0)
    for copy in out_copies(experts - 1):
        copy.wait()


def row_room(cap, blocks, groups, tile):
    most = groups * min(cap + 15 * blocks, SEG * blocks)
    return -(-most // tile) * tile + tile


def own_experts(first, xs, ps, wg, wu, wd, cap):
    nb = len(xs)
    experts, _, width = wg.shape
    toks = xs[0].shape[0]
    room = row_room(cap, nb, 1, TILE_OWN)
    half = nb // 2
    shapes = [
        jax.ShapeDtypeStruct((half, toks, D), bf16),
        jax.ShapeDtypeStruct((half, toks, D), bf16),
        jax.ShapeDtypeStruct((half, toks + TAB, D), bf16),
        jax.ShapeDtypeStruct((half, toks + TAB, D), bf16),
    ]
    return pl.pallas_call(
        functools.partial(own_kernel, nb, TILE_OWN),
        out_shape=shapes,
        in_specs=[SM] + [HB] * (2 * nb + 3),
        out_specs=[HB] * 4,
        scratch_shapes=[
            pltpu.VMEM((nb, toks, D), bf16),
            pltpu.VMEM((nb, toks + TAB, D), bf16),
            pltpu.VMEM(wg.shape, bf16),
            pltpu.VMEM(wu.shape, bf16),
            pltpu.VMEM(wd.shape, bf16),
            pltpu.VMEM((experts, room, 2 * D), bf16),
            pltpu.VMEM((experts, room, 128), f32),
            pltpu.VMEM((TAB, D), f32),
            pltpu.VMEM((2, toks, D), bf16),
            pltpu.VMEM((2, toks + TAB, D), bf16),
            pltpu.SMEM((experts,), jnp.int32),
            pltpu.SMEM((nb, experts), jnp.int32),
            pltpu.SemaphoreType.DMA((2, nb)),
            pltpu.SemaphoreType.DMA((3,)),
            pltpu.SemaphoreType.DMA((2, 2)),
        ],
        compiler_params=params(),
        name="own_experts",
    )(first, *xs, *ps, wg, wu, wd)


def weight_grads(first, xs, ps, wg, wu, wd, cap, groups):
    pieces = tuple(x.shape[0] for x in xs)
    experts, _, width = wg.shape
    toks = xs[0].shape[1]
    ring = 3
    room = row_room(cap, sum(pieces) // groups, groups, TILE_ALL)
    shapes = [
        jax.ShapeDtypeStruct(wg.shape, f32),
        jax.ShapeDtypeStruct(wu.shape, f32),
        jax.ShapeDtypeStruct(wd.shape, f32),
    ]
    return pl.pallas_call(
        functools.partial(weight_kernel, pieces, TILE_ALL),
        out_shape=shapes,
        in_specs=[SM] + [HB] * (2 * len(pieces) + 3),
        out_specs=[HB] * 3,
        scratch_shapes=[
            pltpu.VMEM((ring, toks, D), bf16),
            pltpu.VMEM((ring, toks + TAB, D), bf16),
            pltpu.VMEM(wg.shape, bf16),
            pltpu.VMEM(wu.shape, bf16),
            pltpu.VMEM(wd.shape, bf16),
            pltpu.VMEM((experts, room, 2 * D), bf16),
            pltpu.VMEM((TAB, D), f32),
            pltpu.VMEM(wg.shape[1:], f32),
            pltpu.VMEM(wu.shape[1:], f32),
            pltpu.VMEM(wd.shape[1:], f32),
            pltpu.SMEM((experts,), jnp.int32),
            pltpu.SemaphoreType.DMA((2, ring)),
            pltpu.SemaphoreType.DMA((3,)),
            pltpu.SemaphoreType.DMA((3,)),
        ],
        compiler_params=params(),
        name="weight_grads",
    )(first, *xs, *ps, wg, wu, wd)


def plane_gather(value):
    near = [value, shift(value, "y", 1)]
    wide = list(near)
    for step in range(1, lax.axis_size("x")):
        wide += [shift(v, "x", step) for v in near]
    return wide + [shift(v, "c", 1) for v in wide]


def plane_scatter(keep, send):
    other = shift(send, "c", -1)
    count = lax.axis_size("x")

    def total(a, b):
        return (a.astype(f32) + b.astype(f32)).astype(bf16)

    line = keep[0:2].astype(f32) + other[0:2].astype(f32)
    for step in range(1, count):
        part = total(keep[2 * step : 2 * step + 2], other[2 * step : 2 * step + 2])
        line += shift(part, "x", -step).astype(f32)
    line = line.astype(bf16)
    return total(line[0], shift(line[1], "y", -1))


def all_sum_rows(value):
    for axis in ("c", "y", "x", "dp"):
        count = lax.axis_size(axis)
        total = value
        for step in range(1, count):
            total = total + shift(value, axis, step)
        value = total
    return value


def sum_over(value, axes):
    if not axes:
        return value
    axis = axes[0]
    count = lax.axis_size(axis)
    index = lax.axis_index(axis)
    rows = value.shape[0] // count
    chunks = value.reshape((count, rows) + value.shape[1:])
    total = lax.dynamic_index_in_dim(chunks, index, 0, keepdims=False).astype(f32)
    for step in range(1, count):
        part = lax.dynamic_index_in_dim(chunks, (index + step) % count, 0, keepdims=False)
        total = total + shift(part, axis, step).astype(f32)
    own = sum_over(total.astype(bf16), axes[1:])
    full = jnp.zeros(chunks.shape, bf16)
    full = lax.dynamic_update_index_in_dim(full, own, index, 0)
    for step in range(1, count):
        full = lax.dynamic_update_index_in_dim(
            full, shift(own, axis, step), (index - step) % count, 0
        )
    return full.reshape(value.shape)


def shards(
    inputs,
    cotangent,
    gain_attn,
    gain_ffn,
    attn_in,
    attn_out,
    expert_gate,
    expert_up,
    expert_down,
    const_vectors,
    gate_values,
    routes,
    priority,
    pieces,
):
    toks = inputs.shape[1]
    y_index, c_index = lax.axis_index("y"), lax.axis_index("c")
    x_index, x_count = lax.axis_index("x"), lax.axis_size("x")
    dp_count = lax.axis_size("dp")
    row_count = lax.axis_size("y") * lax.axis_size("c")
    seq = toks * row_count
    heads = attn_in.shape[2] // HEAD_DIM
    width = heads * HEAD_DIM
    group_tokens = routes.shape[1]
    nb = group_tokens // toks
    cap = 5 * group_tokens // 24
    experts = expert_gate.shape[0]
    x_own, cot = inputs[0], cotangent[0]
    gain1, gain2 = gain_attn[None], gain_ffn[None]
    place = jnp.stack(
        [
            ((y_index - ky) % 2) * 2 + (c_index - kc) % 2
            for ky in range(2)
            for kc in range(2)
        ]
    ).astype(jnp.int32)
    first = (x_index * experts).astype(jnp.int32)[None]
    base = (x_index * seq + (y_index * 2 + c_index) * toks).astype(jnp.int32)[None]

    x_y = shift(x_own, "y", 1)
    x_slots = [x_own, shift(x_own, "c", 1), x_y, shift(x_y, "c", 1)]
    w_y = shift(attn_out, "y", 1)
    w_slots = [attn_out, shift(attn_out, "c", 1), w_y, shift(w_y, "c", 1)]

    cosine, sine = rotary_numpy(seq, heads)
    cos_t, sin_t = cosine[:, :HEAD_DIM].T.copy(), sine[:, :HEAD_DIM].T.copy()
    cosine, sine, cos_t, sin_t = (jnp.asarray(a) for a in (cosine, sine, cos_t, sin_t))

    payload = pl.pallas_call(
        functools.partial(route_kernel, cap),
        out_shape=jax.ShapeDtypeStruct((toks + TAB, D), bf16),
        in_specs=[SM, VM, VM, VM, VM],
        out_specs=VM,
        compiler_params=params(),
        name="route",
    )(base, routes[0].T, priority, gate_values[0].T, cot)

    head_shape = jax.ShapeDtypeStruct((heads, seq, HEAD_DIM), bf16)
    mix_shape = jax.ShapeDtypeStruct((toks, width), bf16)
    steps = row_count * heads
    q, k, v, probs, *mixed = pl.pallas_call(
        functools.partial(attn_fwd_kernel, heads),
        out_shape=[head_shape] * 3
        + [jax.ShapeDtypeStruct((steps, seq, toks), bf16)]
        + [mix_shape] * 4,
        in_specs=[SM] + [VM] * 10,
        out_specs=[VM] * 3 + [HB] + [VM] * 4,
        scratch_shapes=[
            pltpu.VMEM((seq, toks), f32),
            pltpu.VMEM((2, seq, toks), bf16),
            pltpu.VMEM((row_count, width, toks), f32),
            pltpu.SemaphoreType.DMA((2,)),
        ],
        compiler_params=params(),
        name="attn_fwd",
    )(place, *x_slots, gain1, attn_in, cosine, sine, pieces, pieces[0][:, None])

    def to_owner(parts):
        return [
            parts[0],
            shift(parts[1], "c", -1),
            shift(parts[2], "y", -1),
            lax.ppermute(parts[3], ("y", "c"), [(i, 3 - i) for i in range(4)]),
        ]

    mixed = to_owner(mixed)
    resid, norm_two = pl.pallas_call(
        out_proj_kernel,
        out_shape=[jax.ShapeDtypeStruct((toks, D), f32), jax.ShapeDtypeStruct((toks, D), bf16)],
        in_specs=[VM] * 10,
        out_specs=[VM] * 2,
        compiler_params=params(),
        name="out_proj",
    )(x_own, *mixed, *w_slots, gain2)

    own_p = plane_gather(payload)
    own_x = plane_gather(norm_two)
    dxa, dxb, ya, yb = own_experts(
        first, own_x, own_p, expert_gate, expert_up, expert_down, cap
    )
    dx = plane_scatter(dxa, dxb)

    def column(array):
        return array[0] if array.ndim == 3 else array

    own_routes = lax.dynamic_slice_in_dim(routes[0], base[0], toks, 0)
    gates = column(gate_values)
    gres, g0, g1, g2, g3, o0, o1, o2, o3, sums = pl.pallas_call(
        mid_kernel,
        out_shape=[jax.ShapeDtypeStruct((toks, D), f32)]
        + [mix_shape] * 4
        + [jax.ShapeDtypeStruct((width, D), bf16)] * 4
        + [jax.ShapeDtypeStruct((8, D), f32)],
        in_specs=[VM] * 14,
        out_specs=[VM] * 10,
        compiler_params=params(),
        name="mid",
    )(dx, cot, resid, own_routes, gates, gain2, *mixed, *w_slots)
    grads = to_owner([g0, g1, g2, g3])
    gno_keep, gno_send, dw_in, gain_part = pl.pallas_call(
        functools.partial(attn_bwd_kernel, heads),
        out_shape=[
            jax.ShapeDtypeStruct((2, toks, D), bf16),
            jax.ShapeDtypeStruct((2, toks, D), bf16),
            jax.ShapeDtypeStruct((3, width, D), bf16),
            jax.ShapeDtypeStruct((1, D), f32),
        ],
        in_specs=[SM] + [VM] * 17 + [HB],
        out_specs=[VM] * 4,
        scratch_shapes=[
            pltpu.VMEM((seq, D), bf16),
            pltpu.VMEM((heads, seq, HEAD_DIM), bf16),
            pltpu.VMEM((heads, seq, 2 * HEAD_DIM), bf16),
            pltpu.VMEM((heads, 2 * HEAD_DIM, seq), bf16),
            pltpu.VMEM((heads, seq, 2 * HEAD_DIM), f32),
            pltpu.VMEM((heads, seq, HEAD_DIM), f32),
            pltpu.VMEM((row_count, heads, 2 * HEAD_DIM, toks), f32),
            pltpu.VMEM((3, seq, width), bf16),
            pltpu.VMEM((2, seq, toks), bf16),
            pltpu.SemaphoreType.DMA((2,)),
        ],
        compiler_params=params(),
        name="attn_bwd",
    )(
        place,
        *x_slots,
        *grads,
        gain1,
        attn_in,
        cosine,
        sine,
        cos_t,
        sin_t,
        q,
        k,
        v,
        probs,
    )
    gno_other = shift(gno_send, "c", -1)
    gno_far = (gno_keep[1].astype(f32) + gno_other[1].astype(f32)).astype(bf16)
    gno_near = (gno_keep[0].astype(f32) + gno_other[0].astype(f32)).astype(bf16)
    gno_far = shift(gno_far, "y", -1)
    input_grad = pl.pallas_call(
        last_kernel,
        out_shape=jax.ShapeDtypeStruct((toks, D), f32),
        in_specs=[VM] * 5,
        out_specs=VM,
        compiler_params=params(),
        name="last",
    )(gno_near, gno_far, x_own, gres, gain1)

    out_send = jnp.stack([o1, o3])
    out_other = shift(out_send, "c", -1).astype(f32)
    out_far = (o2.astype(f32) + out_other[1]).astype(bf16)
    dw_out = (o0.astype(f32) + out_other[0] + shift(out_far, "y", -1).astype(f32)).astype(bf16)
    attn_grads = jnp.concatenate([dw_in.reshape(3 * width, D), dw_out], axis=0)
    attn_grads = sum_over(attn_grads, ("x", "dp")).astype(f32)
    grad_w_in = attn_grads[: 3 * width].reshape(3, width, D).transpose(0, 2, 1)
    grad_w_out = attn_grads[3 * width :]
    sums = all_sum_rows(jnp.concatenate([sums[:3], gain_part], axis=0))

    y_sum = plane_scatter(ya, yb)
    block_out, grad_gates = pl.pallas_call(
        out_kernel,
        out_shape=[
            jax.ShapeDtypeStruct((toks, D), bf16),
            jax.ShapeDtypeStruct((toks, 2), f32),
        ],
        in_specs=[VM] * 7,
        out_specs=[VM] * 2,
        compiler_params=params(),
        name="block_out",
    )(y_sum, cot, resid, norm_two, own_routes, gates, const_vectors)

    per_call = max(1, min(dp_count, CALL_TOKENS // group_tokens))
    grads_w = None
    for begin in range(0, dp_count, per_call):
        far = [s for s in range(begin, min(begin + per_call, dp_count)) if s > 0]
        xs = [a[None] for a in own_x] if begin == 0 else []
        ps = [a[None] for a in own_p] if begin == 0 else []
        if far:
            seed_x, seed_p = norm_two, payload
            if grads_w is not None:
                seed_x, seed_p, grads_w = lax.optimization_barrier((seed_x, seed_p, grads_w))
            xs += plane_gather(jnp.stack([shift(seed_x, "dp", s) for s in far]))
            ps += plane_gather(jnp.stack([shift(seed_p, "dp", s) for s in far]))
        groups = len(far) + (begin == 0)
        part = weight_grads(first, xs, ps, expert_gate, expert_up, expert_down, cap, groups)
        grads_w = part if grads_w is None else [a + b for a, b in zip(grads_w, part)]
    grad_w_gate, grad_w_up, grad_w_down = grads_w

    return (
        block_out[None],
        input_grad[None],
        sums[3],
        sums[0],
        grad_w_in,
        grad_w_out,
        grad_w_gate,
        grad_w_up,
        grad_w_down,
        sums[1:3],
        grad_gates[None],
    )


def solution(mesh):
    dp, row, col = mesh.devices.shape
    fine = Mesh(mesh.devices.reshape(dp, row // 2, 2, col), ("dp", "y", "c", "x"))
    rows = ("y", "c")
    in_specs = (
        P(("dp", "x"), rows, None),
        P(("dp", "x"), rows, None),
        P(),
        P(),
        P(None, None, rows),
        P(rows, None),
        P("x", None, rows),
        P("x", None, rows),
        P("x", rows, None),
        P(),
        P(("dp", "x"), rows, None),
        P("dp", None, None),
        P("dp", None),
        P(("dp", "x"), None),
    )
    out_specs = (
        P(("dp", "x"), rows, None),
        P(("dp", "x"), rows, None),
        P(),
        P(),
        P(None, None, rows),
        P(rows, None),
        P("x", None, rows),
        P("x", None, rows),
        P("x", rows, None),
        P(),
        P(("dp", "x"), rows, None),
    )
    return jax.shard_map(shards, mesh=fine, in_specs=in_specs, out_specs=out_specs, check_vma=False)
```

```python
import functools

import jax
import jax.numpy as jnp
import numpy as np
from jax import lax
from jax.experimental import pallas as pl
from jax.experimental.pallas import tpu as pltpu
from jax.sharding import Mesh
from jax.sharding import PartitionSpec as P

D = 768
HEAD_DIM = 64
E_FFN = 8
MOST = 88
SHORT = 48
SEG = 96
TAB = 8
TILE_OWN = 192
TILE_BACK = 256
TILE_FAR = 512
CALL_TOKENS = 8192

norm_eps = 1e-05
masked_score = -1e30
bf16 = jnp.bfloat16
f32 = jnp.float32
VMEM_MAX = 60 * 1024 * 1024


def dot(a, b, ca=1, cb=0):
    return lax.dot_general(a, b, (((ca,), (cb,)), ((), ())), preferred_element_type=f32)


def params(**kw):
    return pltpu.CompilerParams(vmem_limit_bytes=VMEM_MAX, **kw)


def cost(micros):
    return pl.CostEstimate(
        flops=int(micros * 1.1e9), transcendentals=0, bytes_accessed=int(micros * 3.5e6)
    )


VM = pl.BlockSpec(memory_space=pltpu.VMEM)
SM = pl.BlockSpec(memory_space=pltpu.SMEM)
HB = pl.BlockSpec(memory_space=pl.ANY)


def shift(value, axis, step):
    count = lax.axis_size(axis)
    return lax.ppermute(value, axis, [(i, (i + step) % count) for i in range(count)])


def gain_row(ref):
    return ref[...].reshape(1, D)


def normed(rows, gain):
    inverse = lax.rsqrt(jnp.mean(rows * rows, axis=-1, keepdims=True) + norm_eps)
    unit = rows * inverse
    return unit, inverse, (unit * gain).astype(bf16)


def rotary_numpy(length, heads):
    half = HEAD_DIM // 2
    frequency = (10000.0 ** (-np.arange(half, dtype=np.float32) / half)).astype(np.float32)
    angles = np.arange(length, dtype=np.float32)[:, None] * frequency[None, :]
    cosine = np.tile(np.cos(angles), (1, 2 * heads)).astype(np.float32)
    sine = np.tile(np.sin(angles), (1, 2 * heads)).astype(np.float32)
    return cosine, sine


def partner_matrix(width):
    i = lax.broadcasted_iota(jnp.int32, (width, width), 0)
    j = lax.broadcasted_iota(jnp.int32, (width, width), 1)
    low = (j % HEAD_DIM) < HEAD_DIM // 2
    minus = jnp.where(low & (i == j + HEAD_DIM // 2), -1.0, 0.0)
    plus = jnp.where((~low) & (i == j - HEAD_DIM // 2), 1.0, 0.0)
    return (minus + plus).astype(bf16)


def eye(width):
    i = lax.broadcasted_iota(jnp.int32, (width, width), 0)
    j = lax.broadcasted_iota(jnp.int32, (width, width), 1)
    return jnp.where(i == j, 1.0, 0.0).astype(bf16)


def route_kernel(cap, base_ref, routes_ref, prio_ref, gates_ref, cot_ref, out_ref, copies_ref):
    total = prio_ref.shape[1]
    toks = cot_ref.shape[0]
    base = pl.multiple_of(base_ref[0], toks)
    prio = prio_ref[...].astype(f32)
    own_row = prio_ref[:, pl.ds(base, toks)].astype(f32)
    own_col = jnp.broadcast_to(own_row, (8, toks)).T[:, :1]
    earlier = jnp.where(prio < own_col, 1.0, 0.0).astype(bf16)
    ids = lax.broadcasted_iota(jnp.int32, (16, total), 0)
    named = (routes_ref[0:1, :] == ids) | (routes_ref[1:2, :] == ids)
    slots = dot(jnp.where(named, 1.0, 0.0).astype(bf16), earlier, 1, 1)
    own_ids = lax.broadcasted_iota(jnp.int32, (16, toks), 0)
    first = routes_ref[0:1, pl.ds(base, toks)] == own_ids
    second = routes_ref[1:2, pl.ds(base, toks)] == own_ids
    kept = (first | second) & (own_ids < E_FFN) & (slots < cap)
    before_i = lax.broadcasted_iota(jnp.int32, (toks, toks), 0)
    before_j = lax.broadcasted_iota(jnp.int32, (toks, toks), 1)
    lower = jnp.where(before_i < before_j, 1.0, 0.0).astype(bf16)
    rank = dot(jnp.where(kept, 1.0, 0.0).astype(bf16), lower)
    rank = jnp.where(kept, rank, -1.0)
    gate = jnp.where(first, gates_ref[0:1, :], 0.0) + jnp.where(second, gates_ref[1:2, :], 0.0)
    high = gate.astype(bf16)
    rest = (gate - high.astype(f32)).astype(bf16)
    table = jnp.concatenate([rank[:TAB].astype(bf16), high[:TAB], rest[:TAB]], axis=1)
    out_ref[0:toks, :] = cot_ref[...]
    out_ref[toks : toks + TAB, :] = table
    for k in range(copies_ref.shape[0]):
        copies_ref[k, 0:toks, :] = cot_ref[...]
        copies_ref[k, toks : toks + TAB, :] = table


def attn_fwd_kernel(
    heads,
    place_ref,
    x0,
    x1,
    x2,
    x3,
    gain_ref,
    w_ref,
    cos_ref,
    sin_ref,
    prow_ref,
    q_ref,
    k_ref,
    v_ref,
    pt_ref,
    m0,
    m1,
    m2,
    m3,
    bias_ref,
    pbuf,
    obuf,
    sems,
):
    toks = x0.shape[0]
    width = heads * HEAD_DIM
    slots = 4
    seq = slots * toks
    swap = partner_matrix(width)
    wq, wk, wv = w_ref[0], w_ref[1], w_ref[2]
    wq_swap = dot(swap, wq, 0, 0).astype(bf16)
    wk_swap = dot(swap, wk, 0, 0).astype(bf16)
    piece_col = jnp.broadcast_to(prow_ref[...].astype(f32), (8, seq)).T[:, :1]
    for slot, x_ref in enumerate((x0, x1, x2, x3)):
        start = pl.multiple_of(place_ref[slot] * toks, toks)
        rows = pl.ds(start, toks)
        _, _, act = normed(x_ref[...].astype(f32), gain_row(gain_ref))
        cosine, sine = cos_ref[rows, :], sin_ref[rows, :]
        queries = (dot(act, wq, 1, 1) * cosine + dot(act, wq_swap, 1, 1) * sine).astype(bf16)
        queries = (queries.astype(f32) * HEAD_DIM**-0.5).astype(bf16)
        keys = (dot(act, wk, 1, 1) * cosine + dot(act, wk_swap, 1, 1) * sine).astype(bf16)
        values = dot(act, wv, 1, 1).astype(bf16)
        for h in range(heads):
            cols = slice(h * HEAD_DIM, (h + 1) * HEAD_DIM)
            q_ref[h, rows, :] = queries[:, cols]
            k_ref[h, rows, :] = keys[:, cols]
            v_ref[h, rows, :] = values[:, cols]

    def copy_out(step):
        return pltpu.make_async_copy(pbuf.at[step % 2], pt_ref.at[step], sems.at[step % 2])

    def step_body(step, carry):
        block = step // heads
        h = step % heads
        cols = pl.ds(pl.multiple_of(block * toks, toks), toks)

        @pl.when(h == 0)
        def _():
            kpos = lax.broadcasted_iota(jnp.int32, (seq, toks), 0)
            qpos = lax.broadcasted_iota(jnp.int32, (seq, toks), 1) + block * toks
            qp = prow_ref[:, cols].astype(f32)
            same = (piece_col == qp) & (qp > 0.0)
            bias_ref[...] = jnp.where((kpos <= qpos) | same, 0.0, masked_score)

        scores = dot(k_ref[h], q_ref[h, cols, :], 1, 1) + bias_ref[...]
        peak = jnp.max(scores, axis=0, keepdims=True)
        weights = jnp.exp(scores - peak)
        mass = jnp.sum(weights, axis=0, keepdims=True)
        probs = (weights * (1.0 / mass)).astype(bf16)

        @pl.when(step >= 2)
        def _():
            copy_out(step - 2).wait()

        pbuf[step % 2] = probs
        copy_out(step).start()
        obuf[block, pl.ds(pl.multiple_of(h * HEAD_DIM, HEAD_DIM), HEAD_DIM), :] = dot(
            v_ref[h], probs, 0, 0
        )
        return carry

    lax.fori_loop(0, slots * heads, step_body, 0)
    for slot, m_ref in enumerate((m0, m1, m2, m3)):
        m_ref[...] = obuf[place_ref[slot]].T.astype(bf16)
    copy_out(slots * heads - 2).wait()
    copy_out(slots * heads - 1).wait()


def attn_bwd_kernel(
    heads,
    place_ref,
    x0,
    x1,
    x2,
    x3,
    g0,
    g1,
    g2,
    g3,
    gain_ref,
    w_ref,
    cos_ref,
    sin_ref,
    cost_ref,
    sint_ref,
    q_ref,
    k_ref,
    v_ref,
    pt_ref,
    keep_ref,
    send_ref,
    dw_ref,
    gg_ref,
    act_ref,
    go_ref,
    qcat_ref,
    kcat_ref,
    dk_ref,
    dv_ref,
    dqt_ref,
    dlin_ref,
    pbuf,
    sems,
):
    toks = x0.shape[0]
    width = heads * HEAD_DIM
    slots = 4
    total_steps = slots * heads

    def copy_in(step):
        return pltpu.make_async_copy(pt_ref.at[step], pbuf.at[step % 2], sems.at[step % 2])

    copy_in(0).start()
    copy_in(1).start()
    swap = partner_matrix(HEAD_DIM)
    both = jnp.concatenate([eye(HEAD_DIM), swap], axis=1)
    swap_i = lax.broadcasted_iota(jnp.int32, (2 * HEAD_DIM, HEAD_DIM), 0)
    swap_j = lax.broadcasted_iota(jnp.int32, (2 * HEAD_DIM, HEAD_DIM), 1)
    low = ((swap_i - HEAD_DIM) < HEAD_DIM // 2) & (swap_i >= HEAD_DIM)
    high = (swap_i - HEAD_DIM) >= HEAD_DIM // 2
    stacked = (
        jnp.where(swap_i == swap_j, 1.0, 0.0)
        + jnp.where(low & (swap_j == swap_i - HEAD_DIM + HEAD_DIM // 2), -1.0, 0.0)
        + jnp.where(high & (swap_j == swap_i - HEAD_DIM - HEAD_DIM // 2), 1.0, 0.0)
    ).astype(bf16)
    for slot, (x_ref, g_ref) in enumerate(zip((x0, x1, x2, x3), (g0, g1, g2, g3))):
        rows = pl.ds(pl.multiple_of(place_ref[slot] * toks, toks), toks)
        _, _, act = normed(x_ref[...].astype(f32), gain_row(gain_ref))
        act_ref[rows, :] = act
        for h in range(heads):
            go_ref[h, rows, :] = g_ref[:, h * HEAD_DIM : (h + 1) * HEAD_DIM]
    for h in range(heads):
        qcat_ref[h] = dot(q_ref[h], both).astype(bf16)
        kcat_ref[h] = dot(stacked, k_ref[h], 1, 1).astype(bf16)
    dk_ref[...] = jnp.zeros(dk_ref.shape, f32)
    dv_ref[...] = jnp.zeros(dv_ref.shape, f32)

    def step_body(step, carry):
        block = step // heads
        h = step % heads
        cols = pl.ds(pl.multiple_of(block * toks, toks), toks)
        copy_in(step).wait()
        probs = pbuf[step % 2]
        grad_out = go_ref[h, cols, :]
        grad_probs = dot(v_ref[h], grad_out, 1, 1)
        probs_f = probs.astype(f32)
        inner = jnp.sum(probs_f * grad_probs, axis=0, keepdims=True)
        grad_scores = (probs_f * (grad_probs - inner)).astype(bf16)
        dv_ref[h] += dot(probs, grad_out)
        dk_ref[h] += dot(grad_scores, qcat_ref[h, cols, :])
        dqt_ref[block, h] = dot(kcat_ref[h], grad_scores)

        @pl.when(step + 2 < total_steps)
        def _():
            copy_in(step + 2).start()

        return carry

    lax.fori_loop(0, total_steps, step_body, 0)
    for h in range(heads):
        cols = slice(h * HEAD_DIM, (h + 1) * HEAD_DIM)
        for block in range(slots):
            rows = slice(block * toks, (block + 1) * toks)
            both_t = dqt_ref[block, h]
            lin_t = (
                both_t[:HEAD_DIM] * cost_ref[:, rows] - both_t[HEAD_DIM:] * sint_ref[:, rows]
            ) * HEAD_DIM**-0.5
            dlin_ref[0, rows, cols] = lin_t.T.astype(bf16)
        cosine, sine = cos_ref[:, :HEAD_DIM], sin_ref[:, :HEAD_DIM]
        dlin_ref[1, :, cols] = (
            dk_ref[h, :, :HEAD_DIM] * cosine - dk_ref[h, :, HEAD_DIM:] * sine
        ).astype(bf16)
        dlin_ref[2, :, cols] = dv_ref[h].astype(bf16)
    for k in range(3):
        dw_ref[k] = dot(dlin_ref[k], act_ref[...], 0, 0).astype(bf16)
    gain_grad = jnp.zeros((1, D), f32)
    for slot, x_ref in enumerate((x0, x1, x2, x3)):
        rows = pl.ds(pl.multiple_of(place_ref[slot] * toks, toks), toks)
        part = dot(dlin_ref[0, rows, :], w_ref[0])
        part += dot(dlin_ref[1, rows, :], w_ref[1])
        part += dot(dlin_ref[2, rows, :], w_ref[2])
        unit, _, _ = normed(x_ref[...].astype(f32), gain_row(gain_ref))
        gain_grad += jnp.sum(part * unit, axis=0, keepdims=True)
        if slot % 2 == 0:
            keep_ref[slot // 2] = part.astype(bf16)
        else:
            send_ref[slot // 2] = part.astype(bf16)
    gg_ref[...] = gain_grad


def out_proj_kernel(
    x_ref, m0, m1, m2, m3, w0, w1, w2, w3, gain_ref, resid_ref, n_ref, top_ref, low_ref, copies_ref
):
    attended = dot(m0[...], w0[...])
    attended += dot(m1[...], w1[...])
    attended += dot(m2[...], w2[...])
    attended += dot(m3[...], w3[...])
    resid = x_ref[...].astype(f32) + attended
    resid_ref[...] = resid
    _, _, act = normed(resid, gain_row(gain_ref))
    half = act.shape[0] // 2
    n_ref[...] = act
    top_ref[...] = act[:half]
    low_ref[...] = act[half:]
    for k in range(copies_ref.shape[0]):
        copies_ref[k] = act


def route_columns(base_ref, routes_ref, gates_ref, toks):
    base = pl.multiple_of(base_ref[0], toks)
    routes = routes_ref[:, pl.ds(base, toks)].astype(f32)
    rows = jnp.concatenate([routes, gates_ref[...], jnp.zeros((4, toks), f32)], axis=0)
    return rows.T, routes


def expert_gate(columns, expert):
    return jnp.where(columns[:, 0:1] == expert, columns[:, 2:3], 0.0) + jnp.where(
        columns[:, 1:2] == expert, columns[:, 3:4], 0.0
    )


def mid_kernel(
    base_ref,
    dx_refs,
    cot_ref,
    resid_ref,
    routes_ref,
    gates_ref,
    gain_ref,
    m_refs,
    w_refs,
    gres_ref,
    g_refs,
    o_refs,
    sums_ref,
):
    toks = cot_ref.shape[0]
    cot = cot_ref[...].astype(f32)
    columns, _ = route_columns(base_ref, routes_ref, gates_ref, toks)
    halves = [dx_refs[k][...].astype(f32) + dx_refs[k + 1][...].astype(f32) for k in (0, 2)]
    grad = jnp.concatenate(halves, axis=0) + expert_gate(columns, E_FFN + 1) * cot
    gain = gain_row(gain_ref)
    unit, inverse, _ = normed(resid_ref[...], gain)
    grad_unit = grad * gain
    grad_resid = cot + inverse * (
        grad_unit - unit * jnp.mean(grad_unit * unit, axis=-1, keepdims=True)
    )
    gres_ref[...] = grad_resid
    grad_att = grad_resid.astype(bf16)
    for m_ref, w_ref, g_ref, o_ref in zip(m_refs, w_refs, g_refs, o_refs):
        g_ref[...] = dot(grad_att, w_ref[...], 1, 1).astype(bf16)
        o_ref[...] = dot(m_ref[...], grad_att, 0, 0).astype(bf16)
    sums_ref[...] = jnp.zeros(sums_ref.shape, f32)
    sums_ref[0:1, :] = jnp.sum(grad * unit, axis=0, keepdims=True)
    for k in range(2):
        weight = expert_gate(columns, E_FFN + 2 + k)
        sums_ref[1 + k : 2 + k, :] = jnp.sum(weight * cot, axis=0, keepdims=True)


def out_kernel(
    base_ref,
    y_refs,
    cot_ref,
    resid_ref,
    n_ref,
    routes_ref,
    gates_ref,
    const_ref,
    out_ref,
    gg_ref,
):
    toks = cot_ref.shape[0]
    half = toks // 2
    cot = cot_ref[...].astype(f32)
    columns, routes = route_columns(base_ref, routes_ref, gates_ref, toks)
    act = n_ref[...].astype(f32)
    consts = const_ref[...].astype(f32)
    top = y_refs[0][...].astype(f32) + y_refs[1][...].astype(f32)
    low = y_refs[2][...].astype(f32) + y_refs[3][...].astype(f32)
    moe = jnp.concatenate([top, low[:half]], axis=0) + expert_gate(columns, E_FFN + 1) * act
    moe += expert_gate(columns, E_FFN + 2) * consts[0:1]
    moe += expert_gate(columns, E_FFN + 3) * consts[1:2]
    out_ref[...] = (resid_ref[...] + moe).astype(bf16)
    dots = [cot * act, cot * consts[0:1], cot * consts[1:2]]
    dots = [jnp.sum(v, axis=1, keepdims=True) for v in dots]
    dots = jnp.concatenate([jnp.broadcast_to(dots[k % 3], (toks, 1)) for k in range(8)], axis=1).T
    table = low[half : half + TAB, 0:toks]
    for pair in range(2):
        route = routes[pair : pair + 1]
        result = jnp.zeros((1, toks), f32)
        for e in range(E_FFN):
            result += jnp.where(route == e, table[e : e + 1], 0.0)
        for k in range(3):
            result += jnp.where(route == E_FFN + 1 + k, dots[k : k + 1], 0.0)
        gg_ref[pair : pair + 1, :] = result


def last_kernel(gno_a, gno_b, x_ref, gres_ref, gain_ref, out_ref):
    grad = gno_a[...].astype(f32) + gno_b[...].astype(f32)
    gain = gain_row(gain_ref)
    unit, inverse, _ = normed(x_ref[...].astype(f32), gain)
    grad_unit = grad * gain
    out_ref[...] = gres_ref[...] + inverse * (
        grad_unit - unit * jnp.mean(grad_unit * unit, axis=-1, keepdims=True)
    )


def dispatch_block(first, experts, x, p_ref, tab_ref, rows_ref, gate_ref, offs, starts, block):
    toks = x.shape[0]
    tab_ref[...] = p_ref[toks : toks + TAB, :].astype(f32)
    want = lax.broadcasted_iota(jnp.int32, (SHORT, toks), 0).astype(f32)
    cot = p_ref[0:toks, :]

    def select(i, begin):
        row = tab_ref[pl.ds(first + i, 1), :]
        match = (want + begin) == row[:, 0:toks]
        gate = row[:, toks : 2 * toks] + row[:, 2 * toks : 3 * toks]
        weight = jnp.sum(jnp.where(match, gate, 0.0), axis=1, keepdims=True)
        return jnp.where(match, 1.0, 0.0).astype(bf16), weight, row[:, 0:toks]

    def put(i, off, rows_x, rows_c, weight):
        at = pl.ds(pl.multiple_of(off, 16), SHORT)
        rows_ref[i, at, 0:D] = rows_x.astype(bf16)
        rows_ref[i, at, D : 2 * D] = (rows_c * weight).astype(bf16)
        if gate_ref is not None:
            gate_ref[i, at, :] = jnp.broadcast_to(weight, (SHORT, 128))

    parts = [select(i, 0.0) for i in range(experts)]
    counts = [jnp.max(rank).astype(jnp.int32) + 1 for _, _, rank in parts]
    hot = jnp.concatenate([p[0] for p in parts], axis=0)
    rows_x, rows_c = dot(hot, x), dot(hot, cot)
    for i in range(experts):
        off = offs[i]
        if starts is not None:
            starts[block, i] = off
        seg = slice(i * SHORT, (i + 1) * SHORT)
        put(i, off, rows_x[seg], rows_c[seg], parts[i][1])

        @pl.when(counts[i] > SHORT)
        def _(i=i, off=off):
            rest, weight, _ = select(i, float(SHORT))
            put(i, off + SHORT, dot(rest, x), dot(rest, cot), weight)

        offs[i] = off + ((counts[i] + 15) // 16) * 16


def expert_acts(rows, wg, wu, wd):
    act, grad = rows[:, :D], rows[:, D:]
    gate_pre = dot(act, wg)
    up_pre = dot(act, wu)
    grad_hidden = dot(grad, wd, 1, 1)
    sig = 1.0 / (1.0 + jnp.exp(-gate_pre))
    silu = gate_pre * sig
    hidden = (silu * up_pre).astype(bf16)
    grad_gate = (grad_hidden * up_pre * sig * (1.0 + gate_pre * (1.0 - sig))).astype(bf16)
    grad_up = (grad_hidden * silu).astype(bf16)
    return act, grad, hidden, grad_hidden, grad_gate, grad_up


def own_kernel(nb, tile, first_ref, *refs):
    tops, lows, ps = refs[:nb], refs[nb : 2 * nb], refs[2 * nb : 3 * nb]
    wg_h, wu_h, wd_h, dxa, dxb, ya, yb, rows_out, used = refs[3 * nb : 3 * nb + 9]
    (
        xbuf,
        pbuf,
        wg,
        wu,
        wd,
        rows_ref,
        back_ref,
        gate_ref,
        tab_ref,
        dxbuf,
        ybuf,
        offs,
        starts,
        tok_sems,
        w_sems,
        out_sems,
        row_sem,
    ) = refs[3 * nb + 9 :]
    experts = wg.shape[0]
    toks = xbuf.shape[1]
    half = nb // 2
    first = first_ref[0]
    mid = toks // 2

    def tok_copies(b, src):
        return (
            pltpu.make_async_copy(tops[src], xbuf.at[b, 0:mid], tok_sems.at[0, b]),
            pltpu.make_async_copy(lows[src], xbuf.at[b, mid:toks], tok_sems.at[1, b]),
            pltpu.make_async_copy(ps[src], pbuf.at[b], tok_sems.at[2, b]),
        )

    w_copies = [
        pltpu.make_async_copy(src, dst, w_sems.at[k])
        for k, (src, dst) in enumerate(((wg_h, wg), (wu_h, wu), (wd_h, wd)))
    ]
    for b in range(nb):
        for copy in tok_copies(b, b):
            copy.start()
    for copy in w_copies:
        copy.start()
    for i in range(experts):
        offs[i] = 0

    def dispatch_body(b, carry):
        for copy in tok_copies(b, 0):
            copy.wait()
        dispatch_block(
            first, experts, xbuf[b], pbuf.at[b], tab_ref, rows_ref, gate_ref, offs, starts, b
        )
        return carry

    lax.fori_loop(0, nb, dispatch_body, 0)
    for i in range(experts):
        at = pl.ds(pl.multiple_of(offs[i], 16), TILE_BACK)
        rows_ref[i, at, :] = jnp.zeros((TILE_BACK, 2 * D), bf16)
        back_ref[i, at, :] = jnp.zeros((TILE_BACK, 2 * D), bf16)
        gate_ref[i, at, :] = jnp.zeros((TILE_BACK, 128), f32)
        used[i] = offs[i]
    rows_copy = pltpu.make_async_copy(rows_ref, rows_out, row_sem)
    rows_copy.start()
    for copy in w_copies:
        copy.wait()

    def expert_body(e, carry):
        def tile_body(j, inner):
            at = pl.ds(pl.multiple_of(j * tile, 16), tile)
            rows = rows_ref[e, at, :]
            _, _, hidden, grad_hidden, grad_gate, grad_up = expert_acts(rows, wg[e], wu[e], wd[e])
            weight = gate_ref[e, at, :]
            product = jnp.sum(hidden.astype(f32) * grad_hidden, axis=1, keepdims=True)
            gate_ref[e, at, :] = jnp.where(weight > 0.0, product / jnp.maximum(weight, 0.125), 0.0)
            back_ref[e, at, 0:D] = (
                dot(grad_gate, wg[e], 1, 1) + dot(grad_up, wu[e], 1, 1)
            ).astype(bf16)
            back_ref[e, at, D : 2 * D] = (dot(hidden, wd[e]) * weight[:, :1]).astype(bf16)
            return inner

        return lax.fori_loop(0, (offs[e] + tile - 1) // tile, tile_body, carry)

    lax.fori_loop(0, experts, expert_body, 0)

    def out_copies(b, slot):
        near = b < half
        return near, (
            pltpu.make_async_copy(dxbuf.at[slot], dxa.at[b % half], out_sems.at[0, slot]),
            pltpu.make_async_copy(ybuf.at[slot], ya.at[b % half], out_sems.at[1, slot]),
        ), (
            pltpu.make_async_copy(dxbuf.at[slot], dxb.at[b % half], out_sems.at[0, slot]),
            pltpu.make_async_copy(ybuf.at[slot], yb.at[b % half], out_sems.at[1, slot]),
        )

    def wait_slot(slot):
        pltpu.make_async_copy(dxbuf.at[slot], dxa.at[0], out_sems.at[0, slot]).wait()
        pltpu.make_async_copy(ybuf.at[slot], ya.at[0], out_sems.at[1, slot]).wait()

    want = lax.broadcasted_iota(jnp.int32, (SEG, toks), 0).astype(f32)
    tab_rows = lax.broadcasted_iota(jnp.int32, (TAB, toks), 0)

    def combine_body(b, carry):
        slot = b % 2

        @pl.when(b >= 2)
        def _():
            wait_slot(slot)

        tab_ref[...] = pbuf[b, toks : toks + TAB, :].astype(f32)
        hots, segs = [], []
        table = jnp.zeros((TAB, toks), f32)
        for i in range(experts):
            rank = tab_ref[pl.ds(first + i, 1), 0:toks]
            match = jnp.where(want == rank, 1.0, 0.0)
            at = pl.ds(pl.multiple_of(starts[b, i], 16), SEG)
            hots.append(match.astype(bf16))
            segs.append(back_ref[i, at, :])
            line = jnp.sum(match * gate_ref[i, at, :][:, :1], axis=0, keepdims=True)
            table += jnp.where(tab_rows == first + i, line, 0.0)
        result = dot(jnp.concatenate(hots, axis=0), jnp.concatenate(segs, axis=0), 0, 0)
        dxbuf[slot] = result[:, :D].astype(bf16)
        ybuf[slot, 0:toks, :] = result[:, D:].astype(bf16)
        ybuf[slot, toks : toks + TAB, 0:toks] = table.astype(bf16)
        ybuf[slot, toks : toks + TAB, toks:] = jnp.zeros((TAB, D - toks), bf16)
        near, here, there = out_copies(b, slot)

        @pl.when(near)
        def _():
            here[0].start()
            here[1].start()

        @pl.when(jnp.logical_not(near))
        def _():
            there[0].start()
            there[1].start()

        return carry

    lax.fori_loop(0, nb, combine_body, 0)
    wait_slot(0)
    wait_slot(1)
    rows_copy.wait()


def dispatch_kernel(pieces, arrays, tile, first_ref, *refs):
    srcs, refs = refs[:arrays], refs[arrays:]
    rows_out, used, xbuf, pbuf, rows_ref, tab_ref, offs, tok_sems, row_sem = refs
    experts = rows_ref.shape[0]
    ring = xbuf.shape[0]
    first = first_ref[0]
    total = sum(p[0] for p in pieces)

    def start_block(b):
        slot = b % ring
        begin = 0
        for blocks, x_parts, p_parts in pieces:

            @pl.when((b >= begin) & (b < begin + blocks))
            def _(begin=begin, x_parts=x_parts, p_parts=p_parts):
                for which, (parts, buf) in enumerate(((x_parts, xbuf), (p_parts, pbuf))):
                    for array, at, lo, hi in parts:
                        pltpu.make_async_copy(
                            srcs[array].at[b - begin + at],
                            buf.at[slot, lo:hi],
                            tok_sems.at[which, slot],
                        ).start()

            begin += blocks

    for b in range(min(ring - 1, total)):
        start_block(jnp.int32(b))
    for i in range(experts):
        offs[i] = 0

    def dispatch_body(b, carry):
        slot = b % ring
        pltpu.make_async_copy(xbuf.at[slot], xbuf.at[slot], tok_sems.at[0, slot]).wait()
        pltpu.make_async_copy(pbuf.at[slot], pbuf.at[slot], tok_sems.at[1, slot]).wait()

        @pl.when(b + ring - 1 < total)
        def _():
            start_block(b + ring - 1)

        dispatch_block(
            first, experts, xbuf[slot], pbuf.at[slot], tab_ref, rows_ref, None, offs, None, b
        )
        return carry

    lax.fori_loop(0, total, dispatch_body, 0)

    def chunk(i, j):
        at = pl.ds(pl.multiple_of(j * tile, tile), tile)
        return pltpu.make_async_copy(rows_ref.at[i, at], rows_out.at[i, at], row_sem)

    def chunks(i):
        return jnp.maximum((offs[i] + tile - 1) // tile, 1)

    def start_chunk(i):
        def body(j, carry):
            chunk(i, j).start()
            return carry

        return body

    def wait_chunk(i):
        def body(j, carry):
            chunk(i, j).wait()
            return carry

        return body

    for i in range(experts):
        rows_ref[i, pl.ds(pl.multiple_of(offs[i], 16), tile), :] = jnp.zeros((tile, 2 * D), bf16)
        used[i] = offs[i]
        lax.fori_loop(0, chunks(i), start_chunk(i), 0)
    for i in range(experts):
        lax.fori_loop(0, chunks(i), wait_chunk(i), 0)


def weight_kernel(tile, begin_e, experts, given, add, used_ref, rows_h, wg_h, wu_h, wd_h, *refs):
    olds, refs = (refs[:3], refs[3:]) if given else ((), refs)
    outs, accs = refs[:3], refs[3:6]
    rbuf, wg, wu, wd, row_sems, w_sems, acc_sems = refs[6:]
    w_copies = [
        pltpu.make_async_copy(src.at[begin_e : begin_e + experts], dst, w_sems.at[k])
        for k, (src, dst) in enumerate(((wg_h, wg), (wu_h, wu), (wd_h, wd)))
    ]

    def tiles(e):
        return jnp.maximum((used_ref[begin_e + e] + tile - 1) // tile, 1)

    def fetch(e, j, slot):
        at = pl.ds(pl.multiple_of(j * tile, tile), tile)
        return pltpu.make_async_copy(
            rows_h.at[begin_e + e, at], rbuf.at[slot], row_sems.at[slot]
        )

    def out_copies(e):
        return [
            pltpu.make_async_copy(src, dst.at[e + begin_e], acc_sems.at[k])
            for k, (src, dst) in enumerate(zip(accs, outs))
        ]

    def old_copies(e):
        return [
            pltpu.make_async_copy(src.at[e + begin_e], dst, acc_sems.at[k])
            for k, (src, dst) in enumerate(zip(olds, accs))
        ]

    fetch(0, 0, 0).start()
    for copy in w_copies:
        copy.start()
    if add:
        for copy in old_copies(0):
            copy.start()
    for copy in w_copies:
        copy.wait()

    def expert_body(e, count):
        last = tiles(e)

        def tile_body(j, step):
            slot = step % 2
            fetch(e, j, slot).wait()

            @pl.when(j + 1 < last)
            def _():
                fetch(e, j + 1, 1 - slot).start()

            @pl.when((j + 1 == last) & (e + 1 < experts))
            def _():
                fetch(e + 1, 0, 1 - slot).start()

            rows = rbuf[slot]
            act, grad, hidden, _, grad_gate, grad_up = expert_acts(rows, wg[e], wu[e], wd[e])
            part = dot(act, jnp.concatenate([grad_gate, grad_up], axis=1), 0, 0)
            width = grad_gate.shape[1]
            down = dot(hidden, grad, 0, 0)
            parts = (part[:, :width], part[:, width:], down)

            @pl.when(j == 0)
            def _():
                @pl.when(e > 0)
                def _():
                    for copy in out_copies(e - 1):
                        copy.wait()
                    if add:
                        for copy in old_copies(e):
                            copy.start()

                if add:
                    for copy, acc, value in zip(old_copies(e), accs, parts):
                        copy.wait()
                        acc[...] += value
                else:
                    for acc, value in zip(accs, parts):
                        acc[...] = value

            @pl.when(j > 0)
            def _():
                for acc, value in zip(accs, parts):
                    acc[...] += value

            return step + 1

        count = lax.fori_loop(0, last, tile_body, count)
        for copy in out_copies(e):
            copy.start()
        return count

    lax.fori_loop(0, experts, expert_body, jnp.int32(0))
    for copy in out_copies(experts - 1):
        copy.wait()


def row_room(cap, blocks, groups, tile):
    most = groups * min(cap + 15 * blocks, SEG * blocks)
    return -(-most // tile) * tile + tile


def own_experts(first, tops, lows, ps, wg, wu, wd, cap):
    nb = len(ps)
    experts = wg.shape[0]
    toks = ps[0].shape[0] - TAB
    room = row_room(cap, nb, 1, TILE_BACK)
    half = nb // 2
    shapes = [
        jax.ShapeDtypeStruct((half, toks, D), bf16),
        jax.ShapeDtypeStruct((half, toks, D), bf16),
        jax.ShapeDtypeStruct((half, toks + TAB, D), bf16),
        jax.ShapeDtypeStruct((half, toks + TAB, D), bf16),
        jax.ShapeDtypeStruct((experts, room, 2 * D), bf16),
        jax.ShapeDtypeStruct((experts,), jnp.int32),
    ]
    return pl.pallas_call(
        functools.partial(own_kernel, nb, TILE_OWN),
        out_shape=shapes,
        in_specs=[SM] + [HB] * (3 * nb + 3),
        out_specs=[HB] * 5 + [SM],
        scratch_shapes=[
            pltpu.VMEM((nb, toks, D), bf16),
            pltpu.VMEM((nb, toks + TAB, D), bf16),
            pltpu.VMEM(wg.shape, bf16),
            pltpu.VMEM(wu.shape, bf16),
            pltpu.VMEM(wd.shape, bf16),
            pltpu.VMEM((experts, room, 2 * D), bf16),
            pltpu.VMEM((experts, room, 2 * D), bf16),
            pltpu.VMEM((experts, room, 128), f32),
            pltpu.VMEM((TAB, D), f32),
            pltpu.VMEM((2, toks, D), bf16),
            pltpu.VMEM((2, toks + TAB, D), bf16),
            pltpu.SMEM((experts,), jnp.int32),
            pltpu.SMEM((nb, experts), jnp.int32),
            pltpu.SemaphoreType.DMA((3, nb)),
            pltpu.SemaphoreType.DMA((3,)),
            pltpu.SemaphoreType.DMA((2, 2)),
            pltpu.SemaphoreType.DMA,
        ],
        compiler_params=params(),
        name="own_experts",
        cost_estimate=cost(29),
    )(first, *tops, *lows, *ps, wg, wu, wd)


def chip_pieces(x_sets, p_sets, blocks, toks):
    flat = [a for sets in (x_sets, p_sets) for arrays in sets for a in arrays]
    half = toks // 2
    x_count = x_sets[0][0].shape[0] // blocks
    pieces = []
    for k in range(4 * x_count):
        core, x, y = k // (2 * x_count), k // 2 % x_count, k % 2
        parts, base = [], 0
        for sets, end in ((x_sets, toks), (p_sets, toks + TAB)):
            top, low = base + core * 2 + y, base + len(sets[0]) + core * x_count + x
            parts.append(((top, x * blocks, 0, half), (low, y * blocks, half, end)))
            base += len(sets[0]) + len(sets[1])
        pieces.append((blocks, *parts))
    return flat, pieces


def dispatch(first, flat, pieces, toks, experts, cap, groups):
    total = sum(p[0] for p in pieces)
    ring = 4
    room = row_room(cap, total // groups, groups, TILE_FAR)
    return pl.pallas_call(
        functools.partial(dispatch_kernel, tuple(pieces), len(flat), TILE_FAR),
        out_shape=[
            jax.ShapeDtypeStruct((experts, room, 2 * D), bf16),
            jax.ShapeDtypeStruct((experts,), jnp.int32),
        ],
        in_specs=[SM] + [HB] * len(flat),
        out_specs=[HB, SM],
        scratch_shapes=[
            pltpu.VMEM((ring, toks, D), bf16),
            pltpu.VMEM((ring, toks + TAB, D), bf16),
            pltpu.VMEM((experts, room, 2 * D), bf16),
            pltpu.VMEM((TAB, D), f32),
            pltpu.SMEM((experts,), jnp.int32),
            pltpu.SemaphoreType.DMA((2, ring)),
            pltpu.SemaphoreType.DMA,
        ],
        compiler_params=params(),
        name="dispatch",
        cost_estimate=cost(20),
    )(first, *flat)


def weight_grads(used, rows, weights, tile, olds=None, add=True, begin_e=0, count_e=None):
    experts = count_e or weights[0].shape[0]
    shapes = [jax.ShapeDtypeStruct(w.shape, f32) for w in weights]
    operands = [used, rows, *weights, *(olds or ())]
    return pl.pallas_call(
        functools.partial(weight_kernel, tile, begin_e, experts, bool(olds), bool(olds) and add),
        out_shape=shapes,
        in_specs=[SM] + [HB] * (len(operands) - 1),
        out_specs=[HB] * 3,
        input_output_aliases={len(operands) - 3 + k: k for k in range(3)} if olds else {},
        scratch_shapes=[
            *[pltpu.VMEM(w.shape[1:], f32) for w in weights],
            pltpu.VMEM((2, tile, 2 * D), bf16),
            *[pltpu.VMEM((experts, *w.shape[1:]), bf16) for w in weights],
            pltpu.SemaphoreType.DMA((2,)),
            pltpu.SemaphoreType.DMA((3,)),
            pltpu.SemaphoreType.DMA((3,)),
        ],
        compiler_params=params(),
        name="weight_grads",
        cost_estimate=cost(14),
    )(*operands)


def after(value, *deps):
    return lax.optimization_barrier((value, *deps))[0]


def after_all(values, *deps):
    return lax.optimization_barrier((*values, *deps))[: len(values)]


def after_tree(tree, *deps):
    return lax.optimization_barrier((tree, *deps))[0]


def other_groups(copies, cut):
    count, index = lax.axis_size("dp"), lax.axis_index("dp")
    blocks = lax.all_to_all(copies, "dp", 0, 0, tiled=True)

    def pick(blocks, rows):
        found = [
            lax.dynamic_index_in_dim(blocks, (index + step) % count, 0)[:, rows]
            for step in range(1, count)
        ]
        return jnp.concatenate(found, axis=0)

    return blocks, lambda b: (pick(b, slice(0, cut)), pick(b, slice(cut, None)))


def gather_line(values, axis):
    out = list(values)
    for step in range(1, lax.axis_size(axis)):
        out += [shift(v, axis, step) for v in values]
    return out


def with_line(values, axis):
    return gather_line([jnp.concatenate(values, axis=0)], axis)


def plane_gather(value, x_first):
    if x_first:
        cols = gather_line([value], "x")
        rows = [shift(v, "y", 1) for v in cols]
        return [v for pair in zip(cols, rows) for v in pair]
    return gather_line(gather_line([value], "y"), "x")


def both_cores(values, *deps):
    return list(values) + [shift(after(v, *deps) if deps else v, "c", 1) for v in values]


def total(*parts):
    return sum(p.astype(f32) for p in parts).astype(bf16)


def scatter_cores(parts):
    return parts[0], shift(parts[1], "c", -1)


def scatter_first(keep, other, cut):
    count = lax.axis_size("x")

    def add(rows, where):
        return total(keep[where][:, rows], other[where][:, rows])

    top, low = slice(0, cut), slice(cut, None)
    x_sent = [add(top, slice(2 * k, 2 * k + 2)) for k in range(1, count)]
    y_sent = add(low, slice(1, None, 2))
    x_kept = add(top, slice(0, 2))
    y_kept = add(low, slice(0, None, 2))
    x_got = [shift(v, "x", -k) for k, v in zip(range(1, count), x_sent)]
    y_got = shift(y_sent, "y", -1)
    return (*x_got, y_got), x_kept, y_kept


def scatter_second(got, x_kept, y_kept):
    x_got, y_got = got[:-1], got[-1]
    count = len(got)
    y_next = total(x_kept[1], *[v[1] for v in x_got])
    x_next = [total(y_kept[k], y_got[k]) for k in range(1, count)]
    top_own = total(x_kept[0], *[v[0] for v in x_got])
    low_own = total(y_kept[0], y_got[0])
    top_far = shift(y_next, "y", -1)
    low_far = [shift(v, "x", -k) for k, v in zip(range(1, count), x_next)]
    if count > 2:
        low_far = [total(*low_far)]
    return top_own, top_far, low_own, low_far[0]


def line_sum(value, axis):
    return sum([shift(value, axis, step) for step in range(1, lax.axis_size(axis))], value)


def scatter_sum(value, axis):
    count, index = lax.axis_size(axis), lax.axis_index(axis)
    chunks = value.reshape((count, value.shape[0] // count) + value.shape[1:])
    result = lax.dynamic_index_in_dim(chunks, index, 0, keepdims=False).astype(f32)
    for step in range(1, count):
        chunk = lax.dynamic_index_in_dim(chunks, (index + step) % count, 0, keepdims=False)
        result = result + shift(chunk, axis, step).astype(f32)
    return result.astype(bf16)


def gather_chunks(own, axis):
    count, index = lax.axis_size(axis), lax.axis_index(axis)
    full = jnp.zeros((count,) + own.shape, bf16)
    full = lax.dynamic_update_index_in_dim(full, own, index, 0)
    for step in range(1, count):
        chunk = shift(own, axis, step)
        full = lax.dynamic_update_index_in_dim(full, chunk, (index - step) % count, 0)
    return full.reshape((count * own.shape[0],) + own.shape[1:])


def shards(
    inputs,
    cotangent,
    gain_attn,
    gain_ffn,
    attn_in,
    attn_out,
    expert_gate,
    expert_up,
    expert_down,
    const_vectors,
    gate_values,
    routes,
    priority,
    pieces,
):
    toks = inputs.shape[1]
    y_index, c_index = lax.axis_index("y"), lax.axis_index("c")
    x_index, x_count = lax.axis_index("x"), lax.axis_size("x")
    dp_count = lax.axis_size("dp")
    row_count = lax.axis_size("y") * lax.axis_size("c")
    seq = toks * row_count
    heads = attn_in.shape[2] // HEAD_DIM
    width = heads * HEAD_DIM
    group_tokens = routes.shape[1]
    nb = group_tokens // toks
    cap = 5 * group_tokens // 24
    experts = expert_gate.shape[0]
    x_own, cot = inputs[0], cotangent[0]
    place = jnp.stack(
        [
            ((y_index - ky) % 2) * 2 + (c_index - kc) % 2
            for ky in range(2)
            for kc in range(2)
        ]
    ).astype(jnp.int32)
    first = (x_index * experts).astype(jnp.int32)[None]
    base = (x_index * seq + (y_index * 2 + c_index) * toks).astype(jnp.int32)[None]

    x_y = shift(x_own, "y", 1)
    w_y = shift(after(attn_out, x_y), "y", 1)
    w_slots = [attn_out, shift(attn_out, "c", 1), w_y, shift(w_y, "c", 1)]

    cosine, sine = rotary_numpy(seq, heads)
    cos_t, sin_t = cosine[:, :HEAD_DIM].T.copy(), sine[:, :HEAD_DIM].T.copy()
    cosine, sine, cos_t, sin_t = (jnp.asarray(a) for a in (cosine, sine, cos_t, sin_t))
    routes_t, gates_t = routes[0].T, gate_values[0].T
    attn_w = attn_in.transpose(0, 2, 1)
    weights = (expert_gate, expert_up, expert_down)
    half = toks // 2
    far = list(range(1, dp_count))
    one_call = dp_count * group_tokens <= CALL_TOKENS

    payload, p_copies = pl.pallas_call(
        functools.partial(route_kernel, cap),
        out_shape=[
            jax.ShapeDtypeStruct((toks + TAB, D), bf16),
            jax.ShapeDtypeStruct((dp_count if one_call else 1, toks + TAB, D), bf16),
        ],
        in_specs=[SM, VM, VM, VM, VM],
        out_specs=[VM, VM],
        compiler_params=params(),
        name="route",
        cost_estimate=cost(2.5),
    )(base, routes_t, priority, gates_t, cot)
    if one_call:
        far_p, split_p = other_groups(p_copies, half)
    x_slots = [x_own, shift(x_own, "c", 1), x_y, shift(after(x_y, payload), "c", 1)]
    p_cols = gather_line([payload], "x")
    p_y = shift(after(payload, x_y), "y", 1)

    head_shape = jax.ShapeDtypeStruct((heads, seq, HEAD_DIM), bf16)
    mix_shape = jax.ShapeDtypeStruct((toks, width), bf16)
    steps = row_count * heads
    q, k, v, probs, *mixed = pl.pallas_call(
        functools.partial(attn_fwd_kernel, heads),
        out_shape=[head_shape] * 3
        + [jax.ShapeDtypeStruct((steps, seq, toks), bf16)]
        + [mix_shape] * 4,
        in_specs=[SM] + [VM] * 9,
        out_specs=[VM] * 3 + [HB] + [VM] * 4,
        scratch_shapes=[
            pltpu.VMEM((seq, toks), f32),
            pltpu.VMEM((2, seq, toks), bf16),
            pltpu.VMEM((row_count, width, toks), f32),
            pltpu.SemaphoreType.DMA((2,)),
        ],
        compiler_params=params(),
        name="attn_fwd",
        cost_estimate=cost(20),
    )(after(place, payload), *x_slots, gain_attn, attn_w, cosine, sine, pieces)

    def to_owner(parts):
        return [
            parts[0],
            shift(parts[1], "c", -1),
            shift(parts[2], "y", -1),
            lax.ppermute(parts[3], ("y", "c"), [(i, 3 - i) for i in range(4)]),
        ]

    started = mixed[0]
    own_p = [p_cols[0], p_y]
    for step, p in enumerate(p_cols[1:], 1):
        own_p += [p, shift(after(p_y, started), "x", step)]
    own_p = both_cores(own_p, started)
    if one_call:
        p_top, p_low = split_p(after(far_p, started))
        p_top_x = gather_line([p_top], "x")
    ready = (p_top, p_low) if one_call else ()
    mixed = to_owner(mixed)
    resid, norm_two, norm_top, norm_low, x_copies = pl.pallas_call(
        out_proj_kernel,
        out_shape=[
            jax.ShapeDtypeStruct((toks, D), f32),
            jax.ShapeDtypeStruct((toks, D), bf16),
            jax.ShapeDtypeStruct((half, D), bf16),
            jax.ShapeDtypeStruct((half, D), bf16),
            jax.ShapeDtypeStruct((dp_count if one_call else 1, toks, D), bf16),
        ],
        in_specs=[VM] * 10,
        out_specs=[VM] * 5,
        compiler_params=params(),
        name="out_proj",
        cost_estimate=cost(3),
    )(x_own, *mixed, *w_slots, after(gain_ffn, *ready))

    tops = plane_gather(norm_top, True)
    lows = plane_gather(norm_low, False)
    arrived = (tops[-1], lows[-1])
    ready = ()
    if one_call:
        far_x, split_x = other_groups(x_copies, half)
        p_low_y = gather_line([p_low], "y")
        ready = (p_top_x[-1], p_low_y[-1])
        p_top = with_line(after_all(p_top_x, *arrived), "y")
        p_low = with_line(after_all(p_low_y, *arrived), "x")
    tops, lows = both_cores(tops), both_cores(lows)
    own_out = own_experts(after(first, *ready), tops, lows, own_p, *weights, cap)
    if one_call:
        own_out = after_all(own_out, *p_top, *p_low, far_x)
    dxa, dxb, ya, yb, rows, used = own_out
    dx_first = scatter_first(*scatter_cores((dxa, dxb)), half)
    dx_stage = dx_first[0][-1]
    dx_parts = scatter_second(*dx_first)
    if one_call:
        p_near = [shift(after(a[0], dxa), "c", 1) for a in (p_top, p_low)]
    front = max(1, experts // 2)
    grads_w = weight_grads(after(used, dx_first[1]), rows, weights, TILE_BACK, count_e=front)
    if one_call:
        x_top, x_low = split_x(after(far_x, dx_stage, grads_w[0]))
        x_top_x = gather_line([x_top], "x")
        x_low_y = gather_line([x_low], "y")
        p_other = [shift(after(a[1], dx_stage), "c", 1) for a in (p_top, p_low)]
    for begin in range(front, experts, front):
        grads_w = weight_grads(
            after(used, dx_stage), rows, weights, TILE_BACK, grads_w, False, begin, front
        )

    gres, *mids = pl.pallas_call(
        lambda base_ref, *refs: mid_kernel(
            base_ref,
            refs[0:4],
            *refs[4:9],
            refs[9:13],
            refs[13:17],
            refs[17],
            refs[18:22],
            refs[22:26],
            refs[26],
        ),
        out_shape=[jax.ShapeDtypeStruct((toks, D), f32)]
        + [mix_shape] * 4
        + [jax.ShapeDtypeStruct((width, D), bf16)] * 4
        + [jax.ShapeDtypeStruct((8, D), f32)],
        in_specs=[SM] + [VM] * 17,
        out_specs=[VM] * 10,
        compiler_params=params(),
        name="mid",
        cost_estimate=cost(5),
    )(
        after(base, grads_w[0]),
        *dx_parts,
        cot,
        resid,
        routes_t,
        gates_t,
        gain_ffn,
        *mixed,
        *w_slots,
    )
    (o0, o1, o2, o3), sums = mids[4:8], mids[8]
    grads = to_owner(mids[:4])
    ready = ()
    if one_call:
        ready = (x_top_x[-1], x_low_y[-1])
        x_top = with_line(after_all(x_top_x, *grads), "y")
        x_low = with_line(after_all(x_low_y, *grads), "x")
        x_near = [shift(a[0], "c", 1) for a in (x_top, x_low)]
    bwd_out = pl.pallas_call(
        functools.partial(attn_bwd_kernel, heads),
        out_shape=[
            jax.ShapeDtypeStruct((2, toks, D), bf16),
            jax.ShapeDtypeStruct((2, toks, D), bf16),
            jax.ShapeDtypeStruct((3, width, D), bf16),
            jax.ShapeDtypeStruct((1, D), f32),
        ],
        in_specs=[SM] + [VM] * 17 + [HB],
        out_specs=[VM] * 4,
        scratch_shapes=[
            pltpu.VMEM((seq, D), bf16),
            pltpu.VMEM((heads, seq, HEAD_DIM), bf16),
            pltpu.VMEM((heads, seq, 2 * HEAD_DIM), bf16),
            pltpu.VMEM((heads, 2 * HEAD_DIM, seq), bf16),
            pltpu.VMEM((heads, seq, 2 * HEAD_DIM), f32),
            pltpu.VMEM((heads, seq, HEAD_DIM), f32),
            pltpu.VMEM((row_count, heads, 2 * HEAD_DIM, toks), f32),
            pltpu.VMEM((3, seq, width), bf16),
            pltpu.VMEM((2, seq, toks), bf16),
            pltpu.SemaphoreType.DMA((2,)),
        ],
        compiler_params=params(),
        name="attn_bwd",
        cost_estimate=cost(22),
    )(
        after(place, *ready),
        *x_slots,
        *grads,
        gain_attn,
        attn_w,
        cosine,
        sine,
        cos_t,
        sin_t,
        q,
        k,
        v,
        probs,
    )
    if one_call:
        bwd_out = after_all(bwd_out, *x_top, *x_low, *x_near)
    gno_keep, gno_send, dw_in, gain_part = bwd_out
    gno_other = shift(gno_send, "c", -1)
    gno_far = (gno_keep[1].astype(f32) + gno_other[1].astype(f32)).astype(bf16)
    gno_near = (gno_keep[0].astype(f32) + gno_other[0].astype(f32)).astype(bf16)

    out_send = jnp.stack([o1, o3])
    out_other = shift(out_send, "c", -1).astype(f32)
    out_far = (o2.astype(f32) + out_other[1]).astype(bf16)
    dw_out = (o0.astype(f32) + out_other[0] + shift(out_far, "y", -1).astype(f32)).astype(bf16)
    sums = jnp.concatenate([sums[:3], gain_part], axis=0)
    sums = line_sum(line_sum(sums, "c"), "y")
    rows_all = 4 * width + sums.shape[0]
    unit = 8 * x_count * dp_count
    padding = jnp.zeros((-rows_all % unit, D), bf16)
    attn_grads = jnp.concatenate(
        [dw_in.reshape(3 * width, D), dw_out, sums.astype(bf16), padding], axis=0
    )
    part = scatter_sum(attn_grads, "x")
    y_stage = scatter_cores(after_all((ya, yb), gain_part))

    if one_call:
        x_other = [shift(after(a[1], gain_part), "c", 1) for a in (x_top, x_low)]
        x_sets = [[*a, n, o] for a, n, o in zip((x_top, x_low), x_near, x_other)]
        p_sets = [[*a, n, o] for a, n, o in zip((p_top, p_low), p_near, p_other)]
        flat, spots = chip_pieces(x_sets, p_sets, len(far), toks)
        rows, used = dispatch(after(first, gain_part), flat, spots, toks, experts, cap, len(far))
        used = after(used, part)
        part, gno_far = after_all((part, gno_far), used)
        part = scatter_sum(part, "dp")
        gno_far = shift(gno_far, "y", -1)
        for e in range(experts):
            grads_w = weight_grads(used, rows, weights, TILE_FAR, grads_w, True, e, 1)
            if e == 0:
                used = after(used, grads_w[0], part, gno_far)
                part, *y_stage = after_tree((part, *y_stage), used)
                part = gather_chunks(part, "dp")
                y_stage = scatter_first(*y_stage, half)
            elif e == 1:
                used = after(used, grads_w[0], part, *y_stage[0])
                part, y_stage = after_tree((part, y_stage), used)
                attn_grads = gather_chunks(part, "x")
                y_parts = scatter_second(*y_stage)
            elif e == 2:
                used = after(used, grads_w[0], attn_grads, *y_parts)
    else:
        gno_far = shift(gno_far, "y", -1)
        part = scatter_sum(part, "dp")
        attn_grads = gather_chunks(gather_chunks(part, "dp"), "x")
        y_parts = scatter_second(*scatter_first(*y_stage, half))
        spots = [(nb, ((0, 0, 0, toks),), ((1, 0, 0, toks + TAB),))]

        def next_group(step, carry):
            x_block, p_block, *sums_w = carry
            x_block, p_block = shift(x_block, "dp", 1), shift(p_block, "dp", 1)
            flat = [lax.all_gather(a, ("y", "c", "x")) for a in (x_block, p_block)]
            rows, used = dispatch(first, flat, spots, toks, experts, cap, 1)
            return x_block, p_block, *weight_grads(used, rows, weights, TILE_FAR, sums_w)

        grads_w = lax.fori_loop(1, dp_count, next_group, (norm_two, payload, *grads_w))[2:]
    grad_w_gate, grad_w_up, grad_w_down = grads_w
    attn_grads = attn_grads.astype(f32)
    grad_w_in = attn_grads[: 3 * width].reshape(3, width, D).transpose(0, 2, 1)
    grad_w_out = attn_grads[3 * width : 4 * width]
    sums = attn_grads[4 * width : 4 * width + 4]
    input_grad = pl.pallas_call(
        last_kernel,
        out_shape=jax.ShapeDtypeStruct((toks, D), f32),
        in_specs=[VM] * 5,
        out_specs=VM,
        compiler_params=params(),
        name="last",
        cost_estimate=cost(3),
    )(gno_near, gno_far, x_own, gres, gain_attn)

    block_out, grad_gates = pl.pallas_call(
        lambda base_ref, *refs: out_kernel(base_ref, refs[0:4], *refs[4:]),
        out_shape=[
            jax.ShapeDtypeStruct((toks, D), bf16),
            jax.ShapeDtypeStruct((2, toks), f32),
        ],
        in_specs=[SM] + [VM] * 10,
        out_specs=[VM] * 2,
        compiler_params=params(),
        name="block_out",
        cost_estimate=cost(3),
    )(base, *y_parts, cot, resid, norm_two, routes_t, gates_t, const_vectors)

    return (
        block_out[None],
        input_grad[None],
        sums[3],
        sums[0],
        grad_w_in,
        grad_w_out,
        grad_w_gate,
        grad_w_up,
        grad_w_down,
        sums[1:3],
        grad_gates.T[None],
    )


def solution(mesh):
    dp, row, col = mesh.devices.shape
    fine = Mesh(mesh.devices.reshape(dp, row // 2, 2, col), ("dp", "y", "c", "x"))
    rows = ("y", "c")
    in_specs = (
        P(("dp", "x"), rows, None),
        P(("dp", "x"), rows, None),
        P(),
        P(),
        P(None, None, rows),
        P(rows, None),
        P("x", None, rows),
        P("x", None, rows),
        P("x", rows, None),
        P(),
        P(("dp", "x"), rows, None),
        P("dp", None, None),
        P("dp", None),
        P(("dp", "x"), None),
    )
    out_specs = (
        P(("dp", "x"), rows, None),
        P(("dp", "x"), rows, None),
        P(),
        P(),
        P(None, None, rows),
        P(rows, None),
        P("x", None, rows),
        P("x", None, rows),
        P("x", rows, None),
        P(),
        P(("dp", "x"), rows, None),
    )
    return jax.shard_map(shards, mesh=fine, in_specs=in_specs, out_specs=out_specs, check_vma=False)
```

```python
import functools

import jax
import jax.numpy as jnp
import numpy as np
from jax import lax
from jax.experimental import pallas as pl
from jax.experimental.pallas import tpu as pltpu
from jax.sharding import Mesh
from jax.sharding import PartitionSpec as P

D = 768
HEAD_DIM = 64
E_FFN = 8
MOST = 88
SHORT = 48
SEG = 96
TAB = 8
TILE_OWN = 192
TILE_BACK = 256
TILE_FAR = 512
CALL_TOKENS = 8192

norm_eps = 1e-05
masked_score = -1e30
bf16 = jnp.bfloat16
f32 = jnp.float32
VMEM_MAX = 60 * 1024 * 1024


def dot(a, b, ca=1, cb=0):
    return lax.dot_general(a, b, (((ca,), (cb,)), ((), ())), preferred_element_type=f32)


def params(**kw):
    return pltpu.CompilerParams(vmem_limit_bytes=VMEM_MAX, **kw)


def cost(micros):
    return pl.CostEstimate(
        flops=int(micros * 1.1e9), transcendentals=0, bytes_accessed=int(micros * 3.5e6)
    )


VM = pl.BlockSpec(memory_space=pltpu.VMEM)
SM = pl.BlockSpec(memory_space=pltpu.SMEM)
HB = pl.BlockSpec(memory_space=pl.ANY)


def shift(value, axis, step):
    count = lax.axis_size(axis)
    return lax.ppermute(value, axis, [(i, (i + step) % count) for i in range(count)])


def gain_row(ref):
    return ref[...].reshape(1, D)


def normed(rows, gain):
    inverse = lax.rsqrt(jnp.mean(rows * rows, axis=-1, keepdims=True) + norm_eps)
    unit = rows * inverse
    return unit, inverse, (unit * gain).astype(bf16)


def rotary_numpy(length, heads):
    half = HEAD_DIM // 2
    frequency = (10000.0 ** (-np.arange(half, dtype=np.float32) / half)).astype(np.float32)
    angles = np.arange(length, dtype=np.float32)[:, None] * frequency[None, :]
    cosine = np.tile(np.cos(angles), (1, 2 * heads)).astype(np.float32)
    sine = np.tile(np.sin(angles), (1, 2 * heads)).astype(np.float32)
    return cosine, sine


def partner_matrix(width):
    i = lax.broadcasted_iota(jnp.int32, (width, width), 0)
    j = lax.broadcasted_iota(jnp.int32, (width, width), 1)
    low = (j % HEAD_DIM) < HEAD_DIM // 2
    minus = jnp.where(low & (i == j + HEAD_DIM // 2), -1.0, 0.0)
    plus = jnp.where((~low) & (i == j - HEAD_DIM // 2), 1.0, 0.0)
    return (minus + plus).astype(bf16)


def eye(width):
    i = lax.broadcasted_iota(jnp.int32, (width, width), 0)
    j = lax.broadcasted_iota(jnp.int32, (width, width), 1)
    return jnp.where(i == j, 1.0, 0.0).astype(bf16)


def route_kernel(cap, base_ref, routes_ref, prio_ref, gates_ref, cot_ref, out_ref, copies_ref):
    total = prio_ref.shape[1]
    toks = cot_ref.shape[0]
    base = pl.multiple_of(base_ref[0], toks)
    prio = prio_ref[...].astype(f32)
    own_row = prio_ref[:, pl.ds(base, toks)].astype(f32)
    own_col = jnp.broadcast_to(own_row, (8, toks)).T[:, :1]
    earlier = jnp.where(prio < own_col, 1.0, 0.0).astype(bf16)
    ids = lax.broadcasted_iota(jnp.int32, (16, total), 0)
    named = (routes_ref[0:1, :] == ids) | (routes_ref[1:2, :] == ids)
    slots = dot(jnp.where(named, 1.0, 0.0).astype(bf16), earlier, 1, 1)
    own_ids = lax.broadcasted_iota(jnp.int32, (16, toks), 0)
    first = routes_ref[0:1, pl.ds(base, toks)] == own_ids
    second = routes_ref[1:2, pl.ds(base, toks)] == own_ids
    kept = (first | second) & (own_ids < E_FFN) & (slots < cap)
    before_i = lax.broadcasted_iota(jnp.int32, (toks, toks), 0)
    before_j = lax.broadcasted_iota(jnp.int32, (toks, toks), 1)
    lower = jnp.where(before_i < before_j, 1.0, 0.0).astype(bf16)
    rank = dot(jnp.where(kept, 1.0, 0.0).astype(bf16), lower)
    rank = jnp.where(kept, rank, -1.0)
    gate = jnp.where(first, gates_ref[0:1, :], 0.0) + jnp.where(second, gates_ref[1:2, :], 0.0)
    high = gate.astype(bf16)
    rest = (gate - high.astype(f32)).astype(bf16)
    table = jnp.concatenate([rank[:TAB].astype(bf16), high[:TAB], rest[:TAB]], axis=1)
    out_ref[0:toks, :] = cot_ref[...]
    out_ref[toks : toks + TAB, :] = table
    for k in range(copies_ref.shape[0]):
        copies_ref[k, 0:toks, :] = cot_ref[...]
        copies_ref[k, toks : toks + TAB, :] = table


def attn_fwd_kernel(
    heads,
    place_ref,
    x0,
    x1,
    x2,
    x3,
    gain_ref,
    w_ref,
    cos_ref,
    sin_ref,
    prow_ref,
    q_ref,
    k_ref,
    v_ref,
    pt_ref,
    m0,
    m1,
    m2,
    m3,
    bias_ref,
    pbuf,
    obuf,
    vt_ref,
    sems,
):
    toks = x0.shape[0]
    width = heads * HEAD_DIM
    slots = 4
    seq = slots * toks
    swap = partner_matrix(width)
    wq, wk, wv = w_ref[0], w_ref[1], w_ref[2]
    wq_swap = dot(swap, wq, 0, 0).astype(bf16)
    wk_swap = dot(swap, wk, 0, 0).astype(bf16)
    piece_col = jnp.broadcast_to(prow_ref[...].astype(f32), (8, seq)).T[:, :1]
    for slot, x_ref in enumerate((x0, x1, x2, x3)):
        start = pl.multiple_of(place_ref[slot] * toks, toks)
        rows = pl.ds(start, toks)
        _, _, act = normed(x_ref[...].astype(f32), gain_row(gain_ref))
        cosine, sine = cos_ref[rows, :], sin_ref[rows, :]
        queries = (dot(act, wq, 1, 1) * cosine + dot(act, wq_swap, 1, 1) * sine).astype(bf16)
        queries = (queries.astype(f32) * HEAD_DIM**-0.5).astype(bf16)
        keys = (dot(act, wk, 1, 1) * cosine + dot(act, wk_swap, 1, 1) * sine).astype(bf16)
        values = dot(act, wv, 1, 1).astype(bf16)
        for h in range(heads):
            cols = slice(h * HEAD_DIM, (h + 1) * HEAD_DIM)
            q_ref[h, rows, :] = queries[:, cols]
            k_ref[h, rows, :] = keys[:, cols]
            v_ref[h, rows, :] = values[:, cols]

    for h in range(heads):
        vt_ref[h] = v_ref[h].astype(f32).T.astype(bf16)

    def copy_out(block, h, slot):
        keys = visible(block, slots) * toks
        return pltpu.make_async_copy(
            pbuf.at[slot, 0:keys], pt_ref.at[block * heads + h, 0:keys], sems.at[slot]
        )

    for block in range(slots):
        keys = visible(block, slots) * toks
        cols = slice(block * toks, (block + 1) * toks)
        kpos = lax.broadcasted_iota(jnp.int32, (keys, toks), 0)
        qpos = lax.broadcasted_iota(jnp.int32, (keys, toks), 1) + block * toks
        qp = prow_ref[:, cols].astype(f32)
        same = (piece_col[:keys] == qp) & (qp > 0.0)
        bias_ref[0:keys] = jnp.where((kpos <= qpos) | same, 0.0, masked_score)

        for h in range(heads):
            step = block * heads + h
            slot = step % 2
            scores = dot(k_ref[h, 0:keys], q_ref[h, cols, :], 1, 1) + bias_ref[0:keys]
            peak = jnp.max(scores, axis=0, keepdims=True)
            weights = jnp.exp(scores - peak)
            mass = jnp.sum(weights, axis=0, keepdims=True)
            probs = (weights * (1.0 / mass)).astype(bf16)
            if step >= 2:
                copy_out((step - 2) // heads, (step - 2) % heads, slot).wait()
            pbuf[slot, 0:keys] = probs
            copy_out(block, h, slot).start()
            obuf[block, h * HEAD_DIM : (h + 1) * HEAD_DIM, :] = dot(vt_ref[h, :, 0:keys], probs)
    for slot, m_ref in enumerate((m0, m1, m2, m3)):
        m_ref[...] = obuf[place_ref[slot]].T.astype(bf16)
    for step in (slots * heads - 2, slots * heads - 1):
        copy_out(step // heads, step % heads, step % 2).wait()


def visible(block, slots):
    return min(block + 2, slots)


def attn_bwd_kernel(
    heads,
    place_ref,
    x0,
    x1,
    x2,
    x3,
    g0,
    g1,
    g2,
    g3,
    gain_ref,
    w_ref,
    cos_ref,
    sin_ref,
    cost_ref,
    sint_ref,
    q_ref,
    k_ref,
    v_ref,
    pt_ref,
    sums_ref,
    keep_ref,
    send_ref,
    dw_ref,
    done_ref,
    act_ref,
    go_ref,
    qcat_ref,
    kcat_ref,
    dk_ref,
    dv_ref,
    dqt_ref,
    dlin_ref,
    pbuf,
    sems,
):
    toks = x0.shape[0]
    width = heads * HEAD_DIM
    slots = 4
    total_steps = slots * heads

    def copy_in(step):
        keys = visible(step // heads, slots) * toks
        return pltpu.make_async_copy(
            pt_ref.at[step, 0:keys], pbuf.at[step % 2, 0:keys], sems.at[step % 2]
        )

    copy_in(0).start()
    copy_in(1).start()
    swap = partner_matrix(HEAD_DIM)
    both = jnp.concatenate([eye(HEAD_DIM), swap], axis=1)
    swap_i = lax.broadcasted_iota(jnp.int32, (2 * HEAD_DIM, HEAD_DIM), 0)
    swap_j = lax.broadcasted_iota(jnp.int32, (2 * HEAD_DIM, HEAD_DIM), 1)
    low = ((swap_i - HEAD_DIM) < HEAD_DIM // 2) & (swap_i >= HEAD_DIM)
    high = (swap_i - HEAD_DIM) >= HEAD_DIM // 2
    stacked = (
        jnp.where(swap_i == swap_j, 1.0, 0.0)
        + jnp.where(low & (swap_j == swap_i - HEAD_DIM + HEAD_DIM // 2), -1.0, 0.0)
        + jnp.where(high & (swap_j == swap_i - HEAD_DIM - HEAD_DIM // 2), 1.0, 0.0)
    ).astype(bf16)
    for slot, (x_ref, g_ref) in enumerate(zip((x0, x1, x2, x3), (g0, g1, g2, g3))):
        rows = pl.ds(pl.multiple_of(place_ref[slot] * toks, toks), toks)
        _, _, act = normed(x_ref[...].astype(f32), gain_row(gain_ref))
        act_ref[rows, :] = act
        for h in range(heads):
            go_ref[h, rows, :] = g_ref[:, h * HEAD_DIM : (h + 1) * HEAD_DIM]
    for h in range(heads):
        qcat_ref[h] = dot(q_ref[h], both).astype(bf16)
        kcat_ref[h] = dot(stacked, k_ref[h], 1, 1).astype(bf16)
    dk_ref[...] = jnp.zeros(dk_ref.shape, f32)
    dv_ref[...] = jnp.zeros(dv_ref.shape, f32)

    for step in range(total_steps):
        block, h = step // heads, step % heads
        keys = visible(block, slots) * toks
        cols = slice(block * toks, (block + 1) * toks)
        copy_in(step).wait()
        probs = pbuf[step % 2, 0:keys]
        grad_out = go_ref[h, cols, :]
        grad_probs = dot(v_ref[h, 0:keys], grad_out, 1, 1)
        probs_f = probs.astype(f32)
        inner = jnp.sum(probs_f * grad_probs, axis=0, keepdims=True)
        grad_scores = (probs_f * (grad_probs - inner)).astype(bf16)
        dv_ref[h, 0:keys] += dot(probs, grad_out)
        dk_ref[h, 0:keys] += dot(grad_scores, qcat_ref[h, cols, :])
        dqt_ref[block, h] = dot(kcat_ref[h, :, 0:keys], grad_scores)
        if step + 2 < total_steps:
            copy_in(step + 2).start()
    for h in range(heads):
        cols = slice(h * HEAD_DIM, (h + 1) * HEAD_DIM)
        for block in range(slots):
            rows = slice(block * toks, (block + 1) * toks)
            both_t = dqt_ref[block, h]
            lin_t = (
                both_t[:HEAD_DIM] * cost_ref[:, rows] - both_t[HEAD_DIM:] * sint_ref[:, rows]
            ) * HEAD_DIM**-0.5
            dlin_ref[0, rows, cols] = lin_t.T.astype(bf16)
        cosine, sine = cos_ref[:, :HEAD_DIM], sin_ref[:, :HEAD_DIM]
        dlin_ref[1, :, cols] = (
            dk_ref[h, :, :HEAD_DIM] * cosine - dk_ref[h, :, HEAD_DIM:] * sine
        ).astype(bf16)
        dlin_ref[2, :, cols] = dv_ref[h].astype(bf16)
    for k in range(3):
        dw_ref[k * width : (k + 1) * width, :] = dot(
            dlin_ref[k], act_ref[...], 0, 0
        ).astype(bf16)
    gain_grad = jnp.zeros((1, D), f32)
    for slot, x_ref in enumerate((x0, x1, x2, x3)):
        rows = pl.ds(pl.multiple_of(place_ref[slot] * toks, toks), toks)
        part = dot(dlin_ref[0, rows, :], w_ref[0])
        part += dot(dlin_ref[1, rows, :], w_ref[1])
        part += dot(dlin_ref[2, rows, :], w_ref[2])
        unit, _, _ = normed(x_ref[...].astype(f32), gain_row(gain_ref))
        gain_grad += jnp.sum(part * unit, axis=0, keepdims=True)
        if slot % 2 == 0:
            keep_ref[slot // 2] = part.astype(bf16)
        else:
            send_ref[slot // 2] = part.astype(bf16)
    rest = dw_ref.shape[0] - 4 * width
    ids = lax.broadcasted_iota(jnp.int32, (8, D), 0)
    tail = jnp.where(ids == 3, gain_grad, sums_ref[...])
    dw_ref[3 * width : 4 * width, :] = jnp.zeros((width, D), bf16)
    dw_ref[4 * width :, :] = jnp.zeros((rest, D), bf16)
    dw_ref[4 * width : 4 * width + 8, :] = tail.astype(bf16)
    done_ref[...] = jnp.zeros(done_ref.shape, f32)


def attn_fwd(place, x_slots, gain, w, cosine, sine, pieces):
    toks, width = x_slots[0].shape[0], w.shape[1]
    slots = len(x_slots)
    seq, heads = slots * toks, width // HEAD_DIM
    head_shape = jax.ShapeDtypeStruct((heads, seq, HEAD_DIM), bf16)
    return pl.pallas_call(
        functools.partial(attn_fwd_kernel, heads),
        out_shape=[head_shape] * 3
        + [jax.ShapeDtypeStruct((slots * heads, seq, toks), bf16)]
        + [jax.ShapeDtypeStruct((toks, width), bf16)] * slots,
        in_specs=[SM] + [VM] * 9,
        out_specs=[VM] * 3 + [HB] + [VM] * slots,
        scratch_shapes=[
            pltpu.VMEM((seq, toks), f32),
            pltpu.VMEM((2, seq, toks), bf16),
            pltpu.VMEM((slots, width, toks), f32),
            pltpu.VMEM((heads, HEAD_DIM, seq), bf16),
            pltpu.SemaphoreType.DMA((2,)),
        ],
        compiler_params=params(),
        name="attn_fwd",
        cost_estimate=cost(20),
    )(place, *x_slots, gain, w, cosine, sine, pieces)


def attn_bwd(place, x_slots, grads, gain, w, tables, saved, sums, dw_rows):
    toks, width = x_slots[0].shape[0], w.shape[1]
    slots = len(x_slots)
    seq, heads = slots * toks, width // HEAD_DIM
    return pl.pallas_call(
        functools.partial(attn_bwd_kernel, heads),
        out_shape=[
            jax.ShapeDtypeStruct((2, toks, D), bf16),
            jax.ShapeDtypeStruct((2, toks, D), bf16),
            jax.ShapeDtypeStruct((dw_rows, D), bf16),
            jax.ShapeDtypeStruct((8, 128), f32),
        ],
        in_specs=[SM] + [VM] * 17 + [HB, VM],
        out_specs=[VM] * 4,
        scratch_shapes=[
            pltpu.VMEM((seq, D), bf16),
            pltpu.VMEM((heads, seq, HEAD_DIM), bf16),
            pltpu.VMEM((heads, seq, 2 * HEAD_DIM), bf16),
            pltpu.VMEM((heads, 2 * HEAD_DIM, seq), bf16),
            pltpu.VMEM((heads, seq, 2 * HEAD_DIM), f32),
            pltpu.VMEM((heads, seq, HEAD_DIM), f32),
            pltpu.VMEM((slots, heads, 2 * HEAD_DIM, toks), f32),
            pltpu.VMEM((3, seq, width), bf16),
            pltpu.VMEM((2, seq, toks), bf16),
            pltpu.SemaphoreType.DMA((2,)),
        ],
        compiler_params=params(),
        name="attn_bwd",
        cost_estimate=cost(22),
    )(place, *x_slots, *grads, gain, w, *tables, *saved, sums)


def out_proj_kernel(
    x_ref, m0, m1, m2, m3, w0, w1, w2, w3, gain_ref, resid_ref, n_ref, top_ref, low_ref, copies_ref
):
    attended = dot(m0[...], w0[...])
    attended += dot(m1[...], w1[...])
    attended += dot(m2[...], w2[...])
    attended += dot(m3[...], w3[...])
    resid = x_ref[...].astype(f32) + attended
    resid_ref[...] = resid
    _, _, act = normed(resid, gain_row(gain_ref))
    half = act.shape[0] // 2
    n_ref[...] = act
    top_ref[...] = act[:half]
    low_ref[...] = act[half:]
    for k in range(copies_ref.shape[0]):
        copies_ref[k] = act


def route_columns(base_ref, routes_ref, gates_ref, toks):
    base = pl.multiple_of(base_ref[0], toks)
    routes = routes_ref[:, pl.ds(base, toks)].astype(f32)
    rows = jnp.concatenate([routes, gates_ref[...], jnp.zeros((4, toks), f32)], axis=0)
    return rows.T, routes


def expert_gate(columns, expert):
    return jnp.where(columns[:, 0:1] == expert, columns[:, 2:3], 0.0) + jnp.where(
        columns[:, 1:2] == expert, columns[:, 3:4], 0.0
    )


def mid_kernel(
    base_ref,
    dx_refs,
    cot_ref,
    resid_ref,
    routes_ref,
    gates_ref,
    gain_ref,
    m_refs,
    w_refs,
    gres_ref,
    g_refs,
    o_refs,
    sums_ref,
):
    toks = cot_ref.shape[0]
    cot = cot_ref[...].astype(f32)
    columns, _ = route_columns(base_ref, routes_ref, gates_ref, toks)
    halves = [dx_refs[k][...].astype(f32) + dx_refs[k + 1][...].astype(f32) for k in (0, 2)]
    grad = jnp.concatenate(halves, axis=0) + expert_gate(columns, E_FFN + 1) * cot
    gain = gain_row(gain_ref)
    unit, inverse, _ = normed(resid_ref[...], gain)
    grad_unit = grad * gain
    grad_resid = cot + inverse * (
        grad_unit - unit * jnp.mean(grad_unit * unit, axis=-1, keepdims=True)
    )
    gres_ref[...] = grad_resid
    grad_att = grad_resid.astype(bf16)
    for k, (m_ref, w_ref, g_ref) in enumerate(zip(m_refs, w_refs, g_refs)):
        g_ref[...] = dot(grad_att, w_ref[...], 1, 1).astype(bf16)
        o_refs[k % 2][k // 2] = dot(m_ref[...], grad_att, 0, 0).astype(bf16)
    sums_ref[...] = jnp.zeros(sums_ref.shape, f32)
    sums_ref[0:1, :] = jnp.sum(grad * unit, axis=0, keepdims=True)
    for k in range(2):
        weight = expert_gate(columns, E_FFN + 2 + k)
        sums_ref[1 + k : 2 + k, :] = jnp.sum(weight * cot, axis=0, keepdims=True)


def out_kernel(
    base_ref,
    y_refs,
    cot_ref,
    resid_ref,
    n_ref,
    routes_ref,
    gates_ref,
    const_ref,
    out_ref,
    gg_ref,
):
    toks = cot_ref.shape[0]
    half = toks // 2
    cot = cot_ref[...].astype(f32)
    columns, routes = route_columns(base_ref, routes_ref, gates_ref, toks)
    act = n_ref[...].astype(f32)
    consts = const_ref[...].astype(f32)
    top = y_refs[0][...].astype(f32) + y_refs[1][...].astype(f32)
    low = y_refs[2][...].astype(f32) + y_refs[3][...].astype(f32)
    moe = jnp.concatenate([top, low[:half]], axis=0) + expert_gate(columns, E_FFN + 1) * act
    moe += expert_gate(columns, E_FFN + 2) * consts[0:1]
    moe += expert_gate(columns, E_FFN + 3) * consts[1:2]
    out_ref[...] = (resid_ref[...] + moe).astype(bf16)
    dots = [cot * act, cot * consts[0:1], cot * consts[1:2]]
    dots = [jnp.sum(v, axis=1, keepdims=True) for v in dots]
    dots = jnp.concatenate([jnp.broadcast_to(dots[k % 3], (toks, 1)) for k in range(8)], axis=1).T
    table = low[half : half + TAB, 0:toks]
    for pair in range(2):
        route = routes[pair : pair + 1]
        result = jnp.zeros((1, toks), f32)
        for e in range(E_FFN):
            result += jnp.where(route == e, table[e : e + 1], 0.0)
        for k in range(3):
            result += jnp.where(route == E_FFN + 1 + k, dots[k : k + 1], 0.0)
        gg_ref[pair : pair + 1, :] = result


def last_kernel(gno_a, gno_b, x_ref, gres_ref, gain_ref, out_ref):
    grad = gno_a[...].astype(f32) + gno_b[...].astype(f32)
    gain = gain_row(gain_ref)
    unit, inverse, _ = normed(x_ref[...].astype(f32), gain)
    grad_unit = grad * gain
    out_ref[...] = gres_ref[...] + inverse * (
        grad_unit - unit * jnp.mean(grad_unit * unit, axis=-1, keepdims=True)
    )


def dispatch_block(first, experts, x, p_ref, tab_ref, rows_ref, gate_ref, offs, starts, block):
    toks = x.shape[0]
    tab_ref[...] = p_ref[toks : toks + TAB, :].astype(f32)
    want = lax.broadcasted_iota(jnp.int32, (SHORT, toks), 0).astype(f32)
    cot = p_ref[0:toks, :]

    def select(i, begin):
        row = tab_ref[pl.ds(first + i, 1), :]
        match = (want + begin) == row[:, 0:toks]
        gate = row[:, toks : 2 * toks] + row[:, 2 * toks : 3 * toks]
        weight = jnp.sum(jnp.where(match, gate, 0.0), axis=1, keepdims=True)
        return jnp.where(match, 1.0, 0.0).astype(bf16), weight, row[:, 0:toks]

    def put(i, off, rows_x, rows_c, weight):
        at = pl.ds(pl.multiple_of(off, 16), SHORT)
        rows_ref[i, at, 0:D] = rows_x.astype(bf16)
        rows_ref[i, at, D : 2 * D] = (rows_c * weight).astype(bf16)
        if gate_ref is not None:
            gate_ref[i, at, :] = jnp.broadcast_to(weight, (SHORT, 128))

    parts = [select(i, 0.0) for i in range(experts)]
    counts = [jnp.max(rank).astype(jnp.int32) + 1 for _, _, rank in parts]
    hot = jnp.concatenate([p[0] for p in parts], axis=0)
    rows_x, rows_c = dot(hot, x), dot(hot, cot)
    for i in range(experts):
        off = offs[i]
        if starts is not None:
            starts[block, i] = off
        seg = slice(i * SHORT, (i + 1) * SHORT)
        put(i, off, rows_x[seg], rows_c[seg], parts[i][1])

        @pl.when(counts[i] > SHORT)
        def _(i=i, off=off):
            rest, weight, _ = select(i, float(SHORT))
            put(i, off + SHORT, dot(rest, x), dot(rest, cot), weight)

        offs[i] = off + ((counts[i] + 15) // 16) * 16


def expert_acts(rows, wg, wu, wd):
    act, grad = rows[:, :D], rows[:, D:]
    gate_pre = dot(act, wg)
    up_pre = dot(act, wu)
    grad_hidden = dot(grad, wd, 1, 1)
    sig = 1.0 / (1.0 + jnp.exp(-gate_pre))
    silu = gate_pre * sig
    hidden = (silu * up_pre).astype(bf16)
    grad_gate = (grad_hidden * up_pre * sig * (1.0 + gate_pre * (1.0 - sig))).astype(bf16)
    grad_up = (grad_hidden * silu).astype(bf16)
    return act, grad, hidden, grad_hidden, grad_gate, grad_up


def own_kernel(nb, tile, first_ref, *refs):
    tops, lows, ps = refs[:nb], refs[nb : 2 * nb], refs[2 * nb : 3 * nb]
    wg_h, wu_h, wd_h, dxa, dxb, ya, yb, rows_out, used = refs[3 * nb : 3 * nb + 9]
    (
        xbuf,
        pbuf,
        wg,
        wu,
        wd,
        rows_ref,
        back_ref,
        gate_ref,
        tab_ref,
        dxbuf,
        ybuf,
        offs,
        starts,
        tok_sems,
        w_sems,
        out_sems,
        row_sem,
    ) = refs[3 * nb + 9 :]
    experts = wg.shape[0]
    toks = xbuf.shape[1]
    half = nb // 2
    first = first_ref[0]
    mid = toks // 2

    def tok_copies(b, src):
        return (
            pltpu.make_async_copy(tops[src], xbuf.at[b, 0:mid], tok_sems.at[0, b]),
            pltpu.make_async_copy(lows[src], xbuf.at[b, mid:toks], tok_sems.at[1, b]),
            pltpu.make_async_copy(ps[src], pbuf.at[b], tok_sems.at[2, b]),
        )

    w_copies = [
        pltpu.make_async_copy(src, dst, w_sems.at[k])
        for k, (src, dst) in enumerate(((wg_h, wg), (wu_h, wu), (wd_h, wd)))
    ]
    for b in range(nb):
        for copy in tok_copies(b, b):
            copy.start()
    for copy in w_copies:
        copy.start()
    for i in range(experts):
        offs[i] = 0

    def dispatch_body(b, carry):
        for copy in tok_copies(b, 0):
            copy.wait()
        dispatch_block(
            first, experts, xbuf[b], pbuf.at[b], tab_ref, rows_ref, gate_ref, offs, starts, b
        )
        return carry

    lax.fori_loop(0, nb, dispatch_body, 0)
    for i in range(experts):
        at = pl.ds(pl.multiple_of(offs[i], 16), TILE_BACK)
        rows_ref[i, at, :] = jnp.zeros((TILE_BACK, 2 * D), bf16)
        back_ref[i, at, :] = jnp.zeros((TILE_BACK, 2 * D), bf16)
        gate_ref[i, at, :] = jnp.zeros((TILE_BACK, 128), f32)
        used[i] = offs[i]
    rows_copy = pltpu.make_async_copy(rows_ref, rows_out, row_sem)
    rows_copy.start()
    for copy in w_copies:
        copy.wait()

    def expert_body(e, carry):
        def tile_body(j, inner):
            at = pl.ds(pl.multiple_of(j * tile, 16), tile)
            rows = rows_ref[e, at, :]
            _, _, hidden, grad_hidden, grad_gate, grad_up = expert_acts(rows, wg[e], wu[e], wd[e])
            weight = gate_ref[e, at, :]
            product = jnp.sum(hidden.astype(f32) * grad_hidden, axis=1, keepdims=True)
            gate_ref[e, at, :] = jnp.where(weight > 0.0, product / jnp.maximum(weight, 0.125), 0.0)
            back_ref[e, at, 0:D] = (
                dot(grad_gate, wg[e], 1, 1) + dot(grad_up, wu[e], 1, 1)
            ).astype(bf16)
            back_ref[e, at, D : 2 * D] = (dot(hidden, wd[e]) * weight[:, :1]).astype(bf16)
            return inner

        return lax.fori_loop(0, (offs[e] + tile - 1) // tile, tile_body, carry)

    lax.fori_loop(0, experts, expert_body, 0)

    def out_copies(b, slot):
        near = b < half
        return near, (
            pltpu.make_async_copy(dxbuf.at[slot], dxa.at[b % half], out_sems.at[0, slot]),
            pltpu.make_async_copy(ybuf.at[slot], ya.at[b % half], out_sems.at[1, slot]),
        ), (
            pltpu.make_async_copy(dxbuf.at[slot], dxb.at[b % half], out_sems.at[0, slot]),
            pltpu.make_async_copy(ybuf.at[slot], yb.at[b % half], out_sems.at[1, slot]),
        )

    def wait_slot(slot):
        pltpu.make_async_copy(dxbuf.at[slot], dxa.at[0], out_sems.at[0, slot]).wait()
        pltpu.make_async_copy(ybuf.at[slot], ya.at[0], out_sems.at[1, slot]).wait()

    want = lax.broadcasted_iota(jnp.int32, (SEG, toks), 0).astype(f32)
    tab_rows = lax.broadcasted_iota(jnp.int32, (TAB, toks), 0)

    def combine_body(b, carry):
        slot = b % 2

        @pl.when(b >= 2)
        def _():
            wait_slot(slot)

        tab_ref[...] = pbuf[b, toks : toks + TAB, :].astype(f32)
        hots, segs = [], []
        table = jnp.zeros((TAB, toks), f32)
        for i in range(experts):
            rank = tab_ref[pl.ds(first + i, 1), 0:toks]
            match = jnp.where(want == rank, 1.0, 0.0)
            at = pl.ds(pl.multiple_of(starts[b, i], 16), SEG)
            hots.append(match.astype(bf16))
            segs.append(back_ref[i, at, :])
            line = jnp.sum(match * gate_ref[i, at, :][:, :1], axis=0, keepdims=True)
            table += jnp.where(tab_rows == first + i, line, 0.0)
        result = dot(jnp.concatenate(hots, axis=0), jnp.concatenate(segs, axis=0), 0, 0)
        dxbuf[slot] = result[:, :D].astype(bf16)
        ybuf[slot, 0:toks, :] = result[:, D:].astype(bf16)
        ybuf[slot, toks : toks + TAB, 0:toks] = table.astype(bf16)
        ybuf[slot, toks : toks + TAB, toks:] = jnp.zeros((TAB, D - toks), bf16)
        near, here, there = out_copies(b, slot)

        @pl.when(near)
        def _():
            here[0].start()
            here[1].start()

        @pl.when(jnp.logical_not(near))
        def _():
            there[0].start()
            there[1].start()

        return carry

    lax.fori_loop(0, nb, combine_body, 0)
    wait_slot(0)
    wait_slot(1)
    rows_copy.wait()


def dispatch_kernel(pieces, arrays, tile, first_ref, *refs):
    srcs, refs = refs[:arrays], refs[arrays:]
    rows_out, used, xbuf, pbuf, rows_ref, tab_ref, offs, tok_sems, row_sem = refs
    experts = rows_ref.shape[0]
    ring = xbuf.shape[0]
    first = first_ref[0]
    total = sum(p[0] for p in pieces)

    def start_block(b):
        slot = b % ring
        begin = 0
        for blocks, x_parts, p_parts in pieces:

            @pl.when((b >= begin) & (b < begin + blocks))
            def _(begin=begin, x_parts=x_parts, p_parts=p_parts):
                for which, (parts, buf) in enumerate(((x_parts, xbuf), (p_parts, pbuf))):
                    for array, at, lo, hi in parts:
                        pltpu.make_async_copy(
                            srcs[array].at[b - begin + at],
                            buf.at[slot, lo:hi],
                            tok_sems.at[which, slot],
                        ).start()

            begin += blocks

    for b in range(min(ring - 1, total)):
        start_block(jnp.int32(b))
    for i in range(experts):
        offs[i] = 0

    def dispatch_body(b, carry):
        slot = b % ring
        pltpu.make_async_copy(xbuf.at[slot], xbuf.at[slot], tok_sems.at[0, slot]).wait()
        pltpu.make_async_copy(pbuf.at[slot], pbuf.at[slot], tok_sems.at[1, slot]).wait()

        @pl.when(b + ring - 1 < total)
        def _():
            start_block(b + ring - 1)

        dispatch_block(
            first, experts, xbuf[slot], pbuf.at[slot], tab_ref, rows_ref, None, offs, None, b
        )
        return carry

    lax.fori_loop(0, total, dispatch_body, 0)

    def chunk(i, j):
        at = pl.ds(pl.multiple_of(j * tile, tile), tile)
        return pltpu.make_async_copy(rows_ref.at[i, at], rows_out.at[i, at], row_sem)

    def chunks(i):
        return jnp.maximum((offs[i] + tile - 1) // tile, 1)

    def start_chunk(i):
        def body(j, carry):
            chunk(i, j).start()
            return carry

        return body

    def wait_chunk(i):
        def body(j, carry):
            chunk(i, j).wait()
            return carry

        return body

    for i in range(experts):
        rows_ref[i, pl.ds(pl.multiple_of(offs[i], 16), tile), :] = jnp.zeros((tile, 2 * D), bf16)
        used[i] = offs[i]
        lax.fori_loop(0, chunks(i), start_chunk(i), 0)
    for i in range(experts):
        lax.fori_loop(0, chunks(i), wait_chunk(i), 0)


def weight_kernel(tile, begin_e, experts, given, add, used_ref, rows_h, wg_h, wu_h, wd_h, *refs):
    olds, refs = (refs[:3], refs[3:]) if given else ((), refs)
    outs, accs = refs[:3], refs[3:6]
    rbuf, wg, wu, wd, row_sems, w_sems, acc_sems = refs[6:]
    w_copies = [
        pltpu.make_async_copy(src.at[begin_e : begin_e + experts], dst, w_sems.at[k])
        for k, (src, dst) in enumerate(((wg_h, wg), (wu_h, wu), (wd_h, wd)))
    ]

    def tiles(e):
        return jnp.maximum((used_ref[begin_e + e] + tile - 1) // tile, 1)

    def fetch(e, j, slot):
        at = pl.ds(pl.multiple_of(j * tile, tile), tile)
        return pltpu.make_async_copy(
            rows_h.at[begin_e + e, at], rbuf.at[slot], row_sems.at[slot]
        )

    def out_copies(e):
        return [
            pltpu.make_async_copy(src, dst.at[e + begin_e], acc_sems.at[k])
            for k, (src, dst) in enumerate(zip(accs, outs))
        ]

    def old_copies(e):
        return [
            pltpu.make_async_copy(src.at[e + begin_e], dst, acc_sems.at[k])
            for k, (src, dst) in enumerate(zip(olds, accs))
        ]

    fetch(0, 0, 0).start()
    for copy in w_copies:
        copy.start()
    if add:
        for copy in old_copies(0):
            copy.start()
    for copy in w_copies:
        copy.wait()

    def expert_body(e, count):
        last = tiles(e)

        def tile_body(j, step):
            slot = step % 2
            fetch(e, j, slot).wait()

            @pl.when(j + 1 < last)
            def _():
                fetch(e, j + 1, 1 - slot).start()

            @pl.when((j + 1 == last) & (e + 1 < experts))
            def _():
                fetch(e + 1, 0, 1 - slot).start()

            rows = rbuf[slot]
            act, grad, hidden, _, grad_gate, grad_up = expert_acts(rows, wg[e], wu[e], wd[e])
            part = dot(act, jnp.concatenate([grad_gate, grad_up], axis=1), 0, 0)
            width = grad_gate.shape[1]
            down = dot(hidden, grad, 0, 0)
            parts = (part[:, :width], part[:, width:], down)

            @pl.when(j == 0)
            def _():
                @pl.when(e > 0)
                def _():
                    for copy in out_copies(e - 1):
                        copy.wait()
                    if add:
                        for copy in old_copies(e):
                            copy.start()

                if add:
                    for copy, acc, value in zip(old_copies(e), accs, parts):
                        copy.wait()
                        acc[...] += value
                else:
                    for acc, value in zip(accs, parts):
                        acc[...] = value

            @pl.when(j > 0)
            def _():
                for acc, value in zip(accs, parts):
                    acc[...] += value

            return step + 1

        count = lax.fori_loop(0, last, tile_body, count)
        for copy in out_copies(e):
            copy.start()
        return count

    lax.fori_loop(0, experts, expert_body, jnp.int32(0))
    for copy in out_copies(experts - 1):
        copy.wait()


def row_room(cap, blocks, groups, tile):
    most = groups * min(cap + 15 * blocks, SEG * blocks)
    return -(-most // tile) * tile + tile


def own_experts(first, tops, lows, ps, wg, wu, wd, cap):
    nb = len(ps)
    experts = wg.shape[0]
    toks = ps[0].shape[0] - TAB
    room = row_room(cap, nb, 1, TILE_BACK)
    half = nb // 2
    shapes = [
        jax.ShapeDtypeStruct((half, toks, D), bf16),
        jax.ShapeDtypeStruct((half, toks, D), bf16),
        jax.ShapeDtypeStruct((half, toks + TAB, D), bf16),
        jax.ShapeDtypeStruct((half, toks + TAB, D), bf16),
        jax.ShapeDtypeStruct((experts, room, 2 * D), bf16),
        jax.ShapeDtypeStruct((experts,), jnp.int32),
    ]
    return pl.pallas_call(
        functools.partial(own_kernel, nb, TILE_OWN),
        out_shape=shapes,
        in_specs=[SM] + [HB] * (3 * nb + 3),
        out_specs=[HB] * 5 + [SM],
        scratch_shapes=[
            pltpu.VMEM((nb, toks, D), bf16),
            pltpu.VMEM((nb, toks + TAB, D), bf16),
            pltpu.VMEM(wg.shape, bf16),
            pltpu.VMEM(wu.shape, bf16),
            pltpu.VMEM(wd.shape, bf16),
            pltpu.VMEM((experts, room, 2 * D), bf16),
            pltpu.VMEM((experts, room, 2 * D), bf16),
            pltpu.VMEM((experts, room, 128), f32),
            pltpu.VMEM((TAB, D), f32),
            pltpu.VMEM((2, toks, D), bf16),
            pltpu.VMEM((2, toks + TAB, D), bf16),
            pltpu.SMEM((experts,), jnp.int32),
            pltpu.SMEM((nb, experts), jnp.int32),
            pltpu.SemaphoreType.DMA((3, nb)),
            pltpu.SemaphoreType.DMA((3,)),
            pltpu.SemaphoreType.DMA((2, 2)),
            pltpu.SemaphoreType.DMA,
        ],
        compiler_params=params(),
        name="own_experts",
        cost_estimate=cost(29),
    )(first, *tops, *lows, *ps, wg, wu, wd)


def chip_pieces(x_sets, p_sets, blocks, toks):
    flat = [a for sets in (x_sets, p_sets) for arrays in sets for a in arrays]
    half = toks // 2
    x_count = x_sets[0][0].shape[0] // blocks
    pieces = []
    for k in range(4 * x_count):
        core, x, y = k // (2 * x_count), k // 2 % x_count, k % 2
        parts, base = [], 0
        for sets, end in ((x_sets, toks), (p_sets, toks + TAB)):
            top, low = base + core * 2 + y, base + len(sets[0]) + core * x_count + x
            parts.append(((top, x * blocks, 0, half), (low, y * blocks, half, end)))
            base += len(sets[0]) + len(sets[1])
        pieces.append((blocks, *parts))
    return flat, pieces


def dispatch(first, flat, pieces, toks, experts, cap, groups):
    total = sum(p[0] for p in pieces)
    ring = 4
    room = row_room(cap, total // groups, groups, TILE_FAR)
    return pl.pallas_call(
        functools.partial(dispatch_kernel, tuple(pieces), len(flat), TILE_FAR),
        out_shape=[
            jax.ShapeDtypeStruct((experts, room, 2 * D), bf16),
            jax.ShapeDtypeStruct((experts,), jnp.int32),
        ],
        in_specs=[SM] + [HB] * len(flat),
        out_specs=[HB, SM],
        scratch_shapes=[
            pltpu.VMEM((ring, toks, D), bf16),
            pltpu.VMEM((ring, toks + TAB, D), bf16),
            pltpu.VMEM((experts, room, 2 * D), bf16),
            pltpu.VMEM((TAB, D), f32),
            pltpu.SMEM((experts,), jnp.int32),
            pltpu.SemaphoreType.DMA((2, ring)),
            pltpu.SemaphoreType.DMA,
        ],
        compiler_params=params(),
        name="dispatch",
        cost_estimate=cost(20),
    )(first, *flat)


def weight_grads(used, rows, weights, tile, olds=None, add=True, begin_e=0, count_e=None):
    experts = count_e or weights[0].shape[0]
    shapes = [jax.ShapeDtypeStruct(w.shape, f32) for w in weights]
    operands = [used, rows, *weights, *(olds or ())]
    return pl.pallas_call(
        functools.partial(weight_kernel, tile, begin_e, experts, bool(olds), bool(olds) and add),
        out_shape=shapes,
        in_specs=[SM] + [HB] * (len(operands) - 1),
        out_specs=[HB] * 3,
        input_output_aliases={len(operands) - 3 + k: k for k in range(3)} if olds else {},
        scratch_shapes=[
            *[pltpu.VMEM(w.shape[1:], f32) for w in weights],
            pltpu.VMEM((2, tile, 2 * D), bf16),
            *[pltpu.VMEM((experts, *w.shape[1:]), bf16) for w in weights],
            pltpu.SemaphoreType.DMA((2,)),
            pltpu.SemaphoreType.DMA((3,)),
            pltpu.SemaphoreType.DMA((3,)),
        ],
        compiler_params=params(),
        name="weight_grads",
        cost_estimate=cost(14),
    )(*operands)


def after(value, *deps):
    return lax.optimization_barrier((value, *deps))[0]


def after_all(values, *deps):
    return lax.optimization_barrier((*values, *deps))[: len(values)]


def after_tree(tree, *deps):
    return lax.optimization_barrier((tree, *deps))[0]


def other_groups(copies, cut):
    count, index = lax.axis_size("dp"), lax.axis_index("dp")
    blocks = lax.all_to_all(copies, "dp", 0, 0, tiled=True)

    def pick(blocks, rows):
        found = [
            lax.dynamic_index_in_dim(blocks, (index + step) % count, 0)[:, rows]
            for step in range(1, count)
        ]
        return jnp.concatenate(found, axis=0)

    return blocks, lambda b: (pick(b, slice(0, cut)), pick(b, slice(cut, None)))


def gather_line(values, axis):
    out = list(values)
    for step in range(1, lax.axis_size(axis)):
        out += [shift(v, axis, step) for v in values]
    return out


def with_line(values, axis):
    return gather_line([jnp.concatenate(values, axis=0)], axis)


def plane_gather(value, x_first):
    if x_first:
        cols = gather_line([value], "x")
        rows = [shift(v, "y", 1) for v in cols]
        return [v for pair in zip(cols, rows) for v in pair]
    return gather_line(gather_line([value], "y"), "x")


def both_cores(values, *deps):
    return list(values) + [shift(after(v, *deps) if deps else v, "c", 1) for v in values]


def total(*parts):
    return sum(p.astype(f32) for p in parts).astype(bf16)


def scatter_cores(parts):
    return parts[0], shift(parts[1], "c", -1)


def scatter_first(keep, other, cut):
    count = lax.axis_size("x")

    def add(rows, where):
        return total(keep[where][:, rows], other[where][:, rows])

    top, low = slice(0, cut), slice(cut, None)
    x_sent = [add(top, slice(2 * k, 2 * k + 2)) for k in range(1, count)]
    y_sent = add(low, slice(1, None, 2))
    x_kept = add(top, slice(0, 2))
    y_kept = add(low, slice(0, None, 2))
    x_got = [shift(v, "x", -k) for k, v in zip(range(1, count), x_sent)]
    y_got = shift(y_sent, "y", -1)
    return (*x_got, y_got), x_kept, y_kept


def scatter_second(got, x_kept, y_kept):
    x_got, y_got = got[:-1], got[-1]
    count = len(got)
    y_next = total(x_kept[1], *[v[1] for v in x_got])
    x_next = [total(y_kept[k], y_got[k]) for k in range(1, count)]
    top_own = total(x_kept[0], *[v[0] for v in x_got])
    low_own = total(y_kept[0], y_got[0])
    top_far = shift(y_next, "y", -1)
    low_far = [shift(v, "x", -k) for k, v in zip(range(1, count), x_next)]
    if count > 2:
        low_far = [total(*low_far)]
    return top_own, top_far, low_own, low_far[0]


def line_sum(value, axis):
    return sum([shift(value, axis, step) for step in range(1, lax.axis_size(axis))], value)


def row_sum(value):
    far = lax.ppermute(value, ("y", "c"), [(i, 3 - i) for i in range(4)])
    return value + shift(value, "c", 1) + shift(value, "y", 1) + far


def scatter_sum(value, axis):
    count, index = lax.axis_size(axis), lax.axis_index(axis)
    chunks = value.reshape((count, value.shape[0] // count) + value.shape[1:])
    result = lax.dynamic_index_in_dim(chunks, index, 0, keepdims=False).astype(f32)
    for step in range(1, count):
        chunk = lax.dynamic_index_in_dim(chunks, (index + step) % count, 0, keepdims=False)
        result = result + shift(chunk, axis, step).astype(f32)
    return result.astype(bf16)


def gather_chunks(own, axis):
    count, index = lax.axis_size(axis), lax.axis_index(axis)
    full = jnp.zeros((count,) + own.shape, bf16)
    full = lax.dynamic_update_index_in_dim(full, own, index, 0)
    for step in range(1, count):
        chunk = shift(own, axis, step)
        full = lax.dynamic_update_index_in_dim(full, chunk, (index - step) % count, 0)
    return full.reshape((count * own.shape[0],) + own.shape[1:])


def shards(
    inputs,
    cotangent,
    gain_attn,
    gain_ffn,
    attn_in,
    attn_out,
    expert_gate,
    expert_up,
    expert_down,
    const_vectors,
    gate_values,
    routes,
    priority,
    pieces,
):
    toks = inputs.shape[1]
    y_index, c_index = lax.axis_index("y"), lax.axis_index("c")
    x_index, x_count = lax.axis_index("x"), lax.axis_size("x")
    dp_count = lax.axis_size("dp")
    row_count = lax.axis_size("y") * lax.axis_size("c")
    seq = toks * row_count
    heads = attn_in.shape[2] // HEAD_DIM
    width = heads * HEAD_DIM
    group_tokens = routes.shape[1]
    nb = group_tokens // toks
    cap = 5 * group_tokens // 24
    experts = expert_gate.shape[0]
    x_own, cot = inputs[0], cotangent[0]
    place = jnp.stack(
        [
            ((y_index - ky) % 2) * 2 + (c_index - kc) % 2
            for ky in range(2)
            for kc in range(2)
        ]
    ).astype(jnp.int32)
    first = (x_index * experts).astype(jnp.int32)[None]
    base = (x_index * seq + (y_index * 2 + c_index) * toks).astype(jnp.int32)[None]

    x_y = shift(x_own, "y", 1)
    w_y = shift(after(attn_out, x_y), "y", 1)

    cosine, sine = rotary_numpy(seq, heads)
    cos_t, sin_t = cosine[:, :HEAD_DIM].T.copy(), sine[:, :HEAD_DIM].T.copy()
    cosine, sine, cos_t, sin_t = (jnp.asarray(a) for a in (cosine, sine, cos_t, sin_t))
    routes_t, gates_t = routes[0].T, gate_values[0].T
    attn_w = attn_in.transpose(0, 2, 1)
    weights = (expert_gate, expert_up, expert_down)
    half = toks // 2
    far = list(range(1, dp_count))
    one_call = dp_count * group_tokens <= CALL_TOKENS

    payload, p_copies = pl.pallas_call(
        functools.partial(route_kernel, cap),
        out_shape=[
            jax.ShapeDtypeStruct((toks + TAB, D), bf16),
            jax.ShapeDtypeStruct((dp_count if one_call else 1, toks + TAB, D), bf16),
        ],
        in_specs=[SM, VM, VM, VM, VM],
        out_specs=[VM, VM],
        compiler_params=params(),
        name="route",
        cost_estimate=cost(2.5),
    )(base, routes_t, priority, gates_t, cot)
    if one_call:
        far_p, split_p = other_groups(p_copies, half)
    x_slots = [x_own, shift(x_own, "c", 1), x_y, shift(after(x_y, payload), "c", 1)]
    p_cols = gather_line([payload], "x")
    p_y = shift(after(payload, x_y), "y", 1)

    mix_shape = jax.ShapeDtypeStruct((toks, width), bf16)
    fwd_out = attn_fwd(after(place, payload), x_slots, gain_attn, attn_w, cosine, sine, pieces)
    fwd_out = after_all(fwd_out, *p_cols, p_y, w_y)
    q, k, v, probs, *mixed = fwd_out

    def to_owner(parts):
        return [
            parts[0],
            shift(parts[1], "c", -1),
            shift(parts[2], "y", -1),
            lax.ppermute(parts[3], ("y", "c"), [(i, 3 - i) for i in range(4)]),
        ]

    started = mixed[0]
    w_slots = [attn_out, w_y]
    w_slots = [v for w in w_slots for v in (w, shift(after(w, started), "c", 1))]
    own_p = [p_cols[0], p_y]
    for step, p in enumerate(p_cols[1:], 1):
        own_p += [p, shift(after(p_y, started), "x", step)]
    own_p = both_cores(own_p, started)
    if one_call:
        p_top, p_low = split_p(after(far_p, started))
        p_top_x = gather_line([p_top], "x")
    mixed = to_owner(mixed)
    resid, norm_two, norm_top, norm_low, x_copies = pl.pallas_call(
        out_proj_kernel,
        out_shape=[
            jax.ShapeDtypeStruct((toks, D), f32),
            jax.ShapeDtypeStruct((toks, D), bf16),
            jax.ShapeDtypeStruct((half, D), bf16),
            jax.ShapeDtypeStruct((half, D), bf16),
            jax.ShapeDtypeStruct((dp_count if one_call else 1, toks, D), bf16),
        ],
        in_specs=[VM] * 10,
        out_specs=[VM] * 5,
        compiler_params=params(),
        name="out_proj",
        cost_estimate=cost(3),
    )(x_own, *mixed, *w_slots, gain_ffn)

    tops = plane_gather(norm_top, True)
    lows = plane_gather(norm_low, False)
    arrived = (tops[-1], lows[-1])
    ready = ()
    if one_call:
        far_x, split_x = other_groups(x_copies, half)
        p_low_y = gather_line([p_low], "y")
        ready = (p_top_x[-1], p_low_y[-1])
        p_top = with_line(after_all(p_top_x, *arrived), "y")
        p_low = with_line(after_all(p_low_y, *arrived), "x")
    tops, lows = both_cores(tops), both_cores(lows)
    own_out = own_experts(after(first, *ready), tops, lows, own_p, *weights, cap)
    if one_call:
        own_out = after_all(own_out, *p_top, *p_low, far_x)
    dxa, dxb, ya, yb, rows, used = own_out
    dx_first = scatter_first(*scatter_cores((dxa, dxb)), half)
    dx_stage = dx_first[0][-1]
    dx_parts = scatter_second(*dx_first)
    if one_call:
        p_near = [shift(after(a[0], dx_first[1]), "c", 1) for a in (p_top, p_low)]
    front = max(1, experts // 2)
    grads_w = weight_grads(after(used, dx_first[1]), rows, weights, TILE_BACK, count_e=front)
    if one_call:
        x_top, x_low = split_x(after(far_x, dx_stage, grads_w[0]))
        x_top_x = gather_line([x_top], "x")
        x_low_y = gather_line([x_low], "y")
        used = after(used, *p_near)
    for begin in range(front, experts, front):
        grads_w = weight_grads(
            after(used, dx_stage), rows, weights, TILE_BACK, grads_w, False, begin, front
        )

    gres, *mids = pl.pallas_call(
        lambda base_ref, *refs: mid_kernel(
            base_ref,
            refs[0:4],
            *refs[4:9],
            refs[9:13],
            refs[13:17],
            refs[17],
            refs[18:22],
            refs[22:24],
            refs[24],
        ),
        out_shape=[jax.ShapeDtypeStruct((toks, D), f32)]
        + [mix_shape] * 4
        + [jax.ShapeDtypeStruct((2, width, D), bf16)] * 2
        + [jax.ShapeDtypeStruct((8, D), f32)],
        in_specs=[SM] + [VM] * 17,
        out_specs=[VM] * 8,
        compiler_params=params(),
        name="mid",
        cost_estimate=cost(5),
    )(
        after(base, grads_w[0], *((*x_top_x, *x_low_y) if one_call else ())),
        *dx_parts,
        cot,
        resid,
        routes_t,
        gates_t,
        gain_ffn,
        *mixed,
        *w_slots,
    )
    out_keep, out_send, sums = mids[4:]
    grads = to_owner(mids[:4])
    out_other = shift(out_send, "c", -1)
    out_sent = total(out_keep[1], out_other[1])
    out_far = shift(out_sent, "y", -1)
    ready = ()
    if one_call:
        ready = (x_top_x[-1], x_low_y[-1])
        x_top = with_line(after_all(x_top_x, *grads, out_sent), "y")
        x_low = with_line(after_all(x_low_y, *grads, out_sent), "x")
        p_other = [shift(after(a[1], *grads), "c", 1) for a in (p_top, p_low)]
    tables = (cosine, sine, cos_t, sin_t)
    unit = 8 * x_count * dp_count
    dw_rows = -(-(4 * width + 8) // unit) * unit
    saved = (q, k, v, probs)
    bwd_out = attn_bwd(
        place, x_slots, grads, gain_attn, attn_w, tables, saved, sums, dw_rows
    )
    if one_call:
        bwd_out = after_all(bwd_out, *x_top, *x_low, *p_other, out_far)
    gno_keep, gno_send, dw_in, gain_part = bwd_out
    gno_other = shift(gno_send, "c", -1)
    gno_far = (gno_keep[1].astype(f32) + gno_other[1].astype(f32)).astype(bf16)
    gno_near = (gno_keep[0].astype(f32) + gno_other[0].astype(f32)).astype(bf16)

    dw_out = total(out_keep[0], out_other[0], out_far)
    attn_grads = lax.dynamic_update_slice(dw_in, dw_out, (3 * width, 0))
    y_stage = scatter_cores(after_all((ya, yb), gno_other))
    gno_far = shift(gno_far, "y", -1)

    if one_call:
        x_near = [shift(after(a[0], gain_part), "c", 1) for a in (x_top, x_low)]
        x_other = [shift(after(a[1], gain_part), "c", 1) for a in (x_top, x_low)]
        x_sets = [[*a, n, o] for a, n, o in zip((x_top, x_low), x_near, x_other)]
        p_sets = [[*a, n, o] for a, n, o in zip((p_top, p_low), p_near, p_other)]
        flat, spots = chip_pieces(x_sets, p_sets, len(far), toks)
        part = scatter_sum(after(attn_grads, *x_near, *x_other), "x")
        rows, used = dispatch(after(first, gain_part), flat, spots, toks, experts, cap, len(far))
        used = after(used, part, gno_far, *y_stage)
        part, y_stage = after_tree((part, y_stage), used)
        part = scatter_sum(part, "dp")
        y_stage = scatter_first(*y_stage, half)
        for e in range(experts):
            grads_w = weight_grads(used, rows, weights, TILE_FAR, grads_w, True, e, 1)
            if e == 0:
                used = after(used, grads_w[0], part, *y_stage[0])
                part = gather_chunks(after(part, used), "dp")
            elif e == 1:
                used = after(used, grads_w[0], part)
                part, y_stage = after_tree((part, y_stage), used)
                attn_grads = gather_chunks(part, "x")
                y_parts = scatter_second(*y_stage)
            elif e == 2:
                used = after(used, grads_w[0], attn_grads, *y_parts)
                sums = row_sum(attn_grads[4 * width : 4 * width + 4].astype(f32))
            elif e == 3:
                grads_w = after_all(grads_w, sums)
    else:
        part = scatter_sum(scatter_sum(attn_grads, "x"), "dp")
        attn_grads = gather_chunks(gather_chunks(part, "dp"), "x")
        sums = row_sum(attn_grads[4 * width : 4 * width + 4].astype(f32))
        y_parts = scatter_second(*scatter_first(*y_stage, half))
        spots = [(nb, ((0, 0, 0, toks),), ((1, 0, 0, toks + TAB),))]

        def next_group(step, carry):
            x_block, p_block, *sums_w = carry
            x_block, p_block = shift(x_block, "dp", 1), shift(p_block, "dp", 1)
            flat = [lax.all_gather(a, ("y", "c", "x")) for a in (x_block, p_block)]
            rows, used = dispatch(first, flat, spots, toks, experts, cap, 1)
            return x_block, p_block, *weight_grads(used, rows, weights, TILE_FAR, sums_w)

        grads_w = lax.fori_loop(1, dp_count, next_group, (norm_two, payload, *grads_w))[2:]
    grad_w_gate, grad_w_up, grad_w_down = grads_w
    grad_w_in = attn_grads[: 3 * width].astype(f32).reshape(3, width, D).transpose(0, 2, 1)
    grad_w_out = attn_grads[3 * width : 4 * width].astype(f32)
    input_grad = pl.pallas_call(
        last_kernel,
        out_shape=jax.ShapeDtypeStruct((toks, D), f32),
        in_specs=[VM] * 5,
        out_specs=VM,
        compiler_params=params(),
        name="last",
        cost_estimate=cost(3),
    )(gno_near, gno_far, x_own, gres, gain_attn)

    block_out, grad_gates = pl.pallas_call(
        lambda base_ref, *refs: out_kernel(base_ref, refs[0:4], *refs[4:]),
        out_shape=[
            jax.ShapeDtypeStruct((toks, D), bf16),
            jax.ShapeDtypeStruct((2, toks), f32),
        ],
        in_specs=[SM] + [VM] * 10,
        out_specs=[VM] * 2,
        compiler_params=params(),
        name="block_out",
        cost_estimate=cost(3),
    )(base, *y_parts, cot, resid, norm_two, routes_t, gates_t, const_vectors)

    return (
        block_out[None],
        input_grad[None],
        sums[3],
        sums[0],
        grad_w_in,
        grad_w_out,
        grad_w_gate,
        grad_w_up,
        grad_w_down,
        sums[1:3],
        grad_gates.T[None],
    )


def solution(mesh):
    dp, row, col = mesh.devices.shape
    fine = Mesh(mesh.devices.reshape(dp, row // 2, 2, col), ("dp", "y", "c", "x"))
    rows = ("y", "c")
    in_specs = (
        P(("dp", "x"), rows, None),
        P(("dp", "x"), rows, None),
        P(),
        P(),
        P(None, None, rows),
        P(rows, None),
        P("x", None, rows),
        P("x", None, rows),
        P("x", rows, None),
        P(),
        P(("dp", "x"), rows, None),
        P("dp", None, None),
        P("dp", None),
        P(("dp", "x"), None),
    )
    out_specs = (
        P(("dp", "x"), rows, None),
        P(("dp", "x"), rows, None),
        P(),
        P(),
        P(None, None, rows),
        P(rows, None),
        P("x", None, rows),
        P("x", None, rows),
        P("x", rows, None),
        P(),
        P(("dp", "x"), rows, None),
    )
    return jax.shard_map(shards, mesh=fine, in_specs=in_specs, out_specs=out_specs, check_vma=False)
```

```python
import functools

import jax
import jax.numpy as jnp
import numpy as np
from jax import lax
from jax.experimental import pallas as pl
from jax.experimental.pallas import tpu as pltpu
from jax.sharding import Mesh
from jax.sharding import PartitionSpec as P

D = 768
HEAD_DIM = 64
E_FFN = 8
MOST = 88
SHORT = 48
SEG = 96
TAB = 8
TILE_OWN = 192
TILE_BACK = 256
TILE_FAR = 512
CALL_TOKENS = 8192

norm_eps = 1e-05
masked_score = -1e30
bf16 = jnp.bfloat16
f32 = jnp.float32
VMEM_MAX = 60 * 1024 * 1024


def dot(a, b, ca=1, cb=0):
    return lax.dot_general(a, b, (((ca,), (cb,)), ((), ())), preferred_element_type=f32)


def params(**kw):
    return pltpu.CompilerParams(vmem_limit_bytes=VMEM_MAX, **kw)


def cost(micros):
    return pl.CostEstimate(
        flops=int(micros * 1.1e9), transcendentals=0, bytes_accessed=int(micros * 3.5e6)
    )


VM = pl.BlockSpec(memory_space=pltpu.VMEM)
SM = pl.BlockSpec(memory_space=pltpu.SMEM)
HB = pl.BlockSpec(memory_space=pl.ANY)


def shift(value, axis, step):
    count = lax.axis_size(axis)
    return lax.ppermute(value, axis, [(i, (i + step) % count) for i in range(count)])


def gain_row(ref):
    return ref[...].reshape(1, D)


def normed(rows, gain):
    inverse = lax.rsqrt(jnp.mean(rows * rows, axis=-1, keepdims=True) + norm_eps)
    unit = rows * inverse
    return unit, inverse, (unit * gain).astype(bf16)


def rotary_numpy(length):
    half = HEAD_DIM // 2
    frequency = (10000.0 ** (-np.arange(half, dtype=np.float32) / half)).astype(np.float32)
    angles = frequency[:, None] * np.arange(length, dtype=np.float32)[None, :]
    cosine = np.tile(np.cos(angles), (2, 1)).astype(np.float32)
    sine = np.tile(np.sin(angles), (2, 1)).astype(np.float32)
    return cosine, sine


def partner_matrix(width):
    i = lax.broadcasted_iota(jnp.int32, (width, width), 0)
    j = lax.broadcasted_iota(jnp.int32, (width, width), 1)
    low = (j % HEAD_DIM) < HEAD_DIM // 2
    minus = jnp.where(low & (i == j + HEAD_DIM // 2), -1.0, 0.0)
    plus = jnp.where((~low) & (i == j - HEAD_DIM // 2), 1.0, 0.0)
    return (minus + plus).astype(bf16)


def eye(width):
    i = lax.broadcasted_iota(jnp.int32, (width, width), 0)
    j = lax.broadcasted_iota(jnp.int32, (width, width), 1)
    return jnp.where(i == j, 1.0, 0.0).astype(bf16)


def route_kernel(cap, base_ref, routes_ref, prio_ref, gates_ref, cot_ref, out_ref, copies_ref):
    total = prio_ref.shape[1]
    toks = cot_ref.shape[0]
    base = pl.multiple_of(base_ref[0], toks)
    prio = prio_ref[...].astype(f32)
    own_row = prio_ref[:, pl.ds(base, toks)].astype(f32)
    own_col = jnp.broadcast_to(own_row, (8, toks)).T[:, :1]
    earlier = jnp.where(prio < own_col, 1.0, 0.0).astype(bf16)
    ids = lax.broadcasted_iota(jnp.int32, (16, total), 0)
    named = (routes_ref[0:1, :] == ids) | (routes_ref[1:2, :] == ids)
    slots = dot(jnp.where(named, 1.0, 0.0).astype(bf16), earlier, 1, 1)
    own_ids = lax.broadcasted_iota(jnp.int32, (16, toks), 0)
    first = routes_ref[0:1, pl.ds(base, toks)] == own_ids
    second = routes_ref[1:2, pl.ds(base, toks)] == own_ids
    kept = (first | second) & (own_ids < E_FFN) & (slots < cap)
    before_i = lax.broadcasted_iota(jnp.int32, (toks, toks), 0)
    before_j = lax.broadcasted_iota(jnp.int32, (toks, toks), 1)
    lower = jnp.where(before_i < before_j, 1.0, 0.0).astype(bf16)
    rank = dot(jnp.where(kept, 1.0, 0.0).astype(bf16), lower)
    rank = jnp.where(kept, rank, -1.0)
    gate = jnp.where(first, gates_ref[0:1, :], 0.0) + jnp.where(second, gates_ref[1:2, :], 0.0)
    high = gate.astype(bf16)
    rest = (gate - high.astype(f32)).astype(bf16)
    table = jnp.concatenate([rank[:TAB].astype(bf16), high[:TAB], rest[:TAB]], axis=1)
    out_ref[0:toks, :] = cot_ref[...]
    out_ref[toks : toks + TAB, :] = table
    for k in range(copies_ref.shape[0]):
        copies_ref[k, 0:toks, :] = cot_ref[...]
        copies_ref[k, toks : toks + TAB, :] = table


def attn_fwd_kernel(
    heads,
    place_ref,
    x0,
    x1,
    x2,
    x3,
    gain_ref,
    w_ref,
    cos_ref,
    sin_ref,
    prow_ref,
    q_ref,
    k_ref,
    v_ref,
    pt_ref,
    m0,
    m1,
    m2,
    m3,
    bias_ref,
    pbuf,
    obuf,
    vt_ref,
    sems,
):
    toks = x0.shape[0]
    width = heads * HEAD_DIM
    slots = 4
    seq = slots * toks
    swap = partner_matrix(width)
    wq, wk, wv = w_ref[0], w_ref[1], w_ref[2]
    wq_swap = dot(swap, wq, 0, 0).astype(bf16)
    wk_swap = dot(swap, wk, 0, 0).astype(bf16)
    piece_col = jnp.broadcast_to(prow_ref[...].astype(f32), (8, seq)).T[:, :1]
    for slot, x_ref in enumerate((x0, x1, x2, x3)):
        start = pl.multiple_of(place_ref[slot] * toks, toks)
        rows = pl.ds(start, toks)
        _, _, act = normed(x_ref[...].astype(f32), gain_row(gain_ref))
        cosine = jnp.concatenate([cos_ref[:, rows].T] * heads, axis=1)
        sine = jnp.concatenate([sin_ref[:, rows].T] * heads, axis=1)
        queries = (dot(act, wq, 1, 1) * cosine + dot(act, wq_swap, 1, 1) * sine).astype(bf16)
        queries = (queries.astype(f32) * HEAD_DIM**-0.5).astype(bf16)
        keys = (dot(act, wk, 1, 1) * cosine + dot(act, wk_swap, 1, 1) * sine).astype(bf16)
        values = dot(act, wv, 1, 1).astype(bf16)
        for h in range(heads):
            cols = slice(h * HEAD_DIM, (h + 1) * HEAD_DIM)
            q_ref[h, rows, :] = queries[:, cols]
            k_ref[h, rows, :] = keys[:, cols]
            v_ref[h, rows, :] = values[:, cols]

    for h in range(heads):
        vt_ref[h] = v_ref[h].astype(f32).T.astype(bf16)

    def copy_out(block, h):
        keys = visible(block, slots) * toks
        return pltpu.make_async_copy(
            pbuf.at[h, 0:keys], pt_ref.at[block * heads + h, 0:keys], sems.at[h]
        )

    for block in range(slots):
        keys = visible(block, slots) * toks
        cols = slice(block * toks, (block + 1) * toks)
        kpos = lax.broadcasted_iota(jnp.int32, (keys, toks), 0)
        qpos = lax.broadcasted_iota(jnp.int32, (keys, toks), 1) + block * toks
        qp = prow_ref[:, cols].astype(f32)
        same = (piece_col[:keys] == qp) & (qp > 0.0)
        bias_ref[0:keys] = jnp.where((kpos <= qpos) | same, 0.0, masked_score)

        def head_body(h, carry, block=block, keys=keys, cols=cols):
            scores = dot(k_ref[h, 0:keys], q_ref[h, cols, :], 1, 1) + bias_ref[0:keys]
            peak = jnp.max(scores, axis=0, keepdims=True)
            weights = jnp.exp(scores - peak)
            mass = jnp.sum(weights, axis=0, keepdims=True)
            probs = (weights * (1.0 / mass)).astype(bf16)
            if block > 0:
                copy_out(block - 1, h).wait()
            pbuf[h, 0:keys] = probs
            copy_out(block, h).start()
            at = pl.ds(pl.multiple_of(h * HEAD_DIM, HEAD_DIM), HEAD_DIM)
            obuf[block, at, :] = dot(vt_ref[h, :, 0:keys], probs)
            return carry

        lax.fori_loop(0, heads, head_body, 0)
    for slot, m_ref in enumerate((m0, m1, m2, m3)):
        m_ref[...] = obuf[place_ref[slot]].T.astype(bf16)
    for h in range(heads):
        copy_out(slots - 1, h).wait()


def visible(block, slots):
    return min(block + 2, slots)


def attn_bwd_kernel(
    heads,
    place_ref,
    x0,
    x1,
    x2,
    x3,
    g0,
    g1,
    g2,
    g3,
    gain_ref,
    w_ref,
    cost_ref,
    sint_ref,
    q_ref,
    k_ref,
    v_ref,
    pt_ref,
    sums_ref,
    keep_ref,
    send_ref,
    dw_ref,
    done_ref,
    act_ref,
    go_ref,
    qcat_ref,
    kcat_ref,
    dk_ref,
    dv_ref,
    dqt_ref,
    dlin_ref,
    pbuf,
    sems,
):
    toks = x0.shape[0]
    width = heads * HEAD_DIM
    slots = 4

    def copy_in(block, h):
        keys = visible(block, slots) * toks
        return pltpu.make_async_copy(
            pt_ref.at[block * heads + h, 0:keys], pbuf.at[h, 0:keys], sems.at[h]
        )

    for h in range(heads):
        copy_in(0, h).start()
    swap = partner_matrix(HEAD_DIM)
    both = jnp.concatenate([eye(HEAD_DIM), swap], axis=1)
    swap_i = lax.broadcasted_iota(jnp.int32, (2 * HEAD_DIM, HEAD_DIM), 0)
    swap_j = lax.broadcasted_iota(jnp.int32, (2 * HEAD_DIM, HEAD_DIM), 1)
    low = ((swap_i - HEAD_DIM) < HEAD_DIM // 2) & (swap_i >= HEAD_DIM)
    high = (swap_i - HEAD_DIM) >= HEAD_DIM // 2
    stacked = (
        jnp.where(swap_i == swap_j, 1.0, 0.0)
        + jnp.where(low & (swap_j == swap_i - HEAD_DIM + HEAD_DIM // 2), -1.0, 0.0)
        + jnp.where(high & (swap_j == swap_i - HEAD_DIM - HEAD_DIM // 2), 1.0, 0.0)
    ).astype(bf16)
    for slot, (x_ref, g_ref) in enumerate(zip((x0, x1, x2, x3), (g0, g1, g2, g3))):
        rows = pl.ds(pl.multiple_of(place_ref[slot] * toks, toks), toks)
        _, _, act = normed(x_ref[...].astype(f32), gain_row(gain_ref))
        act_ref[rows, :] = act
        for h in range(heads):
            go_ref[h, rows, :] = g_ref[:, h * HEAD_DIM : (h + 1) * HEAD_DIM]
    for h in range(heads):
        qcat_ref[h] = dot(q_ref[h], both).astype(bf16)
        kcat_ref[h] = dot(stacked, k_ref[h], 1, 1).astype(bf16)
    dk_ref[...] = jnp.zeros(dk_ref.shape, f32)
    dv_ref[...] = jnp.zeros(dv_ref.shape, f32)

    for block in range(slots):
        keys = visible(block, slots) * toks
        cols = slice(block * toks, (block + 1) * toks)

        def head_body(h, carry, block=block, keys=keys, cols=cols):
            copy_in(block, h).wait()
            probs = pbuf[h, 0:keys]
            grad_out = go_ref[h, cols, :]
            grad_probs = dot(v_ref[h, 0:keys], grad_out, 1, 1)
            probs_f = probs.astype(f32)
            inner = jnp.sum(probs_f * grad_probs, axis=0, keepdims=True)
            grad_scores = (probs_f * (grad_probs - inner)).astype(bf16)
            dv_ref[h, 0:keys] += dot(probs, grad_out)
            dk_ref[h, 0:keys] += dot(grad_scores, qcat_ref[h, cols, :])
            dqt_ref[block, h] = dot(kcat_ref[h, :, 0:keys], grad_scores)
            if block + 1 < slots:
                copy_in(block + 1, h).start()
            return carry

        lax.fori_loop(0, heads, head_body, 0)
    cosine, sine = cost_ref[...].T, sint_ref[...].T
    for h in range(heads):
        cols = slice(h * HEAD_DIM, (h + 1) * HEAD_DIM)
        for block in range(slots):
            rows = slice(block * toks, (block + 1) * toks)
            both_t = dqt_ref[block, h]
            lin_t = (
                both_t[:HEAD_DIM] * cost_ref[:, rows] - both_t[HEAD_DIM:] * sint_ref[:, rows]
            ) * HEAD_DIM**-0.5
            dlin_ref[0, rows, cols] = lin_t.T.astype(bf16)
        dlin_ref[1, :, cols] = (
            dk_ref[h, :, :HEAD_DIM] * cosine - dk_ref[h, :, HEAD_DIM:] * sine
        ).astype(bf16)
        dlin_ref[2, :, cols] = dv_ref[h].astype(bf16)
    for k in range(3):
        dw_ref[k * width : (k + 1) * width, :] = dot(
            dlin_ref[k], act_ref[...], 0, 0
        ).astype(bf16)
    gain_grad = jnp.zeros((1, D), f32)
    for slot, x_ref in enumerate((x0, x1, x2, x3)):
        rows = pl.ds(pl.multiple_of(place_ref[slot] * toks, toks), toks)
        part = dot(dlin_ref[0, rows, :], w_ref[0])
        part += dot(dlin_ref[1, rows, :], w_ref[1])
        part += dot(dlin_ref[2, rows, :], w_ref[2])
        unit, _, _ = normed(x_ref[...].astype(f32), gain_row(gain_ref))
        gain_grad += jnp.sum(part * unit, axis=0, keepdims=True)
        if slot % 2 == 0:
            keep_ref[slot // 2] = part.astype(bf16)
        else:
            send_ref[slot // 2] = part.astype(bf16)
    rest = dw_ref.shape[0] - 4 * width
    ids = lax.broadcasted_iota(jnp.int32, (8, D), 0)
    tail = jnp.where(ids == 3, gain_grad, sums_ref[...])
    dw_ref[3 * width : 4 * width, :] = jnp.zeros((width, D), bf16)
    dw_ref[4 * width :, :] = jnp.zeros((rest, D), bf16)
    dw_ref[4 * width : 4 * width + 8, :] = tail.astype(bf16)
    done_ref[...] = jnp.zeros(done_ref.shape, f32)


def attn_fwd(place, x_slots, gain, w, cosine, sine, pieces):
    toks, width = x_slots[0].shape[0], w.shape[1]
    slots = len(x_slots)
    seq, heads = slots * toks, width // HEAD_DIM
    head_shape = jax.ShapeDtypeStruct((heads, seq, HEAD_DIM), bf16)
    return pl.pallas_call(
        functools.partial(attn_fwd_kernel, heads),
        out_shape=[head_shape] * 3
        + [jax.ShapeDtypeStruct((slots * heads, seq, toks), bf16)]
        + [jax.ShapeDtypeStruct((toks, width), bf16)] * slots,
        in_specs=[SM] + [VM] * 9,
        out_specs=[VM] * 3 + [HB] + [VM] * slots,
        scratch_shapes=[
            pltpu.VMEM((seq, toks), f32),
            pltpu.VMEM((heads, seq, toks), bf16),
            pltpu.VMEM((slots, width, toks), f32),
            pltpu.VMEM((heads, HEAD_DIM, seq), bf16),
            pltpu.SemaphoreType.DMA((heads,)),
        ],
        compiler_params=params(),
        name="attn_fwd",
        cost_estimate=cost(20),
    )(place, *x_slots, gain, w, cosine, sine, pieces)


def attn_bwd(place, x_slots, grads, gain, w, tables, saved, sums, dw_rows):
    toks, width = x_slots[0].shape[0], w.shape[1]
    slots = len(x_slots)
    seq, heads = slots * toks, width // HEAD_DIM
    return pl.pallas_call(
        functools.partial(attn_bwd_kernel, heads),
        out_shape=[
            jax.ShapeDtypeStruct((2, toks, D), bf16),
            jax.ShapeDtypeStruct((2, toks, D), bf16),
            jax.ShapeDtypeStruct((dw_rows, D), bf16),
            jax.ShapeDtypeStruct((8, 128), f32),
        ],
        in_specs=[SM] + [VM] * 15 + [HB, VM],
        out_specs=[VM] * 4,
        scratch_shapes=[
            pltpu.VMEM((seq, D), bf16),
            pltpu.VMEM((heads, seq, HEAD_DIM), bf16),
            pltpu.VMEM((heads, seq, 2 * HEAD_DIM), bf16),
            pltpu.VMEM((heads, 2 * HEAD_DIM, seq), bf16),
            pltpu.VMEM((heads, seq, 2 * HEAD_DIM), f32),
            pltpu.VMEM((heads, seq, HEAD_DIM), f32),
            pltpu.VMEM((slots, heads, 2 * HEAD_DIM, toks), f32),
            pltpu.VMEM((3, seq, width), bf16),
            pltpu.VMEM((heads, seq, toks), bf16),
            pltpu.SemaphoreType.DMA((heads,)),
        ],
        compiler_params=params(),
        name="attn_bwd",
        cost_estimate=cost(22),
    )(place, *x_slots, *grads, gain, w, *tables, *saved, sums)


def out_proj_kernel(
    x_ref, m0, m1, m2, m3, w0, w1, w2, w3, gain_ref, resid_ref, n_ref, top_ref, low_ref, copies_ref
):
    attended = dot(m0[...], w0[...])
    attended += dot(m1[...], w1[...])
    attended += dot(m2[...], w2[...])
    attended += dot(m3[...], w3[...])
    resid = x_ref[...].astype(f32) + attended
    resid_ref[...] = resid
    _, _, act = normed(resid, gain_row(gain_ref))
    half = act.shape[0] // 2
    n_ref[...] = act
    top_ref[...] = act[:half]
    low_ref[...] = act[half:]
    for k in range(copies_ref.shape[0]):
        copies_ref[k] = act


def route_columns(base_ref, routes_ref, gates_ref, toks):
    base = pl.multiple_of(base_ref[0], toks)
    routes = routes_ref[:, pl.ds(base, toks)].astype(f32)
    rows = jnp.concatenate([routes, gates_ref[...], jnp.zeros((4, toks), f32)], axis=0)
    return rows.T, routes


def expert_gate(columns, expert):
    return jnp.where(columns[:, 0:1] == expert, columns[:, 2:3], 0.0) + jnp.where(
        columns[:, 1:2] == expert, columns[:, 3:4], 0.0
    )


def mid_kernel(
    base_ref,
    dx_refs,
    cot_ref,
    resid_ref,
    routes_ref,
    gates_ref,
    gain_ref,
    m_refs,
    w_refs,
    gres_ref,
    g_refs,
    o_refs,
    sums_ref,
):
    toks = cot_ref.shape[0]
    cot = cot_ref[...].astype(f32)
    columns, _ = route_columns(base_ref, routes_ref, gates_ref, toks)
    halves = [dx_refs[k][...].astype(f32) + dx_refs[k + 1][...].astype(f32) for k in (0, 2)]
    grad = jnp.concatenate(halves, axis=0) + expert_gate(columns, E_FFN + 1) * cot
    gain = gain_row(gain_ref)
    unit, inverse, _ = normed(resid_ref[...], gain)
    grad_unit = grad * gain
    grad_resid = cot + inverse * (
        grad_unit - unit * jnp.mean(grad_unit * unit, axis=-1, keepdims=True)
    )
    gres_ref[...] = grad_resid
    grad_att = grad_resid.astype(bf16)
    for k, (m_ref, w_ref, g_ref) in enumerate(zip(m_refs, w_refs, g_refs)):
        g_ref[...] = dot(grad_att, w_ref[...], 1, 1).astype(bf16)
        o_refs[k % 2][k // 2] = dot(m_ref[...], grad_att, 0, 0).astype(bf16)
    sums_ref[...] = jnp.zeros(sums_ref.shape, f32)
    sums_ref[0:1, :] = jnp.sum(grad * unit, axis=0, keepdims=True)
    for k in range(2):
        weight = expert_gate(columns, E_FFN + 2 + k)
        sums_ref[1 + k : 2 + k, :] = jnp.sum(weight * cot, axis=0, keepdims=True)


def out_kernel(
    base_ref,
    y_refs,
    cot_ref,
    resid_ref,
    n_ref,
    routes_ref,
    gates_ref,
    const_ref,
    out_ref,
    gg_ref,
):
    toks = cot_ref.shape[0]
    half = toks // 2
    cot = cot_ref[...].astype(f32)
    columns, routes = route_columns(base_ref, routes_ref, gates_ref, toks)
    act = n_ref[...].astype(f32)
    consts = const_ref[...].astype(f32)
    top = y_refs[0][...].astype(f32) + y_refs[1][...].astype(f32)
    low = y_refs[2][...].astype(f32) + y_refs[3][...].astype(f32)
    moe = jnp.concatenate([top, low[:half]], axis=0) + expert_gate(columns, E_FFN + 1) * act
    moe += expert_gate(columns, E_FFN + 2) * consts[0:1]
    moe += expert_gate(columns, E_FFN + 3) * consts[1:2]
    out_ref[...] = (resid_ref[...] + moe).astype(bf16)
    dots = [cot * act, cot * consts[0:1], cot * consts[1:2]]
    dots = [jnp.sum(v, axis=1, keepdims=True) for v in dots]
    dots = jnp.concatenate([jnp.broadcast_to(dots[k % 3], (toks, 1)) for k in range(8)], axis=1).T
    table = low[half : half + TAB, 0:toks]
    for pair in range(2):
        route = routes[pair : pair + 1]
        result = jnp.zeros((1, toks), f32)
        for e in range(E_FFN):
            result += jnp.where(route == e, table[e : e + 1], 0.0)
        for k in range(3):
            result += jnp.where(route == E_FFN + 1 + k, dots[k : k + 1], 0.0)
        gg_ref[pair : pair + 1, :] = result


def last_kernel(gno_a, gno_b, x_ref, gres_ref, gain_ref, out_ref):
    grad = gno_a[...].astype(f32) + gno_b[...].astype(f32)
    gain = gain_row(gain_ref)
    unit, inverse, _ = normed(x_ref[...].astype(f32), gain)
    grad_unit = grad * gain
    out_ref[...] = gres_ref[...] + inverse * (
        grad_unit - unit * jnp.mean(grad_unit * unit, axis=-1, keepdims=True)
    )


def dispatch_block(first, experts, x, p_ref, tab_ref, rows_ref, gate_ref, offs, starts, block):
    toks = x.shape[0]
    tab_ref[...] = p_ref[toks : toks + TAB, :].astype(f32)
    want = lax.broadcasted_iota(jnp.int32, (SHORT, toks), 0).astype(f32)
    cot = p_ref[0:toks, :]

    def select(i, begin):
        row = tab_ref[pl.ds(first + i, 1), :]
        match = (want + begin) == row[:, 0:toks]
        gate = row[:, toks : 2 * toks] + row[:, 2 * toks : 3 * toks]
        weight = jnp.sum(jnp.where(match, gate, 0.0), axis=1, keepdims=True)
        return jnp.where(match, 1.0, 0.0).astype(bf16), weight, row[:, 0:toks]

    def put(i, off, rows_x, rows_c, weight):
        at = pl.ds(pl.multiple_of(off, 16), SHORT)
        rows_ref[i, at, 0:D] = rows_x.astype(bf16)
        rows_ref[i, at, D : 2 * D] = (rows_c * weight).astype(bf16)
        if gate_ref is not None:
            gate_ref[i, at, :] = jnp.broadcast_to(weight, (SHORT, 128))

    parts = [select(i, 0.0) for i in range(experts)]
    counts = [jnp.max(rank).astype(jnp.int32) + 1 for _, _, rank in parts]
    hot = jnp.concatenate([p[0] for p in parts], axis=0)
    rows_x, rows_c = dot(hot, x), dot(hot, cot)
    for i in range(experts):
        off = offs[i]
        if starts is not None:
            starts[block, i] = off
        seg = slice(i * SHORT, (i + 1) * SHORT)
        put(i, off, rows_x[seg], rows_c[seg], parts[i][1])

        @pl.when(counts[i] > SHORT)
        def _(i=i, off=off):
            rest, weight, _ = select(i, float(SHORT))
            put(i, off + SHORT, dot(rest, x), dot(rest, cot), weight)

        offs[i] = off + ((counts[i] + 15) // 16) * 16


def expert_acts(rows, wg, wu, wd):
    act, grad = rows[:, :D], rows[:, D:]
    gate_pre = dot(act, wg)
    up_pre = dot(act, wu)
    grad_hidden = dot(grad, wd, 1, 1)
    sig = 1.0 / (1.0 + jnp.exp(-gate_pre))
    silu = gate_pre * sig
    hidden = (silu * up_pre).astype(bf16)
    grad_gate = (grad_hidden * up_pre * sig * (1.0 + gate_pre * (1.0 - sig))).astype(bf16)
    grad_up = (grad_hidden * silu).astype(bf16)
    return act, grad, hidden, grad_hidden, grad_gate, grad_up


def own_kernel(nb, tile, first_ref, *refs):
    tops, lows, ps = refs[:nb], refs[nb : 2 * nb], refs[2 * nb : 3 * nb]
    wg_h, wu_h, wd_h, dxa, dxb, ya, yb, rows_out, used = refs[3 * nb : 3 * nb + 9]
    (
        xbuf,
        pbuf,
        wg,
        wu,
        wd,
        rows_ref,
        back_ref,
        gate_ref,
        tab_ref,
        dxbuf,
        ybuf,
        offs,
        starts,
        tok_sems,
        w_sems,
        out_sems,
        row_sem,
    ) = refs[3 * nb + 9 :]
    experts = wg.shape[0]
    toks = xbuf.shape[1]
    half = nb // 2
    first = first_ref[0]
    mid = toks // 2

    def tok_copies(b, src):
        return (
            pltpu.make_async_copy(tops[src], xbuf.at[b, 0:mid], tok_sems.at[0, b]),
            pltpu.make_async_copy(lows[src], xbuf.at[b, mid:toks], tok_sems.at[1, b]),
            pltpu.make_async_copy(ps[src], pbuf.at[b], tok_sems.at[2, b]),
        )

    w_copies = [
        pltpu.make_async_copy(src, dst, w_sems.at[k])
        for k, (src, dst) in enumerate(((wg_h, wg), (wu_h, wu), (wd_h, wd)))
    ]
    for b in range(nb):
        for copy in tok_copies(b, b):
            copy.start()
    for copy in w_copies:
        copy.start()
    for i in range(experts):
        offs[i] = 0

    def dispatch_body(b, carry):
        for copy in tok_copies(b, 0):
            copy.wait()
        dispatch_block(
            first, experts, xbuf[b], pbuf.at[b], tab_ref, rows_ref, gate_ref, offs, starts, b
        )
        return carry

    lax.fori_loop(0, nb, dispatch_body, 0)
    for i in range(experts):
        at = pl.ds(pl.multiple_of(offs[i], 16), TILE_BACK)
        rows_ref[i, at, :] = jnp.zeros((TILE_BACK, 2 * D), bf16)
        back_ref[i, at, :] = jnp.zeros((TILE_BACK, 2 * D), bf16)
        gate_ref[i, at, :] = jnp.zeros((TILE_BACK, 128), f32)
        used[i] = offs[i]
    rows_copy = pltpu.make_async_copy(rows_ref, rows_out, row_sem)
    rows_copy.start()
    for copy in w_copies:
        copy.wait()

    def expert_body(e, carry):
        def tile_body(j, inner):
            at = pl.ds(pl.multiple_of(j * tile, 16), tile)
            rows = rows_ref[e, at, :]
            _, _, hidden, grad_hidden, grad_gate, grad_up = expert_acts(rows, wg[e], wu[e], wd[e])
            weight = gate_ref[e, at, :]
            product = jnp.sum(hidden.astype(f32) * grad_hidden, axis=1, keepdims=True)
            gate_ref[e, at, :] = jnp.where(weight > 0.0, product / jnp.maximum(weight, 0.125), 0.0)
            back_ref[e, at, 0:D] = (
                dot(grad_gate, wg[e], 1, 1) + dot(grad_up, wu[e], 1, 1)
            ).astype(bf16)
            back_ref[e, at, D : 2 * D] = (dot(hidden, wd[e]) * weight[:, :1]).astype(bf16)
            return inner

        return lax.fori_loop(0, (offs[e] + tile - 1) // tile, tile_body, carry)

    lax.fori_loop(0, experts, expert_body, 0)

    def out_copies(b, slot):
        near = b < half
        return near, (
            pltpu.make_async_copy(dxbuf.at[slot], dxa.at[b % half], out_sems.at[0, slot]),
            pltpu.make_async_copy(ybuf.at[slot], ya.at[b % half], out_sems.at[1, slot]),
        ), (
            pltpu.make_async_copy(dxbuf.at[slot], dxb.at[b % half], out_sems.at[0, slot]),
            pltpu.make_async_copy(ybuf.at[slot], yb.at[b % half], out_sems.at[1, slot]),
        )

    def wait_slot(slot):
        pltpu.make_async_copy(dxbuf.at[slot], dxa.at[0], out_sems.at[0, slot]).wait()
        pltpu.make_async_copy(ybuf.at[slot], ya.at[0], out_sems.at[1, slot]).wait()

    want = lax.broadcasted_iota(jnp.int32, (SEG, toks), 0).astype(f32)
    tab_rows = lax.broadcasted_iota(jnp.int32, (TAB, toks), 0)

    def combine_body(b, carry):
        slot = b % 2

        @pl.when(b >= 2)
        def _():
            wait_slot(slot)

        tab_ref[...] = pbuf[b, toks : toks + TAB, :].astype(f32)
        hots, segs = [], []
        table = jnp.zeros((TAB, toks), f32)
        for i in range(experts):
            rank = tab_ref[pl.ds(first + i, 1), 0:toks]
            match = jnp.where(want == rank, 1.0, 0.0)
            at = pl.ds(pl.multiple_of(starts[b, i], 16), SEG)
            hots.append(match.astype(bf16))
            segs.append(back_ref[i, at, :])
            line = jnp.sum(match * gate_ref[i, at, :][:, :1], axis=0, keepdims=True)
            table += jnp.where(tab_rows == first + i, line, 0.0)
        result = dot(jnp.concatenate(hots, axis=0), jnp.concatenate(segs, axis=0), 0, 0)
        dxbuf[slot] = result[:, :D].astype(bf16)
        ybuf[slot, 0:toks, :] = result[:, D:].astype(bf16)
        ybuf[slot, toks : toks + TAB, 0:toks] = table.astype(bf16)
        ybuf[slot, toks : toks + TAB, toks:] = jnp.zeros((TAB, D - toks), bf16)
        near, here, there = out_copies(b, slot)

        @pl.when(near)
        def _():
            here[0].start()
            here[1].start()

        @pl.when(jnp.logical_not(near))
        def _():
            there[0].start()
            there[1].start()

        return carry

    lax.fori_loop(0, nb, combine_body, 0)
    wait_slot(0)
    wait_slot(1)
    rows_copy.wait()


def dispatch_kernel(pieces, arrays, tile, first_ref, *refs):
    srcs, refs = refs[:arrays], refs[arrays:]
    rows_out, used, xbuf, pbuf, rows_ref, tab_ref, offs, tok_sems, row_sem = refs
    experts = rows_ref.shape[0]
    ring = xbuf.shape[0]
    first = first_ref[0]
    total = sum(p[0] for p in pieces)

    def start_block(b):
        slot = b % ring
        begin = 0
        for blocks, x_parts, p_parts in pieces:

            @pl.when((b >= begin) & (b < begin + blocks))
            def _(begin=begin, x_parts=x_parts, p_parts=p_parts):
                for which, (parts, buf) in enumerate(((x_parts, xbuf), (p_parts, pbuf))):
                    for array, at, lo, hi in parts:
                        pltpu.make_async_copy(
                            srcs[array].at[b - begin + at],
                            buf.at[slot, lo:hi],
                            tok_sems.at[which, slot],
                        ).start()

            begin += blocks

    def start_body(b, carry):
        start_block(b)
        return carry

    lax.fori_loop(0, min(ring - 1, total), start_body, 0)
    for i in range(experts):
        offs[i] = 0

    def dispatch_body(b, carry):
        slot = b % ring
        pltpu.make_async_copy(xbuf.at[slot], xbuf.at[slot], tok_sems.at[0, slot]).wait()
        pltpu.make_async_copy(pbuf.at[slot], pbuf.at[slot], tok_sems.at[1, slot]).wait()

        @pl.when(b + ring - 1 < total)
        def _():
            start_block(b + ring - 1)

        dispatch_block(
            first, experts, xbuf[slot], pbuf.at[slot], tab_ref, rows_ref, None, offs, None, b
        )
        return carry

    lax.fori_loop(0, total, dispatch_body, 0)

    def chunk(i, j):
        at = pl.ds(pl.multiple_of(j * tile, tile), tile)
        return pltpu.make_async_copy(rows_ref.at[i, at], rows_out.at[i, at], row_sem)

    def chunks(i):
        return jnp.maximum((offs[i] + tile - 1) // tile, 1)

    def start_chunk(i):
        def body(j, carry):
            chunk(i, j).start()
            return carry

        return body

    def wait_chunk(i):
        def body(j, carry):
            chunk(i, j).wait()
            return carry

        return body

    for i in range(experts):
        rows_ref[i, pl.ds(pl.multiple_of(offs[i], 16), tile), :] = jnp.zeros((tile, 2 * D), bf16)
        used[i] = offs[i]
        lax.fori_loop(0, chunks(i), start_chunk(i), 0)
    for i in range(experts):
        lax.fori_loop(0, chunks(i), wait_chunk(i), 0)


def weight_kernel(tile, experts, given, add, begin_ref, used_ref, rows_h, wg_h, wu_h, wd_h, *refs):
    begin_e = begin_ref[0]
    olds, refs = (refs[:3], refs[3:]) if given else ((), refs)
    outs, accs = refs[:3], refs[3:6]
    rbuf, wg, wu, wd, row_sems, w_sems, acc_sems = refs[6:]
    w_copies = [
        pltpu.make_async_copy(src.at[pl.ds(begin_e, experts)], dst, w_sems.at[k])
        for k, (src, dst) in enumerate(((wg_h, wg), (wu_h, wu), (wd_h, wd)))
    ]

    def tiles(e):
        return jnp.maximum((used_ref[begin_e + e] + tile - 1) // tile, 1)

    def fetch(e, j, slot):
        at = pl.ds(pl.multiple_of(j * tile, tile), tile)
        return pltpu.make_async_copy(
            rows_h.at[begin_e + e, at], rbuf.at[slot], row_sems.at[slot]
        )

    def out_copies(e):
        return [
            pltpu.make_async_copy(src, dst.at[e + begin_e], acc_sems.at[k])
            for k, (src, dst) in enumerate(zip(accs, outs))
        ]

    def old_copies(e):
        return [
            pltpu.make_async_copy(src.at[e + begin_e], dst, acc_sems.at[k])
            for k, (src, dst) in enumerate(zip(olds, accs))
        ]

    fetch(0, 0, 0).start()
    for copy in w_copies:
        copy.start()
    if add:
        for copy in old_copies(0):
            copy.start()
    for copy in w_copies:
        copy.wait()

    def expert_body(e, count):
        last = tiles(e)

        def tile_body(j, step):
            slot = step % 2
            fetch(e, j, slot).wait()

            @pl.when(j + 1 < last)
            def _():
                fetch(e, j + 1, 1 - slot).start()

            @pl.when((j + 1 == last) & (e + 1 < experts))
            def _():
                fetch(e + 1, 0, 1 - slot).start()

            rows = rbuf[slot]
            act, grad, hidden, _, grad_gate, grad_up = expert_acts(rows, wg[e], wu[e], wd[e])
            part = dot(act, jnp.concatenate([grad_gate, grad_up], axis=1), 0, 0)
            width = grad_gate.shape[1]
            down = dot(hidden, grad, 0, 0)
            parts = (part[:, :width], part[:, width:], down)

            @pl.when(j == 0)
            def _():
                @pl.when(e > 0)
                def _():
                    for copy in out_copies(e - 1):
                        copy.wait()
                    if add:
                        for copy in old_copies(e):
                            copy.start()

                if add:
                    for copy, acc, value in zip(old_copies(e), accs, parts):
                        copy.wait()
                        acc[...] += value
                else:
                    for acc, value in zip(accs, parts):
                        acc[...] = value

            @pl.when(j > 0)
            def _():
                for acc, value in zip(accs, parts):
                    acc[...] += value

            return step + 1

        count = lax.fori_loop(0, last, tile_body, count)
        for copy in out_copies(e):
            copy.start()
        return count

    lax.fori_loop(0, experts, expert_body, jnp.int32(0))
    for copy in out_copies(experts - 1):
        copy.wait()


def row_room(cap, blocks, groups, tile):
    most = groups * min(cap + 15 * blocks, SEG * blocks)
    return -(-most // tile) * tile + tile


def own_experts(first, tops, lows, ps, wg, wu, wd, cap):
    nb = len(ps)
    experts = wg.shape[0]
    toks = ps[0].shape[0] - TAB
    room = row_room(cap, nb, 1, TILE_BACK)
    half = nb // 2
    shapes = [
        jax.ShapeDtypeStruct((half, toks, D), bf16),
        jax.ShapeDtypeStruct((half, toks, D), bf16),
        jax.ShapeDtypeStruct((half, toks + TAB, D), bf16),
        jax.ShapeDtypeStruct((half, toks + TAB, D), bf16),
        jax.ShapeDtypeStruct((experts, room, 2 * D), bf16),
        jax.ShapeDtypeStruct((experts,), jnp.int32),
    ]
    return pl.pallas_call(
        functools.partial(own_kernel, nb, TILE_OWN),
        out_shape=shapes,
        in_specs=[SM] + [HB] * (3 * nb + 3),
        out_specs=[HB] * 5 + [SM],
        scratch_shapes=[
            pltpu.VMEM((nb, toks, D), bf16),
            pltpu.VMEM((nb, toks + TAB, D), bf16),
            pltpu.VMEM(wg.shape, bf16),
            pltpu.VMEM(wu.shape, bf16),
            pltpu.VMEM(wd.shape, bf16),
            pltpu.VMEM((experts, room, 2 * D), bf16),
            pltpu.VMEM((experts, room, 2 * D), bf16),
            pltpu.VMEM((experts, room, 128), f32),
            pltpu.VMEM((TAB, D), f32),
            pltpu.VMEM((2, toks, D), bf16),
            pltpu.VMEM((2, toks + TAB, D), bf16),
            pltpu.SMEM((experts,), jnp.int32),
            pltpu.SMEM((nb, experts), jnp.int32),
            pltpu.SemaphoreType.DMA((3, nb)),
            pltpu.SemaphoreType.DMA((3,)),
            pltpu.SemaphoreType.DMA((2, 2)),
            pltpu.SemaphoreType.DMA,
        ],
        compiler_params=params(),
        name="own_experts",
        cost_estimate=cost(29),
    )(first, *tops, *lows, *ps, wg, wu, wd)


def chip_pieces(x_sets, p_sets, blocks, toks):
    flat = [a for sets in (x_sets, p_sets) for arrays in sets for a in arrays]
    half = toks // 2
    x_count = x_sets[0][0].shape[0] // blocks
    pieces = []
    for k in range(4 * x_count):
        core, x, y = k // (2 * x_count), k // 2 % x_count, k % 2
        parts, base = [], 0
        for sets, end in ((x_sets, toks), (p_sets, toks + TAB)):
            top, low = base + core * 2 + y, base + len(sets[0]) + core * x_count + x
            parts.append(((top, x * blocks, 0, half), (low, y * blocks, half, end)))
            base += len(sets[0]) + len(sets[1])
        pieces.append((blocks, *parts))
    return flat, pieces


def dispatch(first, flat, pieces, toks, experts, cap, groups):
    total = sum(p[0] for p in pieces)
    ring = 4
    room = row_room(cap, total // groups, groups, TILE_FAR)
    return pl.pallas_call(
        functools.partial(dispatch_kernel, tuple(pieces), len(flat), TILE_FAR),
        out_shape=[
            jax.ShapeDtypeStruct((experts, room, 2 * D), bf16),
            jax.ShapeDtypeStruct((experts,), jnp.int32),
        ],
        in_specs=[SM] + [HB] * len(flat),
        out_specs=[HB, SM],
        scratch_shapes=[
            pltpu.VMEM((ring, toks, D), bf16),
            pltpu.VMEM((ring, toks + TAB, D), bf16),
            pltpu.VMEM((experts, room, 2 * D), bf16),
            pltpu.VMEM((TAB, D), f32),
            pltpu.SMEM((experts,), jnp.int32),
            pltpu.SemaphoreType.DMA((2, ring)),
            pltpu.SemaphoreType.DMA,
        ],
        compiler_params=params(),
        name="dispatch",
        cost_estimate=cost(20),
    )(first, *flat)


def weight_grads(used, rows, weights, tile, olds=None, add=True, begin_e=0, count_e=None):
    experts = count_e or weights[0].shape[0]
    shapes = [jax.ShapeDtypeStruct(w.shape, f32) for w in weights]
    operands = [jnp.full((1,), begin_e, jnp.int32), used, rows, *weights, *(olds or ())]
    return pl.pallas_call(
        functools.partial(weight_kernel, tile, experts, bool(olds), bool(olds) and add),
        out_shape=shapes,
        in_specs=[SM, SM] + [HB] * (len(operands) - 2),
        out_specs=[HB] * 3,
        input_output_aliases={len(operands) - 3 + k: k for k in range(3)} if olds else {},
        scratch_shapes=[
            *[pltpu.VMEM(w.shape[1:], f32) for w in weights],
            pltpu.VMEM((2, tile, 2 * D), bf16),
            *[pltpu.VMEM((experts, *w.shape[1:]), bf16) for w in weights],
            pltpu.SemaphoreType.DMA((2,)),
            pltpu.SemaphoreType.DMA((3,)),
            pltpu.SemaphoreType.DMA((3,)),
        ],
        compiler_params=params(),
        name="weight_grads",
        cost_estimate=cost(14),
    )(*operands)


def after(value, *deps):
    return lax.optimization_barrier((value, *deps))[0]


def after_all(values, *deps):
    return lax.optimization_barrier((*values, *deps))[: len(values)]


def after_tree(tree, *deps):
    return lax.optimization_barrier((tree, *deps))[0]


def other_groups(copies, cut):
    count, index = lax.axis_size("dp"), lax.axis_index("dp")
    blocks = lax.all_to_all(copies, "dp", 0, 0, tiled=True)

    def pick(blocks, rows):
        found = [
            lax.dynamic_index_in_dim(blocks, (index + step) % count, 0)[:, rows]
            for step in range(1, count)
        ]
        return jnp.concatenate(found, axis=0)

    return blocks, lambda b: (pick(b, slice(0, cut)), pick(b, slice(cut, None)))


def gather_line(values, axis):
    out = list(values)
    for step in range(1, lax.axis_size(axis)):
        out += [shift(v, axis, step) for v in values]
    return out


def with_line(values, axis):
    return gather_line([jnp.concatenate(values, axis=0)], axis)


def plane_gather(value, x_first):
    if x_first:
        cols = gather_line([value], "x")
        rows = [shift(v, "y", 1) for v in cols]
        return [v for pair in zip(cols, rows) for v in pair]
    return gather_line(gather_line([value], "y"), "x")


def both_cores(values, *deps):
    return list(values) + [shift(after(v, *deps) if deps else v, "c", 1) for v in values]


def total(*parts):
    return sum(p.astype(f32) for p in parts).astype(bf16)


def scatter_cores(parts):
    return parts[0], shift(parts[1], "c", -1)


def scatter_first(keep, other, cut):
    count = lax.axis_size("x")

    def add(rows, where):
        return total(keep[where][:, rows], other[where][:, rows])

    top, low = slice(0, cut), slice(cut, None)
    x_sent = [add(top, slice(2 * k, 2 * k + 2)) for k in range(1, count)]
    y_sent = add(low, slice(1, None, 2))
    x_kept = add(top, slice(0, 2))
    y_kept = add(low, slice(0, None, 2))
    x_got = [shift(v, "x", -k) for k, v in zip(range(1, count), x_sent)]
    y_got = shift(y_sent, "y", -1)
    return (*x_got, y_got), x_kept, y_kept


def scatter_second(got, x_kept, y_kept):
    x_got, y_got = got[:-1], got[-1]
    count = len(got)
    y_next = total(x_kept[1], *[v[1] for v in x_got])
    x_next = [total(y_kept[k], y_got[k]) for k in range(1, count)]
    top_own = total(x_kept[0], *[v[0] for v in x_got])
    low_own = total(y_kept[0], y_got[0])
    top_far = shift(y_next, "y", -1)
    low_far = [shift(v, "x", -k) for k, v in zip(range(1, count), x_next)]
    if count > 2:
        low_far = [total(*low_far)]
    return top_own, top_far, low_own, low_far[0]


def line_sum(value, axis):
    return sum([shift(value, axis, step) for step in range(1, lax.axis_size(axis))], value)


def row_sum(value):
    far = lax.ppermute(value, ("y", "c"), [(i, 3 - i) for i in range(4)])
    return value + shift(value, "c", 1) + shift(value, "y", 1) + far


def scatter_sum(value, axis):
    count, index = lax.axis_size(axis), lax.axis_index(axis)
    chunks = value.reshape((count, value.shape[0] // count) + value.shape[1:])
    result = lax.dynamic_index_in_dim(chunks, index, 0, keepdims=False).astype(f32)
    for step in range(1, count):
        chunk = lax.dynamic_index_in_dim(chunks, (index + step) % count, 0, keepdims=False)
        result = result + shift(chunk, axis, step).astype(f32)
    return result.astype(bf16)


def gather_chunks(own, axis):
    count, index = lax.axis_size(axis), lax.axis_index(axis)
    full = jnp.zeros((count,) + own.shape, bf16)
    full = lax.dynamic_update_index_in_dim(full, own, index, 0)
    for step in range(1, count):
        chunk = shift(own, axis, step)
        full = lax.dynamic_update_index_in_dim(full, chunk, (index - step) % count, 0)
    return full.reshape((count * own.shape[0],) + own.shape[1:])


def shards(
    inputs,
    cotangent,
    gain_attn,
    gain_ffn,
    attn_in,
    attn_out,
    expert_gate,
    expert_up,
    expert_down,
    const_vectors,
    gate_values,
    routes,
    priority,
    pieces,
):
    toks = inputs.shape[1]
    y_index, c_index = lax.axis_index("y"), lax.axis_index("c")
    x_index, x_count = lax.axis_index("x"), lax.axis_size("x")
    dp_count = lax.axis_size("dp")
    row_count = lax.axis_size("y") * lax.axis_size("c")
    seq = toks * row_count
    heads = attn_in.shape[2] // HEAD_DIM
    width = heads * HEAD_DIM
    group_tokens = routes.shape[1]
    nb = group_tokens // toks
    cap = 5 * group_tokens // 24
    experts = expert_gate.shape[0]
    x_own, cot = inputs[0], cotangent[0]
    place = jnp.stack(
        [
            ((y_index - ky) % 2) * 2 + (c_index - kc) % 2
            for ky in range(2)
            for kc in range(2)
        ]
    ).astype(jnp.int32)
    first = (x_index * experts).astype(jnp.int32)[None]
    base = (x_index * seq + (y_index * 2 + c_index) * toks).astype(jnp.int32)[None]

    x_y = shift(x_own, "y", 1)
    w_y = shift(after(attn_out, x_y), "y", 1)
    w_c = shift(attn_out, "c", 1)

    cosine, sine = (jnp.asarray(a) for a in rotary_numpy(seq))
    routes_t, gates_t = routes[0].T, gate_values[0].T
    attn_w = attn_in.transpose(0, 2, 1)
    weights = (expert_gate, expert_up, expert_down)
    half = toks // 2
    far = list(range(1, dp_count))
    one_call = dp_count * group_tokens <= CALL_TOKENS

    payload, p_copies = pl.pallas_call(
        functools.partial(route_kernel, cap),
        out_shape=[
            jax.ShapeDtypeStruct((toks + TAB, D), bf16),
            jax.ShapeDtypeStruct((dp_count if one_call else 1, toks + TAB, D), bf16),
        ],
        in_specs=[SM, VM, VM, VM, VM],
        out_specs=[VM, VM],
        compiler_params=params(),
        name="route",
        cost_estimate=cost(2.5),
    )(base, routes_t, priority, gates_t, cot)
    if one_call:
        far_p, split_p = other_groups(p_copies, half)
    x_slots = [x_own, shift(x_own, "c", 1), x_y, shift(after(x_y, payload), "c", 1)]
    p_cols = gather_line([payload], "x")
    p_y = shift(after(payload, x_y), "y", 1)

    mix_shape = jax.ShapeDtypeStruct((toks, width), bf16)
    fwd_out = attn_fwd(after(place, payload), x_slots, gain_attn, attn_w, cosine, sine, pieces)
    fwd_out = after_all(fwd_out, *p_cols, p_y, w_y, w_c)
    q, k, v, probs, *mixed = fwd_out

    def to_owner(parts):
        return [
            parts[0],
            shift(parts[1], "c", -1),
            shift(parts[2], "y", -1),
            lax.ppermute(parts[3], ("y", "c"), [(i, 3 - i) for i in range(4)]),
        ]

    started = mixed[0]
    w_slots = [attn_out, w_c, w_y, shift(after(w_y, started), "c", 1)]
    own_p = [p_cols[0], p_y]
    for step, p in enumerate(p_cols[1:], 1):
        own_p += [p, shift(after(p_y, started), "x", step)]
    own_p = both_cores(own_p, started)
    if one_call:
        p_top, p_low = split_p(after(far_p, started))
    mixed = to_owner(mixed)
    resid, norm_two, norm_top, norm_low, x_copies = pl.pallas_call(
        out_proj_kernel,
        out_shape=[
            jax.ShapeDtypeStruct((toks, D), f32),
            jax.ShapeDtypeStruct((toks, D), bf16),
            jax.ShapeDtypeStruct((half, D), bf16),
            jax.ShapeDtypeStruct((half, D), bf16),
            jax.ShapeDtypeStruct((dp_count if one_call else 1, toks, D), bf16),
        ],
        in_specs=[VM] * 10,
        out_specs=[VM] * 5,
        compiler_params=params(),
        name="out_proj",
        cost_estimate=cost(3),
    )(x_own, *mixed, *w_slots, after(gain_ffn, own_p[2 * x_count - 1]))

    tops = plane_gather(norm_top, True)
    lows = plane_gather(norm_low, False)
    arrived = (tops[-1], lows[-1])
    ready = ()
    if one_call:
        far_x, split_x = other_groups(x_copies, half)
        first_in = (tops[1], tops[2], lows[1], lows[2])
        p_top_x = gather_line([after(p_top, *first_in)], "x")
        p_low_y = gather_line([after(p_low, *first_in)], "y")
        ready = (p_top_x[-1], p_low_y[-1])
        p_top = with_line(after_all(p_top_x, *arrived), "y")
        p_low = with_line(after_all(p_low_y, *arrived), "x")
    tops, lows = both_cores(tops), both_cores(lows)
    own_out = own_experts(after(first, *ready), tops, lows, own_p, *weights, cap)
    if one_call:
        own_out = after_all(own_out, *p_top, *p_low, far_x)
    dxa, dxb, ya, yb, rows, used = own_out
    dx_first = scatter_first(*scatter_cores((dxa, dxb)), half)
    dx_stage = dx_first[0][-1]
    dx_parts = scatter_second(*dx_first)
    if one_call:
        p_near = [shift(after(a[0], dx_first[1]), "c", 1) for a in (p_top, p_low)]
    front = max(1, experts // 2)
    grads_w = weight_grads(after(used, dx_first[1]), rows, weights, TILE_BACK, count_e=front)
    if one_call:
        x_top, x_low = split_x(after(far_x, dx_stage, grads_w[0]))
        x_top_x = gather_line([x_top], "x")
        x_low_y = gather_line([x_low], "y")
        used = after(used, *p_near)
    for begin in range(front, experts, front):
        grads_w = weight_grads(
            after(used, dx_stage), rows, weights, TILE_BACK, grads_w, False, begin, front
        )

    gres, *mids = pl.pallas_call(
        lambda base_ref, *refs: mid_kernel(
            base_ref,
            refs[0:4],
            *refs[4:9],
            refs[9:13],
            refs[13:17],
            refs[17],
            refs[18:22],
            refs[22:24],
            refs[24],
        ),
        out_shape=[jax.ShapeDtypeStruct((toks, D), f32)]
        + [mix_shape] * 4
        + [jax.ShapeDtypeStruct((2, width, D), bf16)] * 2
        + [jax.ShapeDtypeStruct((8, D), f32)],
        in_specs=[SM] + [VM] * 17,
        out_specs=[VM] * 8,
        compiler_params=params(),
        name="mid",
        cost_estimate=cost(5),
    )(
        after(base, grads_w[0], *((*x_top_x, *x_low_y) if one_call else ())),
        *dx_parts,
        cot,
        resid,
        routes_t,
        gates_t,
        gain_ffn,
        *mixed,
        *w_slots,
    )
    out_keep, out_send, sums = mids[4:]
    grads = to_owner(mids[:4])
    out_other = shift(out_send, "c", -1)
    out_sent = total(out_keep[1], out_other[1])
    out_far = shift(out_sent, "y", -1)
    ready = ()
    if one_call:
        ready = (x_top_x[-1], x_low_y[-1])
        x_top = with_line(after_all(x_top_x, *grads, out_sent), "y")
        x_low = with_line(after_all(x_low_y, *grads, out_sent), "x")
        p_other = [shift(after(a[1], *grads), "c", 1) for a in (p_top, p_low)]
    tables = (cosine, sine)
    unit = 8 * x_count * dp_count
    dw_rows = -(-(4 * width + 8) // unit) * unit
    saved = (q, k, v, probs)
    bwd_out = attn_bwd(
        place, x_slots, grads, gain_attn, attn_w, tables, saved, sums, dw_rows
    )
    if one_call:
        bwd_out = after_all(bwd_out, *x_top, *x_low, *p_other, out_far)
    gno_keep, gno_send, dw_in, gain_part = bwd_out
    gno_other = shift(gno_send, "c", -1)
    gno_far = (gno_keep[1].astype(f32) + gno_other[1].astype(f32)).astype(bf16)
    gno_near = (gno_keep[0].astype(f32) + gno_other[0].astype(f32)).astype(bf16)

    dw_out = total(out_keep[0], out_other[0], out_far)
    attn_grads = lax.dynamic_update_slice(dw_in, dw_out, (3 * width, 0))
    y_stage = scatter_cores(after_all((ya, yb), gno_other))
    gno_far = shift(gno_far, "y", -1)

    if one_call:
        x_near = [shift(after(a[0], gain_part), "c", 1) for a in (x_top, x_low)]
        x_other = [shift(after(a[1], gain_part), "c", 1) for a in (x_top, x_low)]
        x_sets = [[*a, n, o] for a, n, o in zip((x_top, x_low), x_near, x_other)]
        p_sets = [[*a, n, o] for a, n, o in zip((p_top, p_low), p_near, p_other)]
        flat, spots = chip_pieces(x_sets, p_sets, len(far), toks)
        part = scatter_sum(after(attn_grads, *x_near, *x_other), "x")
        rows, used = dispatch(after(first, gain_part), flat, spots, toks, experts, cap, len(far))
        used = after(used, part, gno_far, *y_stage)
        part, y_stage = after_tree((part, y_stage), used)
        part = scatter_sum(part, "dp")
        y_stage = scatter_first(*y_stage, half)
        for e in range(experts):
            grads_w = weight_grads(used, rows, weights, TILE_FAR, grads_w, True, e, 1)
            if e == 0:
                used = after(used, grads_w[0], part, *y_stage[0])
                part = gather_chunks(after(part, used), "dp")
            elif e == 1:
                used = after(used, grads_w[0], part)
                part, y_stage = after_tree((part, y_stage), used)
                attn_grads = gather_chunks(part, "x")
                y_parts = scatter_second(*y_stage)
            elif e == 2:
                used = after(used, grads_w[0], attn_grads, *y_parts)
                sums = row_sum(attn_grads[4 * width : 4 * width + 4].astype(f32))
            elif e == 3:
                grads_w = after_all(grads_w, sums)
    else:
        part = scatter_sum(scatter_sum(attn_grads, "x"), "dp")
        attn_grads = gather_chunks(gather_chunks(part, "dp"), "x")
        sums = row_sum(attn_grads[4 * width : 4 * width + 4].astype(f32))
        y_parts = scatter_second(*scatter_first(*y_stage, half))
        spots = [(nb, ((0, 0, 0, toks),), ((1, 0, 0, toks + TAB),))]

        def next_group(step, carry):
            x_block, p_block, *sums_w = carry
            x_block, p_block = shift(x_block, "dp", 1), shift(p_block, "dp", 1)
            flat = [lax.all_gather(a, ("y", "c", "x")) for a in (x_block, p_block)]
            rows, used = dispatch(first, flat, spots, toks, experts, cap, 1)
            return x_block, p_block, *weight_grads(used, rows, weights, TILE_FAR, sums_w)

        grads_w = lax.fori_loop(1, dp_count, next_group, (norm_two, payload, *grads_w))[2:]
    grad_w_gate, grad_w_up, grad_w_down = grads_w
    grad_w_in = attn_grads[: 3 * width].astype(f32).reshape(3, width, D).transpose(0, 2, 1)
    grad_w_out = attn_grads[3 * width : 4 * width].astype(f32)
    input_grad = pl.pallas_call(
        last_kernel,
        out_shape=jax.ShapeDtypeStruct((toks, D), f32),
        in_specs=[VM] * 5,
        out_specs=VM,
        compiler_params=params(),
        name="last",
        cost_estimate=cost(3),
    )(gno_near, gno_far, x_own, gres, gain_attn)

    block_out, grad_gates = pl.pallas_call(
        lambda base_ref, *refs: out_kernel(base_ref, refs[0:4], *refs[4:]),
        out_shape=[
            jax.ShapeDtypeStruct((toks, D), bf16),
            jax.ShapeDtypeStruct((2, toks), f32),
        ],
        in_specs=[SM] + [VM] * 10,
        out_specs=[VM] * 2,
        compiler_params=params(),
        name="block_out",
        cost_estimate=cost(3),
    )(base, *y_parts, cot, resid, norm_two, routes_t, gates_t, const_vectors)

    return (
        block_out[None],
        input_grad[None],
        sums[3],
        sums[0],
        grad_w_in,
        grad_w_out,
        grad_w_gate,
        grad_w_up,
        grad_w_down,
        sums[1:3],
        grad_gates.T[None],
    )


def solution(mesh):
    dp, row, col = mesh.devices.shape
    fine = Mesh(mesh.devices.reshape(dp, row // 2, 2, col), ("dp", "y", "c", "x"))
    rows = ("y", "c")
    in_specs = (
        P(("dp", "x"), rows, None),
        P(("dp", "x"), rows, None),
        P(),
        P(),
        P(None, None, rows),
        P(rows, None),
        P("x", None, rows),
        P("x", None, rows),
        P("x", rows, None),
        P(),
        P(("dp", "x"), rows, None),
        P("dp", None, None),
        P("dp", None),
        P(("dp", "x"), None),
    )
    out_specs = (
        P(("dp", "x"), rows, None),
        P(("dp", "x"), rows, None),
        P(),
        P(),
        P(None, None, rows),
        P(rows, None),
        P("x", None, rows),
        P("x", None, rows),
        P("x", rows, None),
        P(),
        P(("dp", "x"), rows, None),
    )
    return jax.shard_map(shards, mesh=fine, in_specs=in_specs, out_specs=out_specs, check_vma=False)
```

```python
import functools

import jax
import jax.numpy as jnp
import numpy as np
from jax import lax
from jax.experimental import pallas as pl
from jax.experimental.pallas import tpu as pltpu
from jax.sharding import Mesh
from jax.sharding import PartitionSpec as P

D = 768
HEAD_DIM = 64
E_FFN = 8
MOST = 88
SHORT = 48
SEG = 96
TAB = 8
TILE_OWN = 192
TILE_BACK = 256
TILE_FAR = 512
CALL_TOKENS = 8192

norm_eps = 1e-05
masked_score = -1e30
bf16 = jnp.bfloat16
f32 = jnp.float32
VMEM_MAX = 60 * 1024 * 1024


def dot(a, b, ca=1, cb=0):
    return lax.dot_general(a, b, (((ca,), (cb,)), ((), ())), preferred_element_type=f32)


def params(**kw):
    return pltpu.CompilerParams(vmem_limit_bytes=VMEM_MAX, **kw)


def cost(micros):
    return pl.CostEstimate(
        flops=int(micros * 1.1e9), transcendentals=0, bytes_accessed=int(micros * 3.5e6)
    )


VM = pl.BlockSpec(memory_space=pltpu.VMEM)
SM = pl.BlockSpec(memory_space=pltpu.SMEM)
HB = pl.BlockSpec(memory_space=pl.ANY)


def shift(value, axis, step):
    count = lax.axis_size(axis)
    return lax.ppermute(value, axis, [(i, (i + step) % count) for i in range(count)])


def gain_row(ref):
    return ref[...].reshape(1, D)


def normed(rows, gain):
    inverse = lax.rsqrt(jnp.mean(rows * rows, axis=-1, keepdims=True) + norm_eps)
    unit = rows * inverse
    return unit, inverse, (unit * gain).astype(bf16)


def rotary_numpy(length):
    half = HEAD_DIM // 2
    frequency = (10000.0 ** (-np.arange(half, dtype=np.float32) / half)).astype(np.float32)
    angles = frequency[:, None] * np.arange(length, dtype=np.float32)[None, :]
    cosine = np.tile(np.cos(angles), (2, 1)).astype(np.float32)
    sine = np.tile(np.sin(angles), (2, 1)).astype(np.float32)
    return cosine, sine


def partner_matrix(width):
    i = lax.broadcasted_iota(jnp.int32, (width, width), 0)
    j = lax.broadcasted_iota(jnp.int32, (width, width), 1)
    low = (j % HEAD_DIM) < HEAD_DIM // 2
    minus = jnp.where(low & (i == j + HEAD_DIM // 2), -1.0, 0.0)
    plus = jnp.where((~low) & (i == j - HEAD_DIM // 2), 1.0, 0.0)
    return (minus + plus).astype(bf16)


def eye(width):
    i = lax.broadcasted_iota(jnp.int32, (width, width), 0)
    j = lax.broadcasted_iota(jnp.int32, (width, width), 1)
    return jnp.where(i == j, 1.0, 0.0).astype(bf16)


def route_kernel(cap, base_ref, routes_ref, prio_ref, gates_ref, cot_ref, out_ref, copies_ref):
    total = prio_ref.shape[1]
    toks = cot_ref.shape[0]
    base = pl.multiple_of(base_ref[0], toks)
    prio = prio_ref[...].astype(f32)
    own_row = prio_ref[:, pl.ds(base, toks)].astype(f32)
    own_col = jnp.broadcast_to(own_row, (8, toks)).T[:, :1]
    earlier = jnp.where(prio < own_col, 1.0, 0.0).astype(bf16)
    ids = lax.broadcasted_iota(jnp.int32, (16, total), 0)
    named = (routes_ref[0:1, :] == ids) | (routes_ref[1:2, :] == ids)
    slots = dot(jnp.where(named, 1.0, 0.0).astype(bf16), earlier, 1, 1)
    own_ids = lax.broadcasted_iota(jnp.int32, (16, toks), 0)
    first = routes_ref[0:1, pl.ds(base, toks)] == own_ids
    second = routes_ref[1:2, pl.ds(base, toks)] == own_ids
    kept = (first | second) & (own_ids < E_FFN) & (slots < cap)
    before_i = lax.broadcasted_iota(jnp.int32, (toks, toks), 0)
    before_j = lax.broadcasted_iota(jnp.int32, (toks, toks), 1)
    lower = jnp.where(before_i < before_j, 1.0, 0.0).astype(bf16)
    rank = dot(jnp.where(kept, 1.0, 0.0).astype(bf16), lower)
    rank = jnp.where(kept, rank, -1.0)
    gate = jnp.where(first, gates_ref[0:1, :], 0.0) + jnp.where(second, gates_ref[1:2, :], 0.0)
    high = gate.astype(bf16)
    rest = (gate - high.astype(f32)).astype(bf16)
    table = jnp.concatenate([rank[:TAB].astype(bf16), high[:TAB], rest[:TAB]], axis=1)
    out_ref[0:toks, :] = cot_ref[...]
    out_ref[toks : toks + TAB, :] = table
    for k in range(copies_ref.shape[0]):
        copies_ref[k, 0:toks, :] = cot_ref[...]
        copies_ref[k, toks : toks + TAB, :] = table


def attn_fwd_kernel(
    heads,
    place_ref,
    x0,
    x1,
    x2,
    x3,
    gain_ref,
    w_ref,
    cos_ref,
    sin_ref,
    prow_ref,
    q_ref,
    k_ref,
    v_ref,
    pt_ref,
    m0,
    m1,
    m2,
    m3,
    bias_ref,
    pbuf,
    obuf,
    vt_ref,
    sems,
):
    toks = x0.shape[0]
    width = heads * HEAD_DIM
    slots = 4
    seq = slots * toks
    swap = partner_matrix(width)
    wq, wk, wv = w_ref[0], w_ref[1], w_ref[2]
    wq_swap = dot(swap, wq, 0, 0).astype(bf16)
    wk_swap = dot(swap, wk, 0, 0).astype(bf16)
    piece_col = jnp.broadcast_to(prow_ref[...].astype(f32), (8, seq)).T[:, :1]
    for slot, x_ref in enumerate((x0, x1, x2, x3)):
        start = pl.multiple_of(place_ref[slot] * toks, toks)
        rows = pl.ds(start, toks)
        _, _, act = normed(x_ref[...].astype(f32), gain_row(gain_ref))
        cosine = jnp.concatenate([cos_ref[:, rows].T] * heads, axis=1)
        sine = jnp.concatenate([sin_ref[:, rows].T] * heads, axis=1)
        queries = (dot(act, wq, 1, 1) * cosine + dot(act, wq_swap, 1, 1) * sine).astype(bf16)
        queries = (queries.astype(f32) * HEAD_DIM**-0.5).astype(bf16)
        keys = (dot(act, wk, 1, 1) * cosine + dot(act, wk_swap, 1, 1) * sine).astype(bf16)
        values = dot(act, wv, 1, 1).astype(bf16)
        for h in range(heads):
            cols = slice(h * HEAD_DIM, (h + 1) * HEAD_DIM)
            q_ref[h, rows, :] = queries[:, cols]
            k_ref[h, rows, :] = keys[:, cols]
            v_ref[h, rows, :] = values[:, cols]

    for h in range(heads):
        vt_ref[h] = v_ref[h].astype(f32).T.astype(bf16)

    def copy_out(block, h):
        keys = visible(block, slots) * toks
        return pltpu.make_async_copy(
            pbuf.at[h, 0:keys], pt_ref.at[block * heads + h, 0:keys], sems.at[h]
        )

    for block in range(slots):
        keys = visible(block, slots) * toks
        cols = slice(block * toks, (block + 1) * toks)
        kpos = lax.broadcasted_iota(jnp.int32, (keys, toks), 0)
        qpos = lax.broadcasted_iota(jnp.int32, (keys, toks), 1) + block * toks
        qp = prow_ref[:, cols].astype(f32)
        same = (piece_col[:keys] == qp) & (qp > 0.0)
        bias_ref[0:keys] = jnp.where((kpos <= qpos) | same, 0.0, masked_score)

        def head_body(h, carry, block=block, keys=keys, cols=cols):
            scores = dot(k_ref[h, 0:keys], q_ref[h, cols, :], 1, 1) + bias_ref[0:keys]
            peak = jnp.max(scores, axis=0, keepdims=True)
            weights = jnp.exp(scores - peak)
            mass = jnp.sum(weights, axis=0, keepdims=True)
            probs = (weights * (1.0 / mass)).astype(bf16)
            if block > 0:
                copy_out(block - 1, h).wait()
            pbuf[h, 0:keys] = probs
            copy_out(block, h).start()
            at = pl.ds(pl.multiple_of(h * HEAD_DIM, HEAD_DIM), HEAD_DIM)
            obuf[block, at, :] = dot(vt_ref[h, :, 0:keys], probs)
            return carry

        lax.fori_loop(0, heads, head_body, 0)
    for slot, m_ref in enumerate((m0, m1, m2, m3)):
        m_ref[...] = obuf[place_ref[slot]].T.astype(bf16)
    for h in range(heads):
        copy_out(slots - 1, h).wait()


def visible(block, slots):
    return min(block + 2, slots)


def attn_bwd_kernel(
    heads,
    place_ref,
    x0,
    x1,
    x2,
    x3,
    g0,
    g1,
    g2,
    g3,
    gain_ref,
    w_ref,
    cost_ref,
    sint_ref,
    q_ref,
    k_ref,
    v_ref,
    pt_ref,
    sums_ref,
    keep_ref,
    send_ref,
    dw_ref,
    done_ref,
    act_ref,
    go_ref,
    qcat_ref,
    kcat_ref,
    dk_ref,
    dv_ref,
    dqt_ref,
    dlin_ref,
    pbuf,
    sems,
):
    toks = x0.shape[0]
    width = heads * HEAD_DIM
    slots = 4

    def copy_in(block, h):
        keys = visible(block, slots) * toks
        return pltpu.make_async_copy(
            pt_ref.at[block * heads + h, 0:keys], pbuf.at[h, 0:keys], sems.at[h]
        )

    for h in range(heads):
        copy_in(0, h).start()
    swap = partner_matrix(HEAD_DIM)
    both = jnp.concatenate([eye(HEAD_DIM), swap], axis=1)
    swap_i = lax.broadcasted_iota(jnp.int32, (2 * HEAD_DIM, HEAD_DIM), 0)
    swap_j = lax.broadcasted_iota(jnp.int32, (2 * HEAD_DIM, HEAD_DIM), 1)
    low = ((swap_i - HEAD_DIM) < HEAD_DIM // 2) & (swap_i >= HEAD_DIM)
    high = (swap_i - HEAD_DIM) >= HEAD_DIM // 2
    stacked = (
        jnp.where(swap_i == swap_j, 1.0, 0.0)
        + jnp.where(low & (swap_j == swap_i - HEAD_DIM + HEAD_DIM // 2), -1.0, 0.0)
        + jnp.where(high & (swap_j == swap_i - HEAD_DIM - HEAD_DIM // 2), 1.0, 0.0)
    ).astype(bf16)
    for slot, (x_ref, g_ref) in enumerate(zip((x0, x1, x2, x3), (g0, g1, g2, g3))):
        rows = pl.ds(pl.multiple_of(place_ref[slot] * toks, toks), toks)
        _, _, act = normed(x_ref[...].astype(f32), gain_row(gain_ref))
        act_ref[rows, :] = act
        for h in range(heads):
            go_ref[h, rows, :] = g_ref[:, h * HEAD_DIM : (h + 1) * HEAD_DIM]
    for h in range(heads):
        qcat_ref[h] = dot(q_ref[h], both).astype(bf16)
        kcat_ref[h] = dot(stacked, k_ref[h], 1, 1).astype(bf16)
    dk_ref[...] = jnp.zeros(dk_ref.shape, f32)
    dv_ref[...] = jnp.zeros(dv_ref.shape, f32)

    for block in range(slots):
        keys = visible(block, slots) * toks
        cols = slice(block * toks, (block + 1) * toks)

        def head_body(h, carry, block=block, keys=keys, cols=cols):
            copy_in(block, h).wait()
            probs = pbuf[h, 0:keys]
            grad_out = go_ref[h, cols, :]
            grad_probs = dot(v_ref[h, 0:keys], grad_out, 1, 1)
            probs_f = probs.astype(f32)
            inner = jnp.sum(probs_f * grad_probs, axis=0, keepdims=True)
            grad_scores = (probs_f * (grad_probs - inner)).astype(bf16)
            dv_ref[h, 0:keys] += dot(probs, grad_out)
            dk_ref[h, 0:keys] += dot(grad_scores, qcat_ref[h, cols, :])
            dqt_ref[block, h] = dot(kcat_ref[h, :, 0:keys], grad_scores)
            if block + 1 < slots:
                copy_in(block + 1, h).start()
            return carry

        lax.fori_loop(0, heads, head_body, 0)
    cosine, sine = cost_ref[...].T, sint_ref[...].T
    for h in range(heads):
        cols = slice(h * HEAD_DIM, (h + 1) * HEAD_DIM)
        for block in range(slots):
            rows = slice(block * toks, (block + 1) * toks)
            both_t = dqt_ref[block, h]
            lin_t = (
                both_t[:HEAD_DIM] * cost_ref[:, rows] - both_t[HEAD_DIM:] * sint_ref[:, rows]
            ) * HEAD_DIM**-0.5
            dlin_ref[0, rows, cols] = lin_t.T.astype(bf16)
        dlin_ref[1, :, cols] = (
            dk_ref[h, :, :HEAD_DIM] * cosine - dk_ref[h, :, HEAD_DIM:] * sine
        ).astype(bf16)
        dlin_ref[2, :, cols] = dv_ref[h].astype(bf16)
    for k in range(3):
        dw_ref[k * width : (k + 1) * width, :] = dot(
            dlin_ref[k], act_ref[...], 0, 0
        ).astype(bf16)
    gain_grad = jnp.zeros((1, D), f32)
    for slot, x_ref in enumerate((x0, x1, x2, x3)):
        rows = pl.ds(pl.multiple_of(place_ref[slot] * toks, toks), toks)
        part = dot(dlin_ref[0, rows, :], w_ref[0])
        part += dot(dlin_ref[1, rows, :], w_ref[1])
        part += dot(dlin_ref[2, rows, :], w_ref[2])
        unit, _, _ = normed(x_ref[...].astype(f32), gain_row(gain_ref))
        gain_grad += jnp.sum(part * unit, axis=0, keepdims=True)
        if slot % 2 == 0:
            keep_ref[slot // 2] = part.astype(bf16)
        else:
            send_ref[slot // 2] = part.astype(bf16)
    rest = dw_ref.shape[0] - 4 * width
    ids = lax.broadcasted_iota(jnp.int32, (8, D), 0)
    tail = jnp.where(ids == 3, gain_grad, sums_ref[...])
    dw_ref[3 * width : 4 * width, :] = jnp.zeros((width, D), bf16)
    dw_ref[4 * width :, :] = jnp.zeros((rest, D), bf16)
    dw_ref[4 * width : 4 * width + 8, :] = tail.astype(bf16)
    done_ref[...] = jnp.zeros(done_ref.shape, f32)


def attn_fwd(place, x_slots, gain, w, cosine, sine, pieces):
    toks, width = x_slots[0].shape[0], w.shape[1]
    slots = len(x_slots)
    seq, heads = slots * toks, width // HEAD_DIM
    head_shape = jax.ShapeDtypeStruct((heads, seq, HEAD_DIM), bf16)
    return pl.pallas_call(
        functools.partial(attn_fwd_kernel, heads),
        out_shape=[head_shape] * 3
        + [jax.ShapeDtypeStruct((slots * heads, seq, toks), bf16)]
        + [jax.ShapeDtypeStruct((toks, width), bf16)] * slots,
        in_specs=[SM] + [VM] * 9,
        out_specs=[VM] * 3 + [HB] + [VM] * slots,
        scratch_shapes=[
            pltpu.VMEM((seq, toks), f32),
            pltpu.VMEM((heads, seq, toks), bf16),
            pltpu.VMEM((slots, width, toks), f32),
            pltpu.VMEM((heads, HEAD_DIM, seq), bf16),
            pltpu.SemaphoreType.DMA((heads,)),
        ],
        compiler_params=params(),
        name="attn_fwd",
        cost_estimate=cost(20),
    )(place, *x_slots, gain, w, cosine, sine, pieces)


def attn_bwd(place, x_slots, grads, gain, w, tables, saved, sums, dw_rows):
    toks, width = x_slots[0].shape[0], w.shape[1]
    slots = len(x_slots)
    seq, heads = slots * toks, width // HEAD_DIM
    return pl.pallas_call(
        functools.partial(attn_bwd_kernel, heads),
        out_shape=[
            jax.ShapeDtypeStruct((2, toks, D), bf16),
            jax.ShapeDtypeStruct((2, toks, D), bf16),
            jax.ShapeDtypeStruct((dw_rows, D), bf16),
            jax.ShapeDtypeStruct((8, 128), f32),
        ],
        in_specs=[SM] + [VM] * 15 + [HB, VM],
        out_specs=[VM] * 4,
        scratch_shapes=[
            pltpu.VMEM((seq, D), bf16),
            pltpu.VMEM((heads, seq, HEAD_DIM), bf16),
            pltpu.VMEM((heads, seq, 2 * HEAD_DIM), bf16),
            pltpu.VMEM((heads, 2 * HEAD_DIM, seq), bf16),
            pltpu.VMEM((heads, seq, 2 * HEAD_DIM), f32),
            pltpu.VMEM((heads, seq, HEAD_DIM), f32),
            pltpu.VMEM((slots, heads, 2 * HEAD_DIM, toks), f32),
            pltpu.VMEM((3, seq, width), bf16),
            pltpu.VMEM((heads, seq, toks), bf16),
            pltpu.SemaphoreType.DMA((heads,)),
        ],
        compiler_params=params(),
        name="attn_bwd",
        cost_estimate=cost(22),
    )(place, *x_slots, *grads, gain, w, *tables, *saved, sums)


def out_proj_kernel(
    x_ref, m0, m1, m2, m3, w0, w1, w2, w3, gain_ref, resid_ref, n_ref, top_ref, low_ref, copies_ref
):
    attended = dot(m0[...], w0[...])
    attended += dot(m1[...], w1[...])
    attended += dot(m2[...], w2[...])
    attended += dot(m3[...], w3[...])
    resid = x_ref[...].astype(f32) + attended
    resid_ref[...] = resid
    _, _, act = normed(resid, gain_row(gain_ref))
    half = act.shape[0] // 2
    n_ref[...] = act
    top_ref[...] = act[:half]
    low_ref[...] = act[half:]
    for k in range(copies_ref.shape[0]):
        copies_ref[k] = act


def route_columns(base_ref, routes_ref, gates_ref, toks):
    base = pl.multiple_of(base_ref[0], toks)
    routes = routes_ref[:, pl.ds(base, toks)].astype(f32)
    rows = jnp.concatenate([routes, gates_ref[...], jnp.zeros((4, toks), f32)], axis=0)
    return rows.T, routes


def expert_gate(columns, expert):
    return jnp.where(columns[:, 0:1] == expert, columns[:, 2:3], 0.0) + jnp.where(
        columns[:, 1:2] == expert, columns[:, 3:4], 0.0
    )


def mid_kernel(
    base_ref,
    dx_refs,
    cot_ref,
    resid_ref,
    routes_ref,
    gates_ref,
    gain_ref,
    m_refs,
    w_refs,
    gres_ref,
    g_refs,
    o_refs,
    sums_ref,
):
    toks = cot_ref.shape[0]
    cot = cot_ref[...].astype(f32)
    columns, _ = route_columns(base_ref, routes_ref, gates_ref, toks)
    halves = [dx_refs[k][...].astype(f32) + dx_refs[k + 1][...].astype(f32) for k in (0, 2)]
    grad = jnp.concatenate(halves, axis=0) + expert_gate(columns, E_FFN + 1) * cot
    gain = gain_row(gain_ref)
    unit, inverse, _ = normed(resid_ref[...], gain)
    grad_unit = grad * gain
    grad_resid = cot + inverse * (
        grad_unit - unit * jnp.mean(grad_unit * unit, axis=-1, keepdims=True)
    )
    gres_ref[...] = grad_resid
    grad_att = grad_resid.astype(bf16)
    for k, (m_ref, w_ref, g_ref) in enumerate(zip(m_refs, w_refs, g_refs)):
        g_ref[...] = dot(grad_att, w_ref[...], 1, 1).astype(bf16)
        o_refs[k % 2][k // 2] = dot(m_ref[...], grad_att, 0, 0).astype(bf16)
    sums_ref[...] = jnp.zeros(sums_ref.shape, f32)
    sums_ref[0:1, :] = jnp.sum(grad * unit, axis=0, keepdims=True)
    for k in range(2):
        weight = expert_gate(columns, E_FFN + 2 + k)
        sums_ref[1 + k : 2 + k, :] = jnp.sum(weight * cot, axis=0, keepdims=True)


def out_kernel(
    base_ref,
    y_refs,
    cot_ref,
    resid_ref,
    n_ref,
    routes_ref,
    gates_ref,
    const_ref,
    out_ref,
    gg_ref,
):
    toks = cot_ref.shape[0]
    half = toks // 2
    cot = cot_ref[...].astype(f32)
    columns, routes = route_columns(base_ref, routes_ref, gates_ref, toks)
    act = n_ref[...].astype(f32)
    consts = const_ref[...].astype(f32)
    top = y_refs[0][...].astype(f32) + y_refs[1][...].astype(f32)
    low = y_refs[2][...].astype(f32) + y_refs[3][...].astype(f32)
    moe = jnp.concatenate([top, low[:half]], axis=0) + expert_gate(columns, E_FFN + 1) * act
    moe += expert_gate(columns, E_FFN + 2) * consts[0:1]
    moe += expert_gate(columns, E_FFN + 3) * consts[1:2]
    out_ref[...] = (resid_ref[...] + moe).astype(bf16)
    dots = [cot * act, cot * consts[0:1], cot * consts[1:2]]
    dots = [jnp.sum(v, axis=1, keepdims=True) for v in dots]
    dots = jnp.concatenate([jnp.broadcast_to(dots[k % 3], (toks, 1)) for k in range(8)], axis=1).T
    table = low[half : half + TAB, 0:toks]
    for pair in range(2):
        route = routes[pair : pair + 1]
        result = jnp.zeros((1, toks), f32)
        for e in range(E_FFN):
            result += jnp.where(route == e, table[e : e + 1], 0.0)
        for k in range(3):
            result += jnp.where(route == E_FFN + 1 + k, dots[k : k + 1], 0.0)
        gg_ref[pair : pair + 1, :] = result


def last_kernel(gno_a, gno_b, x_ref, gres_ref, gain_ref, out_ref):
    grad = gno_a[...].astype(f32) + gno_b[...].astype(f32)
    gain = gain_row(gain_ref)
    unit, inverse, _ = normed(x_ref[...].astype(f32), gain)
    grad_unit = grad * gain
    out_ref[...] = gres_ref[...] + inverse * (
        grad_unit - unit * jnp.mean(grad_unit * unit, axis=-1, keepdims=True)
    )


def dispatch_block(first, experts, x, p_ref, tab_ref, rows_ref, gate_ref, offs, starts, block):
    toks = x.shape[0]
    tab_ref[...] = p_ref[toks : toks + TAB, :].astype(f32)
    want = lax.broadcasted_iota(jnp.int32, (SHORT, toks), 0).astype(f32)
    cot = p_ref[0:toks, :]

    def select(i, begin):
        row = tab_ref[pl.ds(first + i, 1), :]
        match = (want + begin) == row[:, 0:toks]
        gate = row[:, toks : 2 * toks] + row[:, 2 * toks : 3 * toks]
        weight = jnp.sum(jnp.where(match, gate, 0.0), axis=1, keepdims=True)
        return jnp.where(match, 1.0, 0.0).astype(bf16), weight, row[:, 0:toks]

    def put(i, off, rows_x, rows_c, weight):
        at = pl.ds(pl.multiple_of(off, 16), SHORT)
        rows_ref[i, at, 0:D] = rows_x.astype(bf16)
        rows_ref[i, at, D : 2 * D] = (rows_c * weight).astype(bf16)
        if gate_ref is not None:
            gate_ref[i, at, :] = jnp.broadcast_to(weight, (SHORT, 128))

    parts = [select(i, 0.0) for i in range(experts)]
    counts = [jnp.max(rank).astype(jnp.int32) + 1 for _, _, rank in parts]
    hot = jnp.concatenate([p[0] for p in parts], axis=0)
    rows_x, rows_c = dot(hot, x), dot(hot, cot)
    for i in range(experts):
        off = offs[i]
        if starts is not None:
            starts[block, i] = off
        seg = slice(i * SHORT, (i + 1) * SHORT)
        put(i, off, rows_x[seg], rows_c[seg], parts[i][1])

        @pl.when(counts[i] > SHORT)
        def _(i=i, off=off):
            rest, weight, _ = select(i, float(SHORT))
            put(i, off + SHORT, dot(rest, x), dot(rest, cot), weight)

        offs[i] = off + ((counts[i] + 15) // 16) * 16


def expert_acts(rows, wg, wu, wd):
    act, grad = rows[:, :D], rows[:, D:]
    gate_pre = dot(act, wg)
    up_pre = dot(act, wu)
    grad_hidden = dot(grad, wd, 1, 1)
    sig = 1.0 / (1.0 + jnp.exp(-gate_pre))
    silu = gate_pre * sig
    hidden = (silu * up_pre).astype(bf16)
    grad_gate = (grad_hidden * up_pre * sig * (1.0 + gate_pre * (1.0 - sig))).astype(bf16)
    grad_up = (grad_hidden * silu).astype(bf16)
    return act, grad, hidden, grad_hidden, grad_gate, grad_up


def own_kernel(nb, tile, first_ref, *refs):
    tops, lows, ps = refs[:nb], refs[nb : 2 * nb], refs[2 * nb : 3 * nb]
    wg_h, wu_h, wd_h, dxa, dxb, ya, yb, rows_out, used = refs[3 * nb : 3 * nb + 9]
    (
        xbuf,
        pbuf,
        wg,
        wu,
        wd,
        rows_ref,
        back_ref,
        gate_ref,
        tab_ref,
        dxbuf,
        ybuf,
        offs,
        starts,
        tok_sems,
        w_sems,
        out_sems,
        row_sem,
    ) = refs[3 * nb + 9 :]
    experts = wg.shape[0]
    toks = xbuf.shape[1]
    half = nb // 2
    first = first_ref[0]
    mid = toks // 2

    def tok_copies(b, src):
        return (
            pltpu.make_async_copy(tops[src], xbuf.at[b, 0:mid], tok_sems.at[0, b]),
            pltpu.make_async_copy(lows[src], xbuf.at[b, mid:toks], tok_sems.at[1, b]),
            pltpu.make_async_copy(ps[src], pbuf.at[b], tok_sems.at[2, b]),
        )

    w_copies = [
        pltpu.make_async_copy(src, dst, w_sems.at[k])
        for k, (src, dst) in enumerate(((wg_h, wg), (wu_h, wu), (wd_h, wd)))
    ]
    for b in range(nb):
        for copy in tok_copies(b, b):
            copy.start()
    for copy in w_copies:
        copy.start()
    for i in range(experts):
        offs[i] = 0

    def dispatch_body(b, carry):
        for copy in tok_copies(b, 0):
            copy.wait()
        dispatch_block(
            first, experts, xbuf[b], pbuf.at[b], tab_ref, rows_ref, gate_ref, offs, starts, b
        )
        return carry

    lax.fori_loop(0, nb, dispatch_body, 0)
    for i in range(experts):
        at = pl.ds(pl.multiple_of(offs[i], 16), TILE_BACK)
        rows_ref[i, at, :] = jnp.zeros((TILE_BACK, 2 * D), bf16)
        back_ref[i, at, :] = jnp.zeros((TILE_BACK, 2 * D), bf16)
        gate_ref[i, at, :] = jnp.zeros((TILE_BACK, 128), f32)
        used[i] = offs[i]
    rows_copy = pltpu.make_async_copy(rows_ref, rows_out, row_sem)
    rows_copy.start()
    for copy in w_copies:
        copy.wait()

    def expert_body(e, carry):
        def tile_body(j, inner):
            at = pl.ds(pl.multiple_of(j * tile, 16), tile)
            rows = rows_ref[e, at, :]
            _, _, hidden, grad_hidden, grad_gate, grad_up = expert_acts(rows, wg[e], wu[e], wd[e])
            weight = gate_ref[e, at, :]
            product = jnp.sum(hidden.astype(f32) * grad_hidden, axis=1, keepdims=True)
            gate_ref[e, at, :] = jnp.where(weight > 0.0, product / jnp.maximum(weight, 0.125), 0.0)
            back_ref[e, at, 0:D] = (
                dot(grad_gate, wg[e], 1, 1) + dot(grad_up, wu[e], 1, 1)
            ).astype(bf16)
            back_ref[e, at, D : 2 * D] = (dot(hidden, wd[e]) * weight[:, :1]).astype(bf16)
            return inner

        return lax.fori_loop(0, (offs[e] + tile - 1) // tile, tile_body, carry)

    lax.fori_loop(0, experts, expert_body, 0)

    def out_copies(b, slot):
        near = b < half
        return near, (
            pltpu.make_async_copy(dxbuf.at[slot], dxa.at[b % half], out_sems.at[0, slot]),
            pltpu.make_async_copy(ybuf.at[slot], ya.at[b % half], out_sems.at[1, slot]),
        ), (
            pltpu.make_async_copy(dxbuf.at[slot], dxb.at[b % half], out_sems.at[0, slot]),
            pltpu.make_async_copy(ybuf.at[slot], yb.at[b % half], out_sems.at[1, slot]),
        )

    def wait_slot(slot):
        pltpu.make_async_copy(dxbuf.at[slot], dxa.at[0], out_sems.at[0, slot]).wait()
        pltpu.make_async_copy(ybuf.at[slot], ya.at[0], out_sems.at[1, slot]).wait()

    want = lax.broadcasted_iota(jnp.int32, (SEG, toks), 0).astype(f32)
    tab_rows = lax.broadcasted_iota(jnp.int32, (TAB, toks), 0)

    def combine_body(b, carry):
        slot = b % 2

        @pl.when(b >= 2)
        def _():
            wait_slot(slot)

        tab_ref[...] = pbuf[b, toks : toks + TAB, :].astype(f32)
        hots, segs = [], []
        table = jnp.zeros((TAB, toks), f32)
        for i in range(experts):
            rank = tab_ref[pl.ds(first + i, 1), 0:toks]
            match = jnp.where(want == rank, 1.0, 0.0)
            at = pl.ds(pl.multiple_of(starts[b, i], 16), SEG)
            hots.append(match.astype(bf16))
            segs.append(back_ref[i, at, :])
            line = jnp.sum(match * gate_ref[i, at, :][:, :1], axis=0, keepdims=True)
            table += jnp.where(tab_rows == first + i, line, 0.0)
        result = dot(jnp.concatenate(hots, axis=0), jnp.concatenate(segs, axis=0), 0, 0)
        dxbuf[slot] = result[:, :D].astype(bf16)
        ybuf[slot, 0:toks, :] = result[:, D:].astype(bf16)
        ybuf[slot, toks : toks + TAB, 0:toks] = table.astype(bf16)
        ybuf[slot, toks : toks + TAB, toks:] = jnp.zeros((TAB, D - toks), bf16)
        near, here, there = out_copies(b, slot)

        @pl.when(near)
        def _():
            here[0].start()
            here[1].start()

        @pl.when(jnp.logical_not(near))
        def _():
            there[0].start()
            there[1].start()

        return carry

    lax.fori_loop(0, nb, combine_body, 0)
    wait_slot(0)
    wait_slot(1)
    rows_copy.wait()


def dispatch_kernel(pieces, arrays, tile, first_ref, *refs):
    srcs, refs = refs[:arrays], refs[arrays:]
    rows_out, used, xbuf, pbuf, rows_ref, tab_ref, offs, tok_sems, row_sem = refs
    experts = rows_ref.shape[0]
    ring = xbuf.shape[0]
    first = first_ref[0]
    total = sum(p[0] for p in pieces)

    def start_block(b):
        slot = b % ring
        begin = 0
        for blocks, x_parts, p_parts in pieces:

            @pl.when((b >= begin) & (b < begin + blocks))
            def _(begin=begin, x_parts=x_parts, p_parts=p_parts):
                for which, (parts, buf) in enumerate(((x_parts, xbuf), (p_parts, pbuf))):
                    for array, at, lo, hi in parts:
                        pltpu.make_async_copy(
                            srcs[array].at[b - begin + at],
                            buf.at[slot, lo:hi],
                            tok_sems.at[which, slot],
                        ).start()

            begin += blocks

    def start_body(b, carry):
        start_block(b)
        return carry

    lax.fori_loop(0, min(ring - 1, total), start_body, 0)
    for i in range(experts):
        offs[i] = 0

    def dispatch_body(b, carry):
        slot = b % ring
        pltpu.make_async_copy(xbuf.at[slot], xbuf.at[slot], tok_sems.at[0, slot]).wait()
        pltpu.make_async_copy(pbuf.at[slot], pbuf.at[slot], tok_sems.at[1, slot]).wait()

        @pl.when(b + ring - 1 < total)
        def _():
            start_block(b + ring - 1)

        dispatch_block(
            first, experts, xbuf[slot], pbuf.at[slot], tab_ref, rows_ref, None, offs, None, b
        )
        return carry

    lax.fori_loop(0, total, dispatch_body, 0)

    def chunk(i, j):
        at = pl.ds(pl.multiple_of(j * tile, tile), tile)
        return pltpu.make_async_copy(rows_ref.at[i, at], rows_out.at[i, at], row_sem)

    def chunks(i):
        return jnp.maximum((offs[i] + tile - 1) // tile, 1)

    def start_chunk(i):
        def body(j, carry):
            chunk(i, j).start()
            return carry

        return body

    def wait_chunk(i):
        def body(j, carry):
            chunk(i, j).wait()
            return carry

        return body

    for i in range(experts):
        rows_ref[i, pl.ds(pl.multiple_of(offs[i], 16), tile), :] = jnp.zeros((tile, 2 * D), bf16)
        used[i] = offs[i]
        lax.fori_loop(0, chunks(i), start_chunk(i), 0)
    for i in range(experts):
        lax.fori_loop(0, chunks(i), wait_chunk(i), 0)


def weight_kernel(tile, experts, given, add, begin_ref, used_ref, rows_h, wg_h, wu_h, wd_h, *refs):
    begin_e = begin_ref[0]
    small = max(tile // 2, TILE_BACK)
    olds, refs = (refs[:3], refs[3:]) if given else ((), refs)
    outs, accs = refs[:3], refs[3:6]
    rbuf, wg, wu, wd, row_sems, w_sems, acc_sems = refs[6:]
    w_copies = [
        pltpu.make_async_copy(src.at[pl.ds(begin_e, experts)], dst, w_sems.at[k])
        for k, (src, dst) in enumerate(((wg_h, wg), (wu_h, wu), (wd_h, wd)))
    ]

    def tiles(e):
        return jnp.maximum((used_ref[begin_e + e] + tile - 1) // tile, 1)

    def fetch(e, j, slot):
        at = pl.ds(pl.multiple_of(j * tile, tile), tile)
        return pltpu.make_async_copy(
            rows_h.at[begin_e + e, at], rbuf.at[slot], row_sems.at[slot]
        )

    def out_copies(e):
        return [
            pltpu.make_async_copy(src, dst.at[e + begin_e], acc_sems.at[k])
            for k, (src, dst) in enumerate(zip(accs, outs))
        ]

    def old_copies(e):
        return [
            pltpu.make_async_copy(src.at[e + begin_e], dst, acc_sems.at[k])
            for k, (src, dst) in enumerate(zip(olds, accs))
        ]

    fetch(0, 0, 0).start()
    for copy in w_copies:
        copy.start()
    if add:
        for copy in old_copies(0):
            copy.start()
    for copy in w_copies:
        copy.wait()

    def expert_body(e, count):
        last = tiles(e)

        def tile_body(j, step):
            slot = step % 2
            fetch(e, j, slot).wait()

            @pl.when(j + 1 < last)
            def _():
                fetch(e, j + 1, 1 - slot).start()

            @pl.when((j + 1 == last) & (e + 1 < experts))
            def _():
                fetch(e + 1, 0, 1 - slot).start()


            @pl.when(j == 0)
            def _():
                @pl.when(e > 0)
                def _():
                    for copy in out_copies(e - 1):
                        copy.wait()
                    if add:
                        for copy in old_copies(e):
                            copy.start()

                if add:
                    for copy in old_copies(e):
                        copy.wait()
                else:
                    for acc in accs:
                        acc[...] = jnp.zeros(acc.shape, f32)

            def work(size):
                rows = rbuf[slot, 0:size]
                act, grad, hidden, _, grad_gate, grad_up = expert_acts(rows, wg[e], wu[e], wd[e])
                part = dot(act, jnp.concatenate([grad_gate, grad_up], axis=1), 0, 0)
                width = grad_gate.shape[1]
                accs[0][...] += part[:, :width]
                accs[1][...] += part[:, width:]
                accs[2][...] += dot(hidden, grad, 0, 0)

            if small < tile:
                little = used_ref[begin_e + e] - j * tile <= small

                @pl.when(little)
                def _():
                    work(small)

                @pl.when(jnp.logical_not(little))
                def _():
                    work(tile)

            else:
                work(tile)
            return step + 1

        count = lax.fori_loop(0, last, tile_body, count)
        for copy in out_copies(e):
            copy.start()
        return count

    lax.fori_loop(0, experts, expert_body, jnp.int32(0))
    for copy in out_copies(experts - 1):
        copy.wait()


def row_room(cap, blocks, groups, tile):
    most = groups * min(cap + 15 * blocks, SEG * blocks)
    return -(-most // tile) * tile + tile


def own_experts(first, tops, lows, ps, wg, wu, wd, cap):
    nb = len(ps)
    experts = wg.shape[0]
    toks = ps[0].shape[0] - TAB
    room = row_room(cap, nb, 1, TILE_BACK)
    half = nb // 2
    shapes = [
        jax.ShapeDtypeStruct((half, toks, D), bf16),
        jax.ShapeDtypeStruct((half, toks, D), bf16),
        jax.ShapeDtypeStruct((half, toks + TAB, D), bf16),
        jax.ShapeDtypeStruct((half, toks + TAB, D), bf16),
        jax.ShapeDtypeStruct((experts, room, 2 * D), bf16),
        jax.ShapeDtypeStruct((experts,), jnp.int32),
    ]
    return pl.pallas_call(
        functools.partial(own_kernel, nb, TILE_OWN),
        out_shape=shapes,
        in_specs=[SM] + [HB] * (3 * nb + 3),
        out_specs=[HB] * 5 + [SM],
        scratch_shapes=[
            pltpu.VMEM((nb, toks, D), bf16),
            pltpu.VMEM((nb, toks + TAB, D), bf16),
            pltpu.VMEM(wg.shape, bf16),
            pltpu.VMEM(wu.shape, bf16),
            pltpu.VMEM(wd.shape, bf16),
            pltpu.VMEM((experts, room, 2 * D), bf16),
            pltpu.VMEM((experts, room, 2 * D), bf16),
            pltpu.VMEM((experts, room, 128), f32),
            pltpu.VMEM((TAB, D), f32),
            pltpu.VMEM((2, toks, D), bf16),
            pltpu.VMEM((2, toks + TAB, D), bf16),
            pltpu.SMEM((experts,), jnp.int32),
            pltpu.SMEM((nb, experts), jnp.int32),
            pltpu.SemaphoreType.DMA((3, nb)),
            pltpu.SemaphoreType.DMA((3,)),
            pltpu.SemaphoreType.DMA((2, 2)),
            pltpu.SemaphoreType.DMA,
        ],
        compiler_params=params(),
        name="own_experts",
        cost_estimate=cost(29),
    )(first, *tops, *lows, *ps, wg, wu, wd)


def chip_pieces(x_sets, p_sets, blocks, toks):
    flat = [a for sets in (x_sets, p_sets) for arrays in sets for a in arrays]
    half = toks // 2
    x_count = x_sets[0][0].shape[0] // blocks
    pieces = []
    for k in range(4 * x_count):
        core, x, y = k // (2 * x_count), k // 2 % x_count, k % 2
        parts, base = [], 0
        for sets, end in ((x_sets, toks), (p_sets, toks + TAB)):
            top, low = base + core * 2 + y, base + len(sets[0]) + core * x_count + x
            parts.append(((top, x * blocks, 0, half), (low, y * blocks, half, end)))
            base += len(sets[0]) + len(sets[1])
        pieces.append((blocks, *parts))
    return flat, pieces


def dispatch(first, flat, pieces, toks, experts, cap, groups):
    total = sum(p[0] for p in pieces)
    ring = 4
    room = row_room(cap, total // groups, groups, TILE_FAR)
    return pl.pallas_call(
        functools.partial(dispatch_kernel, tuple(pieces), len(flat), TILE_FAR),
        out_shape=[
            jax.ShapeDtypeStruct((experts, room, 2 * D), bf16),
            jax.ShapeDtypeStruct((experts,), jnp.int32),
        ],
        in_specs=[SM] + [HB] * len(flat),
        out_specs=[HB, SM],
        scratch_shapes=[
            pltpu.VMEM((ring, toks, D), bf16),
            pltpu.VMEM((ring, toks + TAB, D), bf16),
            pltpu.VMEM((experts, room, 2 * D), bf16),
            pltpu.VMEM((TAB, D), f32),
            pltpu.SMEM((experts,), jnp.int32),
            pltpu.SemaphoreType.DMA((2, ring)),
            pltpu.SemaphoreType.DMA,
        ],
        compiler_params=params(),
        name="dispatch",
        cost_estimate=cost(20),
    )(first, *flat)


def weight_grads(used, rows, weights, tile, olds=None, add=True, begin_e=0, count_e=None):
    experts = count_e or weights[0].shape[0]
    shapes = [jax.ShapeDtypeStruct(w.shape, f32) for w in weights]
    operands = [jnp.full((1,), begin_e, jnp.int32), used, rows, *weights, *(olds or ())]
    return pl.pallas_call(
        functools.partial(weight_kernel, tile, experts, bool(olds), bool(olds) and add),
        out_shape=shapes,
        in_specs=[SM, SM] + [HB] * (len(operands) - 2),
        out_specs=[HB] * 3,
        input_output_aliases={len(operands) - 3 + k: k for k in range(3)} if olds else {},
        scratch_shapes=[
            *[pltpu.VMEM(w.shape[1:], f32) for w in weights],
            pltpu.VMEM((2, tile, 2 * D), bf16),
            *[pltpu.VMEM((experts, *w.shape[1:]), bf16) for w in weights],
            pltpu.SemaphoreType.DMA((2,)),
            pltpu.SemaphoreType.DMA((3,)),
            pltpu.SemaphoreType.DMA((3,)),
        ],
        compiler_params=params(),
        name="weight_grads",
        cost_estimate=cost(14),
    )(*operands)


def after(value, *deps):
    return lax.optimization_barrier((value, *deps))[0]


def after_all(values, *deps):
    return lax.optimization_barrier((*values, *deps))[: len(values)]


def after_tree(tree, *deps):
    return lax.optimization_barrier((tree, *deps))[0]


def other_groups(copies, cut):
    count, index = lax.axis_size("dp"), lax.axis_index("dp")
    blocks = lax.all_to_all(copies, "dp", 0, 0, tiled=True)

    def pick(blocks, rows):
        found = [
            lax.dynamic_index_in_dim(blocks, (index + step) % count, 0)[:, rows]
            for step in range(1, count)
        ]
        return jnp.concatenate(found, axis=0)

    return blocks, lambda b: (pick(b, slice(0, cut)), pick(b, slice(cut, None)))


def gather_line(values, axis):
    out = list(values)
    for step in range(1, lax.axis_size(axis)):
        out += [shift(v, axis, step) for v in values]
    return out


def with_line(values, axis):
    return gather_line([jnp.concatenate(values, axis=0)], axis)


def plane_gather(value, x_first):
    if x_first:
        cols = gather_line([value], "x")
        rows = [shift(v, "y", 1) for v in cols]
        return [v for pair in zip(cols, rows) for v in pair]
    return gather_line(gather_line([value], "y"), "x")


def both_cores(values, *deps):
    return list(values) + [shift(after(v, *deps) if deps else v, "c", 1) for v in values]


def total(*parts):
    return sum(p.astype(f32) for p in parts).astype(bf16)


def scatter_cores(parts):
    return parts[0], shift(parts[1], "c", -1)


def scatter_first(keep, other, cut):
    count = lax.axis_size("x")

    def add(rows, where):
        return total(keep[where][:, rows], other[where][:, rows])

    top, low = slice(0, cut), slice(cut, None)
    x_sent = [add(top, slice(2 * k, 2 * k + 2)) for k in range(1, count)]
    y_sent = add(low, slice(1, None, 2))
    x_kept = add(top, slice(0, 2))
    y_kept = add(low, slice(0, None, 2))
    x_got = [shift(v, "x", -k) for k, v in zip(range(1, count), x_sent)]
    y_got = shift(y_sent, "y", -1)
    return (*x_got, y_got), x_kept, y_kept


def scatter_second(got, x_kept, y_kept):
    x_got, y_got = got[:-1], got[-1]
    count = len(got)
    y_next = total(x_kept[1], *[v[1] for v in x_got])
    x_next = [total(y_kept[k], y_got[k]) for k in range(1, count)]
    top_own = total(x_kept[0], *[v[0] for v in x_got])
    low_own = total(y_kept[0], y_got[0])
    top_far = shift(y_next, "y", -1)
    low_far = [shift(v, "x", -k) for k, v in zip(range(1, count), x_next)]
    if count > 2:
        low_far = [total(*low_far)]
    return top_own, top_far, low_own, low_far[0]


def line_sum(value, axis):
    return sum([shift(value, axis, step) for step in range(1, lax.axis_size(axis))], value)


def row_sum(value):
    far = lax.ppermute(value, ("y", "c"), [(i, 3 - i) for i in range(4)])
    return value + shift(value, "c", 1) + shift(value, "y", 1) + far


def scatter_sum(value, axis):
    count, index = lax.axis_size(axis), lax.axis_index(axis)
    chunks = value.reshape((count, value.shape[0] // count) + value.shape[1:])
    result = lax.dynamic_index_in_dim(chunks, index, 0, keepdims=False).astype(f32)
    for step in range(1, count):
        chunk = lax.dynamic_index_in_dim(chunks, (index + step) % count, 0, keepdims=False)
        result = result + shift(chunk, axis, step).astype(f32)
    return result.astype(bf16)


def gather_chunks(own, axis):
    count, index = lax.axis_size(axis), lax.axis_index(axis)
    full = jnp.zeros((count,) + own.shape, bf16)
    full = lax.dynamic_update_index_in_dim(full, own, index, 0)
    for step in range(1, count):
        chunk = shift(own, axis, step)
        full = lax.dynamic_update_index_in_dim(full, chunk, (index - step) % count, 0)
    return full.reshape((count * own.shape[0],) + own.shape[1:])


def shards(
    inputs,
    cotangent,
    gain_attn,
    gain_ffn,
    attn_in,
    attn_out,
    expert_gate,
    expert_up,
    expert_down,
    const_vectors,
    gate_values,
    routes,
    priority,
    pieces,
):
    toks = inputs.shape[1]
    y_index, c_index = lax.axis_index("y"), lax.axis_index("c")
    x_index, x_count = lax.axis_index("x"), lax.axis_size("x")
    dp_count = lax.axis_size("dp")
    row_count = lax.axis_size("y") * lax.axis_size("c")
    seq = toks * row_count
    heads = attn_in.shape[2] // HEAD_DIM
    width = heads * HEAD_DIM
    group_tokens = routes.shape[1]
    nb = group_tokens // toks
    cap = 5 * group_tokens // 24
    experts = expert_gate.shape[0]
    x_own, cot = inputs[0], cotangent[0]
    place = jnp.stack(
        [
            ((y_index - ky) % 2) * 2 + (c_index - kc) % 2
            for ky in range(2)
            for kc in range(2)
        ]
    ).astype(jnp.int32)
    first = (x_index * experts).astype(jnp.int32)[None]
    base = (x_index * seq + (y_index * 2 + c_index) * toks).astype(jnp.int32)[None]

    x_y = shift(x_own, "y", 1)
    w_y = shift(after(attn_out, x_y), "y", 1)
    w_c = shift(attn_out, "c", 1)

    cosine, sine = (jnp.asarray(a) for a in rotary_numpy(seq))
    routes_t, gates_t = routes[0].T, gate_values[0].T
    attn_w = attn_in.transpose(0, 2, 1)
    weights = (expert_gate, expert_up, expert_down)
    half = toks // 2
    far = list(range(1, dp_count))
    one_call = dp_count * group_tokens <= CALL_TOKENS

    payload, p_copies = pl.pallas_call(
        functools.partial(route_kernel, cap),
        out_shape=[
            jax.ShapeDtypeStruct((toks + TAB, D), bf16),
            jax.ShapeDtypeStruct((dp_count if one_call else 1, toks + TAB, D), bf16),
        ],
        in_specs=[SM, VM, VM, VM, VM],
        out_specs=[VM, VM],
        compiler_params=params(),
        name="route",
        cost_estimate=cost(2.5),
    )(base, routes_t, priority, gates_t, cot)
    if one_call:
        far_p, split_p = other_groups(p_copies, half)
    x_slots = [x_own, shift(x_own, "c", 1), x_y, shift(after(x_y, payload), "c", 1)]
    p_cols = gather_line([payload], "x")
    p_y = shift(after(payload, x_y), "y", 1)

    mix_shape = jax.ShapeDtypeStruct((toks, width), bf16)
    fwd_out = attn_fwd(after(place, payload), x_slots, gain_attn, attn_w, cosine, sine, pieces)
    fwd_out = after_all(fwd_out, *p_cols, p_y, w_y, w_c)
    q, k, v, probs, *mixed = fwd_out

    def to_owner(parts):
        return [
            parts[0],
            shift(parts[1], "c", -1),
            shift(parts[2], "y", -1),
            lax.ppermute(parts[3], ("y", "c"), [(i, 3 - i) for i in range(4)]),
        ]

    started = mixed[0]
    w_slots = [attn_out, w_c, w_y, shift(after(w_y, started), "c", 1)]
    own_p = [p_cols[0], p_y]
    for step, p in enumerate(p_cols[1:], 1):
        own_p += [p, shift(after(p_y, started), "x", step)]
    own_p = both_cores(own_p, started)
    if one_call:
        p_top, p_low = split_p(after(far_p, started))
    mixed = to_owner(mixed)
    resid, norm_two, norm_top, norm_low, x_copies = pl.pallas_call(
        out_proj_kernel,
        out_shape=[
            jax.ShapeDtypeStruct((toks, D), f32),
            jax.ShapeDtypeStruct((toks, D), bf16),
            jax.ShapeDtypeStruct((half, D), bf16),
            jax.ShapeDtypeStruct((half, D), bf16),
            jax.ShapeDtypeStruct((dp_count if one_call else 1, toks, D), bf16),
        ],
        in_specs=[VM] * 10,
        out_specs=[VM] * 5,
        compiler_params=params(),
        name="out_proj",
        cost_estimate=cost(3),
    )(x_own, *mixed, *w_slots, after(gain_ffn, own_p[2 * x_count - 1]))

    tops = plane_gather(norm_top, True)
    lows = plane_gather(norm_low, False)
    arrived = (tops[-1], lows[-1])
    ready = ()
    if one_call:
        far_x, split_x = other_groups(x_copies, half)
        first_in = (tops[1], tops[2], lows[1], lows[2])
        p_top_x = gather_line([after(p_top, *first_in)], "x")
        p_low_y = gather_line([after(p_low, *first_in)], "y")
        ready = (p_top_x[-1], p_low_y[-1])
        p_top = with_line(after_all(p_top_x, *arrived), "y")
        p_low = with_line(after_all(p_low_y, *arrived), "x")
    tops, lows = both_cores(tops), both_cores(lows)
    own_out = own_experts(after(first, *ready), tops, lows, own_p, *weights, cap)
    if one_call:
        own_out = after_all(own_out, *p_top, *p_low, far_x)
    dxa, dxb, ya, yb, rows, used = own_out
    dx_first = scatter_first(*scatter_cores((dxa, dxb)), half)
    dx_stage = dx_first[0][-1]
    dx_parts = scatter_second(*dx_first)
    if one_call:
        p_near = [shift(after(a[0], dx_first[1]), "c", 1) for a in (p_top, p_low)]
    front = max(1, experts // 2)
    grads_w = weight_grads(after(used, dx_first[1]), rows, weights, TILE_BACK, count_e=front)
    if one_call:
        x_top, x_low = split_x(after(far_x, dx_stage, grads_w[0]))
        x_top_x = gather_line([x_top], "x")
        x_low_y = gather_line([x_low], "y")
        used = after(used, *p_near)
    for begin in range(front, experts, front):
        grads_w = weight_grads(
            after(used, dx_stage), rows, weights, TILE_BACK, grads_w, False, begin, front
        )

    gres, *mids = pl.pallas_call(
        lambda base_ref, *refs: mid_kernel(
            base_ref,
            refs[0:4],
            *refs[4:9],
            refs[9:13],
            refs[13:17],
            refs[17],
            refs[18:22],
            refs[22:24],
            refs[24],
        ),
        out_shape=[jax.ShapeDtypeStruct((toks, D), f32)]
        + [mix_shape] * 4
        + [jax.ShapeDtypeStruct((2, width, D), bf16)] * 2
        + [jax.ShapeDtypeStruct((8, D), f32)],
        in_specs=[SM] + [VM] * 17,
        out_specs=[VM] * 8,
        compiler_params=params(),
        name="mid",
        cost_estimate=cost(5),
    )(
        after(base, grads_w[0], *((*x_top_x, *x_low_y) if one_call else ())),
        *dx_parts,
        cot,
        resid,
        routes_t,
        gates_t,
        gain_ffn,
        *mixed,
        *w_slots,
    )
    out_keep, out_send, sums = mids[4:]
    grads = to_owner(mids[:4])
    out_other = shift(out_send, "c", -1)
    out_sent = total(out_keep[1], out_other[1])
    out_far = shift(out_sent, "y", -1)
    ready = ()
    if one_call:
        ready = (x_top_x[-1], x_low_y[-1])
        x_top = with_line(after_all(x_top_x, out_other), "y")
        x_low = with_line(after_all(x_low_y, out_other), "x")
        p_other = [shift(after(a[1], *grads), "c", 1) for a in (p_top, p_low)]
    tables = (cosine, sine)
    unit = 8 * x_count * dp_count
    dw_rows = -(-(4 * width + 8) // unit) * unit
    saved = (q, k, v, probs)
    bwd_out = attn_bwd(
        place, x_slots, grads, gain_attn, attn_w, tables, saved, sums, dw_rows
    )
    if one_call:
        bwd_out = after_all(bwd_out, *x_top, *x_low, *p_other, out_far)
    gno_keep, gno_send, dw_in, gain_part = bwd_out
    gno_other = shift(gno_send, "c", -1)
    gno_far = (gno_keep[1].astype(f32) + gno_other[1].astype(f32)).astype(bf16)
    gno_near = (gno_keep[0].astype(f32) + gno_other[0].astype(f32)).astype(bf16)

    dw_out = total(out_keep[0], out_other[0], out_far)
    attn_grads = lax.dynamic_update_slice(dw_in, dw_out, (3 * width, 0))
    y_stage = scatter_cores(after_all((ya, yb), gno_other))
    gno_far = shift(gno_far, "y", -1)

    if one_call:
        x_near = [shift(after(a[0], gain_part), "c", 1) for a in (x_top, x_low)]
        x_other = [shift(after(a[1], gain_part), "c", 1) for a in (x_top, x_low)]
        x_sets = [[*a, n, o] for a, n, o in zip((x_top, x_low), x_near, x_other)]
        p_sets = [[*a, n, o] for a, n, o in zip((p_top, p_low), p_near, p_other)]
        flat, spots = chip_pieces(x_sets, p_sets, len(far), toks)
        part = scatter_sum(after(attn_grads, *x_near, *x_other), "x")
        rows, used = dispatch(after(first, gain_part), flat, spots, toks, experts, cap, len(far))
        used = after(used, part, gno_far, *y_stage)
        part, y_stage = after_tree((part, y_stage), used)
        part = scatter_sum(part, "dp")
        y_stage = scatter_first(*y_stage, half)
        for e in range(min(experts, 3)):
            many = experts - e if e == 2 else 1
            grads_w = weight_grads(used, rows, weights, TILE_FAR, grads_w, True, e, many)
            if e == 0:
                used = after(used, grads_w[0], part, *y_stage[0])
                part = gather_chunks(after(part, used), "dp")
            elif e == 1:
                used = after(used, grads_w[0], part)
                part, y_stage = after_tree((part, y_stage), used)
                attn_grads = gather_chunks(part, "x")
                y_parts = scatter_second(*y_stage)
            elif e == 2:
                attn_grads, *y_parts = after_all((attn_grads, *y_parts), grads_w[0])
                sums = row_sum(attn_grads[4 * width : 4 * width + 4].astype(f32))
    else:
        part = scatter_sum(scatter_sum(attn_grads, "x"), "dp")
        attn_grads = gather_chunks(gather_chunks(part, "dp"), "x")
        sums = row_sum(attn_grads[4 * width : 4 * width + 4].astype(f32))
        y_parts = scatter_second(*scatter_first(*y_stage, half))
        spots = [(nb, ((0, 0, 0, toks),), ((1, 0, 0, toks + TAB),))]

        def next_group(step, carry):
            x_block, p_block, *sums_w = carry
            x_block, p_block = shift(x_block, "dp", 1), shift(p_block, "dp", 1)
            flat = [lax.all_gather(a, ("y", "c", "x")) for a in (x_block, p_block)]
            rows, used = dispatch(first, flat, spots, toks, experts, cap, 1)
            return x_block, p_block, *weight_grads(used, rows, weights, TILE_FAR, sums_w)

        grads_w = lax.fori_loop(1, dp_count, next_group, (norm_two, payload, *grads_w))[2:]
    grad_w_gate, grad_w_up, grad_w_down = grads_w
    grad_w_in = attn_grads[: 3 * width].astype(f32).reshape(3, width, D).transpose(0, 2, 1)
    grad_w_out = attn_grads[3 * width : 4 * width].astype(f32)
    input_grad = pl.pallas_call(
        last_kernel,
        out_shape=jax.ShapeDtypeStruct((toks, D), f32),
        in_specs=[VM] * 5,
        out_specs=VM,
        compiler_params=params(),
        name="last",
        cost_estimate=cost(3),
    )(gno_near, gno_far, x_own, gres, gain_attn)

    block_out, grad_gates = pl.pallas_call(
        lambda base_ref, *refs: out_kernel(base_ref, refs[0:4], *refs[4:]),
        out_shape=[
            jax.ShapeDtypeStruct((toks, D), bf16),
            jax.ShapeDtypeStruct((2, toks), f32),
        ],
        in_specs=[SM] + [VM] * 10,
        out_specs=[VM] * 2,
        compiler_params=params(),
        name="block_out",
        cost_estimate=cost(3),
    )(base, *y_parts, cot, resid, norm_two, routes_t, gates_t, const_vectors)

    return (
        block_out[None],
        input_grad[None],
        sums[3],
        sums[0],
        grad_w_in,
        grad_w_out,
        grad_w_gate,
        grad_w_up,
        grad_w_down,
        sums[1:3],
        grad_gates.T[None],
    )


def solution(mesh):
    dp, row, col = mesh.devices.shape
    fine = Mesh(mesh.devices.reshape(dp, row // 2, 2, col), ("dp", "y", "c", "x"))
    rows = ("y", "c")
    in_specs = (
        P(("dp", "x"), rows, None),
        P(("dp", "x"), rows, None),
        P(),
        P(),
        P(None, None, rows),
        P(rows, None),
        P("x", None, rows),
        P("x", None, rows),
        P("x", rows, None),
        P(),
        P(("dp", "x"), rows, None),
        P("dp", None, None),
        P("dp", None),
        P(("dp", "x"), None),
    )
    out_specs = (
        P(("dp", "x"), rows, None),
        P(("dp", "x"), rows, None),
        P(),
        P(),
        P(None, None, rows),
        P(rows, None),
        P("x", None, rows),
        P("x", None, rows),
        P("x", rows, None),
        P(),
        P(("dp", "x"), rows, None),
    )
    return jax.shard_map(shards, mesh=fine, in_specs=in_specs, out_specs=out_specs, check_vma=False)
```

```python
import functools

import jax
import jax.numpy as jnp
import numpy as np
from jax import lax
from jax.experimental import pallas as pl
from jax.experimental.pallas import tpu as pltpu
from jax.sharding import Mesh
from jax.sharding import PartitionSpec as P

D = 768
HEAD_DIM = 64
E_FFN = 8
MOST = 88
SHORT = 48
SEG = 96
TAB = 8
TILE_OWN = 192
TILE_BACK = 256
TILE_FAR = 512
CALL_TOKENS = 8192

norm_eps = 1e-05
masked_score = -1e30
bf16 = jnp.bfloat16
f32 = jnp.float32
VMEM_MAX = 60 * 1024 * 1024


def dot(a, b, ca=1, cb=0):
    return lax.dot_general(a, b, (((ca,), (cb,)), ((), ())), preferred_element_type=f32)


def params(**kw):
    return pltpu.CompilerParams(vmem_limit_bytes=VMEM_MAX, **kw)


def cost(micros):
    return pl.CostEstimate(
        flops=int(micros * 1.1e9), transcendentals=0, bytes_accessed=int(micros * 3.5e6)
    )


VM = pl.BlockSpec(memory_space=pltpu.VMEM)
SM = pl.BlockSpec(memory_space=pltpu.SMEM)
HB = pl.BlockSpec(memory_space=pl.ANY)


def shift(value, axis, step):
    count = lax.axis_size(axis)
    return lax.ppermute(value, axis, [(i, (i + step) % count) for i in range(count)])


def gain_row(ref):
    return ref[...].reshape(1, D)


def normed(rows, gain):
    inverse = lax.rsqrt(jnp.mean(rows * rows, axis=-1, keepdims=True) + norm_eps)
    unit = rows * inverse
    return unit, inverse, (unit * gain).astype(bf16)


def rotary_numpy(length):
    half = HEAD_DIM // 2
    frequency = (10000.0 ** (-np.arange(half, dtype=np.float32) / half)).astype(np.float32)
    angles = frequency[:, None] * np.arange(length, dtype=np.float32)[None, :]
    cosine = np.tile(np.cos(angles), (2, 1)).astype(np.float32)
    sine = np.tile(np.sin(angles), (2, 1)).astype(np.float32)
    return cosine, sine


def partner_matrix(width):
    i = lax.broadcasted_iota(jnp.int32, (width, width), 0)
    j = lax.broadcasted_iota(jnp.int32, (width, width), 1)
    low = (j % HEAD_DIM) < HEAD_DIM // 2
    minus = jnp.where(low & (i == j + HEAD_DIM // 2), -1.0, 0.0)
    plus = jnp.where((~low) & (i == j - HEAD_DIM // 2), 1.0, 0.0)
    return (minus + plus).astype(bf16)


def eye(width):
    i = lax.broadcasted_iota(jnp.int32, (width, width), 0)
    j = lax.broadcasted_iota(jnp.int32, (width, width), 1)
    return jnp.where(i == j, 1.0, 0.0).astype(bf16)


def route_kernel(cap, base_ref, routes_ref, prio_ref, gates_ref, cot_ref, out_ref, copies_ref):
    total = prio_ref.shape[1]
    toks = cot_ref.shape[0]
    base = pl.multiple_of(base_ref[0], toks)
    prio = prio_ref[...].astype(f32)
    own_row = prio_ref[:, pl.ds(base, toks)].astype(f32)
    own_col = jnp.broadcast_to(own_row, (8, toks)).T[:, :1]
    earlier = jnp.where(prio < own_col, 1.0, 0.0).astype(bf16)
    ids = lax.broadcasted_iota(jnp.int32, (16, total), 0)
    named = (routes_ref[0:1, :] == ids) | (routes_ref[1:2, :] == ids)
    slots = dot(jnp.where(named, 1.0, 0.0).astype(bf16), earlier, 1, 1)
    own_ids = lax.broadcasted_iota(jnp.int32, (16, toks), 0)
    first = routes_ref[0:1, pl.ds(base, toks)] == own_ids
    second = routes_ref[1:2, pl.ds(base, toks)] == own_ids
    kept = (first | second) & (own_ids < E_FFN) & (slots < cap)
    before_i = lax.broadcasted_iota(jnp.int32, (toks, toks), 0)
    before_j = lax.broadcasted_iota(jnp.int32, (toks, toks), 1)
    lower = jnp.where(before_i < before_j, 1.0, 0.0).astype(bf16)
    rank = dot(jnp.where(kept, 1.0, 0.0).astype(bf16), lower)
    rank = jnp.where(kept, rank, -1.0)
    gate = jnp.where(first, gates_ref[0:1, :], 0.0) + jnp.where(second, gates_ref[1:2, :], 0.0)
    high = gate.astype(bf16)
    rest = (gate - high.astype(f32)).astype(bf16)
    table = jnp.concatenate([rank[:TAB].astype(bf16), high[:TAB], rest[:TAB]], axis=1)
    out_ref[0:toks, :] = cot_ref[...]
    out_ref[toks : toks + TAB, :] = table
    for k in range(copies_ref.shape[0]):
        copies_ref[k, 0:toks, :] = cot_ref[...]
        copies_ref[k, toks : toks + TAB, :] = table


def attn_fwd_kernel(
    heads,
    place_ref,
    x0,
    x1,
    x2,
    x3,
    gain_ref,
    w_ref,
    cos_ref,
    sin_ref,
    prow_ref,
    q_ref,
    k_ref,
    v_ref,
    pt_ref,
    m0,
    m1,
    m2,
    m3,
    bias_ref,
    pbuf,
    obuf,
    vt_ref,
    sems,
):
    toks = x0.shape[0]
    width = heads * HEAD_DIM
    slots = 4
    seq = slots * toks
    swap = partner_matrix(width)
    wq, wk, wv = w_ref[0], w_ref[1], w_ref[2]
    wq_swap = dot(swap, wq, 0, 0).astype(bf16)
    wk_swap = dot(swap, wk, 0, 0).astype(bf16)
    piece_col = jnp.broadcast_to(prow_ref[...].astype(f32), (8, seq)).T[:, :1]
    for slot, x_ref in enumerate((x0, x1, x2, x3)):
        start = pl.multiple_of(place_ref[slot] * toks, toks)
        rows = pl.ds(start, toks)
        _, _, act = normed(x_ref[...].astype(f32), gain_row(gain_ref))
        cosine = jnp.concatenate([cos_ref[:, rows].T] * heads, axis=1)
        sine = jnp.concatenate([sin_ref[:, rows].T] * heads, axis=1)
        queries = (dot(act, wq, 1, 1) * cosine + dot(act, wq_swap, 1, 1) * sine).astype(bf16)
        queries = (queries.astype(f32) * HEAD_DIM**-0.5).astype(bf16)
        keys = (dot(act, wk, 1, 1) * cosine + dot(act, wk_swap, 1, 1) * sine).astype(bf16)
        values = dot(act, wv, 1, 1).astype(bf16)
        for h in range(heads):
            cols = slice(h * HEAD_DIM, (h + 1) * HEAD_DIM)
            q_ref[h, rows, :] = queries[:, cols]
            k_ref[h, rows, :] = keys[:, cols]
            v_ref[h, rows, :] = values[:, cols]

    for h in range(heads):
        vt_ref[h] = v_ref[h].astype(f32).T.astype(bf16)

    def copy_out(block, h):
        keys = visible(block, slots) * toks
        return pltpu.make_async_copy(
            pbuf.at[h, 0:keys], pt_ref.at[block * heads + h, 0:keys], sems.at[h]
        )

    for block in range(slots):
        keys = visible(block, slots) * toks
        cols = slice(block * toks, (block + 1) * toks)
        kpos = lax.broadcasted_iota(jnp.int32, (keys, toks), 0)
        qpos = lax.broadcasted_iota(jnp.int32, (keys, toks), 1) + block * toks
        qp = prow_ref[:, cols].astype(f32)
        same = (piece_col[:keys] == qp) & (qp > 0.0)
        bias_ref[0:keys] = jnp.where((kpos <= qpos) | same, 0.0, masked_score)

        def head_body(h, carry, block=block, keys=keys, cols=cols):
            scores = dot(k_ref[h, 0:keys], q_ref[h, cols, :], 1, 1) + bias_ref[0:keys]
            peak = jnp.max(scores, axis=0, keepdims=True)
            weights = jnp.exp(scores - peak)
            mass = jnp.sum(weights, axis=0, keepdims=True)
            probs = (weights * (1.0 / mass)).astype(bf16)
            if block > 0:
                copy_out(block - 1, h).wait()
            pbuf[h, 0:keys] = probs
            copy_out(block, h).start()
            at = pl.ds(pl.multiple_of(h * HEAD_DIM, HEAD_DIM), HEAD_DIM)
            obuf[block, at, :] = dot(vt_ref[h, :, 0:keys], probs)
            return carry

        lax.fori_loop(0, heads, head_body, 0)
    for slot, m_ref in enumerate((m0, m1, m2, m3)):
        m_ref[...] = obuf[place_ref[slot]].T.astype(bf16)
    for h in range(heads):
        copy_out(slots - 1, h).wait()


def visible(block, slots):
    return min(block + 2, slots)


def attn_bwd_kernel(
    heads,
    place_ref,
    x0,
    x1,
    x2,
    x3,
    g0,
    g1,
    g2,
    g3,
    gain_ref,
    w_ref,
    cost_ref,
    sint_ref,
    q_ref,
    k_ref,
    v_ref,
    pt_ref,
    sums_ref,
    keep_ref,
    send_ref,
    dw_ref,
    done_ref,
    act_ref,
    go_ref,
    qcat_ref,
    kcat_ref,
    dk_ref,
    dv_ref,
    dqt_ref,
    dlin_ref,
    pbuf,
    sems,
):
    toks = x0.shape[0]
    width = heads * HEAD_DIM
    slots = 4

    def copy_in(block, h):
        keys = visible(block, slots) * toks
        return pltpu.make_async_copy(
            pt_ref.at[block * heads + h, 0:keys], pbuf.at[h, 0:keys], sems.at[h]
        )

    for h in range(heads):
        copy_in(0, h).start()
    swap = partner_matrix(HEAD_DIM)
    both = jnp.concatenate([eye(HEAD_DIM), swap], axis=1)
    swap_i = lax.broadcasted_iota(jnp.int32, (2 * HEAD_DIM, HEAD_DIM), 0)
    swap_j = lax.broadcasted_iota(jnp.int32, (2 * HEAD_DIM, HEAD_DIM), 1)
    low = ((swap_i - HEAD_DIM) < HEAD_DIM // 2) & (swap_i >= HEAD_DIM)
    high = (swap_i - HEAD_DIM) >= HEAD_DIM // 2
    stacked = (
        jnp.where(swap_i == swap_j, 1.0, 0.0)
        + jnp.where(low & (swap_j == swap_i - HEAD_DIM + HEAD_DIM // 2), -1.0, 0.0)
        + jnp.where(high & (swap_j == swap_i - HEAD_DIM - HEAD_DIM // 2), 1.0, 0.0)
    ).astype(bf16)
    for slot, (x_ref, g_ref) in enumerate(zip((x0, x1, x2, x3), (g0, g1, g2, g3))):
        rows = pl.ds(pl.multiple_of(place_ref[slot] * toks, toks), toks)
        _, _, act = normed(x_ref[...].astype(f32), gain_row(gain_ref))
        act_ref[rows, :] = act
        for h in range(heads):
            go_ref[h, rows, :] = g_ref[:, h * HEAD_DIM : (h + 1) * HEAD_DIM]
    for h in range(heads):
        qcat_ref[h] = dot(q_ref[h], both).astype(bf16)
        kcat_ref[h] = dot(stacked, k_ref[h], 1, 1).astype(bf16)
    dk_ref[...] = jnp.zeros(dk_ref.shape, f32)
    dv_ref[...] = jnp.zeros(dv_ref.shape, f32)

    for block in range(slots):
        keys = visible(block, slots) * toks
        cols = slice(block * toks, (block + 1) * toks)

        def head_body(h, carry, block=block, keys=keys, cols=cols):
            copy_in(block, h).wait()
            probs = pbuf[h, 0:keys]
            grad_out = go_ref[h, cols, :]
            grad_probs = dot(v_ref[h, 0:keys], grad_out, 1, 1)
            probs_f = probs.astype(f32)
            inner = jnp.sum(probs_f * grad_probs, axis=0, keepdims=True)
            grad_scores = (probs_f * (grad_probs - inner)).astype(bf16)
            dv_ref[h, 0:keys] += dot(probs, grad_out)
            dk_ref[h, 0:keys] += dot(grad_scores, qcat_ref[h, cols, :])
            dqt_ref[block, h] = dot(kcat_ref[h, :, 0:keys], grad_scores)
            if block + 1 < slots:
                copy_in(block + 1, h).start()
            return carry

        lax.fori_loop(0, heads, head_body, 0)
    cosine, sine = cost_ref[...].T, sint_ref[...].T
    for h in range(heads):
        cols = slice(h * HEAD_DIM, (h + 1) * HEAD_DIM)
        for block in range(slots):
            rows = slice(block * toks, (block + 1) * toks)
            both_t = dqt_ref[block, h]
            lin_t = (
                both_t[:HEAD_DIM] * cost_ref[:, rows] - both_t[HEAD_DIM:] * sint_ref[:, rows]
            ) * HEAD_DIM**-0.5
            dlin_ref[0, rows, cols] = lin_t.T.astype(bf16)
        dlin_ref[1, :, cols] = (
            dk_ref[h, :, :HEAD_DIM] * cosine - dk_ref[h, :, HEAD_DIM:] * sine
        ).astype(bf16)
        dlin_ref[2, :, cols] = dv_ref[h].astype(bf16)
    for k in range(3):
        dw_ref[k * width : (k + 1) * width, :] = dot(
            dlin_ref[k], act_ref[...], 0, 0
        ).astype(bf16)
    gain_grad = jnp.zeros((1, D), f32)
    for slot, x_ref in enumerate((x0, x1, x2, x3)):
        rows = pl.ds(pl.multiple_of(place_ref[slot] * toks, toks), toks)
        part = dot(dlin_ref[0, rows, :], w_ref[0])
        part += dot(dlin_ref[1, rows, :], w_ref[1])
        part += dot(dlin_ref[2, rows, :], w_ref[2])
        unit, _, _ = normed(x_ref[...].astype(f32), gain_row(gain_ref))
        gain_grad += jnp.sum(part * unit, axis=0, keepdims=True)
        if slot % 2 == 0:
            keep_ref[slot // 2] = part.astype(bf16)
        else:
            send_ref[slot // 2] = part.astype(bf16)
    rest = dw_ref.shape[0] - 4 * width
    ids = lax.broadcasted_iota(jnp.int32, (8, D), 0)
    tail = jnp.where(ids == 3, gain_grad, sums_ref[...])
    dw_ref[3 * width : 4 * width, :] = jnp.zeros((width, D), bf16)
    dw_ref[4 * width :, :] = jnp.zeros((rest, D), bf16)
    dw_ref[4 * width : 4 * width + 8, :] = tail.astype(bf16)
    done_ref[...] = jnp.zeros(done_ref.shape, f32)


def attn_fwd(place, x_slots, gain, w, cosine, sine, pieces):
    toks, width = x_slots[0].shape[0], w.shape[1]
    slots = len(x_slots)
    seq, heads = slots * toks, width // HEAD_DIM
    head_shape = jax.ShapeDtypeStruct((heads, seq, HEAD_DIM), bf16)
    return pl.pallas_call(
        functools.partial(attn_fwd_kernel, heads),
        out_shape=[head_shape] * 3
        + [jax.ShapeDtypeStruct((slots * heads, seq, toks), bf16)]
        + [jax.ShapeDtypeStruct((toks, width), bf16)] * slots,
        in_specs=[SM] + [VM] * 9,
        out_specs=[VM] * 3 + [HB] + [VM] * slots,
        scratch_shapes=[
            pltpu.VMEM((seq, toks), f32),
            pltpu.VMEM((heads, seq, toks), bf16),
            pltpu.VMEM((slots, width, toks), f32),
            pltpu.VMEM((heads, HEAD_DIM, seq), bf16),
            pltpu.SemaphoreType.DMA((heads,)),
        ],
        compiler_params=params(),
        name="attn_fwd",
        cost_estimate=cost(20),
    )(place, *x_slots, gain, w, cosine, sine, pieces)


def attn_bwd(place, x_slots, grads, gain, w, tables, saved, sums, dw_rows):
    toks, width = x_slots[0].shape[0], w.shape[1]
    slots = len(x_slots)
    seq, heads = slots * toks, width // HEAD_DIM
    return pl.pallas_call(
        functools.partial(attn_bwd_kernel, heads),
        out_shape=[
            jax.ShapeDtypeStruct((2, toks, D), bf16),
            jax.ShapeDtypeStruct((2, toks, D), bf16),
            jax.ShapeDtypeStruct((dw_rows, D), bf16),
            jax.ShapeDtypeStruct((8, 128), f32),
        ],
        in_specs=[SM] + [VM] * 15 + [HB, VM],
        out_specs=[VM] * 4,
        scratch_shapes=[
            pltpu.VMEM((seq, D), bf16),
            pltpu.VMEM((heads, seq, HEAD_DIM), bf16),
            pltpu.VMEM((heads, seq, 2 * HEAD_DIM), bf16),
            pltpu.VMEM((heads, 2 * HEAD_DIM, seq), bf16),
            pltpu.VMEM((heads, seq, 2 * HEAD_DIM), f32),
            pltpu.VMEM((heads, seq, HEAD_DIM), f32),
            pltpu.VMEM((slots, heads, 2 * HEAD_DIM, toks), f32),
            pltpu.VMEM((3, seq, width), bf16),
            pltpu.VMEM((heads, seq, toks), bf16),
            pltpu.SemaphoreType.DMA((heads,)),
        ],
        compiler_params=params(),
        name="attn_bwd",
        cost_estimate=cost(22),
    )(place, *x_slots, *grads, gain, w, *tables, *saved, sums)


def out_proj_kernel(
    x_ref, m0, m1, m2, m3, w0, w1, w2, w3, gain_ref, resid_ref, n_ref, top_ref, low_ref, copies_ref
):
    attended = dot(m0[...], w0[...])
    attended += dot(m1[...], w1[...])
    attended += dot(m2[...], w2[...])
    attended += dot(m3[...], w3[...])
    resid = x_ref[...].astype(f32) + attended
    resid_ref[...] = resid
    _, _, act = normed(resid, gain_row(gain_ref))
    half = act.shape[0] // 2
    n_ref[...] = act
    top_ref[...] = act[:half]
    low_ref[...] = act[half:]
    for k in range(copies_ref.shape[0]):
        copies_ref[k] = act


def route_columns(base_ref, routes_ref, gates_ref, toks):
    base = pl.multiple_of(base_ref[0], toks)
    routes = routes_ref[:, pl.ds(base, toks)].astype(f32)
    rows = jnp.concatenate([routes, gates_ref[...], jnp.zeros((4, toks), f32)], axis=0)
    return rows.T, routes


def expert_gate(columns, expert):
    return jnp.where(columns[:, 0:1] == expert, columns[:, 2:3], 0.0) + jnp.where(
        columns[:, 1:2] == expert, columns[:, 3:4], 0.0
    )


def mid_kernel(
    base_ref,
    dx_refs,
    cot_ref,
    resid_ref,
    routes_ref,
    gates_ref,
    gain_ref,
    m_refs,
    w_refs,
    gres_ref,
    g_refs,
    o_refs,
    sums_ref,
):
    toks = cot_ref.shape[0]
    cot = cot_ref[...].astype(f32)
    columns, _ = route_columns(base_ref, routes_ref, gates_ref, toks)
    halves = [dx_refs[k][...].astype(f32) + dx_refs[k + 1][...].astype(f32) for k in (0, 2)]
    grad = jnp.concatenate(halves, axis=0) + expert_gate(columns, E_FFN + 1) * cot
    gain = gain_row(gain_ref)
    unit, inverse, _ = normed(resid_ref[...], gain)
    grad_unit = grad * gain
    grad_resid = cot + inverse * (
        grad_unit - unit * jnp.mean(grad_unit * unit, axis=-1, keepdims=True)
    )
    gres_ref[...] = grad_resid
    grad_att = grad_resid.astype(bf16)
    for k, (m_ref, w_ref, g_ref) in enumerate(zip(m_refs, w_refs, g_refs)):
        g_ref[...] = dot(grad_att, w_ref[...], 1, 1).astype(bf16)
        o_refs[k % 2][k // 2] = dot(m_ref[...], grad_att, 0, 0).astype(bf16)
    sums_ref[...] = jnp.zeros(sums_ref.shape, f32)
    sums_ref[0:1, :] = jnp.sum(grad * unit, axis=0, keepdims=True)
    for k in range(2):
        weight = expert_gate(columns, E_FFN + 2 + k)
        sums_ref[1 + k : 2 + k, :] = jnp.sum(weight * cot, axis=0, keepdims=True)


def out_kernel(
    base_ref,
    y_refs,
    cot_ref,
    resid_ref,
    n_ref,
    routes_ref,
    gates_ref,
    const_ref,
    out_ref,
    gg_ref,
):
    toks = cot_ref.shape[0]
    half = toks // 2
    cot = cot_ref[...].astype(f32)
    columns, routes = route_columns(base_ref, routes_ref, gates_ref, toks)
    act = n_ref[...].astype(f32)
    consts = const_ref[...].astype(f32)
    top = y_refs[0][...].astype(f32) + y_refs[1][...].astype(f32)
    low = y_refs[2][...].astype(f32) + y_refs[3][...].astype(f32)
    moe = jnp.concatenate([top, low[:half]], axis=0) + expert_gate(columns, E_FFN + 1) * act
    moe += expert_gate(columns, E_FFN + 2) * consts[0:1]
    moe += expert_gate(columns, E_FFN + 3) * consts[1:2]
    out_ref[...] = (resid_ref[...] + moe).astype(bf16)
    dots = [cot * act, cot * consts[0:1], cot * consts[1:2]]
    dots = [jnp.sum(v, axis=1, keepdims=True) for v in dots]
    dots = jnp.concatenate([jnp.broadcast_to(dots[k % 3], (toks, 1)) for k in range(8)], axis=1).T
    table = low[half : half + TAB, 0:toks]
    for pair in range(2):
        route = routes[pair : pair + 1]
        result = jnp.zeros((1, toks), f32)
        for e in range(E_FFN):
            result += jnp.where(route == e, table[e : e + 1], 0.0)
        for k in range(3):
            result += jnp.where(route == E_FFN + 1 + k, dots[k : k + 1], 0.0)
        gg_ref[pair : pair + 1, :] = result


def last_kernel(gno_a, gno_b, x_ref, gres_ref, gain_ref, out_ref):
    grad = gno_a[...].astype(f32) + gno_b[...].astype(f32)
    gain = gain_row(gain_ref)
    unit, inverse, _ = normed(x_ref[...].astype(f32), gain)
    grad_unit = grad * gain
    out_ref[...] = gres_ref[...] + inverse * (
        grad_unit - unit * jnp.mean(grad_unit * unit, axis=-1, keepdims=True)
    )


def dispatch_block(first, experts, x, p_ref, tab_ref, rows_ref, gate_ref, offs, starts, block):
    toks = x.shape[0]
    tab_ref[...] = p_ref[toks : toks + TAB, :].astype(f32)
    want = lax.broadcasted_iota(jnp.int32, (SHORT, toks), 0).astype(f32)
    cot = p_ref[0:toks, :]

    def select(i, begin):
        row = tab_ref[pl.ds(first + i, 1), :]
        match = (want + begin) == row[:, 0:toks]
        gate = row[:, toks : 2 * toks] + row[:, 2 * toks : 3 * toks]
        weight = jnp.sum(jnp.where(match, gate, 0.0), axis=1, keepdims=True)
        return jnp.where(match, 1.0, 0.0).astype(bf16), weight, row[:, 0:toks]

    def put(i, off, rows_x, rows_c, weight):
        at = pl.ds(pl.multiple_of(off, 16), SHORT)
        rows_ref[i, at, 0:D] = rows_x.astype(bf16)
        rows_ref[i, at, D : 2 * D] = (rows_c * weight).astype(bf16)
        if gate_ref is not None:
            gate_ref[i, at, :] = jnp.broadcast_to(weight, (SHORT, 128))

    parts = [select(i, 0.0) for i in range(experts)]
    counts = [jnp.max(rank).astype(jnp.int32) + 1 for _, _, rank in parts]
    hot = jnp.concatenate([p[0] for p in parts], axis=0)
    rows_x, rows_c = dot(hot, x), dot(hot, cot)
    for i in range(experts):
        off = offs[i]
        if starts is not None:
            starts[block, i] = off
        seg = slice(i * SHORT, (i + 1) * SHORT)
        put(i, off, rows_x[seg], rows_c[seg], parts[i][1])

        @pl.when(counts[i] > SHORT)
        def _(i=i, off=off):
            rest, weight, _ = select(i, float(SHORT))
            put(i, off + SHORT, dot(rest, x), dot(rest, cot), weight)

        offs[i] = off + ((counts[i] + 15) // 16) * 16


def expert_acts(rows, wg, wu, wd):
    act, grad = rows[:, :D], rows[:, D:]
    gate_pre = dot(act, wg)
    up_pre = dot(act, wu)
    grad_hidden = dot(grad, wd, 1, 1)
    sig = 1.0 / (1.0 + jnp.exp(-gate_pre))
    silu = gate_pre * sig
    hidden = (silu * up_pre).astype(bf16)
    grad_gate = (grad_hidden * up_pre * sig * (1.0 + gate_pre * (1.0 - sig))).astype(bf16)
    grad_up = (grad_hidden * silu).astype(bf16)
    return act, grad, hidden, grad_hidden, grad_gate, grad_up


def own_kernel(nb, tile, first_ref, *refs):
    tops, lows, ps = refs[:nb], refs[nb : 2 * nb], refs[2 * nb : 3 * nb]
    wg_h, wu_h, wd_h, dxa, dxb, ya, yb, rows_out, used = refs[3 * nb : 3 * nb + 9]
    (
        xbuf,
        pbuf,
        wg,
        wu,
        wd,
        rows_ref,
        back_ref,
        gate_ref,
        tab_ref,
        dxbuf,
        ybuf,
        offs,
        starts,
        tok_sems,
        w_sems,
        out_sems,
        row_sem,
    ) = refs[3 * nb + 9 :]
    experts = wg.shape[0]
    toks = xbuf.shape[1]
    half = nb // 2
    first = first_ref[0]
    mid = toks // 2

    def tok_copies(b, src):
        return (
            pltpu.make_async_copy(tops[src], xbuf.at[b, 0:mid], tok_sems.at[0, b]),
            pltpu.make_async_copy(lows[src], xbuf.at[b, mid:toks], tok_sems.at[1, b]),
            pltpu.make_async_copy(ps[src], pbuf.at[b], tok_sems.at[2, b]),
        )

    w_copies = [
        pltpu.make_async_copy(src, dst, w_sems.at[k])
        for k, (src, dst) in enumerate(((wg_h, wg), (wu_h, wu), (wd_h, wd)))
    ]
    for b in range(nb):
        for copy in tok_copies(b, b):
            copy.start()
    for copy in w_copies:
        copy.start()
    for i in range(experts):
        offs[i] = 0

    def dispatch_body(b, carry):
        for copy in tok_copies(b, 0):
            copy.wait()
        dispatch_block(
            first, experts, xbuf[b], pbuf.at[b], tab_ref, rows_ref, gate_ref, offs, starts, b
        )
        return carry

    lax.fori_loop(0, nb, dispatch_body, 0)
    for i in range(experts):
        at = pl.ds(pl.multiple_of(offs[i], 16), TILE_BACK)
        rows_ref[i, at, :] = jnp.zeros((TILE_BACK, 2 * D), bf16)
        back_ref[i, at, :] = jnp.zeros((TILE_BACK, 2 * D), bf16)
        gate_ref[i, at, :] = jnp.zeros((TILE_BACK, 128), f32)
        used[i] = offs[i]
    rows_copy = pltpu.make_async_copy(rows_ref, rows_out, row_sem)
    rows_copy.start()
    for copy in w_copies:
        copy.wait()

    def expert_body(e, carry):
        def tile_body(j, inner):
            at = pl.ds(pl.multiple_of(j * tile, 16), tile)
            rows = rows_ref[e, at, :]
            _, _, hidden, grad_hidden, grad_gate, grad_up = expert_acts(rows, wg[e], wu[e], wd[e])
            weight = gate_ref[e, at, :]
            product = jnp.sum(hidden.astype(f32) * grad_hidden, axis=1, keepdims=True)
            gate_ref[e, at, :] = jnp.where(weight > 0.0, product / jnp.maximum(weight, 0.125), 0.0)
            back_ref[e, at, 0:D] = (
                dot(grad_gate, wg[e], 1, 1) + dot(grad_up, wu[e], 1, 1)
            ).astype(bf16)
            back_ref[e, at, D : 2 * D] = (dot(hidden, wd[e]) * weight[:, :1]).astype(bf16)
            return inner

        return lax.fori_loop(0, (offs[e] + tile - 1) // tile, tile_body, carry)

    lax.fori_loop(0, experts, expert_body, 0)

    def out_copies(b, slot):
        near = b < half
        return near, (
            pltpu.make_async_copy(dxbuf.at[slot], dxa.at[b % half], out_sems.at[0, slot]),
            pltpu.make_async_copy(ybuf.at[slot], ya.at[b % half], out_sems.at[1, slot]),
        ), (
            pltpu.make_async_copy(dxbuf.at[slot], dxb.at[b % half], out_sems.at[0, slot]),
            pltpu.make_async_copy(ybuf.at[slot], yb.at[b % half], out_sems.at[1, slot]),
        )

    def wait_slot(slot):
        pltpu.make_async_copy(dxbuf.at[slot], dxa.at[0], out_sems.at[0, slot]).wait()
        pltpu.make_async_copy(ybuf.at[slot], ya.at[0], out_sems.at[1, slot]).wait()

    want = lax.broadcasted_iota(jnp.int32, (SEG, toks), 0).astype(f32)
    tab_rows = lax.broadcasted_iota(jnp.int32, (TAB, toks), 0)

    def combine_body(b, carry):
        slot = b % 2

        @pl.when(b >= 2)
        def _():
            wait_slot(slot)

        tab_ref[...] = pbuf[b, toks : toks + TAB, :].astype(f32)
        hots, segs = [], []
        table = jnp.zeros((TAB, toks), f32)
        for i in range(experts):
            rank = tab_ref[pl.ds(first + i, 1), 0:toks]
            match = jnp.where(want == rank, 1.0, 0.0)
            at = pl.ds(pl.multiple_of(starts[b, i], 16), SEG)
            hots.append(match.astype(bf16))
            segs.append(back_ref[i, at, :])
            line = jnp.sum(match * gate_ref[i, at, :][:, :1], axis=0, keepdims=True)
            table += jnp.where(tab_rows == first + i, line, 0.0)
        result = dot(jnp.concatenate(hots, axis=0), jnp.concatenate(segs, axis=0), 0, 0)
        dxbuf[slot] = result[:, :D].astype(bf16)
        ybuf[slot, 0:toks, :] = result[:, D:].astype(bf16)
        ybuf[slot, toks : toks + TAB, 0:toks] = table.astype(bf16)
        ybuf[slot, toks : toks + TAB, toks:] = jnp.zeros((TAB, D - toks), bf16)
        near, here, there = out_copies(b, slot)

        @pl.when(near)
        def _():
            here[0].start()
            here[1].start()

        @pl.when(jnp.logical_not(near))
        def _():
            there[0].start()
            there[1].start()

        return carry

    lax.fori_loop(0, nb, combine_body, 0)
    wait_slot(0)
    wait_slot(1)
    rows_copy.wait()


def dispatch_kernel(pieces, arrays, tile, first_ref, *refs):
    srcs, refs = refs[:arrays], refs[arrays:]
    rows_out, used, xbuf, pbuf, rows_ref, tab_ref, offs, tok_sems, row_sem = refs
    experts = rows_ref.shape[0]
    ring = xbuf.shape[0]
    first = first_ref[0]
    total = sum(p[0] for p in pieces)

    def start_block(b):
        slot = b % ring
        begin = 0
        for blocks, x_parts, p_parts in pieces:

            @pl.when((b >= begin) & (b < begin + blocks))
            def _(begin=begin, x_parts=x_parts, p_parts=p_parts):
                for which, (parts, buf) in enumerate(((x_parts, xbuf), (p_parts, pbuf))):
                    for array, at, lo, hi in parts:
                        pltpu.make_async_copy(
                            srcs[array].at[b - begin + at],
                            buf.at[slot, lo:hi],
                            tok_sems.at[which, slot],
                        ).start()

            begin += blocks

    def start_body(b, carry):
        start_block(b)
        return carry

    lax.fori_loop(0, min(ring - 1, total), start_body, 0)
    for i in range(experts):
        offs[i] = 0

    def dispatch_body(b, carry):
        slot = b % ring
        pltpu.make_async_copy(xbuf.at[slot], xbuf.at[slot], tok_sems.at[0, slot]).wait()
        pltpu.make_async_copy(pbuf.at[slot], pbuf.at[slot], tok_sems.at[1, slot]).wait()

        @pl.when(b + ring - 1 < total)
        def _():
            start_block(b + ring - 1)

        dispatch_block(
            first, experts, xbuf[slot], pbuf.at[slot], tab_ref, rows_ref, None, offs, None, b
        )
        return carry

    lax.fori_loop(0, total, dispatch_body, 0)

    def chunk(i, j):
        at = pl.ds(pl.multiple_of(j * tile, tile), tile)
        return pltpu.make_async_copy(rows_ref.at[i, at], rows_out.at[i, at], row_sem)

    def chunks(i):
        return jnp.maximum((offs[i] + tile - 1) // tile, 1)

    def start_chunk(i):
        def body(j, carry):
            chunk(i, j).start()
            return carry

        return body

    def wait_chunk(i):
        def body(j, carry):
            chunk(i, j).wait()
            return carry

        return body

    for i in range(experts):
        rows_ref[i, pl.ds(pl.multiple_of(offs[i], 16), tile), :] = jnp.zeros((tile, 2 * D), bf16)
        used[i] = offs[i]
        lax.fori_loop(0, chunks(i), start_chunk(i), 0)
    for i in range(experts):
        lax.fori_loop(0, chunks(i), wait_chunk(i), 0)


def weight_kernel(tile, experts, given, add, begin_ref, used_ref, rows_h, wg_h, wu_h, wd_h, *refs):
    begin_e = begin_ref[0]
    small = max(tile // 2, TILE_BACK)
    olds, refs = (refs[:3], refs[3:]) if given else ((), refs)
    outs, accs = refs[:3], refs[3:6]
    rbuf, wg, wu, wd, row_sems, w_sems, acc_sems = refs[6:]
    w_copies = [
        pltpu.make_async_copy(src.at[pl.ds(begin_e, experts)], dst, w_sems.at[k])
        for k, (src, dst) in enumerate(((wg_h, wg), (wu_h, wu), (wd_h, wd)))
    ]

    def tiles(e):
        return jnp.maximum((used_ref[begin_e + e] + tile - 1) // tile, 1)

    def fetch(e, j, slot):
        at = pl.ds(pl.multiple_of(j * tile, tile), tile)
        return pltpu.make_async_copy(
            rows_h.at[begin_e + e, at], rbuf.at[slot], row_sems.at[slot]
        )

    def out_copies(e):
        return [
            pltpu.make_async_copy(src, dst.at[e + begin_e], acc_sems.at[k])
            for k, (src, dst) in enumerate(zip(accs, outs))
        ]

    def old_copies(e):
        return [
            pltpu.make_async_copy(src.at[e + begin_e], dst, acc_sems.at[k])
            for k, (src, dst) in enumerate(zip(olds, accs))
        ]

    fetch(0, 0, 0).start()
    for copy in w_copies:
        copy.start()
    if add:
        for copy in old_copies(0):
            copy.start()
    for copy in w_copies:
        copy.wait()

    def expert_body(e, count):
        last = tiles(e)

        def tile_body(j, step):
            slot = step % 2
            fetch(e, j, slot).wait()

            @pl.when(j + 1 < last)
            def _():
                fetch(e, j + 1, 1 - slot).start()

            @pl.when((j + 1 == last) & (e + 1 < experts))
            def _():
                fetch(e + 1, 0, 1 - slot).start()


            @pl.when(j == 0)
            def _():
                @pl.when(e > 0)
                def _():
                    for copy in out_copies(e - 1):
                        copy.wait()
                    if add:
                        for copy in old_copies(e):
                            copy.start()

                if add:
                    for copy in old_copies(e):
                        copy.wait()
                else:
                    for acc in accs:
                        acc[...] = jnp.zeros(acc.shape, f32)

            def work(size):
                rows = rbuf[slot, 0:size]
                act, grad, hidden, _, grad_gate, grad_up = expert_acts(rows, wg[e], wu[e], wd[e])
                part = dot(act, jnp.concatenate([grad_gate, grad_up], axis=1), 0, 0)
                width = grad_gate.shape[1]
                accs[0][...] += part[:, :width]
                accs[1][...] += part[:, width:]
                accs[2][...] += dot(hidden, grad, 0, 0)

            if small < tile:
                little = used_ref[begin_e + e] - j * tile <= small

                @pl.when(little)
                def _():
                    work(small)

                @pl.when(jnp.logical_not(little))
                def _():
                    work(tile)

            else:
                work(tile)
            return step + 1

        count = lax.fori_loop(0, last, tile_body, count)
        for copy in out_copies(e):
            copy.start()
        return count

    lax.fori_loop(0, experts, expert_body, jnp.int32(0))
    for copy in out_copies(experts - 1):
        copy.wait()


def row_room(cap, blocks, groups, tile):
    most = groups * min(cap + 15 * blocks, SEG * blocks)
    return -(-most // tile) * tile + tile


def own_experts(first, tops, lows, ps, wg, wu, wd, cap):
    nb = len(ps)
    experts = wg.shape[0]
    toks = ps[0].shape[0] - TAB
    room = row_room(cap, nb, 1, TILE_BACK)
    half = nb // 2
    shapes = [
        jax.ShapeDtypeStruct((half, toks, D), bf16),
        jax.ShapeDtypeStruct((half, toks, D), bf16),
        jax.ShapeDtypeStruct((half, toks + TAB, D), bf16),
        jax.ShapeDtypeStruct((half, toks + TAB, D), bf16),
        jax.ShapeDtypeStruct((experts, room, 2 * D), bf16),
        jax.ShapeDtypeStruct((experts,), jnp.int32),
    ]
    return pl.pallas_call(
        functools.partial(own_kernel, nb, TILE_OWN),
        out_shape=shapes,
        in_specs=[SM] + [HB] * (3 * nb + 3),
        out_specs=[HB] * 5 + [SM],
        scratch_shapes=[
            pltpu.VMEM((nb, toks, D), bf16),
            pltpu.VMEM((nb, toks + TAB, D), bf16),
            pltpu.VMEM(wg.shape, bf16),
            pltpu.VMEM(wu.shape, bf16),
            pltpu.VMEM(wd.shape, bf16),
            pltpu.VMEM((experts, room, 2 * D), bf16),
            pltpu.VMEM((experts, room, 2 * D), bf16),
            pltpu.VMEM((experts, room, 128), f32),
            pltpu.VMEM((TAB, D), f32),
            pltpu.VMEM((2, toks, D), bf16),
            pltpu.VMEM((2, toks + TAB, D), bf16),
            pltpu.SMEM((experts,), jnp.int32),
            pltpu.SMEM((nb, experts), jnp.int32),
            pltpu.SemaphoreType.DMA((3, nb)),
            pltpu.SemaphoreType.DMA((3,)),
            pltpu.SemaphoreType.DMA((2, 2)),
            pltpu.SemaphoreType.DMA,
        ],
        compiler_params=params(),
        name="own_experts",
        cost_estimate=cost(29),
    )(first, *tops, *lows, *ps, wg, wu, wd)


def chip_pieces(x_sets, p_sets, blocks, toks):
    flat = [a for sets in (x_sets, p_sets) for arrays in sets for a in arrays]
    half = toks // 2
    x_count = x_sets[0][0].shape[0] // blocks
    pieces = []
    for k in range(4 * x_count):
        core, x, y = k // (2 * x_count), k // 2 % x_count, k % 2
        parts, base = [], 0
        for sets, end in ((x_sets, toks), (p_sets, toks + TAB)):
            top, low = base + core * 2 + y, base + len(sets[0]) + core * x_count + x
            parts.append(((top, x * blocks, 0, half), (low, y * blocks, half, end)))
            base += len(sets[0]) + len(sets[1])
        pieces.append((blocks, *parts))
    return flat, pieces


def dispatch(first, flat, pieces, toks, experts, cap, groups):
    total = sum(p[0] for p in pieces)
    ring = 4
    room = row_room(cap, total // groups, groups, TILE_FAR)
    return pl.pallas_call(
        functools.partial(dispatch_kernel, tuple(pieces), len(flat), TILE_FAR),
        out_shape=[
            jax.ShapeDtypeStruct((experts, room, 2 * D), bf16),
            jax.ShapeDtypeStruct((experts,), jnp.int32),
        ],
        in_specs=[SM] + [HB] * len(flat),
        out_specs=[HB, SM],
        scratch_shapes=[
            pltpu.VMEM((ring, toks, D), bf16),
            pltpu.VMEM((ring, toks + TAB, D), bf16),
            pltpu.VMEM((experts, room, 2 * D), bf16),
            pltpu.VMEM((TAB, D), f32),
            pltpu.SMEM((experts,), jnp.int32),
            pltpu.SemaphoreType.DMA((2, ring)),
            pltpu.SemaphoreType.DMA,
        ],
        compiler_params=params(),
        name="dispatch",
        cost_estimate=cost(20),
    )(first, *flat)


def weight_grads(used, rows, weights, tile, olds=None, add=True, begin_e=0, count_e=None):
    experts = count_e or weights[0].shape[0]
    shapes = [jax.ShapeDtypeStruct(w.shape, f32) for w in weights]
    operands = [jnp.full((1,), begin_e, jnp.int32), used, rows, *weights, *(olds or ())]
    return pl.pallas_call(
        functools.partial(weight_kernel, tile, experts, bool(olds), bool(olds) and add),
        out_shape=shapes,
        in_specs=[SM, SM] + [HB] * (len(operands) - 2),
        out_specs=[HB] * 3,
        input_output_aliases={len(operands) - 3 + k: k for k in range(3)} if olds else {},
        scratch_shapes=[
            *[pltpu.VMEM(w.shape[1:], f32) for w in weights],
            pltpu.VMEM((2, tile, 2 * D), bf16),
            *[pltpu.VMEM((experts, *w.shape[1:]), bf16) for w in weights],
            pltpu.SemaphoreType.DMA((2,)),
            pltpu.SemaphoreType.DMA((3,)),
            pltpu.SemaphoreType.DMA((3,)),
        ],
        compiler_params=params(),
        name="weight_grads",
        cost_estimate=cost(14),
    )(*operands)


def after(value, *deps):
    return lax.optimization_barrier((value, *deps))[0]


def after_all(values, *deps):
    return lax.optimization_barrier((*values, *deps))[: len(values)]


def after_tree(tree, *deps):
    return lax.optimization_barrier((tree, *deps))[0]


def other_groups(copies, cut):
    count, index = lax.axis_size("dp"), lax.axis_index("dp")
    blocks = lax.all_to_all(copies, "dp", 0, 0, tiled=True)

    def pick(blocks, rows):
        found = [
            lax.dynamic_index_in_dim(blocks, (index + step) % count, 0)[:, rows]
            for step in range(1, count)
        ]
        return jnp.concatenate(found, axis=0)

    return blocks, lambda b: (pick(b, slice(0, cut)), pick(b, slice(cut, None)))


def gather_line(values, axis):
    out = list(values)
    for step in range(1, lax.axis_size(axis)):
        out += [shift(v, axis, step) for v in values]
    return out


def with_line(values, axis):
    return gather_line([jnp.concatenate(values, axis=0)], axis)


def plane_gather(value, x_first):
    if x_first:
        cols = gather_line([value], "x")
        rows = [shift(v, "y", 1) for v in cols]
        return [v for pair in zip(cols, rows) for v in pair]
    return gather_line(gather_line([value], "y"), "x")


def both_cores(values, *deps):
    return list(values) + [shift(after(v, *deps) if deps else v, "c", 1) for v in values]


def total(*parts):
    return sum(p.astype(f32) for p in parts).astype(bf16)


def scatter_cores(parts):
    return parts[0], shift(parts[1], "c", -1)


def scatter_first(keep, other, cut):
    count = lax.axis_size("x")

    def add(rows, where):
        return total(keep[where][:, rows], other[where][:, rows])

    top, low = slice(0, cut), slice(cut, None)
    x_sent = [add(top, slice(2 * k, 2 * k + 2)) for k in range(1, count)]
    y_sent = add(low, slice(1, None, 2))
    x_kept = add(top, slice(0, 2))
    y_kept = add(low, slice(0, None, 2))
    x_got = [shift(v, "x", -k) for k, v in zip(range(1, count), x_sent)]
    y_got = shift(y_sent, "y", -1)
    return (*x_got, y_got), x_kept, y_kept


def scatter_second(got, x_kept, y_kept):
    x_got, y_got = got[:-1], got[-1]
    count = len(got)
    y_next = total(x_kept[1], *[v[1] for v in x_got])
    x_next = [total(y_kept[k], y_got[k]) for k in range(1, count)]
    top_own = total(x_kept[0], *[v[0] for v in x_got])
    low_own = total(y_kept[0], y_got[0])
    top_far = shift(y_next, "y", -1)
    low_far = [shift(v, "x", -k) for k, v in zip(range(1, count), x_next)]
    if count > 2:
        low_far = [total(*low_far)]
    return top_own, top_far, low_own, low_far[0]


def line_sum(value, axis):
    return sum([shift(value, axis, step) for step in range(1, lax.axis_size(axis))], value)


def row_sum(value):
    far = lax.ppermute(value, ("y", "c"), [(i, 3 - i) for i in range(4)])
    return value + shift(value, "c", 1) + shift(value, "y", 1) + far


def scatter_sum(value, axis):
    count, index = lax.axis_size(axis), lax.axis_index(axis)
    chunks = value.reshape((count, value.shape[0] // count) + value.shape[1:])
    result = lax.dynamic_index_in_dim(chunks, index, 0, keepdims=False).astype(f32)
    for step in range(1, count):
        chunk = lax.dynamic_index_in_dim(chunks, (index + step) % count, 0, keepdims=False)
        result = result + shift(chunk, axis, step).astype(f32)
    return result.astype(bf16)


def gather_chunks(own, axis):
    count, index = lax.axis_size(axis), lax.axis_index(axis)
    full = jnp.zeros((count,) + own.shape, bf16)
    full = lax.dynamic_update_index_in_dim(full, own, index, 0)
    for step in range(1, count):
        chunk = shift(own, axis, step)
        full = lax.dynamic_update_index_in_dim(full, chunk, (index - step) % count, 0)
    return full.reshape((count * own.shape[0],) + own.shape[1:])


def shards(
    inputs,
    cotangent,
    gain_attn,
    gain_ffn,
    attn_in,
    attn_out,
    expert_gate,
    expert_up,
    expert_down,
    const_vectors,
    gate_values,
    routes,
    priority,
    pieces,
):
    toks = inputs.shape[1]
    y_index, c_index = lax.axis_index("y"), lax.axis_index("c")
    x_index, x_count = lax.axis_index("x"), lax.axis_size("x")
    dp_count = lax.axis_size("dp")
    row_count = lax.axis_size("y") * lax.axis_size("c")
    seq = toks * row_count
    heads = attn_in.shape[2] // HEAD_DIM
    width = heads * HEAD_DIM
    group_tokens = routes.shape[1]
    nb = group_tokens // toks
    cap = 5 * group_tokens // 24
    experts = expert_gate.shape[0]
    x_own, cot = inputs[0], cotangent[0]
    place = jnp.stack(
        [
            ((y_index - ky) % 2) * 2 + (c_index - kc) % 2
            for ky in range(2)
            for kc in range(2)
        ]
    ).astype(jnp.int32)
    first = (x_index * experts).astype(jnp.int32)[None]
    base = (x_index * seq + (y_index * 2 + c_index) * toks).astype(jnp.int32)[None]

    x_y = shift(x_own, "y", 1)
    w_y = shift(after(attn_out, x_y), "y", 1)
    w_c = shift(attn_out, "c", 1)

    cosine, sine = (jnp.asarray(a) for a in rotary_numpy(seq))
    routes_t, gates_t = routes[0].T, gate_values[0].T
    attn_w = attn_in.transpose(0, 2, 1)
    weights = (expert_gate, expert_up, expert_down)
    half = toks // 2
    far = list(range(1, dp_count))
    one_call = dp_count * group_tokens <= CALL_TOKENS

    payload, p_copies = pl.pallas_call(
        functools.partial(route_kernel, cap),
        out_shape=[
            jax.ShapeDtypeStruct((toks + TAB, D), bf16),
            jax.ShapeDtypeStruct((dp_count if one_call else 1, toks + TAB, D), bf16),
        ],
        in_specs=[SM, VM, VM, VM, VM],
        out_specs=[VM, VM],
        compiler_params=params(),
        name="route",
        cost_estimate=cost(2.5),
    )(base, routes_t, priority, gates_t, cot)
    if one_call:
        far_p, split_p = other_groups(p_copies, half)
    x_slots = [x_own, shift(x_own, "c", 1), x_y, shift(after(x_y, payload), "c", 1)]
    p_cols = gather_line([payload], "x")
    p_y = shift(after(payload, x_y), "y", 1)

    mix_shape = jax.ShapeDtypeStruct((toks, width), bf16)
    fwd_out = attn_fwd(after(place, payload), x_slots, gain_attn, attn_w, cosine, sine, pieces)
    fwd_out = after_all(fwd_out, *p_cols, p_y, w_y, w_c)
    q, k, v, probs, *mixed = fwd_out

    def to_owner(parts):
        return [
            parts[0],
            shift(parts[1], "c", -1),
            shift(parts[2], "y", -1),
            lax.ppermute(parts[3], ("y", "c"), [(i, 3 - i) for i in range(4)]),
        ]

    started = mixed[0]
    w_slots = [attn_out, w_c, w_y, shift(after(w_y, started), "c", 1)]
    own_p = [p_cols[0], p_y]
    for step, p in enumerate(p_cols[1:], 1):
        own_p += [p, shift(after(p_y, started), "x", step)]
    own_p = both_cores(own_p, started)
    if one_call:
        p_top, p_low = split_p(after(far_p, started))
    mixed = to_owner(mixed)
    resid, norm_two, norm_top, norm_low, x_copies = pl.pallas_call(
        out_proj_kernel,
        out_shape=[
            jax.ShapeDtypeStruct((toks, D), f32),
            jax.ShapeDtypeStruct((toks, D), bf16),
            jax.ShapeDtypeStruct((half, D), bf16),
            jax.ShapeDtypeStruct((half, D), bf16),
            jax.ShapeDtypeStruct((dp_count if one_call else 1, toks, D), bf16),
        ],
        in_specs=[VM] * 10,
        out_specs=[VM] * 5,
        compiler_params=params(),
        name="out_proj",
        cost_estimate=cost(3),
    )(x_own, *mixed, *w_slots, after(gain_ffn, own_p[2 * x_count - 1]))

    tops = plane_gather(norm_top, True)
    lows = plane_gather(norm_low, False)
    arrived = (tops[-1], lows[-1])
    ready = ()
    if one_call:
        far_x, split_x = other_groups(x_copies, half)
        first_in = (tops[1], tops[2], lows[1], lows[2])
        p_top_x = gather_line([after(p_top, *first_in)], "x")
        p_low_y = gather_line([after(p_low, *first_in)], "y")
        ready = (p_top_x[-1], p_low_y[-1])
        p_top = with_line(after_all(p_top_x, *arrived), "y")
        p_low = with_line(after_all(p_low_y, *arrived), "x")
    tops, lows = both_cores(tops), both_cores(lows)
    own_out = own_experts(after(first, *ready), tops, lows, own_p, *weights, cap)
    if one_call:
        own_out = after_all(own_out, *p_top, *p_low, far_x)
    dxa, dxb, ya, yb, rows, used = own_out
    dx_first = scatter_first(*scatter_cores((dxa, dxb)), half)
    dx_stage = dx_first[0][-1]
    dx_parts = scatter_second(*dx_first)
    if one_call:
        p_near = [shift(after(a[0], dx_first[1]), "c", 1) for a in (p_top, p_low)]
    front = max(1, experts // 2)
    grads_w = weight_grads(after(used, dx_first[1]), rows, weights, TILE_BACK, count_e=front)
    if one_call:
        x_top, x_low = split_x(after(far_x, dx_stage, grads_w[0]))
        x_top_x = gather_line([x_top], "x")
        x_low_y = gather_line([x_low], "y")
        used = after(used, *p_near)
    for begin in range(front, experts, front):
        grads_w = weight_grads(
            after(used, dx_stage), rows, weights, TILE_BACK, grads_w, False, begin, front
        )

    gres, *mids = pl.pallas_call(
        lambda base_ref, *refs: mid_kernel(
            base_ref,
            refs[0:4],
            *refs[4:9],
            refs[9:13],
            refs[13:17],
            refs[17],
            refs[18:22],
            refs[22:24],
            refs[24],
        ),
        out_shape=[jax.ShapeDtypeStruct((toks, D), f32)]
        + [mix_shape] * 4
        + [jax.ShapeDtypeStruct((2, width, D), bf16)] * 2
        + [jax.ShapeDtypeStruct((8, D), f32)],
        in_specs=[SM] + [VM] * 17,
        out_specs=[VM] * 8,
        compiler_params=params(),
        name="mid",
        cost_estimate=cost(5),
    )(
        after(base, grads_w[0], *((*x_top_x, *x_low_y) if one_call else ())),
        *dx_parts,
        cot,
        resid,
        routes_t,
        gates_t,
        gain_ffn,
        *mixed,
        *w_slots,
    )
    out_keep, out_send, sums = mids[4:]
    grads = to_owner(mids[:4])
    out_other = shift(after(out_send, grads[2]), "c", -1)
    out_sent = total(out_keep[1], out_other[1])
    out_far = shift(out_sent, "y", -1)
    ready = ()
    if one_call:
        ready = (x_top_x[-1], x_low_y[-1])
        x_top = with_line(after_all(x_top_x, gres), "y")
        x_low = with_line(after_all(x_low_y, gres), "x")
        p_other = [shift(after(a[1], *grads), "c", 1) for a in (p_top, p_low)]
    tables = (cosine, sine)
    unit = 8 * x_count * dp_count
    dw_rows = -(-(4 * width + 8) // unit) * unit
    saved = (q, k, v, probs)
    bwd_out = attn_bwd(
        place, x_slots, grads, gain_attn, attn_w, tables, saved, sums, dw_rows
    )
    if one_call:
        bwd_out = after_all(bwd_out, *x_top, *x_low, *p_other)
    gno_keep, gno_send, dw_in, gain_part = bwd_out
    gno_other = shift(gno_send, "c", -1)
    gno_far = (gno_keep[1].astype(f32) + gno_other[1].astype(f32)).astype(bf16)
    gno_near = (gno_keep[0].astype(f32) + gno_other[0].astype(f32)).astype(bf16)

    dw_out = total(out_keep[0], out_other[0], out_far)
    attn_grads = lax.dynamic_update_slice(dw_in, dw_out, (3 * width, 0))
    y_stage = scatter_cores(after_all((ya, yb), gno_other))
    gno_far = shift(gno_far, "y", -1)

    if one_call:
        x_near = [shift(after(a[0], gain_part), "c", 1) for a in (x_top, x_low)]
        x_other = [shift(after(a[1], gain_part), "c", 1) for a in (x_top, x_low)]
        x_sets = [[*a, n, o] for a, n, o in zip((x_top, x_low), x_near, x_other)]
        p_sets = [[*a, n, o] for a, n, o in zip((p_top, p_low), p_near, p_other)]
        flat, spots = chip_pieces(x_sets, p_sets, len(far), toks)
        part = scatter_sum(after(attn_grads, *x_near, *x_other), "x")
        rows, used = dispatch(after(first, gain_part), flat, spots, toks, experts, cap, len(far))
        used = after(used, part, gno_far, *y_stage)
        part, y_stage = after_tree((part, y_stage), used)
        part = scatter_sum(part, "dp")
        y_stage = scatter_first(*y_stage, half)
        for e in range(min(experts, 3)):
            many = experts - e if e == 2 else 1
            grads_w = weight_grads(used, rows, weights, TILE_FAR, grads_w, True, e, many)
            if e == 0:
                used = after(used, grads_w[0], part, *y_stage[0])
                part = gather_chunks(after(part, used), "dp")
            elif e == 1:
                used = after(used, grads_w[0], part)
                part, y_stage = after_tree((part, y_stage), used)
                attn_grads = gather_chunks(part, "x")
                y_parts = scatter_second(*y_stage)
            elif e == 2:
                attn_grads, *y_parts = after_all((attn_grads, *y_parts), grads_w[0])
                sums = row_sum(attn_grads[4 * width : 4 * width + 4].astype(f32))
    else:
        part = scatter_sum(scatter_sum(attn_grads, "x"), "dp")
        attn_grads = gather_chunks(gather_chunks(part, "dp"), "x")
        sums = row_sum(attn_grads[4 * width : 4 * width + 4].astype(f32))
        y_parts = scatter_second(*scatter_first(*y_stage, half))
        spots = [(nb, ((0, 0, 0, toks),), ((1, 0, 0, toks + TAB),))]

        def next_group(step, carry):
            x_block, p_block, *sums_w = carry
            x_block, p_block = shift(x_block, "dp", 1), shift(p_block, "dp", 1)
            flat = [lax.all_gather(a, ("y", "c", "x")) for a in (x_block, p_block)]
            rows, used = dispatch(first, flat, spots, toks, experts, cap, 1)
            return x_block, p_block, *weight_grads(used, rows, weights, TILE_FAR, sums_w)

        grads_w = lax.fori_loop(1, dp_count, next_group, (norm_two, payload, *grads_w))[2:]
    grad_w_gate, grad_w_up, grad_w_down = grads_w
    grad_w_in = attn_grads[: 3 * width].astype(f32).reshape(3, width, D).transpose(0, 2, 1)
    grad_w_out = attn_grads[3 * width : 4 * width].astype(f32)
    input_grad = pl.pallas_call(
        last_kernel,
        out_shape=jax.ShapeDtypeStruct((toks, D), f32),
        in_specs=[VM] * 5,
        out_specs=VM,
        compiler_params=params(),
        name="last",
        cost_estimate=cost(3),
    )(gno_near, gno_far, x_own, gres, gain_attn)

    block_out, grad_gates = pl.pallas_call(
        lambda base_ref, *refs: out_kernel(base_ref, refs[0:4], *refs[4:]),
        out_shape=[
            jax.ShapeDtypeStruct((toks, D), bf16),
            jax.ShapeDtypeStruct((2, toks), f32),
        ],
        in_specs=[SM] + [VM] * 10,
        out_specs=[VM] * 2,
        compiler_params=params(),
        name="block_out",
        cost_estimate=cost(3),
    )(base, *y_parts, cot, resid, norm_two, routes_t, gates_t, const_vectors)

    return (
        block_out[None],
        input_grad[None],
        sums[3],
        sums[0],
        grad_w_in,
        grad_w_out,
        grad_w_gate,
        grad_w_up,
        grad_w_down,
        sums[1:3],
        grad_gates.T[None],
    )


def solution(mesh):
    dp, row, col = mesh.devices.shape
    fine = Mesh(mesh.devices.reshape(dp, row // 2, 2, col), ("dp", "y", "c", "x"))
    rows = ("y", "c")
    in_specs = (
        P(("dp", "x"), rows, None),
        P(("dp", "x"), rows, None),
        P(),
        P(),
        P(None, None, rows),
        P(rows, None),
        P("x", None, rows),
        P("x", None, rows),
        P("x", rows, None),
        P(),
        P(("dp", "x"), rows, None),
        P("dp", None, None),
        P("dp", None),
        P(("dp", "x"), None),
    )
    out_specs = (
        P(("dp", "x"), rows, None),
        P(("dp", "x"), rows, None),
        P(),
        P(),
        P(None, None, rows),
        P(rows, None),
        P("x", None, rows),
        P("x", None, rows),
        P("x", rows, None),
        P(),
        P(("dp", "x"), rows, None),
    )
    return jax.shard_map(shards, mesh=fine, in_specs=in_specs, out_specs=out_specs, check_vma=False)
```

```python
import functools

import jax
import jax.numpy as jnp
import numpy as np
from jax import lax
from jax.experimental import pallas as pl
from jax.experimental.pallas import tpu as pltpu
from jax.sharding import Mesh
from jax.sharding import PartitionSpec as P

D = 768
HEAD_DIM = 64
E_FFN = 8
MOST = 88
SHORT = 48
SEG = 96
TAB = 8
TILE_OWN = 192
TILE_BACK = 256
TILE_FAR = 512
CALL_TOKENS = 8192

norm_eps = 1e-05
masked_score = -1e30
bf16 = jnp.bfloat16
f32 = jnp.float32
VMEM_MAX = 60 * 1024 * 1024


def dot(a, b, ca=1, cb=0):
    return lax.dot_general(a, b, (((ca,), (cb,)), ((), ())), preferred_element_type=f32)


def params(**kw):
    return pltpu.CompilerParams(vmem_limit_bytes=VMEM_MAX, **kw)


def cost(micros):
    return pl.CostEstimate(
        flops=int(micros * 1.1e9), transcendentals=0, bytes_accessed=int(micros * 3.5e6)
    )


VM = pl.BlockSpec(memory_space=pltpu.VMEM)
SM = pl.BlockSpec(memory_space=pltpu.SMEM)
HB = pl.BlockSpec(memory_space=pl.ANY)


def shift(value, axis, step):
    count = lax.axis_size(axis)
    return lax.ppermute(value, axis, [(i, (i + step) % count) for i in range(count)])


def gain_row(ref):
    return ref[...].reshape(1, D)


def normed(rows, gain):
    inverse = lax.rsqrt(jnp.mean(rows * rows, axis=-1, keepdims=True) + norm_eps)
    unit = rows * inverse
    return unit, inverse, (unit * gain).astype(bf16)


def rotary_numpy(length):
    half = HEAD_DIM // 2
    frequency = (10000.0 ** (-np.arange(half, dtype=np.float32) / half)).astype(np.float32)
    angles = frequency[:, None] * np.arange(length, dtype=np.float32)[None, :]
    cosine = np.tile(np.cos(angles), (2, 1)).astype(np.float32)
    sine = np.tile(np.sin(angles), (2, 1)).astype(np.float32)
    return cosine, sine


def partner_matrix(width):
    i = lax.broadcasted_iota(jnp.int32, (width, width), 0)
    j = lax.broadcasted_iota(jnp.int32, (width, width), 1)
    low = (j % HEAD_DIM) < HEAD_DIM // 2
    minus = jnp.where(low & (i == j + HEAD_DIM // 2), -1.0, 0.0)
    plus = jnp.where((~low) & (i == j - HEAD_DIM // 2), 1.0, 0.0)
    return (minus + plus).astype(bf16)


def eye(width):
    i = lax.broadcasted_iota(jnp.int32, (width, width), 0)
    j = lax.broadcasted_iota(jnp.int32, (width, width), 1)
    return jnp.where(i == j, 1.0, 0.0).astype(bf16)


def route_kernel(cap, base_ref, routes_ref, prio_ref, gates_ref, cot_ref, out_ref, copies_ref):
    total = prio_ref.shape[1]
    toks = cot_ref.shape[0]
    base = pl.multiple_of(base_ref[0], toks)
    prio = prio_ref[...].astype(f32)
    own_row = prio_ref[:, pl.ds(base, toks)].astype(f32)
    own_col = jnp.broadcast_to(own_row, (8, toks)).T[:, :1]
    earlier = jnp.where(prio < own_col, 1.0, 0.0).astype(bf16)
    ids = lax.broadcasted_iota(jnp.int32, (16, total), 0)
    named = (routes_ref[0:1, :] == ids) | (routes_ref[1:2, :] == ids)
    slots = dot(jnp.where(named, 1.0, 0.0).astype(bf16), earlier, 1, 1)
    own_ids = lax.broadcasted_iota(jnp.int32, (16, toks), 0)
    first = routes_ref[0:1, pl.ds(base, toks)] == own_ids
    second = routes_ref[1:2, pl.ds(base, toks)] == own_ids
    kept = (first | second) & (own_ids < E_FFN) & (slots < cap)
    before_i = lax.broadcasted_iota(jnp.int32, (toks, toks), 0)
    before_j = lax.broadcasted_iota(jnp.int32, (toks, toks), 1)
    lower = jnp.where(before_i < before_j, 1.0, 0.0).astype(bf16)
    rank = dot(jnp.where(kept, 1.0, 0.0).astype(bf16), lower)
    rank = jnp.where(kept, rank, -1.0)
    gate = jnp.where(first, gates_ref[0:1, :], 0.0) + jnp.where(second, gates_ref[1:2, :], 0.0)
    high = gate.astype(bf16)
    rest = (gate - high.astype(f32)).astype(bf16)
    table = jnp.concatenate([rank[:TAB].astype(bf16), high[:TAB], rest[:TAB]], axis=1)
    out_ref[0:toks, :] = cot_ref[...]
    out_ref[toks : toks + TAB, :] = table
    for k in range(copies_ref.shape[0]):
        copies_ref[k, 0:toks, :] = cot_ref[...]
        copies_ref[k, toks : toks + TAB, :] = table


def attn_fwd_kernel(
    heads,
    place_ref,
    x0,
    x1,
    x2,
    x3,
    gain_ref,
    w_ref,
    cos_ref,
    sin_ref,
    prow_ref,
    q_ref,
    k_ref,
    v_ref,
    pt_ref,
    m0,
    m1,
    m2,
    m3,
    bias_ref,
    pbuf,
    obuf,
    vt_ref,
    sems,
):
    toks = x0.shape[0]
    width = heads * HEAD_DIM
    slots = 4
    seq = slots * toks
    swap = partner_matrix(width)
    wq, wk, wv = w_ref[0], w_ref[1], w_ref[2]
    wq_swap = dot(swap, wq, 0, 0).astype(bf16)
    wk_swap = dot(swap, wk, 0, 0).astype(bf16)
    piece_col = jnp.broadcast_to(prow_ref[...].astype(f32), (8, seq)).T[:, :1]
    for slot, x_ref in enumerate((x0, x1, x2, x3)):
        start = pl.multiple_of(place_ref[slot] * toks, toks)
        rows = pl.ds(start, toks)
        _, _, act = normed(x_ref[...].astype(f32), gain_row(gain_ref))
        cosine = jnp.concatenate([cos_ref[:, rows].T] * heads, axis=1)
        sine = jnp.concatenate([sin_ref[:, rows].T] * heads, axis=1)
        queries = (dot(act, wq, 1, 1) * cosine + dot(act, wq_swap, 1, 1) * sine).astype(bf16)
        queries = (queries.astype(f32) * HEAD_DIM**-0.5).astype(bf16)
        keys = (dot(act, wk, 1, 1) * cosine + dot(act, wk_swap, 1, 1) * sine).astype(bf16)
        values = dot(act, wv, 1, 1).astype(bf16)
        for h in range(heads):
            cols = slice(h * HEAD_DIM, (h + 1) * HEAD_DIM)
            q_ref[h, rows, :] = queries[:, cols]
            k_ref[h, rows, :] = keys[:, cols]
            v_ref[h, rows, :] = values[:, cols]

    for h in range(heads):
        vt_ref[h] = v_ref[h].astype(f32).T.astype(bf16)

    def copy_out(block, h):
        keys = visible(block, slots) * toks
        return pltpu.make_async_copy(
            pbuf.at[h, 0:keys], pt_ref.at[block * heads + h, 0:keys], sems.at[h]
        )

    for block in range(slots):
        keys = visible(block, slots) * toks
        cols = slice(block * toks, (block + 1) * toks)
        kpos = lax.broadcasted_iota(jnp.int32, (keys, toks), 0)
        qpos = lax.broadcasted_iota(jnp.int32, (keys, toks), 1) + block * toks
        qp = prow_ref[:, cols].astype(f32)
        same = (piece_col[:keys] == qp) & (qp > 0.0)
        bias_ref[0:keys] = jnp.where((kpos <= qpos) | same, 0.0, masked_score)

        def head_body(h, carry, block=block, keys=keys, cols=cols):
            scores = dot(k_ref[h, 0:keys], q_ref[h, cols, :], 1, 1) + bias_ref[0:keys]
            peak = jnp.max(scores, axis=0, keepdims=True)
            weights = jnp.exp(scores - peak)
            mass = jnp.sum(weights, axis=0, keepdims=True)
            probs = (weights * (1.0 / mass)).astype(bf16)
            if block > 0:
                copy_out(block - 1, h).wait()
            pbuf[h, 0:keys] = probs
            copy_out(block, h).start()
            at = pl.ds(pl.multiple_of(h * HEAD_DIM, HEAD_DIM), HEAD_DIM)
            obuf[block, at, :] = dot(vt_ref[h, :, 0:keys], probs)
            return carry

        lax.fori_loop(0, heads, head_body, 0)
    for slot, m_ref in enumerate((m0, m1, m2, m3)):
        m_ref[...] = obuf[place_ref[slot]].T.astype(bf16)
    for h in range(heads):
        copy_out(slots - 1, h).wait()


def visible(block, slots):
    return min(block + 2, slots)


def attn_bwd_kernel(
    heads,
    place_ref,
    x0,
    x1,
    x2,
    x3,
    g0,
    g1,
    g2,
    g3,
    gain_ref,
    w_ref,
    cost_ref,
    sint_ref,
    q_ref,
    k_ref,
    v_ref,
    pt_ref,
    sums_ref,
    keep_ref,
    send_ref,
    dw_ref,
    done_ref,
    act_ref,
    go_ref,
    qcat_ref,
    kcat_ref,
    dk_ref,
    dv_ref,
    dqt_ref,
    dlin_ref,
    pbuf,
    sems,
):
    toks = x0.shape[0]
    width = heads * HEAD_DIM
    slots = 4

    def copy_in(block, h):
        keys = visible(block, slots) * toks
        return pltpu.make_async_copy(
            pt_ref.at[block * heads + h, 0:keys], pbuf.at[h, 0:keys], sems.at[h]
        )

    for h in range(heads):
        copy_in(0, h).start()
    swap = partner_matrix(HEAD_DIM)
    both = jnp.concatenate([eye(HEAD_DIM), swap], axis=1)
    swap_i = lax.broadcasted_iota(jnp.int32, (2 * HEAD_DIM, HEAD_DIM), 0)
    swap_j = lax.broadcasted_iota(jnp.int32, (2 * HEAD_DIM, HEAD_DIM), 1)
    low = ((swap_i - HEAD_DIM) < HEAD_DIM // 2) & (swap_i >= HEAD_DIM)
    high = (swap_i - HEAD_DIM) >= HEAD_DIM // 2
    stacked = (
        jnp.where(swap_i == swap_j, 1.0, 0.0)
        + jnp.where(low & (swap_j == swap_i - HEAD_DIM + HEAD_DIM // 2), -1.0, 0.0)
        + jnp.where(high & (swap_j == swap_i - HEAD_DIM - HEAD_DIM // 2), 1.0, 0.0)
    ).astype(bf16)
    for slot, (x_ref, g_ref) in enumerate(zip((x0, x1, x2, x3), (g0, g1, g2, g3))):
        rows = pl.ds(pl.multiple_of(place_ref[slot] * toks, toks), toks)
        _, _, act = normed(x_ref[...].astype(f32), gain_row(gain_ref))
        act_ref[rows, :] = act
        for h in range(heads):
            go_ref[h, rows, :] = g_ref[:, h * HEAD_DIM : (h + 1) * HEAD_DIM]
    for h in range(heads):
        qcat_ref[h] = dot(q_ref[h], both).astype(bf16)
        kcat_ref[h] = dot(stacked, k_ref[h], 1, 1).astype(bf16)
    dk_ref[...] = jnp.zeros(dk_ref.shape, f32)
    dv_ref[...] = jnp.zeros(dv_ref.shape, f32)

    for block in range(slots):
        keys = visible(block, slots) * toks
        cols = slice(block * toks, (block + 1) * toks)

        def head_body(h, carry, block=block, keys=keys, cols=cols):
            copy_in(block, h).wait()
            probs = pbuf[h, 0:keys]
            grad_out = go_ref[h, cols, :]
            grad_probs = dot(v_ref[h, 0:keys], grad_out, 1, 1)
            probs_f = probs.astype(f32)
            inner = jnp.sum(probs_f * grad_probs, axis=0, keepdims=True)
            grad_scores = (probs_f * (grad_probs - inner)).astype(bf16)
            dv_ref[h, 0:keys] += dot(probs, grad_out)
            dk_ref[h, 0:keys] += dot(grad_scores, qcat_ref[h, cols, :])
            dqt_ref[block, h] = dot(kcat_ref[h, :, 0:keys], grad_scores)
            if block + 1 < slots:
                copy_in(block + 1, h).start()
            return carry

        lax.fori_loop(0, heads, head_body, 0)
    cosine, sine = cost_ref[...].T, sint_ref[...].T
    for h in range(heads):
        cols = slice(h * HEAD_DIM, (h + 1) * HEAD_DIM)
        for block in range(slots):
            rows = slice(block * toks, (block + 1) * toks)
            both_t = dqt_ref[block, h]
            lin_t = (
                both_t[:HEAD_DIM] * cost_ref[:, rows] - both_t[HEAD_DIM:] * sint_ref[:, rows]
            ) * HEAD_DIM**-0.5
            dlin_ref[0, rows, cols] = lin_t.T.astype(bf16)
        dlin_ref[1, :, cols] = (
            dk_ref[h, :, :HEAD_DIM] * cosine - dk_ref[h, :, HEAD_DIM:] * sine
        ).astype(bf16)
        dlin_ref[2, :, cols] = dv_ref[h].astype(bf16)
    for k in range(3):
        dw_ref[k * width : (k + 1) * width, :] = dot(
            dlin_ref[k], act_ref[...], 0, 0
        ).astype(bf16)
    gain_grad = jnp.zeros((1, D), f32)
    for slot, x_ref in enumerate((x0, x1, x2, x3)):
        rows = pl.ds(pl.multiple_of(place_ref[slot] * toks, toks), toks)
        part = dot(dlin_ref[0, rows, :], w_ref[0])
        part += dot(dlin_ref[1, rows, :], w_ref[1])
        part += dot(dlin_ref[2, rows, :], w_ref[2])
        unit, _, _ = normed(x_ref[...].astype(f32), gain_row(gain_ref))
        gain_grad += jnp.sum(part * unit, axis=0, keepdims=True)
        if slot % 2 == 0:
            keep_ref[slot // 2] = part.astype(bf16)
        else:
            send_ref[slot // 2] = part.astype(bf16)
    rest = dw_ref.shape[0] - 4 * width
    ids = lax.broadcasted_iota(jnp.int32, (8, D), 0)
    tail = jnp.where(ids == 3, gain_grad, sums_ref[...])
    dw_ref[3 * width : 4 * width, :] = jnp.zeros((width, D), bf16)
    dw_ref[4 * width :, :] = jnp.zeros((rest, D), bf16)
    dw_ref[4 * width : 4 * width + 8, :] = tail.astype(bf16)
    done_ref[...] = jnp.zeros(done_ref.shape, f32)


def attn_fwd(place, x_slots, gain, w, cosine, sine, pieces):
    toks, width = x_slots[0].shape[0], w.shape[1]
    slots = len(x_slots)
    seq, heads = slots * toks, width // HEAD_DIM
    head_shape = jax.ShapeDtypeStruct((heads, seq, HEAD_DIM), bf16)
    return pl.pallas_call(
        functools.partial(attn_fwd_kernel, heads),
        out_shape=[head_shape] * 3
        + [jax.ShapeDtypeStruct((slots * heads, seq, toks), bf16)]
        + [jax.ShapeDtypeStruct((toks, width), bf16)] * slots,
        in_specs=[SM] + [VM] * 9,
        out_specs=[VM] * 3 + [HB] + [VM] * slots,
        scratch_shapes=[
            pltpu.VMEM((seq, toks), f32),
            pltpu.VMEM((heads, seq, toks), bf16),
            pltpu.VMEM((slots, width, toks), f32),
            pltpu.VMEM((heads, HEAD_DIM, seq), bf16),
            pltpu.SemaphoreType.DMA((heads,)),
        ],
        compiler_params=params(),
        name="attn_fwd",
        cost_estimate=cost(20),
    )(place, *x_slots, gain, w, cosine, sine, pieces)


def attn_bwd(place, x_slots, grads, gain, w, tables, saved, sums, dw_rows):
    toks, width = x_slots[0].shape[0], w.shape[1]
    slots = len(x_slots)
    seq, heads = slots * toks, width // HEAD_DIM
    return pl.pallas_call(
        functools.partial(attn_bwd_kernel, heads),
        out_shape=[
            jax.ShapeDtypeStruct((2, toks, D), bf16),
            jax.ShapeDtypeStruct((2, toks, D), bf16),
            jax.ShapeDtypeStruct((dw_rows, D), bf16),
            jax.ShapeDtypeStruct((8, 128), f32),
        ],
        in_specs=[SM] + [VM] * 15 + [HB, VM],
        out_specs=[VM] * 4,
        scratch_shapes=[
            pltpu.VMEM((seq, D), bf16),
            pltpu.VMEM((heads, seq, HEAD_DIM), bf16),
            pltpu.VMEM((heads, seq, 2 * HEAD_DIM), bf16),
            pltpu.VMEM((heads, 2 * HEAD_DIM, seq), bf16),
            pltpu.VMEM((heads, seq, 2 * HEAD_DIM), f32),
            pltpu.VMEM((heads, seq, HEAD_DIM), f32),
            pltpu.VMEM((slots, heads, 2 * HEAD_DIM, toks), f32),
            pltpu.VMEM((3, seq, width), bf16),
            pltpu.VMEM((heads, seq, toks), bf16),
            pltpu.SemaphoreType.DMA((heads,)),
        ],
        compiler_params=params(),
        name="attn_bwd",
        cost_estimate=cost(22),
    )(place, *x_slots, *grads, gain, w, *tables, *saved, sums)


def out_proj_kernel(
    x_ref, m0, m1, m2, m3, w0, w1, w2, w3, gain_ref, resid_ref, n_ref, top_ref, low_ref, copies_ref
):
    attended = dot(m0[...], w0[...])
    attended += dot(m1[...], w1[...])
    attended += dot(m2[...], w2[...])
    attended += dot(m3[...], w3[...])
    resid = x_ref[...].astype(f32) + attended
    resid_ref[...] = resid
    _, _, act = normed(resid, gain_row(gain_ref))
    half = act.shape[0] // 2
    n_ref[...] = act
    top_ref[...] = act[:half]
    low_ref[...] = act[half:]
    for k in range(copies_ref.shape[0]):
        copies_ref[k] = act


def route_columns(base_ref, routes_ref, gates_ref, toks):
    base = pl.multiple_of(base_ref[0], toks)
    routes = routes_ref[:, pl.ds(base, toks)].astype(f32)
    rows = jnp.concatenate([routes, gates_ref[...], jnp.zeros((4, toks), f32)], axis=0)
    return rows.T, routes


def expert_gate(columns, expert):
    return jnp.where(columns[:, 0:1] == expert, columns[:, 2:3], 0.0) + jnp.where(
        columns[:, 1:2] == expert, columns[:, 3:4], 0.0
    )


def mid_kernel(
    base_ref,
    dx_refs,
    cot_ref,
    resid_ref,
    routes_ref,
    gates_ref,
    gain_ref,
    m_refs,
    w_refs,
    gres_ref,
    g_refs,
    o_refs,
    sums_ref,
):
    toks = cot_ref.shape[0]
    cot = cot_ref[...].astype(f32)
    columns, _ = route_columns(base_ref, routes_ref, gates_ref, toks)
    halves = [dx_refs[k][...].astype(f32) + dx_refs[k + 1][...].astype(f32) for k in (0, 2)]
    grad = jnp.concatenate(halves, axis=0) + expert_gate(columns, E_FFN + 1) * cot
    gain = gain_row(gain_ref)
    unit, inverse, _ = normed(resid_ref[...], gain)
    grad_unit = grad * gain
    grad_resid = cot + inverse * (
        grad_unit - unit * jnp.mean(grad_unit * unit, axis=-1, keepdims=True)
    )
    gres_ref[...] = grad_resid
    grad_att = grad_resid.astype(bf16)
    for k, (m_ref, w_ref, g_ref) in enumerate(zip(m_refs, w_refs, g_refs)):
        g_ref[...] = dot(grad_att, w_ref[...], 1, 1).astype(bf16)
        o_refs[k % 2][k // 2] = dot(m_ref[...], grad_att, 0, 0).astype(bf16)
    sums_ref[...] = jnp.zeros(sums_ref.shape, f32)
    sums_ref[0:1, :] = jnp.sum(grad * unit, axis=0, keepdims=True)
    for k in range(2):
        weight = expert_gate(columns, E_FFN + 2 + k)
        sums_ref[1 + k : 2 + k, :] = jnp.sum(weight * cot, axis=0, keepdims=True)


def out_kernel(
    base_ref,
    y_refs,
    cot_ref,
    resid_ref,
    n_ref,
    routes_ref,
    gates_ref,
    const_ref,
    out_ref,
    gg_ref,
):
    toks = cot_ref.shape[0]
    half = toks // 2
    cot = cot_ref[...].astype(f32)
    columns, routes = route_columns(base_ref, routes_ref, gates_ref, toks)
    act = n_ref[...].astype(f32)
    consts = const_ref[...].astype(f32)
    top = y_refs[0][...].astype(f32) + y_refs[1][...].astype(f32)
    low = y_refs[2][...].astype(f32) + y_refs[3][...].astype(f32)
    moe = jnp.concatenate([top, low[:half]], axis=0) + expert_gate(columns, E_FFN + 1) * act
    moe += expert_gate(columns, E_FFN + 2) * consts[0:1]
    moe += expert_gate(columns, E_FFN + 3) * consts[1:2]
    out_ref[...] = (resid_ref[...] + moe).astype(bf16)
    dots = [cot * act, cot * consts[0:1], cot * consts[1:2]]
    dots = [jnp.sum(v, axis=1, keepdims=True) for v in dots]
    dots = jnp.concatenate([jnp.broadcast_to(dots[k % 3], (toks, 1)) for k in range(8)], axis=1).T
    table = low[half : half + TAB, 0:toks]
    for pair in range(2):
        route = routes[pair : pair + 1]
        result = jnp.zeros((1, toks), f32)
        for e in range(E_FFN):
            result += jnp.where(route == e, table[e : e + 1], 0.0)
        for k in range(3):
            result += jnp.where(route == E_FFN + 1 + k, dots[k : k + 1], 0.0)
        gg_ref[pair : pair + 1, :] = result


def last_kernel(gno_a, gno_b, x_ref, gres_ref, gain_ref, out_ref):
    grad = gno_a[...].astype(f32) + gno_b[...].astype(f32)
    gain = gain_row(gain_ref)
    unit, inverse, _ = normed(x_ref[...].astype(f32), gain)
    grad_unit = grad * gain
    out_ref[...] = gres_ref[...] + inverse * (
        grad_unit - unit * jnp.mean(grad_unit * unit, axis=-1, keepdims=True)
    )


def dispatch_block(first, experts, x, p_ref, tab_ref, rows_ref, gate_ref, offs, starts, block):
    toks = x.shape[0]
    tab_ref[...] = p_ref[toks : toks + TAB, :].astype(f32)
    want = lax.broadcasted_iota(jnp.int32, (SHORT, toks), 0).astype(f32)
    cot = p_ref[0:toks, :]

    def select(i, begin):
        row = tab_ref[pl.ds(first + i, 1), :]
        match = (want + begin) == row[:, 0:toks]
        gate = row[:, toks : 2 * toks] + row[:, 2 * toks : 3 * toks]
        weight = jnp.sum(jnp.where(match, gate, 0.0), axis=1, keepdims=True)
        return jnp.where(match, 1.0, 0.0).astype(bf16), weight, row[:, 0:toks]

    def put(i, off, rows_x, rows_c, weight):
        at = pl.ds(pl.multiple_of(off, 16), SHORT)
        rows_ref[i, at, 0:D] = rows_x.astype(bf16)
        rows_ref[i, at, D : 2 * D] = (rows_c * weight).astype(bf16)
        if gate_ref is not None:
            gate_ref[i, at, :] = jnp.broadcast_to(weight, (SHORT, 128))

    parts = [select(i, 0.0) for i in range(experts)]
    counts = [jnp.max(rank).astype(jnp.int32) + 1 for _, _, rank in parts]
    hot = jnp.concatenate([p[0] for p in parts], axis=0)
    rows_x, rows_c = dot(hot, x), dot(hot, cot)
    for i in range(experts):
        off = offs[i]
        if starts is not None:
            starts[block, i] = off
        seg = slice(i * SHORT, (i + 1) * SHORT)
        put(i, off, rows_x[seg], rows_c[seg], parts[i][1])

        @pl.when(counts[i] > SHORT)
        def _(i=i, off=off):
            rest, weight, _ = select(i, float(SHORT))
            put(i, off + SHORT, dot(rest, x), dot(rest, cot), weight)

        offs[i] = off + ((counts[i] + 15) // 16) * 16


def expert_acts(rows, wg, wu, wd):
    act, grad = rows[:, :D], rows[:, D:]
    gate_pre = dot(act, wg)
    up_pre = dot(act, wu)
    grad_hidden = dot(grad, wd, 1, 1)
    sig = 1.0 / (1.0 + jnp.exp(-gate_pre))
    silu = gate_pre * sig
    hidden = (silu * up_pre).astype(bf16)
    grad_gate = (grad_hidden * up_pre * sig * (1.0 + gate_pre * (1.0 - sig))).astype(bf16)
    grad_up = (grad_hidden * silu).astype(bf16)
    return act, grad, hidden, grad_hidden, grad_gate, grad_up


def own_kernel(nb, tile, first_ref, *refs):
    tops, lows, ps = refs[:nb], refs[nb : 2 * nb], refs[2 * nb : 3 * nb]
    wg_h, wu_h, wd_h, dxa, dxb, ya, yb, rows_out, used = refs[3 * nb : 3 * nb + 9]
    (
        xbuf,
        pbuf,
        wg,
        wu,
        wd,
        rows_ref,
        back_ref,
        gate_ref,
        tab_ref,
        dxbuf,
        ybuf,
        offs,
        starts,
        tok_sems,
        w_sems,
        out_sems,
        row_sem,
    ) = refs[3 * nb + 9 :]
    experts = wg.shape[0]
    toks = xbuf.shape[1]
    half = nb // 2
    first = first_ref[0]
    mid = toks // 2

    def tok_copies(b, src):
        return (
            pltpu.make_async_copy(tops[src], xbuf.at[b, 0:mid], tok_sems.at[0, b]),
            pltpu.make_async_copy(lows[src], xbuf.at[b, mid:toks], tok_sems.at[1, b]),
            pltpu.make_async_copy(ps[src], pbuf.at[b], tok_sems.at[2, b]),
        )

    w_copies = [
        pltpu.make_async_copy(src, dst, w_sems.at[k])
        for k, (src, dst) in enumerate(((wg_h, wg), (wu_h, wu), (wd_h, wd)))
    ]
    for b in range(nb):
        for copy in tok_copies(b, b):
            copy.start()
    for copy in w_copies:
        copy.start()
    for i in range(experts):
        offs[i] = 0

    def dispatch_body(b, carry):
        for copy in tok_copies(b, 0):
            copy.wait()
        dispatch_block(
            first, experts, xbuf[b], pbuf.at[b], tab_ref, rows_ref, gate_ref, offs, starts, b
        )
        return carry

    lax.fori_loop(0, nb, dispatch_body, 0)
    for i in range(experts):
        at = pl.ds(pl.multiple_of(offs[i], 16), TILE_BACK)
        rows_ref[i, at, :] = jnp.zeros((TILE_BACK, 2 * D), bf16)
        back_ref[i, at, :] = jnp.zeros((TILE_BACK, 2 * D), bf16)
        gate_ref[i, at, :] = jnp.zeros((TILE_BACK, 128), f32)
        used[i] = offs[i]
    rows_copy = pltpu.make_async_copy(rows_ref, rows_out, row_sem)
    rows_copy.start()
    for copy in w_copies:
        copy.wait()

    def expert_body(e, carry):
        def tile_body(j, inner):
            at = pl.ds(pl.multiple_of(j * tile, 16), tile)
            rows = rows_ref[e, at, :]
            _, _, hidden, grad_hidden, grad_gate, grad_up = expert_acts(rows, wg[e], wu[e], wd[e])
            weight = gate_ref[e, at, :]
            product = jnp.sum(hidden.astype(f32) * grad_hidden, axis=1, keepdims=True)
            gate_ref[e, at, :] = jnp.where(weight > 0.0, product / jnp.maximum(weight, 0.125), 0.0)
            back_ref[e, at, 0:D] = (
                dot(grad_gate, wg[e], 1, 1) + dot(grad_up, wu[e], 1, 1)
            ).astype(bf16)
            back_ref[e, at, D : 2 * D] = (dot(hidden, wd[e]) * weight[:, :1]).astype(bf16)
            return inner

        return lax.fori_loop(0, (offs[e] + tile - 1) // tile, tile_body, carry)

    lax.fori_loop(0, experts, expert_body, 0)

    def out_copies(b, slot):
        near = b < half
        return near, (
            pltpu.make_async_copy(dxbuf.at[slot], dxa.at[b % half], out_sems.at[0, slot]),
            pltpu.make_async_copy(ybuf.at[slot], ya.at[b % half], out_sems.at[1, slot]),
        ), (
            pltpu.make_async_copy(dxbuf.at[slot], dxb.at[b % half], out_sems.at[0, slot]),
            pltpu.make_async_copy(ybuf.at[slot], yb.at[b % half], out_sems.at[1, slot]),
        )

    def wait_slot(slot):
        pltpu.make_async_copy(dxbuf.at[slot], dxa.at[0], out_sems.at[0, slot]).wait()
        pltpu.make_async_copy(ybuf.at[slot], ya.at[0], out_sems.at[1, slot]).wait()

    want = lax.broadcasted_iota(jnp.int32, (SEG, toks), 0).astype(f32)
    tab_rows = lax.broadcasted_iota(jnp.int32, (TAB, toks), 0)

    def combine_body(b, carry):
        slot = b % 2

        @pl.when(b >= 2)
        def _():
            wait_slot(slot)

        tab_ref[...] = pbuf[b, toks : toks + TAB, :].astype(f32)
        hots, segs = [], []
        table = jnp.zeros((TAB, toks), f32)
        for i in range(experts):
            rank = tab_ref[pl.ds(first + i, 1), 0:toks]
            match = jnp.where(want == rank, 1.0, 0.0)
            at = pl.ds(pl.multiple_of(starts[b, i], 16), SEG)
            hots.append(match.astype(bf16))
            segs.append(back_ref[i, at, :])
            line = jnp.sum(match * gate_ref[i, at, :][:, :1], axis=0, keepdims=True)
            table += jnp.where(tab_rows == first + i, line, 0.0)
        result = dot(jnp.concatenate(hots, axis=0), jnp.concatenate(segs, axis=0), 0, 0)
        dxbuf[slot] = result[:, :D].astype(bf16)
        ybuf[slot, 0:toks, :] = result[:, D:].astype(bf16)
        ybuf[slot, toks : toks + TAB, 0:toks] = table.astype(bf16)
        ybuf[slot, toks : toks + TAB, toks:] = jnp.zeros((TAB, D - toks), bf16)
        near, here, there = out_copies(b, slot)

        @pl.when(near)
        def _():
            here[0].start()
            here[1].start()

        @pl.when(jnp.logical_not(near))
        def _():
            there[0].start()
            there[1].start()

        return carry

    lax.fori_loop(0, nb, combine_body, 0)
    wait_slot(0)
    wait_slot(1)
    rows_copy.wait()


def dispatch_kernel(pieces, arrays, tile, first_ref, *refs):
    srcs, refs = refs[:arrays], refs[arrays:]
    rows_out, used, xbuf, pbuf, rows_ref, tab_ref, offs, tok_sems, row_sem = refs
    experts = rows_ref.shape[0]
    ring = xbuf.shape[0]
    first = first_ref[0]
    total = sum(p[0] for p in pieces)

    def start_block(b):
        slot = b % ring
        begin = 0
        for blocks, x_parts, p_parts in pieces:

            @pl.when((b >= begin) & (b < begin + blocks))
            def _(begin=begin, x_parts=x_parts, p_parts=p_parts):
                for which, (parts, buf) in enumerate(((x_parts, xbuf), (p_parts, pbuf))):
                    for array, at, lo, hi in parts:
                        pltpu.make_async_copy(
                            srcs[array].at[b - begin + at],
                            buf.at[slot, lo:hi],
                            tok_sems.at[which, slot],
                        ).start()

            begin += blocks

    def start_body(b, carry):
        start_block(b)
        return carry

    lax.fori_loop(0, min(ring - 1, total), start_body, 0)
    for i in range(experts):
        offs[i] = 0

    def dispatch_body(b, carry):
        slot = b % ring
        pltpu.make_async_copy(xbuf.at[slot], xbuf.at[slot], tok_sems.at[0, slot]).wait()
        pltpu.make_async_copy(pbuf.at[slot], pbuf.at[slot], tok_sems.at[1, slot]).wait()

        @pl.when(b + ring - 1 < total)
        def _():
            start_block(b + ring - 1)

        dispatch_block(
            first, experts, xbuf[slot], pbuf.at[slot], tab_ref, rows_ref, None, offs, None, b
        )
        return carry

    lax.fori_loop(0, total, dispatch_body, 0)

    def chunk(i, j):
        at = pl.ds(pl.multiple_of(j * tile, tile), tile)
        return pltpu.make_async_copy(rows_ref.at[i, at], rows_out.at[i, at], row_sem)

    def chunks(i):
        return jnp.maximum((offs[i] + tile - 1) // tile, 1)

    def start_chunk(i):
        def body(j, carry):
            chunk(i, j).start()
            return carry

        return body

    def wait_chunk(i):
        def body(j, carry):
            chunk(i, j).wait()
            return carry

        return body

    for i in range(experts):
        rows_ref[i, pl.ds(pl.multiple_of(offs[i], 16), tile), :] = jnp.zeros((tile, 2 * D), bf16)
        used[i] = offs[i]
        lax.fori_loop(0, chunks(i), start_chunk(i), 0)
    for i in range(experts):
        lax.fori_loop(0, chunks(i), wait_chunk(i), 0)


def weight_kernel(tile, experts, given, add, begin_ref, used_ref, rows_h, wg_h, wu_h, wd_h, *refs):
    begin_e = begin_ref[0]
    small = max(tile // 2, TILE_BACK)
    olds, refs = (refs[:3], refs[3:]) if given else ((), refs)
    outs, accs = refs[:3], refs[3:6]
    rbuf, wg, wu, wd, row_sems, w_sems, acc_sems = refs[6:]
    w_copies = [
        pltpu.make_async_copy(src.at[pl.ds(begin_e, experts)], dst, w_sems.at[k])
        for k, (src, dst) in enumerate(((wg_h, wg), (wu_h, wu), (wd_h, wd)))
    ]

    def tiles(e):
        return jnp.maximum((used_ref[begin_e + e] + tile - 1) // tile, 1)

    def fetch(e, j, slot):
        at = pl.ds(pl.multiple_of(j * tile, tile), tile)
        return pltpu.make_async_copy(
            rows_h.at[begin_e + e, at], rbuf.at[slot], row_sems.at[slot]
        )

    def out_copies(e):
        return [
            pltpu.make_async_copy(src, dst.at[e + begin_e], acc_sems.at[k])
            for k, (src, dst) in enumerate(zip(accs, outs))
        ]

    def old_copies(e):
        return [
            pltpu.make_async_copy(src.at[e + begin_e], dst, acc_sems.at[k])
            for k, (src, dst) in enumerate(zip(olds, accs))
        ]

    fetch(0, 0, 0).start()
    for copy in w_copies:
        copy.start()
    if add:
        for copy in old_copies(0):
            copy.start()
    for copy in w_copies:
        copy.wait()

    def expert_body(e, count):
        last = tiles(e)

        def tile_body(j, step):
            slot = step % 2
            fetch(e, j, slot).wait()

            @pl.when(j + 1 < last)
            def _():
                fetch(e, j + 1, 1 - slot).start()

            @pl.when((j + 1 == last) & (e + 1 < experts))
            def _():
                fetch(e + 1, 0, 1 - slot).start()


            @pl.when(j == 0)
            def _():
                @pl.when(e > 0)
                def _():
                    for copy in out_copies(e - 1):
                        copy.wait()
                    if add:
                        for copy in old_copies(e):
                            copy.start()

                if add:
                    for copy in old_copies(e):
                        copy.wait()
                else:
                    for acc in accs:
                        acc[...] = jnp.zeros(acc.shape, f32)

            def work(size):
                rows = rbuf[slot, 0:size]
                act, grad, hidden, _, grad_gate, grad_up = expert_acts(rows, wg[e], wu[e], wd[e])
                part = dot(act, jnp.concatenate([grad_gate, grad_up], axis=1), 0, 0)
                width = grad_gate.shape[1]
                accs[0][...] += part[:, :width]
                accs[1][...] += part[:, width:]
                accs[2][...] += dot(hidden, grad, 0, 0)

            if small < tile:
                little = used_ref[begin_e + e] - j * tile <= small

                @pl.when(little)
                def _():
                    work(small)

                @pl.when(jnp.logical_not(little))
                def _():
                    work(tile)

            else:
                work(tile)
            return step + 1

        count = lax.fori_loop(0, last, tile_body, count)
        for copy in out_copies(e):
            copy.start()
        return count

    lax.fori_loop(0, experts, expert_body, jnp.int32(0))
    for copy in out_copies(experts - 1):
        copy.wait()


def row_room(cap, blocks, groups, tile):
    most = groups * min(cap + 15 * blocks, SEG * blocks)
    return -(-most // tile) * tile + tile


def own_experts(first, tops, lows, ps, wg, wu, wd, cap):
    nb = len(ps)
    experts = wg.shape[0]
    toks = ps[0].shape[0] - TAB
    room = row_room(cap, nb, 1, TILE_BACK)
    half = nb // 2
    shapes = [
        jax.ShapeDtypeStruct((half, toks, D), bf16),
        jax.ShapeDtypeStruct((half, toks, D), bf16),
        jax.ShapeDtypeStruct((half, toks + TAB, D), bf16),
        jax.ShapeDtypeStruct((half, toks + TAB, D), bf16),
        jax.ShapeDtypeStruct((experts, room, 2 * D), bf16),
        jax.ShapeDtypeStruct((experts,), jnp.int32),
    ]
    return pl.pallas_call(
        functools.partial(own_kernel, nb, TILE_OWN),
        out_shape=shapes,
        in_specs=[SM] + [HB] * (3 * nb + 3),
        out_specs=[HB] * 5 + [SM],
        scratch_shapes=[
            pltpu.VMEM((nb, toks, D), bf16),
            pltpu.VMEM((nb, toks + TAB, D), bf16),
            pltpu.VMEM(wg.shape, bf16),
            pltpu.VMEM(wu.shape, bf16),
            pltpu.VMEM(wd.shape, bf16),
            pltpu.VMEM((experts, room, 2 * D), bf16),
            pltpu.VMEM((experts, room, 2 * D), bf16),
            pltpu.VMEM((experts, room, 128), f32),
            pltpu.VMEM((TAB, D), f32),
            pltpu.VMEM((2, toks, D), bf16),
            pltpu.VMEM((2, toks + TAB, D), bf16),
            pltpu.SMEM((experts,), jnp.int32),
            pltpu.SMEM((nb, experts), jnp.int32),
            pltpu.SemaphoreType.DMA((3, nb)),
            pltpu.SemaphoreType.DMA((3,)),
            pltpu.SemaphoreType.DMA((2, 2)),
            pltpu.SemaphoreType.DMA,
        ],
        compiler_params=params(),
        name="own_experts",
        cost_estimate=cost(29),
    )(first, *tops, *lows, *ps, wg, wu, wd)


def chip_pieces(x_sets, p_sets, blocks, toks):
    flat = [a for sets in (x_sets, p_sets) for arrays in sets for a in arrays]
    half = toks // 2
    x_count = x_sets[0][0].shape[0] // blocks
    pieces = []
    for k in range(4 * x_count):
        core, x, y = k // (2 * x_count), k // 2 % x_count, k % 2
        parts, base = [], 0
        for sets, end in ((x_sets, toks), (p_sets, toks + TAB)):
            top, low = base + core * 2 + y, base + len(sets[0]) + core * x_count + x
            parts.append(((top, x * blocks, 0, half), (low, y * blocks, half, end)))
            base += len(sets[0]) + len(sets[1])
        pieces.append((blocks, *parts))
    return flat, pieces


def dispatch(first, flat, pieces, toks, experts, cap, groups):
    total = sum(p[0] for p in pieces)
    ring = 4
    room = row_room(cap, total // groups, groups, TILE_FAR)
    return pl.pallas_call(
        functools.partial(dispatch_kernel, tuple(pieces), len(flat), TILE_FAR),
        out_shape=[
            jax.ShapeDtypeStruct((experts, room, 2 * D), bf16),
            jax.ShapeDtypeStruct((experts,), jnp.int32),
        ],
        in_specs=[SM] + [HB] * len(flat),
        out_specs=[HB, SM],
        scratch_shapes=[
            pltpu.VMEM((ring, toks, D), bf16),
            pltpu.VMEM((ring, toks + TAB, D), bf16),
            pltpu.VMEM((experts, room, 2 * D), bf16),
            pltpu.VMEM((TAB, D), f32),
            pltpu.SMEM((experts,), jnp.int32),
            pltpu.SemaphoreType.DMA((2, ring)),
            pltpu.SemaphoreType.DMA,
        ],
        compiler_params=params(),
        name="dispatch",
        cost_estimate=cost(20),
    )(first, *flat)


def weight_grads(used, rows, weights, tile, olds=None, add=True, begin_e=0, count_e=None):
    experts = count_e or weights[0].shape[0]
    shapes = [jax.ShapeDtypeStruct(w.shape, f32) for w in weights]
    operands = [jnp.full((1,), begin_e, jnp.int32), used, rows, *weights, *(olds or ())]
    return pl.pallas_call(
        functools.partial(weight_kernel, tile, experts, bool(olds), bool(olds) and add),
        out_shape=shapes,
        in_specs=[SM, SM] + [HB] * (len(operands) - 2),
        out_specs=[HB] * 3,
        input_output_aliases={len(operands) - 3 + k: k for k in range(3)} if olds else {},
        scratch_shapes=[
            *[pltpu.VMEM(w.shape[1:], f32) for w in weights],
            pltpu.VMEM((2, tile, 2 * D), bf16),
            *[pltpu.VMEM((experts, *w.shape[1:]), bf16) for w in weights],
            pltpu.SemaphoreType.DMA((2,)),
            pltpu.SemaphoreType.DMA((3,)),
            pltpu.SemaphoreType.DMA((3,)),
        ],
        compiler_params=params(),
        name="weight_grads",
        cost_estimate=cost(14),
    )(*operands)


def after(value, *deps):
    return lax.optimization_barrier((value, *deps))[0]


def after_all(values, *deps):
    return lax.optimization_barrier((*values, *deps))[: len(values)]


def after_tree(tree, *deps):
    return lax.optimization_barrier((tree, *deps))[0]


def other_groups(copies, cut):
    count, index = lax.axis_size("dp"), lax.axis_index("dp")
    blocks = lax.all_to_all(copies, "dp", 0, 0, tiled=True)

    def pick(blocks, rows):
        found = [
            lax.dynamic_index_in_dim(blocks, (index + step) % count, 0)[:, rows]
            for step in range(1, count)
        ]
        return jnp.concatenate(found, axis=0)

    return blocks, lambda b: (pick(b, slice(0, cut)), pick(b, slice(cut, None)))


def gather_line(values, axis):
    out = list(values)
    for step in range(1, lax.axis_size(axis)):
        out += [shift(v, axis, step) for v in values]
    return out


def with_line(values, axis):
    return gather_line([jnp.concatenate(values, axis=0)], axis)


def plane_gather(value, x_first):
    if x_first:
        cols = gather_line([value], "x")
        rows = [shift(v, "y", 1) for v in cols]
        return [v for pair in zip(cols, rows) for v in pair]
    return gather_line(gather_line([value], "y"), "x")


def both_cores(values, *deps):
    return list(values) + [shift(after(v, *deps) if deps else v, "c", 1) for v in values]


def total(*parts):
    return sum(p.astype(f32) for p in parts).astype(bf16)


def scatter_cores(parts):
    return parts[0], shift(parts[1], "c", -1)


def scatter_first(keep, other, cut):
    count = lax.axis_size("x")

    def add(rows, where):
        return total(keep[where][:, rows], other[where][:, rows])

    top, low = slice(0, cut), slice(cut, None)
    x_sent = [add(top, slice(2 * k, 2 * k + 2)) for k in range(1, count)]
    y_sent = add(low, slice(1, None, 2))
    x_kept = add(top, slice(0, 2))
    y_kept = add(low, slice(0, None, 2))
    x_got = [shift(v, "x", -k) for k, v in zip(range(1, count), x_sent)]
    y_got = shift(y_sent, "y", -1)
    return (*x_got, y_got), x_kept, y_kept


def scatter_second(got, x_kept, y_kept):
    x_got, y_got = got[:-1], got[-1]
    count = len(got)
    y_next = total(x_kept[1], *[v[1] for v in x_got])
    x_next = [total(y_kept[k], y_got[k]) for k in range(1, count)]
    top_own = total(x_kept[0], *[v[0] for v in x_got])
    low_own = total(y_kept[0], y_got[0])
    top_far = shift(y_next, "y", -1)
    low_far = [shift(v, "x", -k) for k, v in zip(range(1, count), x_next)]
    if count > 2:
        low_far = [total(*low_far)]
    return top_own, top_far, low_own, low_far[0]


def line_sum(value, axis):
    return sum([shift(value, axis, step) for step in range(1, lax.axis_size(axis))], value)


def row_sum(value):
    far = lax.ppermute(value, ("y", "c"), [(i, 3 - i) for i in range(4)])
    return value + shift(value, "c", 1) + shift(value, "y", 1) + far


def scatter_sum(value, axis):
    count, index = lax.axis_size(axis), lax.axis_index(axis)
    chunks = value.reshape((count, value.shape[0] // count) + value.shape[1:])
    result = lax.dynamic_index_in_dim(chunks, index, 0, keepdims=False).astype(f32)
    for step in range(1, count):
        chunk = lax.dynamic_index_in_dim(chunks, (index + step) % count, 0, keepdims=False)
        result = result + shift(chunk, axis, step).astype(f32)
    return result.astype(bf16)


def gather_chunks(own, axis):
    count, index = lax.axis_size(axis), lax.axis_index(axis)
    full = jnp.zeros((count,) + own.shape, bf16)
    full = lax.dynamic_update_index_in_dim(full, own, index, 0)
    for step in range(1, count):
        chunk = shift(own, axis, step)
        full = lax.dynamic_update_index_in_dim(full, chunk, (index - step) % count, 0)
    return full.reshape((count * own.shape[0],) + own.shape[1:])


def shards(
    inputs,
    cotangent,
    gain_attn,
    gain_ffn,
    attn_in,
    attn_out,
    expert_gate,
    expert_up,
    expert_down,
    const_vectors,
    gate_values,
    routes,
    priority,
    pieces,
):
    toks = inputs.shape[1]
    y_index, c_index = lax.axis_index("y"), lax.axis_index("c")
    x_index, x_count = lax.axis_index("x"), lax.axis_size("x")
    dp_count = lax.axis_size("dp")
    row_count = lax.axis_size("y") * lax.axis_size("c")
    seq = toks * row_count
    heads = attn_in.shape[2] // HEAD_DIM
    width = heads * HEAD_DIM
    group_tokens = routes.shape[1]
    nb = group_tokens // toks
    cap = 5 * group_tokens // 24
    experts = expert_gate.shape[0]
    x_own, cot = inputs[0], cotangent[0]
    place = jnp.stack(
        [
            ((y_index - ky) % 2) * 2 + (c_index - kc) % 2
            for ky in range(2)
            for kc in range(2)
        ]
    ).astype(jnp.int32)
    first = (x_index * experts).astype(jnp.int32)[None]
    base = (x_index * seq + (y_index * 2 + c_index) * toks).astype(jnp.int32)[None]

    x_y = shift(x_own, "y", 1)
    w_y = shift(after(attn_out, x_y), "y", 1)
    w_c = shift(attn_out, "c", 1)

    cosine, sine = (jnp.asarray(a) for a in rotary_numpy(seq))
    routes_t, gates_t = routes[0].T, gate_values[0].T
    attn_w = attn_in.transpose(0, 2, 1)
    weights = (expert_gate, expert_up, expert_down)
    half = toks // 2
    far = list(range(1, dp_count))
    one_call = dp_count * group_tokens <= CALL_TOKENS

    payload, p_copies = pl.pallas_call(
        functools.partial(route_kernel, cap),
        out_shape=[
            jax.ShapeDtypeStruct((toks + TAB, D), bf16),
            jax.ShapeDtypeStruct((dp_count if one_call else 1, toks + TAB, D), bf16),
        ],
        in_specs=[SM, VM, VM, VM, VM],
        out_specs=[VM, VM],
        compiler_params=params(),
        name="route",
        cost_estimate=cost(2.5),
    )(base, routes_t, priority, gates_t, cot)
    if one_call:
        far_p, split_p = other_groups(p_copies, half)
    x_slots = [x_own, shift(x_own, "c", 1), x_y, shift(after(x_y, payload), "c", 1)]
    p_cols = gather_line([payload], "x")
    p_y = shift(after(payload, x_y), "y", 1)

    mix_shape = jax.ShapeDtypeStruct((toks, width), bf16)
    fwd_out = attn_fwd(after(place, payload), x_slots, gain_attn, attn_w, cosine, sine, pieces)
    fwd_out = after_all(fwd_out, *p_cols, p_y, w_y, w_c)
    q, k, v, probs, *mixed = fwd_out

    def to_owner(parts):
        return [
            parts[0],
            shift(parts[1], "c", -1),
            shift(parts[2], "y", -1),
            lax.ppermute(parts[3], ("y", "c"), [(i, 3 - i) for i in range(4)]),
        ]

    started = mixed[0]
    w_slots = [attn_out, w_c, w_y, shift(after(w_y, started), "c", 1)]
    own_p = [p_cols[0], p_y]
    for step, p in enumerate(p_cols[1:], 1):
        own_p += [p, shift(after(p_y, started), "x", step)]
    own_p = both_cores(own_p, started)
    if one_call:
        p_top, p_low = split_p(after(far_p, started))
    mixed = to_owner(mixed)
    resid, norm_two, norm_top, norm_low, x_copies = pl.pallas_call(
        out_proj_kernel,
        out_shape=[
            jax.ShapeDtypeStruct((toks, D), f32),
            jax.ShapeDtypeStruct((toks, D), bf16),
            jax.ShapeDtypeStruct((half, D), bf16),
            jax.ShapeDtypeStruct((half, D), bf16),
            jax.ShapeDtypeStruct((dp_count if one_call else 1, toks, D), bf16),
        ],
        in_specs=[VM] * 10,
        out_specs=[VM] * 5,
        compiler_params=params(),
        name="out_proj",
        cost_estimate=cost(3),
    )(x_own, *mixed, *w_slots, after(gain_ffn, own_p[2 * x_count - 1]))

    tops = plane_gather(norm_top, True)
    lows = plane_gather(norm_low, False)
    arrived = (tops[-1], lows[-1])
    ready = ()
    if one_call:
        far_x, split_x = other_groups(x_copies, half)
        first_in = (tops[1], tops[2], lows[1], lows[2])
        p_top_x = gather_line([after(p_top, *first_in)], "x")
        p_low_y = gather_line([after(p_low, *first_in)], "y")
        ready = (p_top_x[-1], p_low_y[-1])
        p_top = with_line(after_all(p_top_x, *arrived), "y")
        p_low = with_line(after_all(p_low_y, *arrived), "x")
    tops, lows = both_cores(tops), both_cores(lows)
    own_out = own_experts(after(first, *ready), tops, lows, own_p, *weights, cap)
    if one_call:
        own_out = after_all(own_out, *p_top, *p_low, far_x)
    dxa, dxb, ya, yb, rows, used = own_out
    dx_first = scatter_first(*scatter_cores((dxa, dxb)), half)
    dx_stage = dx_first[0][-1]
    dx_parts = scatter_second(*dx_first)
    if one_call:
        p_near = [shift(after(a[0], dx_first[1]), "c", 1) for a in (p_top, p_low)]
    front = max(1, experts // 2)
    grads_w = weight_grads(after(used, dx_first[1]), rows, weights, TILE_BACK, count_e=front)
    if one_call:
        x_top, x_low = split_x(after(far_x, dx_stage, grads_w[0]))
        x_top_x = gather_line([x_top], "x")
        x_low_y = gather_line([x_low], "y")
        used = after(used, *p_near)
    for begin in range(front, experts, front):
        grads_w = weight_grads(
            after(used, dx_stage), rows, weights, TILE_BACK, grads_w, False, begin, front
        )

    gres, *mids = pl.pallas_call(
        lambda base_ref, *refs: mid_kernel(
            base_ref,
            refs[0:4],
            *refs[4:9],
            refs[9:13],
            refs[13:17],
            refs[17],
            refs[18:22],
            refs[22:24],
            refs[24],
        ),
        out_shape=[jax.ShapeDtypeStruct((toks, D), f32)]
        + [mix_shape] * 4
        + [jax.ShapeDtypeStruct((2, width, D), bf16)] * 2
        + [jax.ShapeDtypeStruct((8, D), f32)],
        in_specs=[SM] + [VM] * 17,
        out_specs=[VM] * 8,
        compiler_params=params(),
        name="mid",
        cost_estimate=cost(5),
    )(
        after(base, grads_w[0], *((*x_top_x, *x_low_y) if one_call else ())),
        *dx_parts,
        cot,
        resid,
        routes_t,
        gates_t,
        gain_ffn,
        *mixed,
        *w_slots,
    )
    out_keep, out_send, sums = mids[4:]
    grads = to_owner(mids[:4])
    out_other = shift(after(out_send, grads[2]), "c", -1)
    out_sent = total(out_keep[1], out_other[1])
    out_far = shift(out_sent, "y", -1)
    ready = ()
    if one_call:
        ready = (x_top_x[-1], x_low_y[-1])
        x_top = with_line(after_all(x_top_x, gres), "y")
        x_low = with_line(after_all(x_low_y, gres), "x")
        p_other = [shift(after(a[1], *grads), "c", 1) for a in (p_top, p_low)]
    tables = (cosine, sine)
    unit = 8 * x_count * dp_count
    dw_rows = -(-(4 * width + 8) // unit) * unit
    saved = (q, k, v, probs)
    bwd_out = attn_bwd(
        place, x_slots, grads, gain_attn, attn_w, tables, saved, sums, dw_rows
    )
    if one_call:
        bwd_out = after_all(bwd_out, *x_top, *x_low, *p_other)
    gno_keep, gno_send, dw_in, gain_part = bwd_out
    gno_other = shift(gno_send, "c", -1)
    gno_far = (gno_keep[1].astype(f32) + gno_other[1].astype(f32)).astype(bf16)
    gno_near = (gno_keep[0].astype(f32) + gno_other[0].astype(f32)).astype(bf16)

    dw_out = total(out_keep[0], out_other[0], after(out_far, gno_other))
    attn_grads = lax.dynamic_update_slice(dw_in, dw_out, (3 * width, 0))
    y_stage = scatter_cores(after_all((ya, yb), gno_other))
    gno_far = shift(gno_far, "y", -1)

    if one_call:
        x_near = [shift(after(a[0], gain_part), "c", 1) for a in (x_top, x_low)]
        x_other = [shift(after(a[1], gain_part), "c", 1) for a in (x_top, x_low)]
        x_sets = [[*a, n, o] for a, n, o in zip((x_top, x_low), x_near, x_other)]
        p_sets = [[*a, n, o] for a, n, o in zip((p_top, p_low), p_near, p_other)]
        flat, spots = chip_pieces(x_sets, p_sets, len(far), toks)
        part = scatter_sum(after(attn_grads, *x_near, *x_other), "x")
        rows, used = dispatch(after(first, gain_part), flat, spots, toks, experts, cap, len(far))
        used = after(used, part, gno_far, *y_stage)
        part, y_stage = after_tree((part, y_stage), used)
        part = scatter_sum(part, "dp")
        y_stage = scatter_first(*y_stage, half)
        for e in range(min(experts, 3)):
            many = experts - e if e == 2 else 1
            grads_w = weight_grads(used, rows, weights, TILE_FAR, grads_w, True, e, many)
            if e == 0:
                used = after(used, grads_w[0], part, *y_stage[0])
                part = gather_chunks(after(part, used), "dp")
            elif e == 1:
                used = after(used, grads_w[0], part)
                part, y_stage = after_tree((part, y_stage), used)
                attn_grads = gather_chunks(part, "x")
                y_parts = scatter_second(*y_stage)
            elif e == 2:
                attn_grads, *y_parts = after_all((attn_grads, *y_parts), grads_w[0])
                sums = row_sum(attn_grads[4 * width : 4 * width + 4].astype(f32))
    else:
        part = scatter_sum(scatter_sum(attn_grads, "x"), "dp")
        attn_grads = gather_chunks(gather_chunks(part, "dp"), "x")
        sums = row_sum(attn_grads[4 * width : 4 * width + 4].astype(f32))
        y_parts = scatter_second(*scatter_first(*y_stage, half))
        spots = [(nb, ((0, 0, 0, toks),), ((1, 0, 0, toks + TAB),))]

        def next_group(step, carry):
            x_block, p_block, *sums_w = carry
            x_block, p_block = shift(x_block, "dp", 1), shift(p_block, "dp", 1)
            flat = [lax.all_gather(a, ("y", "c", "x")) for a in (x_block, p_block)]
            rows, used = dispatch(first, flat, spots, toks, experts, cap, 1)
            return x_block, p_block, *weight_grads(used, rows, weights, TILE_FAR, sums_w)

        grads_w = lax.fori_loop(1, dp_count, next_group, (norm_two, payload, *grads_w))[2:]
    grad_w_gate, grad_w_up, grad_w_down = grads_w
    grad_w_in = attn_grads[: 3 * width].astype(f32).reshape(3, width, D).transpose(0, 2, 1)
    grad_w_out = attn_grads[3 * width : 4 * width].astype(f32)
    input_grad = pl.pallas_call(
        last_kernel,
        out_shape=jax.ShapeDtypeStruct((toks, D), f32),
        in_specs=[VM] * 5,
        out_specs=VM,
        compiler_params=params(),
        name="last",
        cost_estimate=cost(3),
    )(gno_near, gno_far, x_own, gres, gain_attn)

    block_out, grad_gates = pl.pallas_call(
        lambda base_ref, *refs: out_kernel(base_ref, refs[0:4], *refs[4:]),
        out_shape=[
            jax.ShapeDtypeStruct((toks, D), bf16),
            jax.ShapeDtypeStruct((2, toks), f32),
        ],
        in_specs=[SM] + [VM] * 10,
        out_specs=[VM] * 2,
        compiler_params=params(),
        name="block_out",
        cost_estimate=cost(3),
    )(base, *y_parts, cot, resid, norm_two, routes_t, gates_t, const_vectors)

    return (
        block_out[None],
        input_grad[None],
        sums[3],
        sums[0],
        grad_w_in,
        grad_w_out,
        grad_w_gate,
        grad_w_up,
        grad_w_down,
        sums[1:3],
        grad_gates.T[None],
    )


def solution(mesh):
    dp, row, col = mesh.devices.shape
    fine = Mesh(mesh.devices.reshape(dp, row // 2, 2, col), ("dp", "y", "c", "x"))
    rows = ("y", "c")
    in_specs = (
        P(("dp", "x"), rows, None),
        P(("dp", "x"), rows, None),
        P(),
        P(),
        P(None, None, rows),
        P(rows, None),
        P("x", None, rows),
        P("x", None, rows),
        P("x", rows, None),
        P(),
        P(("dp", "x"), rows, None),
        P("dp", None, None),
        P("dp", None),
        P(("dp", "x"), None),
    )
    out_specs = (
        P(("dp", "x"), rows, None),
        P(("dp", "x"), rows, None),
        P(),
        P(),
        P(None, None, rows),
        P(rows, None),
        P("x", None, rows),
        P("x", None, rows),
        P("x", rows, None),
        P(),
        P(("dp", "x"), rows, None),
    )
    return jax.shard_map(shards, mesh=fine, in_specs=in_specs, out_specs=out_specs, check_vma=False)
```
